32 devices in a mesh: dp: 8 (over y, x, core), tensor: 4 (over z).
Axes of the slice: x: 2, y: 2, z: 4, core: 2. Of those that a mesh axis runs over, the one named last changes fastest.
Arguments:
- x_doc: bfloat16 [2, 8192, 1024], P(None, ('dp', 'tensor')), may hold values from -6 to 6
- x_query: bfloat16 [2, 1024, 1024], P(None, ('dp', 'tensor')), may hold values from -6 to 6
- doc_cot: float32 [2, 8192, 1024], P(None, ('dp', 'tensor')), may hold values from -6 to 6
- query_cot: float32 [2, 1024, 1024], P(None, ('dp', 'tensor')), may hold values from -6 to 6
- lengths: int32 [2, 8, 5], replicated, may hold values from 1 to 512, 1024 in all within a row
- positives: int32 [2, 32], P(None, 'dp'), may hold values from 0 to 31
- w_qkv: bfloat16 [3, 1024, 1024], P(None, 'dp', 'tensor'), may hold values from -0.1875 to 0.1875
- b_qkv: float32 [3, 1024], P(None, 'tensor'), may hold values from -2 to 2
- w_out: bfloat16 [1024, 1024], P('tensor', 'dp'), may hold values from -1.5 to 1.5
- b_out: float32 [1024], replicated, may hold values from -2 to 2
- gain_one: float32 [1024], replicated, may hold values from 0.5 to 1.5
- shift_one: float32 [1024], replicated, may hold values from -2 to 2
- w_in: bfloat16 [1024, 4096], P('dp', 'tensor'), may hold values from -0.1875 to 0.1875
- b_in: float32 [4096], P('tensor'), may hold values from -2 to 2
- w_back: bfloat16 [4096, 1024], P('tensor', 'dp'), may hold values from -0.125 to 0.125
- b_back: float32 [1024], replicated, may hold values from -2 to 2
- gain_two: float32 [1024], replicated, may hold values from 0.5 to 1.5
- shift_two: float32 [1024], replicated, may hold values from -2 to 2
- w_proj: bfloat16 [1024, 128], P('dp'), may hold values from -0.1875 to 0.1875
Outputs:
- y_doc: bfloat16 [2, 8192, 1024], P(None, ('dp', 'tensor'))
- y_query: bfloat16 [2, 1024, 1024], P(None, ('dp', 'tensor'))
- query_loss: float32 [2, 32], P(None, ('dp', 'tensor'))
- grad_x_doc: float32 [2, 8192, 1024], P(None, ('dp', 'tensor'))
- grad_x_query: float32 [2, 1024, 1024], P(None, ('dp', 'tensor'))
- grad_w_qkv: float32 [3, 1024, 1024], P(None, 'dp', 'tensor')
- grad_b_qkv: float32 [3, 1024], P(None, 'tensor')
- grad_w_out: float32 [1024, 1024], P('tensor', 'dp')
- grad_b_out: float32 [1024], replicated
- grad_gain_one: float32 [1024], replicated
- grad_shift_one: float32 [1024], replicated
- grad_w_in: float32 [1024, 4096], P('dp', 'tensor')
- grad_b_in: float32 [4096], P('tensor')
- grad_w_back: float32 [4096, 1024], P('tensor', 'dp')
- grad_b_back: float32 [1024], replicated
- grad_gain_two: float32 [1024], replicated
- grad_shift_two: float32 [1024], replicated
- grad_w_proj: float32 [1024, 128], P('dp')
The draws below stay inside these ranges and needn't reach their ends.
Inputs may be any that keep to these rules, and one draw needn't show every extreme that they name: Entry s < 4 of lengths[m, r] is the length of document s packed in order in document row r of micro-batch m; entry 4 counts the padding tokens at the row's end; each row sums to 1024. positives[m, q] names document n = r * 4 + s (document s of document row r) of micro-batch m; queries are numbered by index of dp, then in order.
All inputs are finite; a program needn't handle non-finite values.
Results may differ from the reference program's by a relative error of at most 0.014.
Values may be sent and summed in bfloat16 or wider, within the bound.
A program may use at most 192 MiB of HBM per device.

```python
import math
import jax
import jax.numpy as jnp
import numpy as np
from jax import lax

D = 1024
HEADS = 16
HEAD_WIDTH = 64
FF = 4096
PROJ = 128
LEN = 1024
SEGS = 4
QLEN = 32
MB = 2
MOST = 512
NQ = 4
QP = 128
DOCS = 8192
QTOK = 1024
NSEG = 32
N_DP = 8


def with_ends(drawn, rng, smallest, largest):
    dims = drawn.shape
    index_at = [jax.random.randint(jax.random.fold_in(rng, axis), (), 0, dims[axis]) for axis in range(len(dims))]
    drawn = drawn.at[tuple(index_at)].set(smallest)
    longest = dims.index(max(dims))
    index_at[longest] = (index_at[longest] + 1) % dims[longest]
    return drawn.at[tuple(index_at)].set(largest)


def block_levels(key, dims, pieces, least, largest):
    def one(dim, shards_of):
        steps = jax.random.uniform(jax.random.fold_in(jax.random.fold_in(key, 6), dim), (shards_of,), jnp.float32, least / len(pieces), largest / len(pieces))
        return jnp.repeat(jnp.exp(steps), dims[dim] // shards_of).reshape((-1,) + (1,) * (len(dims) - dim - 1))

    level = one(*pieces[0])
    for cut in pieces[1:]:
        level = level * one(*cut)
    return level


def split_up(number_of, total, limit, skew):
    loads = [(1 << 20) // math.isqrt(standing ** skew) + 1 for standing in range(2, number_of + 1)]
    surplus, given = total - limit - (number_of - 1), [1] * (number_of - 1)
    while surplus > 0:
        candidates = [i for i in range(number_of - 1) if given[i] < limit]
        whole, budget = sum([loads[i] for i in candidates]), surplus
        for i in candidates:
            addition = min(limit - given[i], max(1, budget * loads[i] // whole), surplus)
            given[i] = given[i] + addition
            surplus = surplus - addition
    return np.array([limit] + given)


def ragged(key, number_of, total, bound, lean):
    if number_of == 2:
        one = jax.random.randint(key, (), max(1, total - bound), min(bound, total - 1) + 1)
        return jnp.stack([one, total - one])
    sizes = jnp.asarray(split_up(number_of, total, bound, lean), jnp.int32)
    twos = (number_of - 1) // 2
    source_of, sink = sizes[1:1 + 2 * twos:2], sizes[2:2 + 2 * twos:2]
    slack = jnp.minimum(source_of - 1, bound - sink)
    shifted = jax.random.randint(jax.random.fold_in(key, 1), (twos,), 0, 1 << 20) % (slack + 1)
    sizes = sizes.at[1:1 + 2 * twos:2].set(source_of - shifted).at[2:2 + 2 * twos:2].set(sink + shifted)
    return sizes[jax.random.permutation(jax.random.fold_in(key, 2), number_of)]


def scatter_about(key, extent, scale, most, cuts=(), kind=jnp.bfloat16):
    entries = jax.random.normal(key, extent, jnp.float32) * scale
    if len(cuts) > 0:
        entries = block_levels(key, extent, cuts, -0.22, 0.18) * entries
    return jnp.clip(entries, min=-most, max=most).astype(kind)


def setup_inputs(seed: int = 0) -> dict:
    splits = jax.random.split(jax.random.key(seed), 20)
    return {
        "x_doc": scatter_about(splits[0], (MB, DOCS, D), 1.0, 6.0, ((1, 32),)),
        "x_query": scatter_about(splits[1], (MB, QTOK, D), 1.0, 6.0, ((1, 32),)),
        "doc_cot": scatter_about(splits[2], (MB, DOCS, D), 1.0, 6.0, ((1, 32),), jnp.float32),
        "query_cot": scatter_about(splits[3], (MB, QTOK, D), 1.0, 6.0, ((1, 32),), jnp.float32),
        "lengths": jax.vmap(lambda own: ragged(own, SEGS + 1, LEN, MOST, 1))(jax.random.split(splits[4], MB * N_DP)).reshape((MB, N_DP, SEGS + 1)).astype(jnp.int32),
        "positives": with_ends(jax.random.randint(splits[5], (MB, N_DP * NQ), 0, N_DP * SEGS), jax.random.fold_in(splits[5], 1), 0, (N_DP * SEGS) - 1).astype(jnp.int32),
        "w_qkv": scatter_about(splits[6], (3, D, D), D ** -0.5, 0.1875, ((1, 8), (2, 4))),
        "b_qkv": scatter_about(splits[7], (3, D), 0.3, 2.0, ((1, 4),), jnp.float32),
        "w_out": scatter_about(splits[8], (D, D), (D // 64) ** -0.5, 1.5, ((0, 4), (1, 8))),
        "b_out": scatter_about(splits[9], (D,), 0.3, 2.0, (), jnp.float32),
        "gain_one": jnp.clip(1.0 + 0.1 * jax.random.normal(splits[10], (D,), jnp.float32), 0.5, 1.5),
        "shift_one": scatter_about(splits[11], (D,), 0.3, 2.0, (), jnp.float32),
        "w_in": scatter_about(splits[12], (D, FF), D ** -0.5, 0.1875, ((0, 8), (1, 4))),
        "b_in": scatter_about(splits[13], (FF,), 0.3, 2.0, ((0, 4),), jnp.float32),
        "w_back": scatter_about(splits[14], (FF, D), (FF // 2) ** -0.5, 0.125, ((0, 4), (1, 8))),
        "b_back": scatter_about(splits[15], (D,), 0.3, 2.0, (), jnp.float32),
        "gain_two": jnp.clip(1.0 + 0.1 * jax.random.normal(splits[16], (D,), jnp.float32), 0.5, 1.5),
        "shift_two": scatter_about(splits[17], (D,), 0.3, 2.0, (), jnp.float32),
        "w_proj": scatter_about(splits[18], (D, PROJ), D ** -0.5, 0.1875, ((0, 8),)),
    }


FULL_PRECISION = lax.Precision.HIGHEST
TAU = 20.0
EPS = 1e-05
LOGIT_SCALE = 2.0
MASKED = -1e+30

@jax.custom_vjp
def low(v):
    return lax.optimization_barrier(v.astype(jnp.bfloat16)).astype(jnp.float32)

@jax.custom_vjp
def reduced_backward(v):
    return v

def low_keep(v):
    return (low(v), None)

def low_pass(kept, grad):
    return (grad,)

def back_keep(v):
    return (v, None)

def back_low(kept, grad):
    return (low(grad),)
low.defvjp(low_keep, low_pass)
reduced_backward.defvjp(back_keep, back_low)

def layer_norm(values, gain, shift):
    center = values - lax.optimization_barrier(jnp.mean(values, axis=-1, keepdims=True))
    spread = lax.optimization_barrier(jnp.mean(center * center, axis=-1, keepdims=True))
    return center * lax.rsqrt(spread + EPS) * gain + shift

def normalize(values):
    return values * lax.rsqrt(lax.optimization_barrier(jnp.sum(values * values, axis=-1, keepdims=True)) + 1e-06)

def rope_angle(position, width):
    half = width // 2
    rates = 10000.0 ** (-(2.0 * jnp.arange(half, dtype=jnp.float32)) / width)
    return position.astype(jnp.float32)[:, None] * rates[None, :]

def rotate(values, angle):
    half = values.shape[-1] // 2
    cosine = jnp.cos(angle)[:, None, :]
    sine = jnp.sin(angle)[:, None, :]
    first = values[..., :half]
    second = values[..., half:]
    return jnp.concatenate([first * cosine - second * sine, second * cosine + first * sine], axis=-1)

def row_layout(sizes, count):
    ends = jnp.cumsum(sizes[:-1]).astype(jnp.int32)
    index = jnp.arange(count, dtype=jnp.int32)
    segment = lax.optimization_barrier(jnp.sum((index[:, None] >= ends[None, :]).astype(jnp.int32), axis=1))
    starts = jnp.concatenate([jnp.zeros((1,), jnp.int32), ends])
    labels = jnp.arange(starts.shape[0], dtype=jnp.int32)
    begin = lax.optimization_barrier(jnp.sum(jnp.where(segment[:, None] == labels[None, :], starts[None, :], 0), axis=1))
    return (segment, index - begin)

def query_losses(totals, counts, positive):
    best = (jnp.log(totals) - jnp.log(counts)[None, :]) / TAU + 1.0
    score = lax.optimization_barrier(jnp.sum(best.reshape(-1, QLEN, best.shape[-1]), axis=1))
    logits = LOGIT_SCALE * score
    labels = jnp.arange(logits.shape[-1], dtype=jnp.int32)
    picked = lax.optimization_barrier(jnp.sum(jnp.where(labels[None, :] == positive[:, None], logits, 0.0), axis=1))
    return jax.nn.logsumexp(logits, axis=-1) - picked

def attend(query_matrix, key, value_matrix, labels):
    attention_scores = reduced_backward(jnp.einsum('fio,uio->ifu', query_matrix, key, precision=FULL_PRECISION) * HEAD_WIDTH ** (-0.5))
    same = labels[:, None] == labels[None, :]
    probabilities = low(jax.nn.softmax(jnp.where(same[None], attention_scores, MASKED), axis=-1))
    return jnp.einsum('evg,geb->veb', probabilities, value_matrix, precision=FULL_PRECISION)

def block(attention_weights, rows_in, doc_labels, query_labels, places):
    w_qkv, b_qkv, w_out, b_out, gain_one, shift_one, w_in, b_in, w_back, b_back, gain_two, shift_two = attention_weights
    count = rows_in.shape[0]
    angle = rope_angle(places, HEAD_WIDTH)
    projected = [jnp.dot(rows_in, w_qkv[index], precision=FULL_PRECISION) + b_qkv[index] for index in range(3)]
    query_matrix = low(rotate(reduced_backward(projected[0]).reshape(count, HEADS, HEAD_WIDTH), angle))
    key = low(rotate(reduced_backward(projected[1]).reshape(count, HEADS, HEAD_WIDTH), angle))
    value_matrix = reduced_backward(low(projected[2])).reshape(count, HEADS, HEAD_WIDTH)
    mixed_heads = jnp.concatenate([attend(query_matrix[:LEN], key[:LEN], value_matrix[:LEN], doc_labels), attend(query_matrix[LEN:], key[LEN:], value_matrix[LEN:], query_labels)], axis=0)
    mixed_heads = reduced_backward(low(mixed_heads.reshape(count, HEADS * HEAD_WIDTH)))
    branch = reduced_backward(jnp.dot(mixed_heads, w_out, precision=FULL_PRECISION) + b_out)
    normed = layer_norm(rows_in + branch, gain_one, shift_one)
    inner = reduced_backward(jnp.dot(low(normed), w_in, precision=FULL_PRECISION) + b_in)
    active = low(jax.nn.gelu(inner, approximate=False))
    update = reduced_backward(jnp.dot(active, w_back, precision=FULL_PRECISION) + b_back)
    return layer_norm(normed + update, gain_two, shift_two)

def project(values, w_proj):
    return low(normalize(reduced_backward(jnp.einsum('rld,dp->rlp', low(values), w_proj, precision=FULL_PRECISION))))

def query_totals(query_vecs, doc_vecs, member):
    cosines = reduced_backward(jnp.einsum('qp,rlp->qrl', query_vecs, doc_vecs, precision=FULL_PRECISION))
    return jnp.einsum('qrl,rls->qrs', jnp.exp(TAU * (cosines - 1.0)), member, precision=FULL_PRECISION)

def reference(x_doc, x_query, doc_cot, query_cot, lengths, positives, w_qkv, b_qkv, w_out, b_out, gain_one, shift_one, w_in, b_in, w_back, b_back, gain_two, shift_two, w_proj):
    params = tuple((item.astype(jnp.float32) for item in (w_qkv, b_qkv, w_out, b_out, gain_one, shift_one, w_in, b_in, w_back, b_back, gain_two, shift_two, w_proj)))
    query_index = jnp.arange(QP, dtype=jnp.int32)
    query_labels = query_index // QLEN
    query_places = query_index % QLEN
    seg_labels = jnp.arange(SEGS, dtype=jnp.int32)
    doc_outs, query_outs, loss_rows, doc_grads, query_grads = ([], [], [], [], [])
    totals_grad = None
    for step in range(MB):
        doc_labels, doc_places = jax.vmap(lambda sizes: row_layout(sizes, LEN))(lengths[step])
        member = (doc_labels[:, :, None] == seg_labels[None, None, :]).astype(jnp.float32)
        counts = lengths[step][:, :SEGS].reshape(-1).astype(jnp.float32)
        picks = positives[step].reshape(N_DP, NQ)

        def forward(attention_weights, docs_in, queries_in):

            def one_row(pack):
                rows_in, labels_row, places_row = pack
                return block(attention_weights[:12], rows_in, labels_row, query_labels, jnp.concatenate([places_row, query_places]))
            rows = jnp.concatenate([docs_in, queries_in], axis=1)
            outs = lax.map(jax.checkpoint(one_row), (rows, doc_labels, doc_places))
            doc_out = outs[:, :LEN]
            query_out = outs[:, LEN:]
            doc_vecs = project(doc_out, attention_weights[12])
            query_vecs = project(query_out, attention_weights[12])

            def one_group(pack):
                vecs, pick = pack
                totals = query_totals(vecs, doc_vecs, member).reshape(QP, NSEG)
                return query_losses(totals, counts, pick)
            losses = lax.map(jax.checkpoint(one_group), (query_vecs, picks))
            return (doc_out, query_out, losses.reshape(-1))
        docs_in = x_doc[step].reshape(N_DP, LEN, D).astype(jnp.float32)
        queries_in = x_query[step].reshape(N_DP, QP, D).astype(jnp.float32)
        (doc_out, query_out, losses), pull = jax.vjp(forward, params, docs_in, queries_in)
        grads, doc_grad, query_grad = pull((doc_cot[step].reshape(N_DP, LEN, D).astype(jnp.float32), query_cot[step].reshape(N_DP, QP, D).astype(jnp.float32), jnp.ones_like(losses)))
        totals_grad = grads if totals_grad is None else jax.tree.map(lambda left, right: left + right, totals_grad, grads)
        doc_outs.append(doc_out.reshape(DOCS, D).astype(jnp.bfloat16))
        query_outs.append(query_out.reshape(QTOK, D).astype(jnp.bfloat16))
        loss_rows.append(losses)
        doc_grads.append(doc_grad.reshape(DOCS, D))
        query_grads.append(query_grad.reshape(QTOK, D))
    return (jnp.stack(doc_outs), jnp.stack(query_outs), jnp.stack(loss_rows), jnp.stack(doc_grads), jnp.stack(query_grads), totals_grad[0], totals_grad[1], totals_grad[2], totals_grad[3], totals_grad[4], totals_grad[5], totals_grad[6], totals_grad[7], totals_grad[8], totals_grad[9], totals_grad[10], totals_grad[11], totals_grad[12])
```

```python
import functools

import jax
import jax.numpy as jnp
from jax import lax
from jax.experimental import pallas as pl
from jax.experimental.pallas import tpu as pltpu
from jax.sharding import PartitionSpec as P

HEAD_WIDTH = 64
QLEN = 32
FULL_PRECISION = lax.Precision.HIGHEST
TAU = 20.0
EPS = 1e-05
LOGIT_SCALE = 2.0
MASKED = -1e30
AXES = ("dp", "tensor")
BF = jnp.bfloat16
F32 = jnp.float32


def layer_norm(values, gain, shift):
    center = values - jnp.mean(values, axis=-1, keepdims=True)
    spread = jnp.mean(center * center, axis=-1, keepdims=True)
    return center * lax.rsqrt(spread + EPS) * gain + shift


def normalize(values):
    return values * lax.rsqrt(jnp.sum(values * values, axis=-1, keepdims=True) + 1e-06)


def gelu_exact(values):
    return jax.nn.gelu(values, approximate=False)


def dot_nn(a, b):
    return lax.dot_general(a, b, (((1,), (0,)), ((), ())), preferred_element_type=F32)


def dot_nt(a, b):
    return lax.dot_general(a, b, (((1,), (1,)), ((), ())), preferred_element_type=F32)


def dot_tn(a, b):
    return lax.dot_general(a, b, (((0,), (0,)), ((), ())), preferred_element_type=F32)


def half_turn(values):
    lane = lax.broadcasted_iota(jnp.int32, values.shape, 1)
    ahead = jnp.roll(values, -32, axis=1)
    behind = jnp.roll(values, 32, axis=1)
    return jnp.where(lane % HEAD_WIDTH < 32, -ahead, behind)


def attention_forward(q, k_own, v_own, k_far, v_far, col_labels, own_labels, far_labels, docs):
    rows, width = q.shape
    far = k_far.shape[0]
    block = 128
    asked = rows - docs

    def kernel(q_ref, ko_ref, vo_ref, kf_ref, vf_ref, lc_ref, lo_ref, lf_ref, o_ref):
        lane = lax.broadcasted_iota(jnp.int32, (1, 128), 1)

        def part(start, size, keys, sames):
            q_block = q_ref[pl.ds(start, size), :]
            outs = []
            for head in range(2):
                mask = (lane // HEAD_WIDTH) == head
                q_head = jnp.where(mask, q_block, jnp.zeros_like(q_block))
                scores = [
                    jnp.where(same, dot_nt(q_head, key), MASKED)
                    for (key, _), same in zip(keys, sames)
                ]
                top = functools.reduce(
                    jnp.maximum, [jnp.max(s, axis=-1, keepdims=True) for s in scores]
                )
                powers = [jnp.exp(s - top) for s in scores]
                total = functools.reduce(
                    jnp.add, [jnp.sum(p, axis=-1, keepdims=True) for p in powers]
                )
                mixed = functools.reduce(
                    jnp.add, [dot_nn(p.astype(BF), value) for p, (_, value) in zip(powers, keys)]
                )
                outs.append(mixed * (1.0 / total))
            o_ref[pl.ds(start, size), :] = jnp.where(lane < HEAD_WIDTH, outs[0], outs[1]).astype(BF)

        doc_keys = [
            (ko_ref[:docs, :], vo_ref[:docs, :]),
            (kf_ref[...], vf_ref[...]),
        ]
        for at in range(docs // block):
            labels = lc_ref[pl.ds(at * block, block), :]
            part(at * block, block, doc_keys, [labels == lo_ref[...], labels == lf_ref[...]])
        row = lax.broadcasted_iota(jnp.int32, (asked, asked), 0) // QLEN
        col = lax.broadcasted_iota(jnp.int32, (asked, asked), 1) // QLEN
        part(docs, asked, [(ko_ref[docs:, :], vo_ref[docs:, :])], [row == col])

    head_block = lambda n: pl.BlockSpec((n, 128), lambda h: (0, h))
    whole = lambda shape: pl.BlockSpec(shape, lambda h: (0, 0))
    return pl.pallas_call(
        kernel,
        grid=(width // 128,),
        in_specs=[
            head_block(rows),
            head_block(rows),
            head_block(rows),
            head_block(far),
            head_block(far),
            whole((docs, 1)),
            whole((1, docs)),
            whole((1, far)),
        ],
        out_specs=head_block(rows),
        out_shape=jax.ShapeDtypeStruct((rows, width), BF),
        compiler_params=pltpu.CompilerParams(vmem_limit_bytes=40 << 20),
        name="attend_forward",
        cost_estimate=pl.CostEstimate(
            flops=4 * rows * 2 * docs * width,
            bytes_accessed=2 * (4 * rows + 2 * far) * width,
            transcendentals=rows * 2 * docs * width // 64,
        ),
    )(q, k_own, v_own, k_far, v_far, col_labels, own_labels, far_labels)


def attention_backward(
    q, k_own, v_own, k_far, v_far, grad, col_labels, own_labels, far_labels, docs
):
    rows, width = q.shape
    far = k_far.shape[0]
    block = 128
    asked = rows - docs

    def kernel(
        q_ref, ko_ref, vo_ref, kf_ref, vf_ref, g_ref, lc_ref, lo_ref, lf_ref,
        dq_ref, dko_ref, dvo_ref, dkf_ref, dvf_ref, sums_own, sums_far,
    ):
        lane = lax.broadcasted_iota(jnp.int32, (1, 128), 1)
        sums_own[...] = jnp.zeros_like(sums_own)
        sums_far[...] = jnp.zeros_like(sums_far)

        def part(start, size, keys, sames, sums):
            q_block = q_ref[pl.ds(start, size), :]
            g_block = g_ref[pl.ds(start, size), :]
            grads = []
            for head in range(2):
                mask = (lane // HEAD_WIDTH) == head
                q_head = jnp.where(mask, q_block, jnp.zeros_like(q_block))
                g_head = jnp.where(mask, g_block, jnp.zeros_like(g_block))
                scores = [
                    jnp.where(same, dot_nt(q_head, key), MASKED)
                    for (key, _), same in zip(keys, sames)
                ]
                top = functools.reduce(
                    jnp.maximum, [jnp.max(s, axis=-1, keepdims=True) for s in scores]
                )
                powers = [jnp.exp(s - top) for s in scores]
                total = functools.reduce(
                    jnp.add, [jnp.sum(p, axis=-1, keepdims=True) for p in powers]
                )
                inverse = 1.0 / total
                g_head = (g_head.astype(F32) * inverse).astype(BF)
                pulls = [dot_nt(g_head, value) for _, value in keys]
                mean = functools.reduce(
                    jnp.add,
                    [jnp.sum(p * d, axis=-1, keepdims=True) for p, d in zip(powers, pulls)],
                ) * inverse
                turned = [(p * (d - mean)).astype(BF) for p, d in zip(powers, pulls)]
                got = functools.reduce(
                    jnp.add, [dot_nn(s, key) for s, (key, _) in zip(turned, keys)]
                )
                grads.append(got * 0.125)
                for (ref, first, count), s, p in zip(sums, turned, powers):
                    ref[0, pl.ds(first, count), :] += dot_tn(s, q_head)
                    ref[1, pl.ds(first, count), :] += dot_tn(p.astype(BF), g_head)
            dq_ref[pl.ds(start, size), :] = jnp.where(lane < HEAD_WIDTH, grads[0], grads[1])

        doc_keys = [
            (ko_ref[:docs, :], vo_ref[:docs, :]),
            (kf_ref[...], vf_ref[...]),
        ]
        for at in range(docs // block):
            labels = lc_ref[pl.ds(at * block, block), :]
            part(
                at * block,
                block,
                doc_keys,
                [labels == lo_ref[...], labels == lf_ref[...]],
                [(sums_own, 0, docs), (sums_far, 0, far)],
            )
        row = lax.broadcasted_iota(jnp.int32, (asked, asked), 0) // QLEN
        col = lax.broadcasted_iota(jnp.int32, (asked, asked), 1) // QLEN
        part(
            docs,
            asked,
            [(ko_ref[docs:, :], vo_ref[docs:, :])],
            [row == col],
            [(sums_own, docs, asked)],
        )
        dko_ref[...] = sums_own[0]
        dvo_ref[...] = sums_own[1]
        dkf_ref[...] = sums_far[0].astype(BF)
        dvf_ref[...] = sums_far[1].astype(BF)

    head_block = lambda n: pl.BlockSpec((n, 128), lambda h: (0, h))
    whole = lambda shape: pl.BlockSpec(shape, lambda h: (0, 0))
    return pl.pallas_call(
        kernel,
        grid=(width // 128,),
        in_specs=[
            head_block(rows),
            head_block(rows),
            head_block(rows),
            head_block(far),
            head_block(far),
            head_block(rows),
            whole((docs, 1)),
            whole((1, docs)),
            whole((1, far)),
        ],
        out_specs=[
            head_block(rows),
            head_block(rows),
            head_block(rows),
            head_block(far),
            head_block(far),
        ],
        out_shape=[
            jax.ShapeDtypeStruct((rows, width), F32),
            jax.ShapeDtypeStruct((rows, width), F32),
            jax.ShapeDtypeStruct((rows, width), F32),
            jax.ShapeDtypeStruct((far, width), BF),
            jax.ShapeDtypeStruct((far, width), BF),
        ],
        scratch_shapes=[pltpu.VMEM((2, rows, 128), F32), pltpu.VMEM((2, far, 128), F32)],
        compiler_params=pltpu.CompilerParams(vmem_limit_bytes=40 << 20),
        name="attend_backward",
        cost_estimate=pl.CostEstimate(
            flops=10 * rows * 2 * docs * width,
            bytes_accessed=4 * (6 * rows + 4 * far) * width,
            transcendentals=rows * 2 * docs * width // 64,
        ),
    )(q, k_own, v_own, k_far, v_far, grad, col_labels, own_labels, far_labels)


def body(
    x_doc,
    x_query,
    doc_cot,
    query_cot,
    lengths,
    positives,
    w_qkv,
    b_qkv,
    w_out,
    b_out,
    gain_one,
    shift_one,
    w_in,
    b_in,
    w_back,
    b_back,
    gain_two,
    shift_two,
    w_proj,
):
    ways = lax.axis_size("tensor")
    groups = lax.axis_size("dp")
    column = lax.axis_index("tensor")
    rank = lax.axis_index("dp")
    core = rank % 2
    chip = rank // 2
    chips = groups // 2
    micro, quarter, width = x_doc.shape
    asked = x_query.shape[1]
    segments = lengths.shape[2] - 1
    proj_width = w_proj.shape[1]
    heads_local = w_qkv.shape[2]
    units_local = w_in.shape[1]
    block = width // groups
    assert ways == 2 * micro and ways == 4

    def exchange(value, dr=0, dt=0):
        pairs = [
            (r * ways + t, (r ^ dr) * ways + (t ^ dt)) for r in range(groups) for t in range(ways)
        ]
        return lax.ppermute(value, AXES, pairs)

    chip_bits = []
    bit = 2
    while bit < groups:
        chip_bits.append(bit)
        bit *= 2

    def gather_weights(pack, reverse):
        pieces = [pack] + [exchange(pack, dt=j) for j in range(1, ways)]
        pieces = [(0, jnp.concatenate(pieces, axis=-1))]
        order = chip_bits[::-1] if reverse and len(chip_bits) == 2 else chip_bits
        for dr in order:
            pieces = pieces + [(j + dr // 2, exchange(p, dr=dr)) for j, p in pieces]
            if len(pieces) >= 4 or dr == order[-1]:
                pieces.sort(key=lambda item: item[0])
                pieces = [(0, jnp.concatenate([p for _, p in pieces], axis=-2))]
        (_, half), = pieces
        return jnp.concatenate([half, exchange(half, dr=1)], axis=-2)

    def gather_proj(pack):
        for dr in chip_bits + [1]:
            pack = jnp.concatenate([pack, exchange(pack, dr=dr)], axis=0)
        return pack

    unit_micro = column // 2
    unit_row = chip * 2 + column % 2

    def rows_in(docs, queries):
        blocks = jnp.concatenate([docs, queries], axis=1)
        got = []
        for j in range(2):
            send = jnp.where((column + j) % 2 == 0, blocks[0], blocks[1])
            pairs = []
            for r in range(groups):
                for t in range(ways):
                    m = (t + j) % 2
                    pairs.append(
                        (r * ways + t, ((r // 2) * 2 + t // 2) * ways + 2 * m + r % 2)
                    )
            got.append(lax.ppermute(send, AXES, pairs))
        first = jnp.where(unit_micro == 0, got[0], got[1])
        second = jnp.where(unit_micro == 0, got[1], got[0])
        return jnp.concatenate(
            [first[:quarter], second[:quarter], first[quarter:], second[quarter:]], axis=0
        )

    def quarters_out(first, second):
        got = []
        for j in range(2):
            send = jnp.where((unit_micro + j) % 2 == 0, first, second)
            pairs = []
            for r in range(groups):
                for t in range(ways):
                    m = t // 2
                    pairs.append(
                        (
                            r * ways + t,
                            ((r // 2) * 2 + t % 2) * ways + 2 * (r % 2) + (m + j) % 2,
                        )
                    )
            got.append(lax.ppermute(send, AXES, pairs))
        even = jnp.where(column % 2 == 0, got[0], got[1])
        odd = jnp.where(column % 2 == 0, got[1], got[0])
        return jnp.stack([even, odd])

    def rows_out(values):
        docs = 2 * quarter
        first = jnp.concatenate([values[:quarter], values[docs : docs + asked]], axis=0)
        second = jnp.concatenate([values[quarter:docs], values[docs + asked :]], axis=0)
        blocks = quarters_out(first, second)
        return blocks[:, :quarter], blocks[:, quarter:]

    place = jnp.arange(width, dtype=jnp.int32)
    step = place // block
    actual = (rank ^ (2 * (step % chips) + step // chips)) * block + place % block
    turn = (place[:, None] == actual[None, :]).astype(BF)

    pack_one = jnp.stack([w_qkv[0], w_qkv[1]])
    pack_two = jnp.stack([w_qkv[2], w_out.T])
    full_qk = gather_weights(pack_one, False)
    full_vo = gather_weights(pack_two, True)
    bias_pack = jnp.concatenate([b_qkv.reshape(-1), b_in])[None]
    biases = [bias_pack] + [exchange(bias_pack, dt=j) for j in range(1, ways)]
    bias_qkv = jnp.concatenate(
        [b[0, : 3 * heads_local].reshape(3, heads_local) for b in biases], axis=1
    )
    bias_in = jnp.concatenate([b[0, 3 * heads_local :] for b in biases])
    own_x = rows_in(x_doc, x_query)
    own_cot = rows_in(doc_cot.astype(BF), query_cot.astype(BF))
    full_in = gather_weights(w_in, False)
    full_back = gather_weights(w_back.T, True)
    full_proj = gather_proj(w_proj)
    params = jnp.stack(
        [b_out, gain_one, shift_one, b_back, gain_two, shift_two, b_out, b_out]
    )
    params = jnp.dot(params, turn.astype(F32), precision=FULL_PRECISION)
    b_out, gain_one, shift_one, b_back, gain_two, shift_two = [params[i] for i in range(6)]

    docs = 2 * quarter
    queries = 2 * asked
    rows = docs + queries
    sizes_all = lengths[unit_micro]
    sizes = sizes_all[unit_row]
    ends = jnp.cumsum(sizes[:-1])
    starts = jnp.concatenate([jnp.zeros((1,), jnp.int32), ends])

    def layout(first):
        index = first + jnp.arange(docs, dtype=jnp.int32)
        segment = jnp.sum((index[:, None] >= ends[None, :]).astype(jnp.int32), axis=1)
        labels = jnp.arange(starts.shape[0], dtype=jnp.int32)
        begin = jnp.sum(
            jnp.where(segment[:, None] == labels[None, :], starts[None, :], 0), axis=1
        )
        return segment, index - begin

    own_labels, own_places = layout(core * docs)
    far_labels, _ = layout((1 - core) * docs)
    places = jnp.concatenate([own_places, jnp.arange(queries, dtype=jnp.int32) % QLEN])
    half = HEAD_WIDTH // 2
    rates = 10000.0 ** (-(2.0 * jnp.arange(half, dtype=F32)) / HEAD_WIDTH)
    angle = places.astype(F32)[:, None] * rates[None, :]
    cosine = jnp.tile(jnp.cos(angle), (1, width // half))
    sine = jnp.tile(jnp.sin(angle), (1, width // half))

    x_low = dot_nn(own_x, turn).astype(BF)
    parts = [
        dot_nn(x_low, full_qk[0]) + bias_qkv[0],
        dot_nn(x_low, full_qk[1]) + bias_qkv[1],
        dot_nn(x_low, full_vo[0]) + bias_qkv[2],
    ]
    q_rot = (parts[0] * cosine + half_turn(parts[0]) * sine).astype(BF) * 0.125
    k_rot = (parts[1] * cosine + half_turn(parts[1]) * sine).astype(BF)
    v_low = parts[2].astype(BF)
    k_far = exchange(k_rot[:docs], dr=1)
    v_far = exchange(v_low[:docs], dr=1)
    label_args = (own_labels[:, None], own_labels[None, :], far_labels[None, :], docs)
    mixed = attention_forward(q_rot, k_rot, v_low, k_far, v_far, *label_args)
    branch = dot_nt(mixed, full_vo[1])
    resid_one = x_low.astype(F32) + branch + b_out
    normed, norm_one_pull = jax.vjp(layer_norm, resid_one, gain_one, shift_one)
    normed_low = normed.astype(BF)
    inner = dot_nn(normed_low, full_in) + bias_in
    active, gelu_pull = jax.vjp(gelu_exact, inner)
    active_low = active.astype(BF)
    resid_two = normed + dot_nt(active_low, full_back) + b_back
    output, norm_two_pull = jax.vjp(layer_norm, resid_two, gain_two, shift_two)
    output_low = output.astype(BF)
    y_doc, y_query = rows_out(dot_nt(output_low, turn).astype(BF))
    projection = dot_nn(output_low, full_proj)
    unit, unit_pull = jax.vjp(normalize, projection)
    unit_low = unit.astype(BF)

    doc_unit = unit_low[:docs]
    query_unit = unit_low[docs:]

    def bit_of(dr, dt):
        return (rank // dr) % 2 == 1 if dr else (column // dt) % 2 == 1

    def join(value, dr, dt, axis=0):
        got = exchange(value, dr=dr, dt=dt)
        on = bit_of(dr, dt)
        low = jnp.where(on, got, value)
        high = jnp.where(on, value, got)
        return jnp.concatenate([low, high], axis=axis)

    def split_sum(value, dr, dt):
        on = bit_of(dr, dt)
        size = value.shape[0] // 2
        send = jnp.where(on, value[:size], value[size:])
        keep = jnp.where(on, value[size:], value[:size])
        return keep + exchange(send.astype(BF), dr=dr, dt=dt).astype(F32)

    steps = [(1, 0), (0, 1)] + [(dr, 0) for dr in chip_bits]
    all_queries = query_unit
    for dr, dt in steps:
        all_queries = join(all_queries, dr, dt)
    picks = jnp.where(unit_micro == 0, positives[0], positives[1])[None]
    picks = join(picks, 1, 0)
    for dr in chip_bits:
        picks = join(picks, dr, 0)
    picks = picks.reshape(-1)
    seg_labels = jnp.arange(segments, dtype=jnp.int32)
    member = (own_labels[:, None] == seg_labels[None, :]).astype(F32)
    cosines = dot_nt(doc_unit, all_queries)
    weight = jnp.exp(TAU * (cosines - 1.0))
    totals = jnp.einsum("js,ji->si", member, weight, precision=FULL_PRECISION)
    totals = totals + exchange(totals, dr=1)
    for dr, dt in steps[1:]:
        totals = join(totals, dr, dt)
    counts = sizes_all[:, :segments].reshape(-1).astype(F32)
    best = (jnp.log(totals) - jnp.log(counts)[:, None]) / TAU + 1.0
    score = jnp.sum(best.reshape(best.shape[0], -1, QLEN), axis=-1)
    logits = LOGIT_SCALE * score
    documents = jnp.arange(logits.shape[0], dtype=jnp.int32)
    chosen = (documents[:, None] == picks[None, :]).astype(F32)
    peak = jnp.max(logits, axis=0, keepdims=True)
    powers = jnp.exp(logits - peak)
    mass = jnp.sum(powers, axis=0, keepdims=True)
    losses = (peak + jnp.log(mass))[0] - jnp.sum(chosen * logits, axis=0)
    logit_grad = LOGIT_SCALE * (powers / mass - chosen)
    own_grad = lax.dynamic_slice_in_dim(logit_grad, unit_row * segments, segments, axis=0)
    own_total = lax.dynamic_slice_in_dim(totals, unit_row * segments, segments, axis=0)
    coef = jnp.repeat(own_grad, QLEN, axis=1) / own_total
    spread = jnp.einsum("js,si->ji", member, coef, precision=FULL_PRECISION)
    cosine_grad = (weight * spread).astype(BF)
    doc_grad = dot_nn(cosine_grad, all_queries)
    query_grad = dot_tn(cosine_grad, doc_unit)
    for dr, dt in steps[::-1]:
        query_grad = split_sum(query_grad, dr, dt)
    own_losses = lax.dynamic_slice_in_dim(losses, unit_row * (4 * asked // QLEN) + core * 2 * (asked // QLEN), 2 * (asked // QLEN))
    per = asked // QLEN
    loss_tiles = [
        jnp.broadcast_to(own_losses[i * per : (i + 1) * per, None], (per, 128)) for i in range(2)
    ]
    loss_out = quarters_out(loss_tiles[0], loss_tiles[1])[:, :, 0]

    def reduce_weights(left, right, reverse):
        size = left.shape[1] // 2
        send = dot_tn(left[:, size:], right).astype(BF)
        got = exchange(send, dr=1)
        keep = dot_tn(left[:, :size], right) + got.astype(F32)
        order = chip_bits if reverse and len(chip_bits) == 2 else chip_bits[::-1]
        left_bits = sorted(chip_bits)
        for dr in order:
            at = left_bits.index(dr)
            inner_rows = block << at
            view = keep.reshape(-1, 2, inner_rows, keep.shape[-1])
            send = view[:, 1].reshape(-1, keep.shape[-1]).astype(BF)
            stay = view[:, 0].reshape(-1, keep.shape[-1])
            keep = stay + exchange(send, dr=dr).astype(F32)
            left_bits.remove(dr)
        size = keep.shape[1] // ways
        total = keep[:, :size]
        low = keep.astype(BF)
        for j in range(1, ways):
            total = total + exchange(low[:, j * size : (j + 1) * size], dt=j).astype(F32)
        return total

    unit_grad = jnp.concatenate([doc_grad, query_grad], axis=0)
    (proj_grad,) = unit_pull(unit_grad)
    proj_low = proj_grad.astype(BF)
    out_grad = own_cot_turned = dot_nn(own_cot, turn) + dot_nt(proj_low, full_proj)
    resid_two_grad, gain_two_grad, shift_two_grad = norm_two_pull(out_grad)
    update_low = resid_two_grad.astype(BF)
    active_grad = dot_nn(update_low, full_back)
    (inner_grad,) = gelu_pull(active_grad)
    inner_low = inner_grad.astype(BF)
    out_back = reduce_weights(update_low, active_low, True)
    out_in = reduce_weights(normed_low, inner_low, False)
    normed_grad = dot_nt(inner_low, full_in) + resid_two_grad
    resid_one_grad, gain_one_grad, shift_one_grad = norm_one_pull(normed_grad)
    branch_low = resid_one_grad.astype(BF)
    mixed_grad = dot_nn(branch_low, full_vo[1]).astype(BF)
    out_out = reduce_weights(branch_low, mixed, True)
    q_grad, k_grad, v_grad, k_give, v_give = attention_backward(
        q_rot, k_rot, v_low, k_far, v_far, mixed_grad, *label_args
    )
    pad = jnp.zeros((queries, width), F32)
    k_grad = k_grad + jnp.concatenate([exchange(k_give, dr=1).astype(F32), pad], axis=0)
    v_grad = v_grad + jnp.concatenate([exchange(v_give, dr=1).astype(F32), pad], axis=0)
    pre_low = [
        (q_grad * cosine - half_turn(q_grad) * sine).astype(BF),
        (k_grad * cosine - half_turn(k_grad) * sine).astype(BF),
        v_grad.astype(BF),
    ]
    out_qkv = jnp.stack(
        [reduce_weights(x_low, pre_low[i], i == 2) for i in range(3)]
    )
    x_grad = (
        resid_one_grad
        + dot_nt(pre_low[0], full_qk[0])
        + dot_nt(pre_low[1], full_qk[1])
        + dot_nt(pre_low[2], full_vo[0])
    )
    gx_doc, gx_query = rows_out(dot_nt(x_grad.astype(BF), turn).astype(BF))

    grad_proj = dot_tn(output_low, proj_low)
    for dr in [1] + chip_bits[::-1]:
        size = grad_proj.shape[0] // 2
        got = exchange(grad_proj[size:].astype(BF), dr=dr)
        grad_proj = grad_proj[:size] + got.astype(F32)
    for dt in (1, 2):
        grad_proj = grad_proj + exchange(grad_proj, dt=dt)

    vectors = jnp.stack(
        [
            jnp.sum(branch_low.astype(F32), axis=0),
            gain_one_grad,
            shift_one_grad,
            jnp.sum(update_low.astype(F32), axis=0),
            gain_two_grad,
            shift_two_grad,
        ]
    )
    vectors = lax.dot_general(
        vectors, turn.astype(F32), (((1,), (1,)), ((), ())), precision=FULL_PRECISION
    )
    tensor_grads = jnp.concatenate(
        [
            jnp.sum(item.astype(F32), axis=0).reshape(ways, heads_local) for item in pre_low
        ]
        + [jnp.sum(inner_low.astype(F32), axis=0).reshape(ways, units_local)],
        axis=1,
    )
    for dt in (2, 1):
        tensor_grads = tensor_grads[:dt] + exchange(tensor_grads[dt:], dt=dt)
        vectors = vectors + exchange(vectors, dt=dt)
    for dr in [1] + chip_bits:
        tensor_grads = tensor_grads + exchange(tensor_grads, dr=dr)
        vectors = vectors + exchange(vectors, dr=dr)
    tensor_grads = tensor_grads[0]
    return (
        y_doc,
        y_query,
        loss_out,
        gx_doc.astype(F32),
        gx_query.astype(F32),
        out_qkv,
        tensor_grads[: 3 * heads_local].reshape(3, heads_local),
        out_out.T,
        vectors[0],
        vectors[1],
        vectors[2],
        out_in,
        tensor_grads[3 * heads_local :],
        out_back.T,
        vectors[3],
        vectors[4],
        vectors[5],
        grad_proj,
    )


def solution(mesh):
    rows = P(None, ("dp", "tensor"), None)
    in_specs = (
        rows,
        rows,
        rows,
        rows,
        P(),
        P(None, "dp"),
        P(None, "dp", "tensor"),
        P(None, "tensor"),
        P("tensor", "dp"),
        P(),
        P(),
        P(),
        P("dp", "tensor"),
        P("tensor"),
        P("tensor", "dp"),
        P(),
        P(),
        P(),
        P("dp", None),
    )
    out_specs = (
        rows,
        rows,
        P(None, ("dp", "tensor")),
        rows,
        rows,
        P(None, "dp", "tensor"),
        P(None, "tensor"),
        P("tensor", "dp"),
        P(),
        P(),
        P(),
        P("dp", "tensor"),
        P("tensor"),
        P("tensor", "dp"),
        P(),
        P(),
        P(),
        P("dp", None),
    )
    return jax.shard_map(body, mesh=mesh, in_specs=in_specs, out_specs=out_specs, check_vma=False)
```

```python
import functools

import jax
import jax.numpy as jnp
from jax import lax
from jax.experimental import pallas as pl
from jax.experimental.pallas import tpu as pltpu
from jax.sharding import PartitionSpec as P

HEAD_WIDTH = 64
QLEN = 32
FULL_PRECISION = lax.Precision.HIGHEST
TAU = 20.0
EPS = 1e-05
LOGIT_SCALE = 2.0
MASKED = -1e30
AXES = ("dp", "tensor")
MESH = pl.DeviceIdType.MESH
BF = jnp.bfloat16
F32 = jnp.float32


def layer_norm(values, gain, shift):
    center = values - jnp.mean(values, axis=-1, keepdims=True)
    spread = jnp.mean(center * center, axis=-1, keepdims=True)
    return center * lax.rsqrt(spread + EPS) * gain + shift


def normalize(values):
    return values * lax.rsqrt(jnp.sum(values * values, axis=-1, keepdims=True) + 1e-06)


def gelu_exact(values):
    return jax.nn.gelu(values, approximate=False)


def dot_nn(a, b):
    return lax.dot_general(a, b, (((1,), (0,)), ((), ())), preferred_element_type=F32)


def dot_nt(a, b):
    return lax.dot_general(a, b, (((1,), (1,)), ((), ())), preferred_element_type=F32)


def dot_tn(a, b):
    return lax.dot_general(a, b, (((0,), (0,)), ((), ())), preferred_element_type=F32)


def turned(values):
    lane = lax.broadcasted_iota(jnp.int32, (1, 128), 1)
    ahead = pltpu.roll(values, 96, 1)
    behind = pltpu.roll(values, 32, 1)
    return jnp.where(lane % HEAD_WIDTH < HEAD_WIDTH // 2, ahead, behind)


def project_heads(x, weights, bias, cosine, sine):
    rows, width = x.shape
    columns = 256

    def kernel(x_ref, w_ref, b_ref, c_ref, s_ref, o_ref):
        got = dot_nn(x_ref[...], w_ref[0]) + b_ref[0]
        for at in range(0, columns, 128):
            piece = got[:, at : at + 128]
            o_ref[0, :, at : at + 128] = (piece * c_ref[0] + turned(piece) * s_ref[0]).astype(BF)

    return pl.pallas_call(
        kernel,
        grid=(3, width // columns),
        in_specs=[
            pl.BlockSpec((rows, width), lambda j, n: (0, 0)),
            pl.BlockSpec((1, width, columns), lambda j, n: (j, 0, n)),
            pl.BlockSpec((1, 1, columns), lambda j, n: (j, 0, n)),
            pl.BlockSpec((1, rows, 128), lambda j, n: (j, 0, 0)),
            pl.BlockSpec((1, rows, 128), lambda j, n: (j, 0, 0)),
        ],
        out_specs=pl.BlockSpec((1, rows, columns), lambda j, n: (j, 0, n)),
        out_shape=jax.ShapeDtypeStruct((3, rows, width), BF),
        compiler_params=pltpu.CompilerParams(vmem_limit_bytes=40 << 20),
        name="project_heads",
        cost_estimate=pl.CostEstimate(
            flops=6 * rows * width * width, bytes_accessed=6 * width * width, transcendentals=0
        ),
    )(x, weights, bias[:, None, :], cosine, sine)


def attention_forward(qkv, far_kv, col_labels, own_labels, far_labels):
    rows, width = qkv.shape[1:]
    docs = far_kv.shape[1]
    block = 128
    asked = rows - docs

    def kernel(qkv_ref, far_ref, lc_ref, lo_ref, lf_ref, o_ref):
        lane = lax.broadcasted_iota(jnp.int32, (1, 128), 1)

        def part(start, size, keys, sames):
            q_block = qkv_ref[0, pl.ds(start, size), :]
            outs = []
            for head in range(2):
                mask = (lane // HEAD_WIDTH) == head
                q_head = jnp.where(mask, q_block, jnp.zeros_like(q_block))
                scores = [
                    jnp.where(same, dot_nt(q_head, key), MASKED)
                    for (key, _), same in zip(keys, sames)
                ]
                top = functools.reduce(
                    jnp.maximum, [jnp.max(s, axis=-1, keepdims=True) for s in scores]
                )
                powers = [jnp.exp(s - top) for s in scores]
                total = functools.reduce(
                    jnp.add, [jnp.sum(p, axis=-1, keepdims=True) for p in powers]
                )
                mixed = functools.reduce(
                    jnp.add, [dot_nn(p.astype(BF), value) for p, (_, value) in zip(powers, keys)]
                )
                outs.append(mixed * (1.0 / total))
            o_ref[pl.ds(start, size), :] = jnp.where(lane < HEAD_WIDTH, outs[0], outs[1]).astype(BF)

        doc_keys = [
            (qkv_ref[1, :docs, :], qkv_ref[2, :docs, :]),
            (far_ref[0], far_ref[1]),
        ]
        for at in range(docs // block):
            labels = lc_ref[pl.ds(at * block, block), :]
            part(at * block, block, doc_keys, [labels == lo_ref[...], labels == lf_ref[...]])
        row = lax.broadcasted_iota(jnp.int32, (asked, asked), 0) // QLEN
        col = lax.broadcasted_iota(jnp.int32, (asked, asked), 1) // QLEN
        part(docs, asked, [(qkv_ref[1, docs:, :], qkv_ref[2, docs:, :])], [row == col])

    whole = lambda shape: pl.BlockSpec(shape, lambda h: (0, 0))
    return pl.pallas_call(
        kernel,
        grid=(width // 128,),
        in_specs=[
            pl.BlockSpec((3, rows, 128), lambda h: (0, 0, h)),
            pl.BlockSpec((2, docs, 128), lambda h: (0, 0, h)),
            whole((docs, 1)),
            whole((1, docs)),
            whole((1, docs)),
        ],
        out_specs=pl.BlockSpec((rows, 128), lambda h: (0, h)),
        out_shape=jax.ShapeDtypeStruct((rows, width), BF),
        compiler_params=pltpu.CompilerParams(vmem_limit_bytes=40 << 20),
        name="attend_forward",
        cost_estimate=pl.CostEstimate(
            flops=32 * rows * 2 * docs * width,
            bytes_accessed=2 * (4 * rows + 2 * docs) * width,
            transcendentals=rows * 2 * docs * width // 64,
        ),
    )(qkv, far_kv, col_labels, own_labels, far_labels)


def attention_backward(
    first, count, qkv, far_kv, grad, cosine, sine, far_cosine, far_sine,
    col_labels, own_labels, far_labels,
):
    rows = qkv.shape[1]
    docs = far_kv.shape[1]
    width = count * 128
    block = 128
    asked = rows - docs

    def kernel(
        qkv_ref, far_ref, g_ref, c_ref, s_ref, fc_ref, fs_ref, lc_ref, lo_ref, lf_ref,
        dq_ref, own_ref, give_ref, sums_own, sums_far,
    ):
        lane = lax.broadcasted_iota(jnp.int32, (1, 128), 1)
        sums_own[...] = jnp.zeros_like(sums_own)
        sums_far[...] = jnp.zeros_like(sums_far)

        def part(start, size, keys, sames, sums):
            q_block = qkv_ref[0, pl.ds(start, size), :]
            g_block = g_ref[pl.ds(start, size), :]
            grads = []
            for head in range(2):
                mask = (lane // HEAD_WIDTH) == head
                q_head = jnp.where(mask, q_block, jnp.zeros_like(q_block))
                g_head = jnp.where(mask, g_block, jnp.zeros_like(g_block))
                scores = [
                    jnp.where(same, dot_nt(q_head, key), MASKED)
                    for (key, _), same in zip(keys, sames)
                ]
                top = functools.reduce(
                    jnp.maximum, [jnp.max(s, axis=-1, keepdims=True) for s in scores]
                )
                powers = [jnp.exp(s - top) for s in scores]
                total = functools.reduce(
                    jnp.add, [jnp.sum(p, axis=-1, keepdims=True) for p in powers]
                )
                inverse = 1.0 / total
                g_head = (g_head.astype(F32) * inverse).astype(BF)
                pulls = [dot_nt(g_head, value) for _, value in keys]
                mean = functools.reduce(
                    jnp.add,
                    [jnp.sum(p * d, axis=-1, keepdims=True) for p, d in zip(powers, pulls)],
                ) * inverse
                slopes = [(p * (d - mean)).astype(BF) for p, d in zip(powers, pulls)]
                got = functools.reduce(
                    jnp.add, [dot_nn(s, key) for s, (key, _) in zip(slopes, keys)]
                )
                grads.append(got * 0.125)
                for (ref, begin, many), s, p in zip(sums, slopes, powers):
                    ref[0, pl.ds(begin, many), :] += dot_tn(s, q_head)
                    ref[1, pl.ds(begin, many), :] += dot_tn(p.astype(BF), g_head)
            whole = jnp.where(lane < HEAD_WIDTH, grads[0], grads[1])
            at = pl.ds(start, size)
            dq_ref[at, :] = (whole * c_ref[at, :] - turned(whole) * s_ref[at, :]).astype(BF)

        doc_keys = [
            (qkv_ref[1, :docs, :], qkv_ref[2, :docs, :]),
            (far_ref[0], far_ref[1]),
        ]
        for at in range(docs // block):
            labels = lc_ref[pl.ds(at * block, block), :]
            part(
                at * block,
                block,
                doc_keys,
                [labels == lo_ref[...], labels == lf_ref[...]],
                [(sums_own, 0, docs), (sums_far, 0, docs)],
            )
        row = lax.broadcasted_iota(jnp.int32, (asked, asked), 0) // QLEN
        col = lax.broadcasted_iota(jnp.int32, (asked, asked), 1) // QLEN
        part(
            docs,
            asked,
            [(qkv_ref[1, docs:, :], qkv_ref[2, docs:, :])],
            [row == col],
            [(sums_own, docs, asked)],
        )
        own_ref[0] = sums_own[0] * c_ref[...] - turned(sums_own[0]) * s_ref[...]
        own_ref[1] = sums_own[1]
        give_ref[0] = (sums_far[0] * fc_ref[...] - turned(sums_far[0]) * fs_ref[...]).astype(BF)
        give_ref[1] = sums_far[1].astype(BF)

    whole = lambda shape: pl.BlockSpec(shape, lambda h: (0, 0))
    return pl.pallas_call(
        kernel,
        grid=(count,),
        in_specs=[
            pl.BlockSpec((3, rows, 128), lambda h: (0, 0, h + first)),
            pl.BlockSpec((2, docs, 128), lambda h: (0, 0, h + first)),
            pl.BlockSpec((rows, 128), lambda h: (0, h + first)),
            whole((rows, 128)),
            whole((rows, 128)),
            whole((docs, 128)),
            whole((docs, 128)),
            whole((docs, 1)),
            whole((1, docs)),
            whole((1, docs)),
        ],
        out_specs=[
            pl.BlockSpec((rows, 128), lambda h: (0, h)),
            pl.BlockSpec((2, rows, 128), lambda h: (0, 0, h)),
            pl.BlockSpec((2, docs, 128), lambda h: (0, 0, h)),
        ],
        out_shape=[
            jax.ShapeDtypeStruct((rows, width), BF),
            jax.ShapeDtypeStruct((2, rows, width), F32),
            jax.ShapeDtypeStruct((2, docs, width), BF),
        ],
        scratch_shapes=[pltpu.VMEM((2, rows, 128), F32), pltpu.VMEM((2, docs, 128), F32)],
        compiler_params=pltpu.CompilerParams(vmem_limit_bytes=40 << 20),
        name="attend_backward",
        cost_estimate=pl.CostEstimate(
            flops=100 * rows * 2 * docs * width,
            bytes_accessed=4 * (6 * rows + 4 * docs) * width,
            transcendentals=rows * 2 * docs * width // 64,
        ),
    )(
        qkv, far_kv, grad, cosine, sine, far_cosine, far_sine, col_labels, own_labels, far_labels
    )


def differing(a, b, bits):
    total = 0
    for bit in range(bits):
        x, y = (a // 2**bit) % 2, (b // 2**bit) % 2
        total = total + 2**bit * (x + y - 2 * x * y)
    return total


def gather_kernel(x_doc, x_query, qkv, out, up, back, proj, bias, picks):
    chips, ways = 4, 4
    groups = 2 * chips
    weights = [qkv, out, up, back]
    feature_axis = [1, 1, 0, 1]
    tensor_axis = [2, 0, 1, 0]
    first_bits = [(2, 4), (4, 2), (2, 4), (4, 2)]
    count = len(weights)
    quarter, width = x_doc.shape[1:]
    asked = x_query.shape[1]
    docs = 2 * quarter
    slots = 32

    def place(j):
        return (j & 1) * chips + (j >> 1)

    def kernel(*refs):
        xd_ref, xq_ref = refs[:2]
        sources = refs[2 : 2 + count]
        proj_ref, bias_ref, picks_ref = refs[2 + count : 5 + count]
        x_out = refs[5 + count]
        outs = refs[6 + count : 6 + 2 * count]
        proj_out, bias_out, picks_out = refs[6 + 2 * count : 9 + 2 * count]
        send_sem, recv_sem, small_send, small_recv, x_send, x_recv, local_sem = refs[9 + 2 * count :]
        rank = lax.axis_index("dp")
        column = lax.axis_index("tensor")
        core = rank % 2
        base = rank - core

        def other(bit):
            return rank + bit - 2 * bit * ((rank // bit) % 2)

        barrier = pltpu.get_barrier_semaphore()
        for dc in range(2):
            for dt in range(4):
                if dc + dt > 0:
                    pl.semaphore_signal(
                        barrier,
                        inc=1,
                        device_id=(base + (core + dc) % 2, (column + dt) % 4),
                        device_id_type=MESH,
                    )
        for bit in (2, 4):
            pl.semaphore_signal(
                barrier, inc=1, device_id=(other(bit), column), device_id_type=MESH
            )
        pl.semaphore_wait(barrier, 9)

        local = []

        def keep(src, dst):
            copy = pltpu.make_async_copy(src, dst, local_sem.at[len(local)])
            copy.start()
            local.append(copy)

        lonely = 3 * core == column
        x_copies = []
        for m in range(2):
            mine = jnp.logical_and(lonely, column // 2 == m)
            q = column % 2
            for kind, (ref, size, begin) in enumerate(((xd_ref, quarter, 0), (xq_ref, asked, docs))):
                src = ref.at[m]
                dst = x_out.at[pl.ds(pl.multiple_of(begin + q * size, 32), size), :]
                away = pltpu.make_async_remote_copy(
                    src_ref=src,
                    dst_ref=dst,
                    send_sem=x_send.at[m, kind],
                    recv_sem=x_recv.at[q, kind],
                    device_id=(base + column // 2, 2 * m + core),
                    device_id_type=MESH,
                )
                here = pltpu.make_async_copy(src, dst, x_send.at[m, kind])

                @pl.when(mine)
                def _():
                    here.start()

                @pl.when(jnp.logical_not(mine))
                def _():
                    away.start()

                x_copies.append((mine, here, away))

        waits = []

        def remote(a, slot, src, dst, to):
            return pltpu.make_async_remote_copy(
                src_ref=src,
                dst_ref=dst,
                send_sem=send_sem.at[a, slot],
                recv_sem=recv_sem.at[a, slot],
                device_id=to,
                device_id_type=MESH,
            )

        def piece(a, j, source, at=None):
            at = column if at is None else at
            index = [slice(None)] * len(sources[a].shape)
            size = sources[a].shape[feature_axis[a]]
            index[feature_axis[a]] = pl.ds(place(j) * size, size)
            size = sources[a].shape[tensor_axis[a]]
            offset = pl.multiple_of(differing(at, source, 2) * size, size)
            index[tensor_axis[a]] = pl.ds(offset, size)
            return outs[a].at[tuple(index)]

        def line(a, j):
            index = [slice(None)] * len(sources[a].shape)
            size = sources[a].shape[feature_axis[a]]
            index[feature_axis[a]] = pl.ds(place(j) * size, size)
            return outs[a].at[tuple(index)]

        def go(copy, condition):
            if condition is None:
                copy.start()
            else:

                @pl.when(condition)
                def _():
                    copy.start()

            waits.append((condition, copy))

        def origin(kind):
            if kind == 0:
                return column, None
            if kind <= 3:
                return column - kind, column >= kind
            return column + (kind - 3), column + (kind - 3) <= 3

        def both(x, y):
            if x is None:
                return y
            return x if y is None else jnp.logical_and(x, y)

        def spread(a, kind):
            source, there = origin(kind)
            first, second = first_bits[a]
            src = sources[a] if kind == 0 else piece(a, 0, source)
            go(remote(a, 6 + kind, src, piece(a, first, source), (other(first), column)), there)
            go(remote(a, 13 + kind, src, piece(a, second, source), (other(second), column)), there)

        def along(a, kind):
            source, there = origin(kind)
            src = sources[a] if kind == 0 else piece(a, 0, source)
            hops = kind if kind <= 3 else kind - 3
            if kind <= 3 and hops < 3:
                dst = piece(a, 0, source, column + 1)
                go(remote(a, hops, src, dst, (rank, column + 1)), both(there, column < 3))
            if (kind == 0 or kind > 3) and hops < 3:
                dst = piece(a, 0, source, column - 1)
                go(remote(a, 3 + hops, src, dst, (rank, column - 1)), both(there, column > 0))

        def arrived(a, slot, dst, condition):
            copy = remote(a, slot, dst, dst, (rank, column))
            if condition is None:
                copy.wait_recv()
            else:

                @pl.when(condition)
                def _():
                    copy.wait_recv()

        def onward(a, kind):
            source, there = origin(kind)
            first, second = first_bits[a]
            src = piece(a, first, source)
            arrived(a, 6 + kind, src, there)
            dst = piece(a, first | second, source)
            go(remote(a, 20 + kind, src, dst, (other(second), column)), there)

        small = []

        def tiny(src, dst, to):
            at = len(small)
            copy = pltpu.make_async_remote_copy(
                src_ref=src,
                dst_ref=dst,
                send_sem=small_send.at[at],
                recv_sem=small_recv.at[at],
                device_id=to,
                device_id_type=MESH,
            )
            copy.start()
            small.append(copy)
            return copy

        for a in range(count):
            along(a, 0)
            spread(a, 0)
        for a in range(count):
            keep(sources[a], piece(a, 0, column))
        keep(bias_ref, bias_out.at[0])
        for dt in range(1, 4):
            to = differing(column, dt, 2)
            tiny(bias_ref, bias_out.at[dt], (rank, to))
        flat = []
        for ref, out_ref in ((proj_ref, proj_out), (picks_ref, picks_out)):
            keep(ref, out_ref.at[0])
            flat.append(
                (
                    tiny(ref, out_ref.at[place(2)], (other(2), column)),
                    tiny(ref, out_ref.at[place(4)], (other(4), column)),
                    tiny(ref, out_ref.at[place(1)], (other(1), column)),
                    out_ref,
                )
            )

        for hops in range(1, 4):
            for a in range(count):
                for kind in (hops, hops + 3):
                    source, there = origin(kind)
                    slot = hops - 1 if kind <= 3 else 2 + hops
                    arrived(a, slot, piece(a, 0, source), there)
                    along(a, kind)
                    spread(a, kind)
            kinds = (0,) if hops == 1 else (hops - 1, hops + 2)
            for a in range(count):
                for kind in kinds:
                    onward(a, kind)
        for copy in local:
            copy.wait()

        def sibling(a, slot, j):
            go(remote(a, slot, line(a, j), line(a, j | 1), (other(1), column)), None)

        for a in range(count):
            sibling(a, 27, 0)
        for by_two, by_four, _, out_ref in flat:
            by_two.wait_recv()
            tiny(out_ref.at[place(2)], out_ref.at[place(6)], (other(4), column))
            tiny(out_ref.at[place(2)], out_ref.at[place(3)], (other(1), column))
            by_four.wait_recv()
            tiny(out_ref.at[place(4)], out_ref.at[place(5)], (other(1), column))
        for a in range(count):
            for kind in (3, 6):
                onward(a, kind)
            sibling(a, 28, first_bits[a][0])
        for n, (_, _, _, out_ref) in enumerate(flat):
            small[9 + 3 * n].wait_recv()
            tiny(out_ref.at[place(6)], out_ref.at[place(7)], (other(1), column))
        for a in range(count):
            first, second = first_bits[a]
            for base_slot, j, slot in ((13, second, 29), (20, first | second, 30)):
                for kind in range(7):
                    source, there = origin(kind)
                    arrived(a, base_slot + kind, piece(a, j, source), there)
                sibling(a, slot, j)
        for n, copy in enumerate(small):
            if n not in (3, 4, 6, 7, 9, 12):
                copy.wait_recv()
            copy.wait_send()
        for q in range(2):
            mine = jnp.logical_and(lonely, column % 2 == q)
            for kind, (size, begin) in enumerate(((quarter, 0), (asked, docs))):
                dst = x_out.at[pl.ds(begin + q * size, size), :]
                copy = pltpu.make_async_remote_copy(
                    src_ref=dst,
                    dst_ref=dst,
                    send_sem=x_send.at[q, kind],
                    recv_sem=x_recv.at[q, kind],
                    device_id=(rank, column),
                    device_id_type=MESH,
                )

                @pl.when(jnp.logical_not(mine))
                def _():
                    copy.wait_recv()

        for mine, here, away in x_copies:

            @pl.when(mine)
            def _():
                here.wait()

            @pl.when(jnp.logical_not(mine))
            def _():
                away.wait_send()

        for a in range(count):
            for slot, j in ((27, 1), (28, first_bits[a][0] | 1), (29, first_bits[a][1] | 1), (30, 7)):
                arrived(a, slot, line(a, j), None)
        for condition, copy in waits:
            if condition is None:
                copy.wait_send()
            else:

                @pl.when(condition)
                def _():
                    copy.wait_send()

    out_shape = [jax.ShapeDtypeStruct((docs + 2 * asked, width), x_doc.dtype)]
    for w, f, t in zip(weights, feature_axis, tensor_axis):
        shape = list(w.shape)
        shape[f] *= groups
        shape[t] *= ways
        out_shape.append(jax.ShapeDtypeStruct(tuple(shape), w.dtype))
    out_shape += [
        jax.ShapeDtypeStruct((groups,) + proj.shape, proj.dtype),
        jax.ShapeDtypeStruct((ways,) + bias.shape, bias.dtype),
        jax.ShapeDtypeStruct((groups,) + picks.shape, picks.dtype),
    ]
    anywhere = pl.BlockSpec(memory_space=pl.ANY)
    dma = pltpu.SemaphoreType.DMA
    return pl.pallas_call(
        kernel,
        out_shape=out_shape,
        in_specs=[anywhere] * (5 + count),
        out_specs=[anywhere] * (4 + count),
        scratch_shapes=[
            dma((count, slots)),
            dma((count, slots)),
            dma((17,)),
            dma((17,)),
            dma((2, 2)),
            dma((2, 2)),
            dma((count + 3,)),
        ],
        compiler_params=pltpu.CompilerParams(collective_id=0, has_side_effects=True),
        name="gather_weights",
    )(x_doc, x_query, *weights, proj, bias, picks)


def body(
    x_doc,
    x_query,
    doc_cot,
    query_cot,
    lengths,
    positives,
    w_qkv,
    b_qkv,
    w_out,
    b_out,
    gain_one,
    shift_one,
    w_in,
    b_in,
    w_back,
    b_back,
    gain_two,
    shift_two,
    w_proj,
):
    ways = lax.axis_size("tensor")
    groups = lax.axis_size("dp")
    column = lax.axis_index("tensor")
    rank = lax.axis_index("dp")
    core = rank % 2
    chip = rank // 2
    chips = groups // 2
    micro, quarter, width = x_doc.shape
    asked = x_query.shape[1]
    segments = lengths.shape[2] - 1
    proj_width = w_proj.shape[1]
    heads_local = w_qkv.shape[2]
    units_local = w_in.shape[1]
    block = width // groups
    assert ways == 2 * micro and ways == 4

    def exchange(value, dr=0, dt=0):
        pairs = [
            (r * ways + t, (r ^ dr) * ways + (t ^ dt)) for r in range(groups) for t in range(ways)
        ]
        return lax.ppermute(value, AXES, pairs)

    chip_bits = []
    bit = 2
    while bit < groups:
        chip_bits.append(bit)
        bit *= 2

    def gather_weights(pack, reverse):
        pieces = [pack] + [exchange(pack, dt=j) for j in range(1, ways)]
        pieces = [(0, jnp.concatenate(pieces, axis=-1))]
        order = chip_bits[::-1] if reverse and len(chip_bits) == 2 else chip_bits
        for dr in order:
            pieces = pieces + [(j + dr // 2, exchange(p, dr=dr)) for j, p in pieces]
            if len(pieces) >= 4 or dr == order[-1]:
                pieces.sort(key=lambda item: item[0])
                pieces = [(0, jnp.concatenate([p for _, p in pieces], axis=-2))]
        (_, half), = pieces
        return jnp.concatenate([half, exchange(half, dr=1)], axis=-2)

    def gather_proj(pack):
        for dr in chip_bits + [1]:
            pack = jnp.concatenate([pack, exchange(pack, dr=dr)], axis=0)
        return pack

    unit_micro = column // 2
    unit_row = chip * 2 + column % 2

    def rows_in(docs, queries):
        blocks = jnp.concatenate([docs, queries], axis=1)
        got = []
        for j in range(2):
            send = jnp.where((column + j) % 2 == 0, blocks[0], blocks[1])
            pairs = []
            for r in range(groups):
                for t in range(ways):
                    m = (t + j) % 2
                    pairs.append(
                        (r * ways + t, ((r // 2) * 2 + t // 2) * ways + 2 * m + r % 2)
                    )
            got.append(lax.ppermute(send, AXES, pairs))
        first = jnp.where(unit_micro == 0, got[0], got[1])
        second = jnp.where(unit_micro == 0, got[1], got[0])
        return jnp.concatenate(
            [first[:quarter], second[:quarter], first[quarter:], second[quarter:]], axis=0
        )

    def quarters_out(first, second):
        got = []
        for j in range(2):
            send = jnp.where((unit_micro + j) % 2 == 0, first, second)
            pairs = []
            for r in range(groups):
                for t in range(ways):
                    m = t // 2
                    pairs.append(
                        (
                            r * ways + t,
                            ((r // 2) * 2 + t % 2) * ways + 2 * (r % 2) + (m + j) % 2,
                        )
                    )
            got.append(lax.ppermute(send, AXES, pairs))
        even = jnp.where(column % 2 == 0, got[0], got[1])
        odd = jnp.where(column % 2 == 0, got[1], got[0])
        return jnp.stack([even, odd])

    def rows_out(values):
        docs = 2 * quarter
        first = jnp.concatenate([values[:quarter], values[docs : docs + asked]], axis=0)
        second = jnp.concatenate([values[quarter:docs], values[docs + asked :]], axis=0)
        blocks = quarters_out(first, second)
        return blocks[:, :quarter], blocks[:, quarter:]

    place = jnp.arange(width, dtype=jnp.int32)
    step = place // block
    actual = (rank ^ (2 * (step % chips) + step // chips)) * block + place % block
    turn = (place[:, None] == actual[None, :]).astype(BF)

    bias_pack = jnp.concatenate([b_qkv.reshape(-1), b_in])
    own_picks = jnp.zeros((8, 128), jnp.int32).at[:micro, : positives.shape[1]].set(positives)
    if chips == 4:
        own_x, full_qkv, full_out, full_in, full_back, full_proj, biases, picks_rel = gather_kernel(
            x_doc, x_query, w_qkv, w_out, w_in, w_back, w_proj, bias_pack.reshape(-1, 128), own_picks
        )
        biases = [biases[j].reshape(-1) for j in range(ways)]
        full_proj = full_proj.reshape(width, proj_width)
    else:
        own_x = rows_in(x_doc, x_query)
        full_qkv = gather_weights(w_qkv, False)
        full_out = gather_weights(w_out.T, False).T
        full_in = gather_weights(w_in, False)
        full_back = gather_weights(w_back.T, False).T
        full_proj = gather_proj(w_proj)
        picks_rel = gather_proj(own_picks[None])
        biases = [bias_pack] + [exchange(bias_pack[None], dt=j)[0] for j in range(1, ways)]
    picks_rel = picks_rel[:, :micro, : positives.shape[1]].astype(F32)
    own_cot = rows_in(doc_cot.astype(BF), query_cot.astype(BF))
    bias_qkv = jnp.concatenate(
        [b[: 3 * heads_local].reshape(3, heads_local) for b in biases], axis=1
    )
    bias_in = jnp.concatenate([b[3 * heads_local :] for b in biases])
    params = jnp.stack(
        [b_out, gain_one, shift_one, b_back, gain_two, shift_two, b_out, b_out]
    )
    params = jnp.dot(params, turn.astype(F32), precision=FULL_PRECISION)
    b_out, gain_one, shift_one, b_back, gain_two, shift_two = [params[i] for i in range(6)]

    docs = 2 * quarter
    queries = 2 * asked
    rows = docs + queries
    sizes_all = lengths[unit_micro]
    sizes = sizes_all[unit_row]
    ends = jnp.cumsum(sizes[:-1])
    starts = jnp.concatenate([jnp.zeros((1,), jnp.int32), ends])

    def layout(first):
        index = first + jnp.arange(docs, dtype=jnp.int32)
        segment = jnp.sum((index[:, None] >= ends[None, :]).astype(jnp.int32), axis=1)
        labels = jnp.arange(starts.shape[0], dtype=jnp.int32)
        begin = jnp.sum(
            jnp.where(segment[:, None] == labels[None, :], starts[None, :], 0), axis=1
        )
        return segment, index - begin

    own_labels, own_places = layout(core * docs)
    far_labels, far_places = layout((1 - core) * docs)
    own_places = jnp.concatenate([own_places, jnp.arange(queries, dtype=jnp.int32) % QLEN])
    half = HEAD_WIDTH // 2
    rates = 10000.0 ** (-(2.0 * jnp.arange(half, dtype=F32)) / HEAD_WIDTH)

    def rotation(places):
        angle = places.astype(F32)[:, None] * rates[None, :]
        sine = jnp.sin(angle)
        return jnp.tile(jnp.cos(angle), (1, 4)), jnp.concatenate([-sine, sine] * 2, axis=1)

    cosine, sine = rotation(own_places)
    far_cosine, far_sine = rotation(far_places)
    cosines_three = jnp.stack([cosine * 0.125, cosine, jnp.ones_like(cosine)])
    sines_three = jnp.stack([sine * 0.125, sine, jnp.zeros_like(sine)])

    x_low = dot_nn(own_x, turn).astype(BF)
    qkv = project_heads(x_low, full_qkv, bias_qkv, cosines_three, sines_three)
    far_kv = exchange(qkv[1:, :docs], dr=1)
    label_args = (own_labels[:, None], own_labels[None, :], far_labels[None, :])
    mixed = attention_forward(qkv, far_kv, *label_args)
    branch = dot_nn(mixed, full_out)
    resid_one = x_low.astype(F32) + branch + b_out
    normed, norm_one_pull = jax.vjp(layer_norm, resid_one, gain_one, shift_one)
    normed_low = normed.astype(BF)
    inner = dot_nn(normed_low, full_in) + bias_in
    active, gelu_pull = jax.vjp(gelu_exact, inner)
    active_low = active.astype(BF)
    resid_two = normed + dot_nn(active_low, full_back) + b_back
    output, norm_two_pull = jax.vjp(layer_norm, resid_two, gain_two, shift_two)
    output_low = output.astype(BF)
    y_doc, y_query = rows_out(dot_nt(output_low, turn).astype(BF))
    projection = dot_nn(output_low, full_proj)
    unit, unit_pull = jax.vjp(normalize, projection)
    unit_low = unit.astype(BF)

    doc_unit = unit_low[:docs]
    query_unit = unit_low[docs:]

    def bit_of(dr, dt):
        return (rank // dr) % 2 == 1 if dr else (column // dt) % 2 == 1

    def join(value, dr, dt, axis=0):
        got = exchange(value, dr=dr, dt=dt)
        on = bit_of(dr, dt)
        low = jnp.where(on, got, value)
        high = jnp.where(on, value, got)
        return jnp.concatenate([low, high], axis=axis)

    def split_sum(value, dr, dt):
        on = bit_of(dr, dt)
        size = value.shape[0] // 2
        send = jnp.where(on, value[:size], value[size:])
        keep = jnp.where(on, value[size:], value[:size])
        return keep + exchange(send.astype(BF), dr=dr, dt=dt).astype(F32)

    steps = [(1, 0), (0, 1)] + [(dr, 0) for dr in chip_bits]
    all_queries = query_unit
    for dr, dt in steps:
        all_queries = join(all_queries, dr, dt)
    held = jnp.arange(groups, dtype=jnp.int32)
    held = rank ^ (2 * (held % chips) + held // chips)
    order = (jnp.arange(groups, dtype=jnp.int32)[:, None] == held[None, :]).astype(F32)
    picks = jnp.where(unit_micro == 0, picks_rel[:, 0], picks_rel[:, 1])
    picks = jnp.dot(order, picks, precision=FULL_PRECISION).astype(jnp.int32).reshape(-1)
    seg_labels = jnp.arange(segments, dtype=jnp.int32)
    member = (own_labels[:, None] == seg_labels[None, :]).astype(F32)
    cosines = dot_nt(doc_unit, all_queries)
    weight = jnp.exp(TAU * (cosines - 1.0))
    totals = jnp.einsum("js,ji->si", member, weight, precision=FULL_PRECISION)
    totals = totals + exchange(totals, dr=1)
    for dr, dt in steps[1:]:
        totals = join(totals, dr, dt)
    counts = sizes_all[:, :segments].reshape(-1).astype(F32)
    best = (jnp.log(totals) - jnp.log(counts)[:, None]) / TAU + 1.0
    score = jnp.sum(best.reshape(best.shape[0], -1, QLEN), axis=-1)
    logits = LOGIT_SCALE * score
    documents = jnp.arange(logits.shape[0], dtype=jnp.int32)
    chosen = (documents[:, None] == picks[None, :]).astype(F32)
    peak = jnp.max(logits, axis=0, keepdims=True)
    powers = jnp.exp(logits - peak)
    mass = jnp.sum(powers, axis=0, keepdims=True)
    losses = (peak + jnp.log(mass))[0] - jnp.sum(chosen * logits, axis=0)
    logit_grad = LOGIT_SCALE * (powers / mass - chosen)
    own_grad = lax.dynamic_slice_in_dim(logit_grad, unit_row * segments, segments, axis=0)
    own_total = lax.dynamic_slice_in_dim(totals, unit_row * segments, segments, axis=0)
    coef = jnp.repeat(own_grad, QLEN, axis=1) / own_total
    spread = jnp.einsum("js,si->ji", member, coef, precision=FULL_PRECISION)
    cosine_grad = (weight * spread).astype(BF)
    doc_grad = dot_nn(cosine_grad, all_queries)
    query_grad = dot_tn(cosine_grad, doc_unit)
    for dr, dt in steps[::-1]:
        query_grad = split_sum(query_grad, dr, dt)
    own_losses = lax.dynamic_slice_in_dim(losses, unit_row * (4 * asked // QLEN) + core * 2 * (asked // QLEN), 2 * (asked // QLEN))
    per = asked // QLEN
    loss_tiles = [
        jnp.broadcast_to(own_losses[i * per : (i + 1) * per, None], (per, 128)) for i in range(2)
    ]
    loss_out = quarters_out(loss_tiles[0], loss_tiles[1])[:, :, 0]

    class Reduction:
        def __init__(self, half, axis, reverse, last):
            self.bits = chip_bits if reverse and len(chip_bits) == 2 else chip_bits[::-1]
            self.left = sorted(chip_bits)
            self.axis, self.last = axis, last
            self.sends = [half(1).astype(BF)]
            self.hops = [(1, 0)]
            self.kept = lambda: half(0)
            self.stage = 0

        def advance(self):
            total = self.kept()
            for s, (dr, dt) in zip(self.sends, self.hops):
                got = exchange(s, dr=dr, dt=dt).astype(F32)
                total = got if total is None else total + got
            if self.stage == len(self.bits) + 1:
                return total
            if self.stage < len(self.bits):
                dr = self.bits[self.stage]
                at = self.left.index(dr)
                self.left.remove(dr)
                size = block << at
                stay, send = [
                    jnp.concatenate(
                        [
                            lax.slice_in_dim(total, b, b + size, axis=self.axis)
                            for b in range(side * size, total.shape[self.axis], 2 * size)
                        ],
                        axis=self.axis,
                    )
                    for side in (0, 1)
                ]
                self.sends = [send.astype(BF)]
                self.hops = [(dr, 0)]
            else:
                stay, sends = self.last(total)
                self.sends = [piece.astype(BF) for _, piece in sends]
                self.hops = [(0, dt) for dt, _ in sends]
            self.kept = lambda: stay
            self.stage += 1
            return None

        def finish(self):
            total = None
            while total is None:
                total = self.advance()
            return total

    def weight_sum(left, right, axis, reverse):
        size = width // 2

        def half(n):
            if axis == 0:
                return dot_tn(left[:, n * size : (n + 1) * size], right)
            return dot_tn(left, right[:, n * size : (n + 1) * size])

        def last(total):
            size = total.shape[1 - axis] // ways
            pieces = [
                lax.slice_in_dim(total, j * size, (j + 1) * size, axis=1 - axis)
                for j in range(ways)
            ]
            return pieces[0], [(j, pieces[j]) for j in range(1, ways)]

        return Reduction(half, axis, reverse, last)

    def after(value, reductions):
        sends = [r.sends for r in reductions]
        value, sends = lax.optimization_barrier((value, sends))
        for r, s in zip(reductions, sends):
            r.sends = s
        return value

    unit_grad = jnp.concatenate([doc_grad, query_grad], axis=0)
    (proj_grad,) = unit_pull(unit_grad)
    proj_low = proj_grad.astype(BF)
    out_grad = own_cot_turned = dot_nn(own_cot, turn) + dot_nt(proj_low, full_proj)
    resid_two_grad, gain_two_grad, shift_two_grad = norm_two_pull(out_grad)
    update_low = resid_two_grad.astype(BF)
    sum_back = weight_sum(active_low, update_low, 1, True)
    active_grad = dot_nt(update_low, full_back)
    (inner_grad,) = gelu_pull(active_grad)
    inner_low = inner_grad.astype(BF)
    sum_in = weight_sum(normed_low, inner_low, 0, False)
    normed_grad = dot_nt(inner_low, full_in) + resid_two_grad
    resid_one_grad, gain_one_grad, shift_one_grad = norm_one_pull(normed_grad)
    branch_low = resid_one_grad.astype(BF)
    mixed_grad = dot_nt(branch_low, full_out).astype(BF)
    sum_out = weight_sum(mixed, branch_low, 1, False)

    def heads_sum(rights, first_block, blocks, reverse):
        size = width // 2
        many = rights.shape[1] // 3 // blocks

        def half(n):
            return dot_tn(x_low[:, n * size : (n + 1) * size], rights)

        def last(total):
            stay, sends = None, []
            for b in range(blocks):
                piece = jnp.stack(
                    [total[:, (j * blocks + b) * many : (j * blocks + b + 1) * many] for j in range(3)]
                )
                if first_block + b == 0:
                    stay = piece
                else:
                    sends.append((first_block + b, piece))
            return stay, sends

        return Reduction(half, 0, reverse, last)

    head_sums, head_rights = [], []
    running = [sum_back, sum_in]
    per_block = heads_local // 128
    for first_block, blocks in ((0, 2), (2, 1), (3, 1)):
        for item in running:
            item.advance()
        mixed_grad = after(mixed_grad, running)
        dq, own_grads, give = attention_backward(
            first_block * per_block,
            blocks * per_block,
            qkv,
            far_kv,
            mixed_grad,
            cosine,
            sine,
            far_cosine,
            far_sine,
            *label_args,
        )
        got = exchange(give, dr=1).astype(F32)
        rights = [dq] + [
            jnp.concatenate([own_grads[i, :docs] + got[i], own_grads[i, docs:]], axis=0).astype(BF)
            for i in range(2)
        ]
        rights = jnp.concatenate(rights, axis=1)
        head_rights.append((blocks, rights))
        item = heads_sum(rights, first_block, blocks, first_block > 0)
        head_sums.append(item)
        if first_block == 0:
            running += [sum_out]
        elif first_block == 2:
            running += [head_sums[0]]
    out_back = sum_back.finish()
    out_in = sum_in.finish()
    out_out = sum_out.finish()
    out_qkv = functools.reduce(jnp.add, [item.finish() for item in head_sums])
    x_grad = resid_one_grad
    for j in range(3):
        pre = jnp.concatenate(
            [r[:, j * r.shape[1] // 3 : (j + 1) * r.shape[1] // 3] for _, r in head_rights], axis=1
        )
        x_grad = x_grad + dot_nt(pre, full_qkv[j])
    gx_doc, gx_query = rows_out(dot_nt(x_grad.astype(BF), turn).astype(BF))

    grad_proj = dot_tn(output_low, proj_low)
    for dr in [1] + chip_bits[::-1]:
        size = grad_proj.shape[0] // 2
        got = exchange(grad_proj[size:].astype(BF), dr=dr)
        grad_proj = grad_proj[:size] + got.astype(F32)
    for dt in (1, 2):
        grad_proj = grad_proj + exchange(grad_proj, dt=dt)

    vectors = jnp.stack(
        [
            jnp.sum(branch_low.astype(F32), axis=0),
            gain_one_grad,
            shift_one_grad,
            jnp.sum(update_low.astype(F32), axis=0),
            gain_two_grad,
            shift_two_grad,
        ]
    )
    vectors = lax.dot_general(
        vectors, turn.astype(F32), (((1,), (1,)), ((), ())), precision=FULL_PRECISION
    )
    head_bias = []
    for blocks, r in head_rights:
        sums = jnp.sum(r.astype(F32), axis=0).reshape(3, blocks, heads_local)
        head_bias.append(jnp.swapaxes(sums, 0, 1).reshape(blocks, 3 * heads_local))
    tensor_grads = jnp.concatenate(
        [
            jnp.concatenate(head_bias, axis=0),
            jnp.sum(inner_low.astype(F32), axis=0).reshape(ways, units_local),
        ],
        axis=1,
    )
    for dt in (2, 1):
        tensor_grads = tensor_grads[:dt] + exchange(tensor_grads[dt:], dt=dt)
        vectors = vectors + exchange(vectors, dt=dt)
    for dr in [1] + chip_bits:
        tensor_grads = tensor_grads + exchange(tensor_grads, dr=dr)
        vectors = vectors + exchange(vectors, dr=dr)
    tensor_grads = tensor_grads[0]
    return (
        y_doc,
        y_query,
        loss_out,
        gx_doc.astype(F32),
        gx_query.astype(F32),
        out_qkv,
        tensor_grads[: 3 * heads_local].reshape(3, heads_local),
        out_out,
        vectors[0],
        vectors[1],
        vectors[2],
        out_in,
        tensor_grads[3 * heads_local :],
        out_back,
        vectors[3],
        vectors[4],
        vectors[5],
        grad_proj,
    )


def solution(mesh):
    rows = P(None, ("dp", "tensor"), None)
    in_specs = (
        rows,
        rows,
        rows,
        rows,
        P(),
        P(None, "dp"),
        P(None, "dp", "tensor"),
        P(None, "tensor"),
        P("tensor", "dp"),
        P(),
        P(),
        P(),
        P("dp", "tensor"),
        P("tensor"),
        P("tensor", "dp"),
        P(),
        P(),
        P(),
        P("dp", None),
    )
    out_specs = (
        rows,
        rows,
        P(None, ("dp", "tensor")),
        rows,
        rows,
        P(None, "dp", "tensor"),
        P(None, "tensor"),
        P("tensor", "dp"),
        P(),
        P(),
        P(),
        P("dp", "tensor"),
        P("tensor"),
        P("tensor", "dp"),
        P(),
        P(),
        P(),
        P("dp", None),
    )
    return jax.shard_map(body, mesh=mesh, in_specs=in_specs, out_specs=out_specs, check_vma=False)
```

```python
import functools

import jax
import jax.numpy as jnp
from jax import lax
from jax.experimental import pallas as pl
from jax.experimental.pallas import tpu as pltpu
from jax.sharding import PartitionSpec as P

HEAD_WIDTH = 64
QLEN = 32
FULL_PRECISION = lax.Precision.HIGHEST
TAU = 20.0
EPS = 1e-05
LOGIT_SCALE = 2.0
MASKED = -1e30
AXES = ("dp", "tensor")
MESH = pl.DeviceIdType.MESH
BF = jnp.bfloat16
F32 = jnp.float32


def layer_norm(values, gain, shift):
    center = values - jnp.mean(values, axis=-1, keepdims=True)
    spread = jnp.mean(center * center, axis=-1, keepdims=True)
    return center * lax.rsqrt(spread + EPS) * gain + shift


def normalize(values):
    return values * lax.rsqrt(jnp.sum(values * values, axis=-1, keepdims=True) + 1e-06)


def gelu_exact(values):
    return jax.nn.gelu(values, approximate=False)


def dot_nn(a, b):
    return lax.dot_general(a, b, (((1,), (0,)), ((), ())), preferred_element_type=F32)


def dot_nt(a, b):
    return lax.dot_general(a, b, (((1,), (1,)), ((), ())), preferred_element_type=F32)


def dot_tn(a, b):
    return lax.dot_general(a, b, (((0,), (0,)), ((), ())), preferred_element_type=F32)


def turned(values):
    lane = lax.broadcasted_iota(jnp.int32, (1, 128), 1)
    ahead = pltpu.roll(values, 96, 1)
    behind = pltpu.roll(values, 32, 1)
    return jnp.where(lane % HEAD_WIDTH < HEAD_WIDTH // 2, ahead, behind)


def project_heads(x, weights, bias, cosine, sine):
    rows, width = x.shape
    columns = 256

    def kernel(x_ref, w_ref, b_ref, c_ref, s_ref, o_ref):
        got = dot_nn(x_ref[...], w_ref[0]) + b_ref[0]
        for at in range(0, columns, 128):
            piece = got[:, at : at + 128]
            o_ref[0, :, at : at + 128] = (piece * c_ref[0] + turned(piece) * s_ref[0]).astype(BF)

    return pl.pallas_call(
        kernel,
        grid=(3, width // columns),
        in_specs=[
            pl.BlockSpec((rows, width), lambda j, n: (0, 0)),
            pl.BlockSpec((1, width, columns), lambda j, n: (j, 0, n)),
            pl.BlockSpec((1, 1, columns), lambda j, n: (j, 0, n)),
            pl.BlockSpec((1, rows, 128), lambda j, n: (j, 0, 0)),
            pl.BlockSpec((1, rows, 128), lambda j, n: (j, 0, 0)),
        ],
        out_specs=pl.BlockSpec((1, rows, columns), lambda j, n: (j, 0, n)),
        out_shape=jax.ShapeDtypeStruct((3, rows, width), BF),
        compiler_params=pltpu.CompilerParams(vmem_limit_bytes=40 << 20),
        name="project_heads",
        cost_estimate=pl.CostEstimate(
            flops=6 * rows * width * width, bytes_accessed=6 * width * width, transcendentals=0
        ),
    )(x, weights, bias[:, None, :], cosine, sine)


def attention_forward(qkv, far_kv, col_labels, own_labels, far_labels):
    rows, width = qkv.shape[1:]
    docs = far_kv.shape[1]
    block = 128
    asked = rows - docs

    def kernel(qkv_ref, far_ref, lc_ref, lo_ref, lf_ref, o_ref):
        lane = lax.broadcasted_iota(jnp.int32, (1, 128), 1)

        def part(start, size, keys, sames):
            q_block = qkv_ref[0, pl.ds(start, size), :]
            outs = []
            for head in range(2):
                mask = (lane // HEAD_WIDTH) == head
                q_head = jnp.where(mask, q_block, jnp.zeros_like(q_block))
                scores = [
                    jnp.where(same, dot_nt(q_head, key), MASKED)
                    for (key, _), same in zip(keys, sames)
                ]
                top = functools.reduce(
                    jnp.maximum, [jnp.max(s, axis=-1, keepdims=True) for s in scores]
                )
                powers = [jnp.exp(s - top) for s in scores]
                total = functools.reduce(
                    jnp.add, [jnp.sum(p, axis=-1, keepdims=True) for p in powers]
                )
                mixed = functools.reduce(
                    jnp.add, [dot_nn(p.astype(BF), value) for p, (_, value) in zip(powers, keys)]
                )
                outs.append(mixed * (1.0 / total))
            o_ref[pl.ds(start, size), :] = jnp.where(lane < HEAD_WIDTH, outs[0], outs[1]).astype(BF)

        doc_keys = [
            (qkv_ref[1, :docs, :], qkv_ref[2, :docs, :]),
            (far_ref[0], far_ref[1]),
        ]
        for at in range(docs // block):
            labels = lc_ref[pl.ds(at * block, block), :]
            part(at * block, block, doc_keys, [labels == lo_ref[...], labels == lf_ref[...]])
        row = lax.broadcasted_iota(jnp.int32, (asked, asked), 0) // QLEN
        col = lax.broadcasted_iota(jnp.int32, (asked, asked), 1) // QLEN
        part(docs, asked, [(qkv_ref[1, docs:, :], qkv_ref[2, docs:, :])], [row == col])

    whole = lambda shape: pl.BlockSpec(shape, lambda h: (0, 0))
    return pl.pallas_call(
        kernel,
        grid=(width // 128,),
        in_specs=[
            pl.BlockSpec((3, rows, 128), lambda h: (0, 0, h)),
            pl.BlockSpec((2, docs, 128), lambda h: (0, 0, h)),
            whole((docs, 1)),
            whole((1, docs)),
            whole((1, docs)),
        ],
        out_specs=pl.BlockSpec((rows, 128), lambda h: (0, h)),
        out_shape=jax.ShapeDtypeStruct((rows, width), BF),
        compiler_params=pltpu.CompilerParams(vmem_limit_bytes=40 << 20),
        name="attend_forward",
        cost_estimate=pl.CostEstimate(
            flops=32 * rows * 2 * docs * width,
            bytes_accessed=2 * (4 * rows + 2 * docs) * width,
            transcendentals=rows * 2 * docs * width // 64,
        ),
    )(qkv, far_kv, col_labels, own_labels, far_labels)


def attention_backward(
    first, count, qkv, far_kv, grad, cosine, sine, far_cosine, far_sine,
    col_labels, own_labels, far_labels,
):
    rows = qkv.shape[1]
    docs = far_kv.shape[1]
    width = count * 128
    block = 128
    asked = rows - docs

    def kernel(
        qkv_ref, far_ref, g_ref, c_ref, s_ref, fc_ref, fs_ref, lc_ref, lo_ref, lf_ref,
        dq_ref, own_ref, give_ref, sums_own, sums_far,
    ):
        lane = lax.broadcasted_iota(jnp.int32, (1, 128), 1)
        sums_own[...] = jnp.zeros_like(sums_own)
        sums_far[...] = jnp.zeros_like(sums_far)

        def part(start, size, keys, sames, sums):
            q_block = qkv_ref[0, pl.ds(start, size), :]
            g_block = g_ref[pl.ds(start, size), :]
            grads = []
            for head in range(2):
                mask = (lane // HEAD_WIDTH) == head
                q_head = jnp.where(mask, q_block, jnp.zeros_like(q_block))
                g_head = jnp.where(mask, g_block, jnp.zeros_like(g_block))
                scores = [
                    jnp.where(same, dot_nt(q_head, key), MASKED)
                    for (key, _), same in zip(keys, sames)
                ]
                top = functools.reduce(
                    jnp.maximum, [jnp.max(s, axis=-1, keepdims=True) for s in scores]
                )
                powers = [jnp.exp(s - top) for s in scores]
                total = functools.reduce(
                    jnp.add, [jnp.sum(p, axis=-1, keepdims=True) for p in powers]
                )
                inverse = 1.0 / total
                g_head = (g_head.astype(F32) * inverse).astype(BF)
                pulls = [dot_nt(g_head, value) for _, value in keys]
                mean = functools.reduce(
                    jnp.add,
                    [jnp.sum(p * d, axis=-1, keepdims=True) for p, d in zip(powers, pulls)],
                ) * inverse
                slopes = [(p * (d - mean)).astype(BF) for p, d in zip(powers, pulls)]
                got = functools.reduce(
                    jnp.add, [dot_nn(s, key) for s, (key, _) in zip(slopes, keys)]
                )
                grads.append(got * 0.125)
                for (ref, begin, many), s, p in zip(sums, slopes, powers):
                    ref[0, pl.ds(begin, many), :] += dot_tn(s, q_head)
                    ref[1, pl.ds(begin, many), :] += dot_tn(p.astype(BF), g_head)
            whole = jnp.where(lane < HEAD_WIDTH, grads[0], grads[1])
            at = pl.ds(start, size)
            dq_ref[at, :] = (whole * c_ref[at, :] - turned(whole) * s_ref[at, :]).astype(BF)

        doc_keys = [
            (qkv_ref[1, :docs, :], qkv_ref[2, :docs, :]),
            (far_ref[0], far_ref[1]),
        ]
        for at in range(docs // block):
            labels = lc_ref[pl.ds(at * block, block), :]
            part(
                at * block,
                block,
                doc_keys,
                [labels == lo_ref[...], labels == lf_ref[...]],
                [(sums_own, 0, docs), (sums_far, 0, docs)],
            )
        row = lax.broadcasted_iota(jnp.int32, (asked, asked), 0) // QLEN
        col = lax.broadcasted_iota(jnp.int32, (asked, asked), 1) // QLEN
        part(
            docs,
            asked,
            [(qkv_ref[1, docs:, :], qkv_ref[2, docs:, :])],
            [row == col],
            [(sums_own, docs, asked)],
        )
        own_ref[0] = sums_own[0] * c_ref[...] - turned(sums_own[0]) * s_ref[...]
        own_ref[1] = sums_own[1]
        give_ref[0] = (sums_far[0] * fc_ref[...] - turned(sums_far[0]) * fs_ref[...]).astype(BF)
        give_ref[1] = sums_far[1].astype(BF)

    whole = lambda shape: pl.BlockSpec(shape, lambda h: (0, 0))
    return pl.pallas_call(
        kernel,
        grid=(count,),
        in_specs=[
            pl.BlockSpec((3, rows, 128), lambda h: (0, 0, h + first)),
            pl.BlockSpec((2, docs, 128), lambda h: (0, 0, h + first)),
            pl.BlockSpec((rows, 128), lambda h: (0, h + first)),
            whole((rows, 128)),
            whole((rows, 128)),
            whole((docs, 128)),
            whole((docs, 128)),
            whole((docs, 1)),
            whole((1, docs)),
            whole((1, docs)),
        ],
        out_specs=[
            pl.BlockSpec((rows, 128), lambda h: (0, h)),
            pl.BlockSpec((2, rows, 128), lambda h: (0, 0, h)),
            pl.BlockSpec((2, docs, 128), lambda h: (0, 0, h)),
        ],
        out_shape=[
            jax.ShapeDtypeStruct((rows, width), BF),
            jax.ShapeDtypeStruct((2, rows, width), F32),
            jax.ShapeDtypeStruct((2, docs, width), BF),
        ],
        scratch_shapes=[pltpu.VMEM((2, rows, 128), F32), pltpu.VMEM((2, docs, 128), F32)],
        compiler_params=pltpu.CompilerParams(vmem_limit_bytes=40 << 20),
        name="attend_backward",
        cost_estimate=pl.CostEstimate(
            flops=100 * rows * 2 * docs * width,
            bytes_accessed=4 * (6 * rows + 4 * docs) * width,
            transcendentals=rows * 2 * docs * width // 64,
        ),
    )(
        qkv, far_kv, grad, cosine, sine, far_cosine, far_sine, col_labels, own_labels, far_labels
    )


def differing(a, b, bits):
    total = 0
    for bit in range(bits):
        x, y = (a // 2**bit) % 2, (b // 2**bit) % 2
        total = total + 2**bit * (x + y - 2 * x * y)
    return total


def gather_kernel(x_doc, x_query, qkv, out, up, back, proj, bias, picks):
    chips, ways = 4, 4
    groups = 2 * chips
    weights = [qkv, out, up, back]
    feature_axis = [1, 1, 0, 1]
    tensor_axis = [2, 0, 1, 0]
    first_bits = [(2, 4), (4, 2), (2, 4), (4, 2)]
    count = len(weights)
    quarter, width = x_doc.shape[1:]
    asked = x_query.shape[1]
    docs = 2 * quarter
    slots = 32

    def place(j):
        return (j & 1) * chips + (j >> 1)

    def kernel(*refs):
        xd_ref, xq_ref = refs[:2]
        sources = refs[2 : 2 + count]
        proj_ref, bias_ref, picks_ref = refs[2 + count : 5 + count]
        x_out = refs[5 + count]
        outs = refs[6 + count : 6 + 2 * count]
        proj_out, bias_out, picks_out = refs[6 + 2 * count : 9 + 2 * count]
        send_sem, recv_sem, small_send, small_recv, x_send, x_recv, local_sem = refs[9 + 2 * count :]
        rank = lax.axis_index("dp")
        column = lax.axis_index("tensor")
        core = rank % 2
        base = rank - core

        def other(bit):
            return rank + bit - 2 * bit * ((rank // bit) % 2)

        barrier = pltpu.get_barrier_semaphore()
        for dc in range(2):
            for dt in range(4):
                if dc + dt > 0:
                    pl.semaphore_signal(
                        barrier,
                        inc=1,
                        device_id=(base + (core + dc) % 2, (column + dt) % 4),
                        device_id_type=MESH,
                    )
        for bit in (2, 4):
            pl.semaphore_signal(
                barrier, inc=1, device_id=(other(bit), column), device_id_type=MESH
            )
        pl.semaphore_wait(barrier, 9)

        local = []

        def keep(src, dst):
            copy = pltpu.make_async_copy(src, dst, local_sem.at[len(local)])
            copy.start()
            local.append(copy)

        lonely = 3 * core == column
        x_copies = []
        for m in range(2):
            mine = jnp.logical_and(lonely, column // 2 == m)
            q = column % 2
            for kind, (ref, size, begin) in enumerate(((xd_ref, quarter, 0), (xq_ref, asked, docs))):
                src = ref.at[m]
                dst = x_out.at[pl.ds(pl.multiple_of(begin + q * size, 32), size), :]
                away = pltpu.make_async_remote_copy(
                    src_ref=src,
                    dst_ref=dst,
                    send_sem=x_send.at[m, kind],
                    recv_sem=x_recv.at[q, kind],
                    device_id=(base + column // 2, 2 * m + core),
                    device_id_type=MESH,
                )
                here = pltpu.make_async_copy(src, dst, x_send.at[m, kind])

                @pl.when(mine)
                def _():
                    here.start()

                @pl.when(jnp.logical_not(mine))
                def _():
                    away.start()

                x_copies.append((mine, here, away))

        waits = []

        def remote(a, slot, src, dst, to):
            return pltpu.make_async_remote_copy(
                src_ref=src,
                dst_ref=dst,
                send_sem=send_sem.at[a, slot],
                recv_sem=recv_sem.at[a, slot],
                device_id=to,
                device_id_type=MESH,
            )

        def piece(a, j, source, at=None):
            at = column if at is None else at
            index = [slice(None)] * len(sources[a].shape)
            size = sources[a].shape[feature_axis[a]]
            index[feature_axis[a]] = pl.ds(place(j) * size, size)
            size = sources[a].shape[tensor_axis[a]]
            offset = pl.multiple_of(differing(at, source, 2) * size, size)
            index[tensor_axis[a]] = pl.ds(offset, size)
            return outs[a].at[tuple(index)]

        def line(a, j):
            index = [slice(None)] * len(sources[a].shape)
            size = sources[a].shape[feature_axis[a]]
            index[feature_axis[a]] = pl.ds(place(j) * size, size)
            return outs[a].at[tuple(index)]

        def go(copy, condition):
            if condition is None:
                copy.start()
            else:

                @pl.when(condition)
                def _():
                    copy.start()

            waits.append((condition, copy))

        def origin(kind):
            if kind == 0:
                return column, None
            if kind <= 3:
                return column - kind, column >= kind
            return column + (kind - 3), column + (kind - 3) <= 3

        def both(x, y):
            if x is None:
                return y
            return x if y is None else jnp.logical_and(x, y)

        def spread(a, kind):
            source, there = origin(kind)
            first, second = first_bits[a]
            src = sources[a] if kind == 0 else piece(a, 0, source)
            go(remote(a, 6 + kind, src, piece(a, first, source), (other(first), column)), there)
            go(remote(a, 13 + kind, src, piece(a, second, source), (other(second), column)), there)

        def along(a, kind):
            source, there = origin(kind)
            src = sources[a] if kind == 0 else piece(a, 0, source)
            hops = kind if kind <= 3 else kind - 3
            if kind <= 3 and hops < 3:
                dst = piece(a, 0, source, column + 1)
                go(remote(a, hops, src, dst, (rank, column + 1)), both(there, column < 3))
            if (kind == 0 or kind > 3) and hops < 3:
                dst = piece(a, 0, source, column - 1)
                go(remote(a, 3 + hops, src, dst, (rank, column - 1)), both(there, column > 0))

        def arrived(a, slot, dst, condition):
            copy = remote(a, slot, dst, dst, (rank, column))
            if condition is None:
                copy.wait_recv()
            else:

                @pl.when(condition)
                def _():
                    copy.wait_recv()

        def onward(a, kind):
            source, there = origin(kind)
            first, second = first_bits[a]
            src = piece(a, first, source)
            arrived(a, 6 + kind, src, there)
            dst = piece(a, first | second, source)
            go(remote(a, 20 + kind, src, dst, (other(second), column)), there)

        small = []

        def tiny(src, dst, to):
            at = len(small)
            copy = pltpu.make_async_remote_copy(
                src_ref=src,
                dst_ref=dst,
                send_sem=small_send.at[at],
                recv_sem=small_recv.at[at],
                device_id=to,
                device_id_type=MESH,
            )
            copy.start()
            small.append(copy)
            return copy

        for a in range(count):
            along(a, 0)
            spread(a, 0)
        for a in range(count):
            keep(sources[a], piece(a, 0, column))
        keep(bias_ref, bias_out.at[0])
        for dt in range(1, 4):
            to = differing(column, dt, 2)
            tiny(bias_ref, bias_out.at[dt], (rank, to))
        flat = []
        for ref, out_ref in ((proj_ref, proj_out), (picks_ref, picks_out)):
            keep(ref, out_ref.at[0])
            flat.append(
                (
                    tiny(ref, out_ref.at[place(2)], (other(2), column)),
                    tiny(ref, out_ref.at[place(4)], (other(4), column)),
                    tiny(ref, out_ref.at[place(1)], (other(1), column)),
                    out_ref,
                )
            )

        for hops in range(1, 4):
            for a in range(count):
                for kind in (hops, hops + 3):
                    source, there = origin(kind)
                    slot = hops - 1 if kind <= 3 else 2 + hops
                    arrived(a, slot, piece(a, 0, source), there)
                    along(a, kind)
                    spread(a, kind)
            kinds = (0,) if hops == 1 else (hops - 1, hops + 2)
            for a in range(count):
                for kind in kinds:
                    onward(a, kind)
        for copy in local:
            copy.wait()

        def sibling(a, slot, j):
            go(remote(a, slot, line(a, j), line(a, j | 1), (other(1), column)), None)

        for a in range(count):
            sibling(a, 27, 0)
        for by_two, by_four, _, out_ref in flat:
            by_two.wait_recv()
            tiny(out_ref.at[place(2)], out_ref.at[place(6)], (other(4), column))
            tiny(out_ref.at[place(2)], out_ref.at[place(3)], (other(1), column))
            by_four.wait_recv()
            tiny(out_ref.at[place(4)], out_ref.at[place(5)], (other(1), column))
        for a in range(count):
            for kind in (3, 6):
                onward(a, kind)
            sibling(a, 28, first_bits[a][0])
        for n, (_, _, _, out_ref) in enumerate(flat):
            small[9 + 3 * n].wait_recv()
            tiny(out_ref.at[place(6)], out_ref.at[place(7)], (other(1), column))
        for a in range(count):
            first, second = first_bits[a]
            for base_slot, j, slot in ((13, second, 29), (20, first | second, 30)):
                for kind in range(7):
                    source, there = origin(kind)
                    arrived(a, base_slot + kind, piece(a, j, source), there)
                sibling(a, slot, j)
        for n, copy in enumerate(small):
            if n not in (3, 4, 6, 7, 9, 12):
                copy.wait_recv()
            copy.wait_send()
        for q in range(2):
            mine = jnp.logical_and(lonely, column % 2 == q)
            for kind, (size, begin) in enumerate(((quarter, 0), (asked, docs))):
                dst = x_out.at[pl.ds(begin + q * size, size), :]
                copy = pltpu.make_async_remote_copy(
                    src_ref=dst,
                    dst_ref=dst,
                    send_sem=x_send.at[q, kind],
                    recv_sem=x_recv.at[q, kind],
                    device_id=(rank, column),
                    device_id_type=MESH,
                )

                @pl.when(jnp.logical_not(mine))
                def _():
                    copy.wait_recv()

        for mine, here, away in x_copies:

            @pl.when(mine)
            def _():
                here.wait()

            @pl.when(jnp.logical_not(mine))
            def _():
                away.wait_send()

        for a in range(count):
            for slot, j in ((27, 1), (28, first_bits[a][0] | 1), (29, first_bits[a][1] | 1), (30, 7)):
                arrived(a, slot, line(a, j), None)
        for condition, copy in waits:
            if condition is None:
                copy.wait_send()
            else:

                @pl.when(condition)
                def _():
                    copy.wait_send()

    out_shape = [jax.ShapeDtypeStruct((docs + 2 * asked, width), x_doc.dtype)]
    for w, f, t in zip(weights, feature_axis, tensor_axis):
        shape = list(w.shape)
        shape[f] *= groups
        shape[t] *= ways
        out_shape.append(jax.ShapeDtypeStruct(tuple(shape), w.dtype))
    out_shape += [
        jax.ShapeDtypeStruct((groups,) + proj.shape, proj.dtype),
        jax.ShapeDtypeStruct((ways,) + bias.shape, bias.dtype),
        jax.ShapeDtypeStruct((groups,) + picks.shape, picks.dtype),
    ]
    anywhere = pl.BlockSpec(memory_space=pl.ANY)
    dma = pltpu.SemaphoreType.DMA
    return pl.pallas_call(
        kernel,
        out_shape=out_shape,
        in_specs=[anywhere] * (5 + count),
        out_specs=[anywhere] * (4 + count),
        scratch_shapes=[
            dma((count, slots)),
            dma((count, slots)),
            dma((17,)),
            dma((17,)),
            dma((2, 2)),
            dma((2, 2)),
            dma((count + 3,)),
        ],
        compiler_params=pltpu.CompilerParams(collective_id=0, has_side_effects=True),
        name="gather_weights",
    )(x_doc, x_query, *weights, proj, bias, picks)


class Around:
    def __init__(self):
        self.rank = lax.axis_index("dp")
        self.column = lax.axis_index("tensor")
        self.core = self.rank % 2
        self.base = self.rank - self.core

    def other(self, bit):
        rank = self.rank
        return (rank + bit - 2 * bit * ((rank // bit) % 2), self.column)

    def along(self, dt):
        return (self.rank, differing(self.column, dt, 2))

    def meet(self):
        barrier = pltpu.get_barrier_semaphore()
        for dc in range(2):
            for dt in range(4):
                if dc + dt > 0:
                    pl.semaphore_signal(
                        barrier,
                        inc=1,
                        device_id=(self.base + (self.core + dc) % 2, (self.column + dt) % 4),
                        device_id_type=MESH,
                    )
        for bit in (2, 4):
            pl.semaphore_signal(
                barrier, inc=1, device_id=self.other(bit), device_id_type=MESH
            )
        pl.semaphore_wait(barrier, 9)


class Sender:
    def __init__(self, send_sem, recv_sem):
        self.send_sem, self.recv_sem = send_sem, recv_sem
        self.sent = []

    def __call__(self, src, dst, to):
        at = len(self.sent)
        copy = pltpu.make_async_remote_copy(
            src_ref=src,
            dst_ref=dst,
            send_sem=self.send_sem.at[at],
            recv_sem=self.recv_sem.at[at],
            device_id=to,
            device_id_type=MESH,
        )
        self.sent.append(copy)
        return copy

    def drain(self):
        for copy in self.sent:
            copy.wait_send()


class MatrixSum:
    def __init__(
        self, around, send, axis, across, own, got, next_, near, far, home, local_sems, pieces
    ):
        self.axis, self.own, self.got, self.next, self.near = axis, own, got, next_, near
        self.block = own.shape[axis] // 4
        first, second = (2, 4) if across else (4, 2)
        self.gone, self.later = ((1, 3), 2) if across else ((2, 3), 1)
        self.cores = [send(src, dst, around.other(1)) for src, dst in far]
        self.loads = [
            pltpu.make_async_copy(src, dst, sem) for (src, dst), sem in zip(home, local_sems)
        ]
        self.firsts = [
            send(self.at(own, n), self.at(next_, slot), around.other(first))
            for slot, n in enumerate(self.gone)
        ]
        self.second = send(self.at(own, self.later), near, around.other(second))
        self.pieces = [send(own.at[index], dst, around.along(dt)) for dt, index, dst in pieces]

    def at(self, ref, n):
        span = pl.ds(n * self.block, self.block)
        return ref.at[span, :] if self.axis == 0 else ref.at[:, span]

    def begin(self):
        for copy in self.cores + self.loads:
            copy.start()

    def add(self, n, ref, m):
        rows = self.block if self.axis == 0 else self.own.shape[0]
        step = 16 if self.axis == 0 else 128
        block = self.block

        @pl.loop(0, rows // step)
        def _(k):
            if self.axis == 0:
                to = (pl.ds(pl.multiple_of(n * block + k * step, step), step), slice(None))
                fr = (pl.ds(pl.multiple_of(m * block + k * step, step), step), slice(None))
            else:
                at = pl.ds(pl.multiple_of(k * step, step), step)
                to, fr = (at, pl.ds(n * block, block)), (at, pl.ds(m * block, block))
            self.own[to] = (self.own[to].astype(F32) + ref[fr].astype(F32)).astype(BF)

    def first_axis(self):
        for load in self.loads:
            load.wait()
        for copy in self.cores:
            copy.wait_recv()
        for n, copy in zip(self.gone, self.firsts):
            self.add(n, self.got, n)
            copy.start()
        for n in (self.later, 0):
            self.add(n, self.got, n)

    def second_axis(self):
        for copy in self.firsts:
            copy.wait_recv()
        self.add(self.later, self.next, 1)
        self.second.start()
        self.add(0, self.next, 0)

    def tensor(self):
        self.second.wait_recv()
        self.add(0, self.near, 0)
        for copy in self.pieces:
            copy.start()

    def settle(self):
        for copy in self.pieces:
            copy.wait_recv()


class SmallSum:
    def __init__(self, around, send, got, run, bits=(1, 4, 2), tensor=(1, 2)):
        self.got, self.run = got, run
        tos = [around.other(bit) for bit in bits] + [around.along(dt) for dt in tensor]
        self.copies = [send(run.at[n], got.at[n], to) for n, to in enumerate(tos)]

    def begin(self, value):
        self.run[0] = value
        self.copies[0].start()

    def hop(self, n):
        self.copies[n].wait_recv()
        self.run[n + 1] = self.run[n] + self.got[n]
        if n + 1 < len(self.copies):
            self.copies[n + 1].start()


class ProjSum:
    def __init__(self, around, send, ref, run, got):
        self.ref, self.run, self.got = ref, run, got
        rows = ref.shape[0]
        self.half = [rows // 2, rows // 4, rows // 8]
        starts = [0, rows // 2, 3 * rows // 4]
        self.starts = starts
        self.copies = [
            send(ref.at[self.half[0] :, :], got.at[pl.ds(starts[0], self.half[0]), :], around.other(1))
        ]
        for n, bit in ((1, 4), (2, 2)):
            self.copies.append(
                send(
                    run.at[pl.ds(self.half[n], self.half[n]), :],
                    got.at[pl.ds(starts[n], self.half[n]), :],
                    around.other(bit),
                )
            )
        last = self.half[2]
        self.last = last
        base = rows
        for n, dt in ((0, 1), (1, 2)):
            self.copies.append(
                send(
                    run.at[pl.ds(rows // 2 + n * last, last), :],
                    got.at[pl.ds(base + n * last, last), :],
                    around.along(dt),
                )
            )

    def begin(self):
        self.copies[0].start()

    def hop(self, n):
        self.copies[n].wait_recv()
        rows = self.ref.shape[0]
        last = self.last
        if n < 3:
            size = self.half[n]
            old = self.ref if n == 0 else self.run
            total = old[:size, :] + self.got[pl.ds(self.starts[n], size), :]
            if n < 2:
                self.run[:size, :] = total
            else:
                self.run[pl.ds(rows // 2, last), :] = total
        else:
            at = rows // 2 + (n - 3) * last
            got = self.got[pl.ds(rows + (n - 3) * last, last), :]
            self.run[pl.ds(at + last, last), :] = self.run[pl.ds(at, last), :] + got
        if n + 1 < len(self.copies):
            self.copies[n + 1].start()

    def result(self):
        return self.run[pl.ds(self.ref.shape[0] // 2 + 2 * self.last, self.last), :]


def finish_kernel(qkv, out, rows, tensor_sums):
    ways = 4
    width = qkv.shape[0]
    half, block = width // 2, width // 8
    share = width // ways
    docs = rows.shape[0] // 9 * 8
    quarter, asked = docs // 2, (rows.shape[0] - docs) // 2
    chunk = 16
    parts = 4
    part = 3 * share

    def kernel(
        qkv_ref, out_ref, rows_ref, ten_ref,
        qkv_o, out_o, doc_o, ask_o, ten_o,
        qa, q0, q1, q2, q3, oa, o0, o1, o2, o3, gd, ga, t_got, t_run, tz,
        send_sem, recv_sem, local_sem, row_send, row_recv,
    ):
        around = Around()
        rank, column, core, base = around.rank, around.column, around.core, around.base
        around.meet()
        send = Sender(send_sem, recv_sem)
        small = SmallSum(around, send, t_got, t_run, tensor=())
        spread = [send(t_run.at[3, dt], tz.at[dt - 1], around.along(dt)) for dt in range(1, ways)]
        across = (True, False, False, True)
        heads, feats = [], []
        for n in range(parts):
            spans = [(pl.ds(j * width + n * share, share), pl.ds(j * share, share)) for j in range(3)]
            heads.append(
                MatrixSum(
                    around, send, 0, across[n], qa.at[n], q0.at[n], q1.at[n], q2.at[n],
                    [(qkv_ref.at[half:, fr], q0.at[n, :, to]) for fr, to in spans],
                    [(qkv_ref.at[:half, fr], qa.at[n, :, to]) for fr, to in spans],
                    [local_sem.at[3 * n + j] for j in range(3)],
                    [
                        (n, (slice(0, block), pl.ds(j * share, share)), q3.at[n - 1, j])
                        for j in range(3)
                        if n > 0
                    ],
                )
            )
        for n in range(2):
            span = pl.ds(n * half, half)
            feats.append(
                MatrixSum(
                    around, send, 1, n == 0, oa.at[n], o0.at[n], o1.at[n], o2.at[n],
                    [(out_ref.at[span, half:], o0.at[n])],
                    [(out_ref.at[span, :half], oa.at[n])],
                    [local_sem.at[3 * parts + n]],
                    [
                        (dt, (pl.ds((dt % 2) * share, share), slice(0, block)), o3.at[dt - 1])
                        for dt in (2 * n, 2 * n + 1)
                        if dt > 0
                    ],
                )
            )
        items = [heads[2], heads[3], feats[1], heads[0], heads[1], feats[0]]
        small.begin(ten_ref[...])
        for item in items:
            item.begin()

        lonely = 3 * core == column
        row_copies = []
        for q in range(2):
            own = jnp.logical_and(lonely, core == q)
            for kind, (begin, size, buf) in enumerate(((0, quarter, gd), (docs, asked, ga))):
                src = rows_ref.at[pl.ds(begin + q * size, size), :]
                dst = buf.at[column // 2]
                away = pltpu.make_async_remote_copy(
                    src_ref=src,
                    dst_ref=dst,
                    send_sem=row_send.at[q, kind],
                    recv_sem=row_recv.at[column // 2, kind],
                    device_id=(base + column % 2, 2 * core + q),
                    device_id_type=MESH,
                )
                here = pltpu.make_async_copy(src, dst, row_send.at[q, kind])

                @pl.when(own)
                def _():
                    here.start()

                @pl.when(jnp.logical_not(own))
                def _():
                    away.start()

                row_copies.append((own, here, away))

        for n in range(0, len(items) + 4, 2):
            for item in items[n - 2 : n] if n >= 2 else []:
                item.second_axis()
            for item in items[n : n + 2]:
                item.first_axis()
            if n // 2 < 3:
                small.hop(n // 2)
            if n // 2 == 2:
                for copy in spread:
                    copy.start()
            for m in (n - 4, n - 3):
                if 0 <= m < len(items):
                    items[m].tensor()

        for m in range(2):
            own = jnp.logical_and(lonely, column // 2 == m)
            for kind, buf in enumerate((gd, ga)):
                copy = pltpu.make_async_remote_copy(
                    src_ref=buf.at[m],
                    dst_ref=buf.at[m],
                    send_sem=row_send.at[m, kind],
                    recv_sem=row_recv.at[m, kind],
                    device_id=(rank, column),
                    device_id_type=MESH,
                )

                @pl.when(jnp.logical_not(own))
                def _():
                    copy.wait_recv()

        for own, here, away in row_copies:

            @pl.when(own)
            def _():
                here.wait()

            @pl.when(jnp.logical_not(own))
            def _():
                away.wait_send()

        for m in range(2):

            @pl.loop(0, quarter // chunk)
            def _(n):
                at = pl.ds(pl.multiple_of(n * chunk, chunk), chunk)
                doc_o[m, at, :] = gd[m, at, :].astype(F32)

        ask_o[...] = ga[...].astype(F32)
        for copy in spread:
            copy.wait_recv()
        ten_o[...] = t_run[3, 0] + tz[0] + tz[1] + tz[2]
        for item in items:
            item.settle()
        for j in range(3):
            total = qa[0, :block, pl.ds(j * share, share)].astype(F32)
            for dt in range(ways - 1):
                total = total + q3[dt, j].astype(F32)
            qkv_o[j] = total
        total = oa[0, :share, :block].astype(F32)
        for dt in range(ways - 1):
            total = total + o3[dt].astype(F32)
        out_o[...] = total
        send.drain()

    def whole(x):
        return pl.BlockSpec(x.shape, lambda: (0,) * len(x.shape))

    out_shape = [
        jax.ShapeDtypeStruct((3, block, share), F32),
        jax.ShapeDtypeStruct((share, block), F32),
        jax.ShapeDtypeStruct((2, quarter, width), F32),
        jax.ShapeDtypeStruct((2, asked, width), F32),
        jax.ShapeDtypeStruct(tensor_sums.shape[1:], F32),
    ]
    anywhere = pl.BlockSpec(memory_space=pl.ANY)
    vmem = pltpu.VMEM
    dma = pltpu.SemaphoreType.DMA
    count = 6 + parts * 6 + 9 + 2 * 4 + 3
    return pl.pallas_call(
        kernel,
        out_shape=out_shape,
        in_specs=[anywhere] * 3 + [whole(tensor_sums)],
        out_specs=[whole(x) for x in out_shape],
        scratch_shapes=[
            vmem((parts, half, part), BF),
            vmem((parts, half, part), BF),
            vmem((parts, 2 * block, part), BF),
            vmem((parts, block, part), BF),
            vmem((ways - 1, 3, block, share), BF),
            vmem((2, half, half), BF),
            vmem((2, half, half), BF),
            vmem((2, half, 2 * block), BF),
            vmem((2, half, block), BF),
            vmem((ways - 1, share, block), BF),
            vmem((2, quarter, width), BF),
            vmem((2, asked, width), BF),
            vmem((3,) + tensor_sums.shape, F32),
            vmem((4,) + tensor_sums.shape, F32),
            vmem((ways - 1,) + tensor_sums.shape[1:], F32),
            dma((count,)),
            dma((count,)),
            dma((3 * parts + 2,)),
            dma((2, 2)),
            dma((2, 2)),
        ],
        compiler_params=pltpu.CompilerParams(
            collective_id=1, has_side_effects=True, vmem_limit_bytes=48 << 20
        ),
        name="last_sums",
    )(qkv, out, rows, tensor_sums)


def attention_backward_kernel(
    qkv, far_kv, grad, cosine, sine, far_cosine, far_sine, col_labels, own_labels, far_labels,
    up, back, vectors, proj,
):
    rows, width = qkv.shape[1:]
    docs = far_kv.shape[1]
    pairs = width // 128
    block = 128
    asked = rows - docs
    ways = 4
    half, own_block = width // 2, width // 8
    share = up.shape[1] // ways
    assert pairs == 8

    def kernel(
        qkv_ref, far_ref, g_ref, c_ref, s_ref, fc_ref, fs_ref, lc_ref, lo_ref, lf_ref,
        up_ref, back_ref, vec_ref, proj_ref,
        pre_ref, bias_ref, up_o, back_o, vec_o, proj_o,
        sums_own, sums_far, give, kept, got_kv,
        ua, u0, u1, u2, u3, ba, b0, b1, b2, b3, v_got, v_run, p_run, p_got,
        send_sem, recv_sem, local_sem,
    ):
        h = pl.program_id(0)
        around = Around()
        send = Sender(send_sem, recv_sem)
        ups, backs = [], []
        for n in range(ways):
            span = pl.ds(n * share, share)
            ups.append(
                MatrixSum(
                    around, send, 0, False, ua.at[n], u0.at[n], u1.at[n], u2.at[n],
                    [(up_ref.at[half:, span], u0.at[n])],
                    [(up_ref.at[:half, span], ua.at[n])],
                    [local_sem.at[n]],
                    [(n, (slice(0, own_block), slice(None)), u3.at[n - 1])] if n > 0 else [],
                )
            )
            backs.append(
                MatrixSum(
                    around, send, 1, True, ba.at[n], b0.at[n], b1.at[n], b2.at[n],
                    [(back_ref.at[span, half:], b0.at[n])],
                    [(back_ref.at[span, :half], ba.at[n])],
                    [local_sem.at[ways + n]],
                    [(n, (slice(None), slice(0, own_block)), b3.at[n - 1])] if n > 0 else [],
                )
            )
        couples = [(ups[n], backs[n]) for n in (2, 3, 1, 0)]
        small = SmallSum(around, send, v_got, v_run)
        mean_proj = ProjSum(around, send, proj_ref, p_run, p_got)
        gives = [send(give.at[n], got_kv.at[n], around.other(1)) for n in range(pairs)]
        lane = lax.broadcasted_iota(jnp.int32, (1, 128), 1)

        def finish(n):
            gives[n].wait_recv()
            at = pl.ds(n * 128, 128)
            for i in range(2):
                low = (kept[n % 2, i, :docs, :] + got_kv[n, i].astype(F32)).astype(BF)
                tail = kept[n % 2, i, docs:, :].astype(BF)
                pre_ref[i + 1, :docs, at] = low
                pre_ref[i + 1, docs:, at] = tail
                total = jnp.sum(low.astype(F32), axis=0, keepdims=True)
                total = total + jnp.sum(tail.astype(F32), axis=0, keepdims=True)
                bias_ref[i + 1 : i + 2, at] = total

        for step in range(pairs):

            @pl.when(h == step)
            def _(step=step):
                if step == 0:
                    around.meet()
                    small.begin(vec_ref[...])
                    mean_proj.begin()
                    for couple in couples:
                        for item in couple:
                            item.begin()
                else:
                    if 0 <= step - 2 < 4:
                        for item in couples[step - 2]:
                            item.second_axis()
                    if 0 <= step - 1 < 4:
                        for item in couples[step - 1]:
                            item.first_axis()
                    if step <= 5:
                        small.hop(step - 1)
                        mean_proj.hop(step - 1)
                    if 0 <= step - 3 < 4:
                        for item in couples[step - 3]:
                            item.tensor()
                    finish(step - 1)

        sums_own[...] = jnp.zeros_like(sums_own)
        sums_far[...] = jnp.zeros_like(sums_far)

        def part(start, size, keys, sames, sums):
            q_block = qkv_ref[0, pl.ds(start, size), :]
            g_block = g_ref[pl.ds(start, size), :]
            grads = []
            for head in range(2):
                mask = (lane // HEAD_WIDTH) == head
                q_head = jnp.where(mask, q_block, jnp.zeros_like(q_block))
                g_head = jnp.where(mask, g_block, jnp.zeros_like(g_block))
                scores = [
                    jnp.where(same, dot_nt(q_head, key), MASKED)
                    for (key, _), same in zip(keys, sames)
                ]
                top = functools.reduce(
                    jnp.maximum, [jnp.max(s, axis=-1, keepdims=True) for s in scores]
                )
                powers = [jnp.exp(s - top) for s in scores]
                total = functools.reduce(
                    jnp.add, [jnp.sum(p, axis=-1, keepdims=True) for p in powers]
                )
                inverse = 1.0 / total
                g_head = (g_head.astype(F32) * inverse).astype(BF)
                pulls = [dot_nt(g_head, value) for _, value in keys]
                mean = functools.reduce(
                    jnp.add,
                    [jnp.sum(p * d, axis=-1, keepdims=True) for p, d in zip(powers, pulls)],
                ) * inverse
                slopes = [(p * (d - mean)).astype(BF) for p, d in zip(powers, pulls)]
                got = functools.reduce(
                    jnp.add, [dot_nn(s, key) for s, (key, _) in zip(slopes, keys)]
                )
                grads.append(got * 0.125)
                for (ref, begin, many), s, p in zip(sums, slopes, powers):
                    ref[0, pl.ds(begin, many), :] += dot_tn(s, q_head)
                    ref[1, pl.ds(begin, many), :] += dot_tn(p.astype(BF), g_head)
            total = jnp.where(lane < HEAD_WIDTH, grads[0], grads[1])
            at = pl.ds(start, size)
            low = (total * c_ref[at, :] - turned(total) * s_ref[at, :]).astype(BF)
            pre_ref[0, at, pl.ds(pl.multiple_of(h * 128, 128), 128)] = low
            return jnp.sum(low.astype(F32), axis=0, keepdims=True)

        doc_keys = [
            (qkv_ref[1, :docs, :], qkv_ref[2, :docs, :]),
            (far_ref[0], far_ref[1]),
        ]
        bias = jnp.zeros((1, 128), F32)
        for at in range(docs // block):
            labels = lc_ref[pl.ds(at * block, block), :]
            bias = bias + part(
                at * block,
                block,
                doc_keys,
                [labels == lo_ref[...], labels == lf_ref[...]],
                [(sums_own, 0, docs), (sums_far, 0, docs)],
            )
        row = lax.broadcasted_iota(jnp.int32, (asked, asked), 0) // QLEN
        col = lax.broadcasted_iota(jnp.int32, (asked, asked), 1) // QLEN
        bias = bias + part(
            docs,
            asked,
            [(qkv_ref[1, docs:, :], qkv_ref[2, docs:, :])],
            [row == col],
            [(sums_own, docs, asked)],
        )
        bias_ref[0:1, pl.ds(pl.multiple_of(h * 128, 128), 128)] = bias
        side = h % 2
        kept[side, 0] = sums_own[0] * c_ref[...] - turned(sums_own[0]) * s_ref[...]
        kept[side, 1] = sums_own[1]
        give[h, 0] = (sums_far[0] * fc_ref[...] - turned(sums_far[0]) * fs_ref[...]).astype(BF)
        give[h, 1] = sums_far[1].astype(BF)
        for step in range(pairs):

            @pl.when(h == step)
            def _(step=step):
                gives[step].start()

        @pl.when(h == pairs - 1)
        def _():
            finish(pairs - 1)
            for couple in couples:
                for item in couple:
                    item.settle()
            up_o[...] = (
                ua[0, :own_block, :].astype(F32)
                + u3[0].astype(F32)
                + u3[1].astype(F32)
                + u3[2].astype(F32)
            )
            back_o[...] = (
                ba[0, :, :own_block].astype(F32)
                + b3[0].astype(F32)
                + b3[1].astype(F32)
                + b3[2].astype(F32)
            )
            vec_o[...] = v_run[5]
            proj_o[...] = mean_proj.result()
            send.drain()

    def whole(shape):
        return pl.BlockSpec(shape, lambda h: (0,) * len(shape))

    anywhere = pl.BlockSpec(memory_space=pl.ANY)
    vmem = pltpu.VMEM
    dma = pltpu.SemaphoreType.DMA
    columns = proj.shape[1]
    out_shape = [
        jax.ShapeDtypeStruct((3, rows, width), BF),
        jax.ShapeDtypeStruct((8, width), F32),
        jax.ShapeDtypeStruct((own_block, share), F32),
        jax.ShapeDtypeStruct((share, own_block), F32),
        jax.ShapeDtypeStruct(vectors.shape, F32),
        jax.ShapeDtypeStruct((own_block, columns), F32),
    ]
    count = 2 * (ways * 4 + 3) + 5 + 5 + pairs
    return pl.pallas_call(
        kernel,
        grid=(pairs,),
        in_specs=[
            pl.BlockSpec((3, rows, 128), lambda h: (0, 0, h)),
            pl.BlockSpec((2, docs, 128), lambda h: (0, 0, h)),
            pl.BlockSpec((rows, 128), lambda h: (0, h)),
            whole((rows, 128)),
            whole((rows, 128)),
            whole((docs, 128)),
            whole((docs, 128)),
            whole((docs, 1)),
            whole((1, docs)),
            whole((1, docs)),
            anywhere,
            anywhere,
            whole(vectors.shape),
            whole(proj.shape),
        ],
        out_specs=[whole(x.shape) for x in out_shape],
        out_shape=out_shape,
        scratch_shapes=[
            vmem((2, rows, 128), F32),
            vmem((2, docs, 128), F32),
            vmem((pairs, 2, docs, 128), BF),
            vmem((2, 2, rows, 128), F32),
            vmem((pairs, 2, docs, 128), BF),
            vmem((ways, half, share), BF),
            vmem((ways, half, share), BF),
            vmem((ways, 2 * own_block, share), BF),
            vmem((ways, own_block, share), BF),
            vmem((ways - 1, own_block, share), BF),
            vmem((ways, share, half), BF),
            vmem((ways, share, half), BF),
            vmem((ways, share, 2 * own_block), BF),
            vmem((ways, share, own_block), BF),
            vmem((ways - 1, share, own_block), BF),
            vmem((5,) + vectors.shape, F32),
            vmem((6,) + vectors.shape, F32),
            vmem((width, columns), F32),
            vmem((width + 2 * own_block, columns), F32),
            dma((count,)),
            dma((count,)),
            dma((2 * ways,)),
        ],
        compiler_params=pltpu.CompilerParams(
            collective_id=2, has_side_effects=True, vmem_limit_bytes=60 << 20
        ),
        name="attend_backward_and_sum",
        cost_estimate=pl.CostEstimate(
            flops=100 * rows * 2 * docs * width,
            bytes_accessed=4 * (6 * rows + 4 * docs) * width,
            transcendentals=rows * 2 * docs * width // 64,
        ),
    )(
        qkv, far_kv, grad, cosine, sine, far_cosine, far_sine, col_labels, own_labels, far_labels,
        up, back, vectors, proj,
    )


def body(
    x_doc,
    x_query,
    doc_cot,
    query_cot,
    lengths,
    positives,
    w_qkv,
    b_qkv,
    w_out,
    b_out,
    gain_one,
    shift_one,
    w_in,
    b_in,
    w_back,
    b_back,
    gain_two,
    shift_two,
    w_proj,
):
    ways = lax.axis_size("tensor")
    groups = lax.axis_size("dp")
    column = lax.axis_index("tensor")
    rank = lax.axis_index("dp")
    core = rank % 2
    chip = rank // 2
    chips = groups // 2
    micro, quarter, width = x_doc.shape
    asked = x_query.shape[1]
    segments = lengths.shape[2] - 1
    proj_width = w_proj.shape[1]
    heads_local = w_qkv.shape[2]
    units_local = w_in.shape[1]
    block = width // groups
    assert ways == 2 * micro and ways == 4

    def exchange(value, dr=0, dt=0):
        pairs = [
            (r * ways + t, (r ^ dr) * ways + (t ^ dt)) for r in range(groups) for t in range(ways)
        ]
        return lax.ppermute(value, AXES, pairs)

    chip_bits = []
    bit = 2
    while bit < groups:
        chip_bits.append(bit)
        bit *= 2

    def gather_weights(pack, reverse):
        pieces = [pack] + [exchange(pack, dt=j) for j in range(1, ways)]
        pieces = [(0, jnp.concatenate(pieces, axis=-1))]
        order = chip_bits[::-1] if reverse and len(chip_bits) == 2 else chip_bits
        for dr in order:
            pieces = pieces + [(j + dr // 2, exchange(p, dr=dr)) for j, p in pieces]
            if len(pieces) >= 4 or dr == order[-1]:
                pieces.sort(key=lambda item: item[0])
                pieces = [(0, jnp.concatenate([p for _, p in pieces], axis=-2))]
        (_, half), = pieces
        return jnp.concatenate([half, exchange(half, dr=1)], axis=-2)

    def gather_proj(pack):
        for dr in chip_bits + [1]:
            pack = jnp.concatenate([pack, exchange(pack, dr=dr)], axis=0)
        return pack

    unit_micro = column // 2
    unit_row = chip * 2 + column % 2

    def rows_in(docs, queries):
        blocks = jnp.concatenate([docs, queries], axis=1)
        got = []
        for j in range(2):
            send = jnp.where((column + j) % 2 == 0, blocks[0], blocks[1])
            pairs = []
            for r in range(groups):
                for t in range(ways):
                    m = (t + j) % 2
                    pairs.append(
                        (r * ways + t, ((r // 2) * 2 + t // 2) * ways + 2 * m + r % 2)
                    )
            got.append(lax.ppermute(send, AXES, pairs))
        first = jnp.where(unit_micro == 0, got[0], got[1])
        second = jnp.where(unit_micro == 0, got[1], got[0])
        return jnp.concatenate(
            [first[:quarter], second[:quarter], first[quarter:], second[quarter:]], axis=0
        )

    def quarters_out(first, second):
        got = []
        for j in range(2):
            send = jnp.where((unit_micro + j) % 2 == 0, first, second)
            pairs = []
            for r in range(groups):
                for t in range(ways):
                    m = t // 2
                    pairs.append(
                        (
                            r * ways + t,
                            ((r // 2) * 2 + t % 2) * ways + 2 * (r % 2) + (m + j) % 2,
                        )
                    )
            got.append(lax.ppermute(send, AXES, pairs))
        even = jnp.where(column % 2 == 0, got[0], got[1])
        odd = jnp.where(column % 2 == 0, got[1], got[0])
        return jnp.stack([even, odd])

    def rows_out(values):
        docs = 2 * quarter
        first = jnp.concatenate([values[:quarter], values[docs : docs + asked]], axis=0)
        second = jnp.concatenate([values[quarter:docs], values[docs + asked :]], axis=0)
        blocks = quarters_out(first, second)
        return blocks[:, :quarter], blocks[:, quarter:]

    place = jnp.arange(width, dtype=jnp.int32)
    step = place // block
    actual = (rank ^ (2 * (step % chips) + step // chips)) * block + place % block
    turn = (place[:, None] == actual[None, :]).astype(BF)

    bias_pack = jnp.concatenate([b_qkv.reshape(-1), b_in])
    own_picks = jnp.zeros((8, 128), jnp.int32).at[:micro, : positives.shape[1]].set(positives)
    if chips == 4:
        own_x, full_qkv, full_out, full_in, full_back, full_proj, biases, picks_rel = gather_kernel(
            x_doc, x_query, w_qkv, w_out, w_in, w_back, w_proj, bias_pack.reshape(-1, 128), own_picks
        )
        biases = [biases[j].reshape(-1) for j in range(ways)]
        full_proj = full_proj.reshape(width, proj_width)
    else:
        own_x = rows_in(x_doc, x_query)
        full_qkv = gather_weights(w_qkv, False)
        full_out = gather_weights(w_out.T, False).T
        full_in = gather_weights(w_in, False)
        full_back = gather_weights(w_back.T, False).T
        full_proj = gather_proj(w_proj)
        picks_rel = gather_proj(own_picks[None])
        biases = [bias_pack] + [exchange(bias_pack[None], dt=j)[0] for j in range(1, ways)]
    picks_rel = picks_rel[:, :micro, : positives.shape[1]].astype(F32)
    own_cot = rows_in(doc_cot.astype(BF), query_cot.astype(BF))
    bias_qkv = jnp.concatenate(
        [b[: 3 * heads_local].reshape(3, heads_local) for b in biases], axis=1
    )
    bias_in = jnp.concatenate([b[3 * heads_local :] for b in biases])
    params = jnp.stack(
        [b_out, gain_one, shift_one, b_back, gain_two, shift_two, b_out, b_out]
    )
    params = jnp.dot(params, turn.astype(F32), precision=FULL_PRECISION)
    b_out, gain_one, shift_one, b_back, gain_two, shift_two = [params[i] for i in range(6)]

    docs = 2 * quarter
    queries = 2 * asked
    rows = docs + queries
    sizes_all = lengths[unit_micro]
    sizes = sizes_all[unit_row]
    ends = jnp.cumsum(sizes[:-1])
    starts = jnp.concatenate([jnp.zeros((1,), jnp.int32), ends])

    def layout(first):
        index = first + jnp.arange(docs, dtype=jnp.int32)
        segment = jnp.sum((index[:, None] >= ends[None, :]).astype(jnp.int32), axis=1)
        labels = jnp.arange(starts.shape[0], dtype=jnp.int32)
        begin = jnp.sum(
            jnp.where(segment[:, None] == labels[None, :], starts[None, :], 0), axis=1
        )
        return segment, index - begin

    own_labels, own_places = layout(core * docs)
    far_labels, far_places = layout((1 - core) * docs)
    own_places = jnp.concatenate([own_places, jnp.arange(queries, dtype=jnp.int32) % QLEN])
    half = HEAD_WIDTH // 2
    rates = 10000.0 ** (-(2.0 * jnp.arange(half, dtype=F32)) / HEAD_WIDTH)

    def rotation(places):
        angle = places.astype(F32)[:, None] * rates[None, :]
        sine = jnp.sin(angle)
        return jnp.tile(jnp.cos(angle), (1, 4)), jnp.concatenate([-sine, sine] * 2, axis=1)

    cosine, sine = rotation(own_places)
    far_cosine, far_sine = rotation(far_places)
    cosines_three = jnp.stack([cosine * 0.125, cosine, jnp.ones_like(cosine)])
    sines_three = jnp.stack([sine * 0.125, sine, jnp.zeros_like(sine)])

    x_low = dot_nn(own_x, turn).astype(BF)
    qkv = project_heads(x_low, full_qkv, bias_qkv, cosines_three, sines_three)
    far_kv = exchange(qkv[1:, :docs], dr=1)
    label_args = (own_labels[:, None], own_labels[None, :], far_labels[None, :])
    mixed = attention_forward(qkv, far_kv, *label_args)
    branch = dot_nn(mixed, full_out)
    resid_one = x_low.astype(F32) + branch + b_out
    normed, norm_one_pull = jax.vjp(layer_norm, resid_one, gain_one, shift_one)
    normed_low = normed.astype(BF)
    inner = dot_nn(normed_low, full_in) + bias_in
    active, gelu_pull = jax.vjp(gelu_exact, inner)
    active_low = active.astype(BF)
    resid_two = normed + dot_nn(active_low, full_back) + b_back
    output, norm_two_pull = jax.vjp(layer_norm, resid_two, gain_two, shift_two)
    output_low = output.astype(BF)
    y_doc, y_query = rows_out(dot_nt(output_low, turn).astype(BF))
    projection = dot_nn(output_low, full_proj)
    unit, unit_pull = jax.vjp(normalize, projection)
    unit_low = unit.astype(BF)

    doc_unit = unit_low[:docs]
    query_unit = unit_low[docs:]

    def bit_of(dr, dt):
        return (rank // dr) % 2 == 1 if dr else (column // dt) % 2 == 1

    def join(value, dr, dt, axis=0):
        got = exchange(value, dr=dr, dt=dt)
        on = bit_of(dr, dt)
        low = jnp.where(on, got, value)
        high = jnp.where(on, value, got)
        return jnp.concatenate([low, high], axis=axis)

    def split_sum(value, dr, dt):
        on = bit_of(dr, dt)
        size = value.shape[0] // 2
        send = jnp.where(on, value[:size], value[size:])
        keep = jnp.where(on, value[size:], value[:size])
        return keep + exchange(send.astype(BF), dr=dr, dt=dt).astype(F32)

    steps = [(1, 0), (0, 1)] + [(dr, 0) for dr in chip_bits]
    all_queries = query_unit
    for dr, dt in steps:
        all_queries = join(all_queries, dr, dt)
    held = jnp.arange(groups, dtype=jnp.int32)
    held = rank ^ (2 * (held % chips) + held // chips)
    order = (jnp.arange(groups, dtype=jnp.int32)[:, None] == held[None, :]).astype(F32)
    picks = jnp.where(unit_micro == 0, picks_rel[:, 0], picks_rel[:, 1])
    picks = jnp.dot(order, picks, precision=FULL_PRECISION).astype(jnp.int32).reshape(-1)
    seg_labels = jnp.arange(segments, dtype=jnp.int32)
    member = (own_labels[:, None] == seg_labels[None, :]).astype(F32)
    cosines = dot_nt(doc_unit, all_queries)
    weight = jnp.exp(TAU * (cosines - 1.0))
    totals = jnp.einsum("js,ji->si", member, weight, precision=FULL_PRECISION)
    totals = totals + exchange(totals, dr=1)
    for dr, dt in steps[1:]:
        totals = join(totals, dr, dt)
    counts = sizes_all[:, :segments].reshape(-1).astype(F32)
    best = (jnp.log(totals) - jnp.log(counts)[:, None]) / TAU + 1.0
    score = jnp.sum(best.reshape(best.shape[0], -1, QLEN), axis=-1)
    logits = LOGIT_SCALE * score
    documents = jnp.arange(logits.shape[0], dtype=jnp.int32)
    chosen = (documents[:, None] == picks[None, :]).astype(F32)
    peak = jnp.max(logits, axis=0, keepdims=True)
    powers = jnp.exp(logits - peak)
    mass = jnp.sum(powers, axis=0, keepdims=True)
    losses = (peak + jnp.log(mass))[0] - jnp.sum(chosen * logits, axis=0)
    logit_grad = LOGIT_SCALE * (powers / mass - chosen)
    own_grad = lax.dynamic_slice_in_dim(logit_grad, unit_row * segments, segments, axis=0)
    own_total = lax.dynamic_slice_in_dim(totals, unit_row * segments, segments, axis=0)
    coef = jnp.repeat(own_grad, QLEN, axis=1) / own_total
    spread = jnp.einsum("js,si->ji", member, coef, precision=FULL_PRECISION)
    cosine_grad = (weight * spread).astype(BF)
    doc_grad = dot_nn(cosine_grad, all_queries)
    query_grad = dot_tn(cosine_grad, doc_unit)
    for dr, dt in steps[::-1]:
        query_grad = split_sum(query_grad, dr, dt)
    own_losses = lax.dynamic_slice_in_dim(losses, unit_row * (4 * asked // QLEN) + core * 2 * (asked // QLEN), 2 * (asked // QLEN))
    per = asked // QLEN
    loss_tiles = [
        jnp.broadcast_to(own_losses[i * per : (i + 1) * per, None], (per, 128)) for i in range(2)
    ]
    loss_out = quarters_out(loss_tiles[0], loss_tiles[1])[:, :, 0]

    class Reduction:
        def __init__(self, half, axis, reverse, last):
            self.bits = chip_bits if reverse and len(chip_bits) == 2 else chip_bits[::-1]
            self.left = sorted(chip_bits)
            self.axis, self.last = axis, last
            self.sends = [half(1).astype(BF)]
            self.hops = [(1, 0)]
            self.kept = lambda: half(0)
            self.stage = 0

        def advance(self):
            total = self.kept()
            for s, (dr, dt) in zip(self.sends, self.hops):
                got = exchange(s, dr=dr, dt=dt).astype(F32)
                total = got if total is None else total + got
            if self.stage == len(self.bits) + 1:
                return total
            if self.stage < len(self.bits):
                dr = self.bits[self.stage]
                at = self.left.index(dr)
                self.left.remove(dr)
                size = block << at
                stay, send = [
                    jnp.concatenate(
                        [
                            lax.slice_in_dim(total, b, b + size, axis=self.axis)
                            for b in range(side * size, total.shape[self.axis], 2 * size)
                        ],
                        axis=self.axis,
                    )
                    for side in (0, 1)
                ]
                self.sends = [send.astype(BF)]
                self.hops = [(dr, 0)]
            else:
                stay, sends = self.last(total)
                self.sends = [piece.astype(BF) for _, piece in sends]
                self.hops = [(0, dt) for dt, _ in sends]
            self.kept = lambda: stay
            self.stage += 1
            return None

        def finish(self):
            total = None
            while total is None:
                total = self.advance()
            return total

    def weight_sum(left, right, axis, reverse):
        size = width // 2

        def half(n):
            if axis == 0:
                return dot_tn(left[:, n * size : (n + 1) * size], right)
            return dot_tn(left, right[:, n * size : (n + 1) * size])

        def last(total):
            size = total.shape[1 - axis] // ways
            pieces = [
                lax.slice_in_dim(total, j * size, (j + 1) * size, axis=1 - axis)
                for j in range(ways)
            ]
            return pieces[0], [(j, pieces[j]) for j in range(1, ways)]

        return Reduction(half, axis, reverse, last)

    def after(value, reductions):
        sends = [r.sends for r in reductions]
        value, sends = lax.optimization_barrier((value, sends))
        for r, s in zip(reductions, sends):
            r.sends = s
        return value

    unit_grad = jnp.concatenate([doc_grad, query_grad], axis=0)
    (proj_grad,) = unit_pull(unit_grad)
    proj_low = proj_grad.astype(BF)
    out_grad = own_cot_turned = dot_nn(own_cot, turn) + dot_nt(proj_low, full_proj)
    resid_two_grad, gain_two_grad, shift_two_grad = norm_two_pull(out_grad)
    update_low = resid_two_grad.astype(BF)
    whole_path = chips == 4
    if whole_path:
        back_grad = dot_tn(active_low, update_low).astype(BF)
    else:
        sum_back = weight_sum(active_low, update_low, 1, True)
    active_grad = dot_nt(update_low, full_back)
    (inner_grad,) = gelu_pull(active_grad)
    inner_low = inner_grad.astype(BF)
    if whole_path:
        in_grad = dot_tn(normed_low, inner_low).astype(BF)
    else:
        sum_in = weight_sum(normed_low, inner_low, 0, False)
    normed_grad = dot_nt(inner_low, full_in) + resid_two_grad
    resid_one_grad, gain_one_grad, shift_one_grad = norm_one_pull(normed_grad)
    branch_low = resid_one_grad.astype(BF)
    mixed_grad = dot_nt(branch_low, full_out).astype(BF)
    grad_proj = dot_tn(output_low, proj_low)
    zero = jnp.zeros((width,), F32)
    vectors = jnp.stack(
        [
            jnp.sum(branch_low.astype(F32), axis=0),
            gain_one_grad,
            shift_one_grad,
            jnp.sum(update_low.astype(F32), axis=0),
            gain_two_grad,
            shift_two_grad,
            zero,
            zero,
        ]
    )
    vectors = lax.dot_general(
        vectors, turn.astype(F32), (((1,), (1,)), ((), ())), precision=FULL_PRECISION
    )

    def heads_sum(rights, first_block, blocks, reverse):
        size = width // 2
        many = rights.shape[1] // 3 // blocks

        def half(n):
            return dot_tn(x_low[:, n * size : (n + 1) * size], rights)

        def last(total):
            stay, sends = None, []
            for b in range(blocks):
                piece = jnp.stack(
                    [total[:, (j * blocks + b) * many : (j * blocks + b + 1) * many] for j in range(3)]
                )
                if first_block + b == 0:
                    stay = piece
                else:
                    sends.append((first_block + b, piece))
            return stay, sends

        return Reduction(half, 0, reverse, last)

    inner_bias = jnp.sum(inner_low.astype(F32), axis=0).reshape(ways, units_local)
    if whole_path:
        pre, head_bias, out_in, out_back, vectors, grad_proj = attention_backward_kernel(
            qkv,
            far_kv,
            mixed_grad,
            cosine,
            sine,
            far_cosine,
            far_sine,
            *label_args,
            in_grad,
            back_grad,
            vectors,
            grad_proj,
        )
        head_bias = head_bias[:3].reshape(3, ways, heads_local)
        pre = [pre[j] for j in range(3)]
    else:
        head_sums, head_rights = [], []
        running = [sum_back, sum_in]
        per_block = heads_local // 128
        sum_out = weight_sum(mixed, branch_low, 1, False)
        for first_block, blocks in ((0, 2), (2, 1), (3, 1)):
            for item in running:
                item.advance()
            mixed_grad = after(mixed_grad, running)
            dq, own_grads, give = attention_backward(
                first_block * per_block,
                blocks * per_block,
                qkv,
                far_kv,
                mixed_grad,
                cosine,
                sine,
                far_cosine,
                far_sine,
                *label_args,
            )
            got = exchange(give, dr=1).astype(F32)
            rights = [dq] + [
                jnp.concatenate(
                    [own_grads[i, :docs] + got[i], own_grads[i, docs:]], axis=0
                ).astype(BF)
                for i in range(2)
            ]
            head_rights.append(rights)
            head_sums.append(
                heads_sum(jnp.concatenate(rights, axis=1), first_block, blocks, first_block > 0)
            )
        out_back = sum_back.finish()
        out_in = sum_in.finish()
        pre = [jnp.concatenate([part[j] for part in head_rights], axis=1) for j in range(3)]
        head_bias = jnp.stack([jnp.sum(p.astype(F32), axis=0) for p in pre])
        head_bias = head_bias.reshape(3, ways, heads_local)
    x_grad = resid_one_grad
    for j in range(3):
        x_grad = x_grad + dot_nt(pre[j], full_qkv[j])
    x_grad = dot_nt(x_grad.astype(BF), turn).astype(BF)
    tensor_grads = jnp.concatenate(
        [jnp.swapaxes(head_bias, 0, 1).reshape(ways, 3 * heads_local), inner_bias], axis=1
    )
    if whole_path:
        out_qkv, out_out, gx_doc, gx_query, tensor_grads = finish_kernel(
            jnp.concatenate([dot_tn(x_low, p).astype(BF) for p in pre], axis=1),
            dot_tn(mixed, branch_low).astype(BF),
            x_grad,
            tensor_grads.reshape(ways, -1, 128),
        )
        tensor_grads = tensor_grads.reshape(-1)
    else:
        gx_doc, gx_query = rows_out(x_grad)
        gx_doc, gx_query = gx_doc.astype(F32), gx_query.astype(F32)
        out_out = sum_out.finish()
        out_qkv = functools.reduce(jnp.add, [item.finish() for item in head_sums])
        for dr in [1] + chip_bits[::-1]:
            size = grad_proj.shape[0] // 2
            got = exchange(grad_proj[size:].astype(BF), dr=dr)
            grad_proj = grad_proj[:size] + got.astype(F32)
        for dt in (1, 2):
            grad_proj = grad_proj + exchange(grad_proj, dt=dt)
        for dt in (2, 1):
            tensor_grads = tensor_grads[:dt] + exchange(tensor_grads[dt:], dt=dt)
            vectors = vectors + exchange(vectors, dt=dt)
        for dr in [1] + chip_bits:
            tensor_grads = tensor_grads + exchange(tensor_grads, dr=dr)
            vectors = vectors + exchange(vectors, dr=dr)
        tensor_grads = tensor_grads[0]
    return (
        y_doc,
        y_query,
        loss_out,
        gx_doc,
        gx_query,
        out_qkv,
        tensor_grads[: 3 * heads_local].reshape(3, heads_local),
        out_out,
        vectors[0],
        vectors[1],
        vectors[2],
        out_in,
        tensor_grads[3 * heads_local :],
        out_back,
        vectors[3],
        vectors[4],
        vectors[5],
        grad_proj,
    )


def solution(mesh):
    rows = P(None, ("dp", "tensor"), None)
    in_specs = (
        rows,
        rows,
        rows,
        rows,
        P(),
        P(None, "dp"),
        P(None, "dp", "tensor"),
        P(None, "tensor"),
        P("tensor", "dp"),
        P(),
        P(),
        P(),
        P("dp", "tensor"),
        P("tensor"),
        P("tensor", "dp"),
        P(),
        P(),
        P(),
        P("dp", None),
    )
    out_specs = (
        rows,
        rows,
        P(None, ("dp", "tensor")),
        rows,
        rows,
        P(None, "dp", "tensor"),
        P(None, "tensor"),
        P("tensor", "dp"),
        P(),
        P(),
        P(),
        P("dp", "tensor"),
        P("tensor"),
        P("tensor", "dp"),
        P(),
        P(),
        P(),
        P("dp", None),
    )
    return jax.shard_map(body, mesh=mesh, in_specs=in_specs, out_specs=out_specs, check_vma=False)
```

```python
import functools

import jax
import jax.numpy as jnp
from jax import lax
from jax.experimental import pallas as pl
from jax.experimental.pallas import tpu as pltpu
from jax.sharding import PartitionSpec as P

HEAD_WIDTH = 64
QLEN = 32
FULL_PRECISION = lax.Precision.HIGHEST
TAU = 20.0
EPS = 1e-05
LOGIT_SCALE = 2.0
MASKED = -1e30
AXES = ("dp", "tensor")
MESH = pl.DeviceIdType.MESH
BF = jnp.bfloat16
F32 = jnp.float32


def layer_norm(values, gain, shift):
    center = values - jnp.mean(values, axis=-1, keepdims=True)
    spread = jnp.mean(center * center, axis=-1, keepdims=True)
    return center * lax.rsqrt(spread + EPS) * gain + shift


def normalize(values):
    return values * lax.rsqrt(jnp.sum(values * values, axis=-1, keepdims=True) + 1e-06)


def gelu_exact(values):
    return jax.nn.gelu(values, approximate=False)


def dot_nn(a, b):
    return lax.dot_general(a, b, (((1,), (0,)), ((), ())), preferred_element_type=F32)


def dot_nt(a, b):
    return lax.dot_general(a, b, (((1,), (1,)), ((), ())), preferred_element_type=F32)


def dot_tn(a, b):
    return lax.dot_general(a, b, (((0,), (0,)), ((), ())), preferred_element_type=F32)


def differing(a, b, bits):
    total = 0
    for bit in range(bits):
        x, y = (a // 2**bit) % 2, (b // 2**bit) % 2
        total = total + 2**bit * (x + y - 2 * x * y)
    return total


class Around:
    def __init__(self):
        self.rank = lax.axis_index("dp")
        self.column = lax.axis_index("tensor")
        self.core = self.rank % 2
        self.base = self.rank - self.core

    def other(self, bit):
        rank = self.rank
        return (rank + bit - 2 * bit * ((rank // bit) % 2), self.column)

    def along(self, dt):
        return (self.rank, differing(self.column, dt, 2))

    def meet(self):
        barrier = pltpu.get_barrier_semaphore()
        for dc in range(2):
            for dt in range(4):
                if dc + dt > 0:
                    pl.semaphore_signal(
                        barrier,
                        inc=1,
                        device_id=(self.base + (self.core + dc) % 2, (self.column + dt) % 4),
                        device_id_type=MESH,
                    )
        for bit in (2, 4):
            pl.semaphore_signal(
                barrier, inc=1, device_id=self.other(bit), device_id_type=MESH
            )
        pl.semaphore_wait(barrier, 9)


class Sender:
    def __init__(self, send_sem, recv_sem):
        self.send_sem, self.recv_sem = send_sem, recv_sem
        self.sent = []

    def __call__(self, src, dst, to):
        at = len(self.sent)
        copy = pltpu.make_async_remote_copy(
            src_ref=src,
            dst_ref=dst,
            send_sem=self.send_sem.at[at],
            recv_sem=self.recv_sem.at[at],
            device_id=to,
            device_id_type=MESH,
        )
        self.sent.append(copy)
        return copy

    def drain(self):
        for copy in self.sent:
            copy.wait_send()


class RowMoves:
    def __init__(self, around, inward, docs, asked, packed, send_sem, recv_sem):
        core, column, base = around.core, around.column, around.base
        lonely = 3 * core == column
        self.copies, self.arrivals = [], []
        size, few = docs.shape[1], asked.shape[1]
        for n in range(2):
            q, m = (column % 2, n) if inward else (n, column // 2)
            if inward:
                mine = jnp.logical_and(lonely, column // 2 == n)
                to = (base + column // 2, 2 * n + core)
                here = jnp.logical_and(lonely, column % 2 == n)
            else:
                mine = jnp.logical_and(lonely, core == n)
                to = (base + column % 2, 2 * core + n)
                here = jnp.logical_and(lonely, column // 2 == n)
            for kind, (ref, many, begin) in enumerate(((docs, size, 0), (asked, few, 2 * size))):
                rows = packed.at[pl.ds(pl.multiple_of(begin + q * many, few), many), :]
                src, dst = (ref.at[m], rows) if inward else (rows, ref.at[m])
                away = pltpu.make_async_remote_copy(
                    src_ref=src,
                    dst_ref=dst,
                    send_sem=send_sem.at[n, kind],
                    recv_sem=recv_sem.at[q if inward else m, kind],
                    device_id=to,
                    device_id_type=MESH,
                )
                local = pltpu.make_async_copy(src, dst, send_sem.at[n, kind])
                self.copies.append((mine, local, away))
                if inward:
                    land = packed.at[pl.ds(begin + n * many, many), :]
                else:
                    land = ref.at[n]
                came = pltpu.make_async_remote_copy(
                    src_ref=land,
                    dst_ref=land,
                    send_sem=send_sem.at[n, kind],
                    recv_sem=recv_sem.at[n, kind],
                    device_id=to,
                    device_id_type=MESH,
                )
                self.arrivals.append((here, came))

    def start(self):
        for mine, local, away in self.copies:

            @pl.when(mine)
            def _(local=local):
                local.start()

            @pl.when(jnp.logical_not(mine))
            def _(away=away):
                away.start()

    def wait(self):
        for here, came in self.arrivals:

            @pl.when(jnp.logical_not(here))
            def _(came=came):
                came.wait_recv()

        for mine, local, away in self.copies:

            @pl.when(mine)
            def _(local=local):
                local.wait()

            @pl.when(jnp.logical_not(mine))
            def _(away=away):
                away.wait_send()


def turned(values):
    lane = lax.broadcasted_iota(jnp.int32, (1, 128), 1)
    ahead = pltpu.roll(values, 96, 1)
    behind = pltpu.roll(values, 32, 1)
    return jnp.where(lane % HEAD_WIDTH < HEAD_WIDTH // 2, ahead, behind)


def project_heads(x, weights, bias, cosine, sine, docs, remote):
    rows, width = x.shape
    columns = 256
    steps = width // columns

    def kernel(x_ref, w_ref, b_ref, c_ref, s_ref, o_ref, *rest):
        j, n = pl.program_id(0), pl.program_id(1)
        got = dot_nn(x_ref[...], w_ref[0]) + b_ref[0]
        low = []
        for at in range(0, columns, 128):
            piece = got[:, at : at + 128]
            low.append((piece * c_ref[0] + turned(piece) * s_ref[0]).astype(BF))
            o_ref[0, :, at : at + 128] = low[-1]
        if not remote:
            return
        far_ref, held, send_sem, recv_sem = rest
        rank, column = lax.axis_index("dp"), lax.axis_index("tensor")
        sibling = (rank + 1 - 2 * (rank % 2), column)
        copies = [
            pltpu.make_async_remote_copy(
                src_ref=held.at[i, m],
                dst_ref=far_ref.at[i, :, pl.ds(m * columns, columns)],
                send_sem=send_sem.at[i, m],
                recv_sem=recv_sem.at[i, m],
                device_id=sibling,
                device_id_type=MESH,
            )
            for i in range(2)
            for m in range(steps)
        ]

        @pl.when(jnp.logical_and(j == 0, n == 0))
        def _():
            barrier = pltpu.get_barrier_semaphore()
            pl.semaphore_signal(barrier, inc=1, device_id=sibling, device_id_type=MESH)
            pl.semaphore_wait(barrier, 1)

        for i in range(2):
            for m in range(steps):

                @pl.when(jnp.logical_and(j == i, n == m))
                def _(i=i, m=m):
                    for at, piece in enumerate(low):
                        held[i, m, :, at * 128 : (at + 1) * 128] = piece[:docs]
                    copies[i * steps + m].start()

        @pl.when(jnp.logical_and(j == 2, n == steps - 1))
        def _():
            for copy in copies:
                copy.wait()

    order = lambda j: (j + 1) % 3
    out_specs = [pl.BlockSpec((1, rows, columns), lambda j, n: (order(j), 0, n))]
    out_shape = [jax.ShapeDtypeStruct((3, rows, width), BF)]
    extra = {}
    if remote:
        out_specs.append(pl.BlockSpec(memory_space=pl.ANY))
        out_shape.append(jax.ShapeDtypeStruct((2, docs, width), BF))
        extra = dict(
            scratch_shapes=[
                pltpu.VMEM((2, steps, docs, columns), BF),
                pltpu.SemaphoreType.DMA((2, steps)),
                pltpu.SemaphoreType.DMA((2, steps)),
            ]
        )
        params = pltpu.CompilerParams(
            vmem_limit_bytes=40 << 20, collective_id=3, has_side_effects=True
        )
    else:
        params = pltpu.CompilerParams(vmem_limit_bytes=40 << 20)
    return pl.pallas_call(
        kernel,
        grid=(3, steps),
        in_specs=[
            pl.BlockSpec((rows, width), lambda j, n: (0, 0)),
            pl.BlockSpec((1, width, columns), lambda j, n: (order(j), 0, n)),
            pl.BlockSpec((1, 1, columns), lambda j, n: (order(j), 0, n)),
            pl.BlockSpec((1, rows, 128), lambda j, n: (order(j), 0, 0)),
            pl.BlockSpec((1, rows, 128), lambda j, n: (order(j), 0, 0)),
        ],
        out_specs=out_specs,
        out_shape=out_shape,
        compiler_params=params,
        name="project_heads",
        cost_estimate=pl.CostEstimate(
            flops=6 * rows * width * width, bytes_accessed=6 * width * width, transcendentals=0
        ),
        **extra,
    )(x, weights, bias[:, None, :], cosine, sine)


def attention_forward(qkv, far_kv, col_labels, own_labels, far_labels, cots=None):
    rows, width = qkv.shape[1:]
    docs = far_kv.shape[1]
    block = 128
    asked = rows - docs

    def kernel(qkv_ref, far_ref, lc_ref, lo_ref, lf_ref, *rest):
        if cots is None:
            (o_ref,) = rest
        else:
            cd_ref, cq_ref, o_ref, c_ref, send_sem, recv_sem = rest
            around = Around()
            moves = RowMoves(around, True, cd_ref, cq_ref, c_ref, send_sem, recv_sem)

            @pl.when(pl.program_id(0) == 0)
            def _():
                around.meet()
                moves.start()

        lane = lax.broadcasted_iota(jnp.int32, (1, 128), 1)

        def part(start, size, keys, sames):
            q_block = qkv_ref[0, pl.ds(start, size), :]
            outs = []
            for head in range(2):
                mask = (lane // HEAD_WIDTH) == head
                q_head = jnp.where(mask, q_block, jnp.zeros_like(q_block))
                scores = [
                    jnp.where(same, dot_nt(q_head, key), MASKED)
                    for (key, _), same in zip(keys, sames)
                ]
                top = functools.reduce(
                    jnp.maximum, [jnp.max(s, axis=-1, keepdims=True) for s in scores]
                )
                powers = [jnp.exp(s - top) for s in scores]
                total = functools.reduce(
                    jnp.add, [jnp.sum(p, axis=-1, keepdims=True) for p in powers]
                )
                mixed = functools.reduce(
                    jnp.add, [dot_nn(p.astype(BF), value) for p, (_, value) in zip(powers, keys)]
                )
                outs.append(mixed * (1.0 / total))
            o_ref[pl.ds(start, size), :] = jnp.where(lane < HEAD_WIDTH, outs[0], outs[1]).astype(BF)

        doc_keys = [
            (qkv_ref[1, :docs, :], qkv_ref[2, :docs, :]),
            (far_ref[0], far_ref[1]),
        ]
        for at in range(docs // block):
            labels = lc_ref[pl.ds(at * block, block), :]
            part(at * block, block, doc_keys, [labels == lo_ref[...], labels == lf_ref[...]])
        row = lax.broadcasted_iota(jnp.int32, (asked, asked), 0) // QLEN
        col = lax.broadcasted_iota(jnp.int32, (asked, asked), 1) // QLEN
        part(docs, asked, [(qkv_ref[1, docs:, :], qkv_ref[2, docs:, :])], [row == col])
        if cots is not None:

            @pl.when(pl.program_id(0) == width // 128 - 1)
            def _():
                moves.wait()

    in_more, out_more, shape_more, extra = [], [], [], {}
    params = pltpu.CompilerParams(vmem_limit_bytes=40 << 20)
    if cots is not None:
        anywhere = pl.BlockSpec(memory_space=pl.ANY)
        in_more, out_more = [anywhere, anywhere], [anywhere]
        shape_more = [jax.ShapeDtypeStruct((rows, cots[0].shape[2]), cots[0].dtype)]
        dma = pltpu.SemaphoreType.DMA
        extra = dict(scratch_shapes=[dma((2, 2)), dma((2, 2))])
        params = pltpu.CompilerParams(
            vmem_limit_bytes=40 << 20, collective_id=4, has_side_effects=True
        )

    whole = lambda shape: pl.BlockSpec(shape, lambda h: (0, 0))
    return pl.pallas_call(
        kernel,
        grid=(width // 128,),
        in_specs=[
            pl.BlockSpec((3, rows, 128), lambda h: (0, 0, h)),
            pl.BlockSpec((2, docs, 128), lambda h: (0, 0, h)),
            whole((docs, 1)),
            whole((1, docs)),
            whole((1, docs)),
        ]
        + in_more,
        out_specs=[pl.BlockSpec((rows, 128), lambda h: (0, h))] + out_more,
        out_shape=[jax.ShapeDtypeStruct((rows, width), BF)] + shape_more,
        compiler_params=params,
        name="attend_forward",
        cost_estimate=pl.CostEstimate(
            flops=32 * rows * 2 * docs * width,
            bytes_accessed=2 * (4 * rows + 2 * docs) * width,
            transcendentals=rows * 2 * docs * width // 64,
        ),
        **extra,
    )(qkv, far_kv, col_labels, own_labels, far_labels, *(cots or ()))


def attention_backward(
    first, count, qkv, far_kv, grad, cosine, sine, far_cosine, far_sine,
    col_labels, own_labels, far_labels,
):
    rows = qkv.shape[1]
    docs = far_kv.shape[1]
    width = count * 128
    block = 128
    asked = rows - docs

    def kernel(
        qkv_ref, far_ref, g_ref, c_ref, s_ref, fc_ref, fs_ref, lc_ref, lo_ref, lf_ref,
        dq_ref, own_ref, give_ref, sums_own, sums_far,
    ):
        lane = lax.broadcasted_iota(jnp.int32, (1, 128), 1)
        sums_own[...] = jnp.zeros_like(sums_own)
        sums_far[...] = jnp.zeros_like(sums_far)

        def part(start, size, keys, sames, sums):
            q_block = qkv_ref[0, pl.ds(start, size), :]
            g_block = g_ref[pl.ds(start, size), :]
            grads = []
            for head in range(2):
                mask = (lane // HEAD_WIDTH) == head
                q_head = jnp.where(mask, q_block, jnp.zeros_like(q_block))
                g_head = jnp.where(mask, g_block, jnp.zeros_like(g_block))
                scores = [
                    jnp.where(same, dot_nt(q_head, key), MASKED)
                    for (key, _), same in zip(keys, sames)
                ]
                top = functools.reduce(
                    jnp.maximum, [jnp.max(s, axis=-1, keepdims=True) for s in scores]
                )
                powers = [jnp.exp(s - top) for s in scores]
                total = functools.reduce(
                    jnp.add, [jnp.sum(p, axis=-1, keepdims=True) for p in powers]
                )
                inverse = 1.0 / total
                g_head = (g_head.astype(F32) * inverse).astype(BF)
                pulls = [dot_nt(g_head, value) for _, value in keys]
                mean = functools.reduce(
                    jnp.add,
                    [jnp.sum(p * d, axis=-1, keepdims=True) for p, d in zip(powers, pulls)],
                ) * inverse
                slopes = [(p * (d - mean)).astype(BF) for p, d in zip(powers, pulls)]
                got = functools.reduce(
                    jnp.add, [dot_nn(s, key) for s, (key, _) in zip(slopes, keys)]
                )
                grads.append(got * 0.125)
                for (ref, begin, many), s, p in zip(sums, slopes, powers):
                    ref[0, pl.ds(begin, many), :] += dot_tn(s, q_head)
                    ref[1, pl.ds(begin, many), :] += dot_tn(p.astype(BF), g_head)
            whole = jnp.where(lane < HEAD_WIDTH, grads[0], grads[1])
            at = pl.ds(start, size)
            dq_ref[at, :] = (whole * c_ref[at, :] - turned(whole) * s_ref[at, :]).astype(BF)

        doc_keys = [
            (qkv_ref[1, :docs, :], qkv_ref[2, :docs, :]),
            (far_ref[0], far_ref[1]),
        ]
        for at in range(docs // block):
            labels = lc_ref[pl.ds(at * block, block), :]
            part(
                at * block,
                block,
                doc_keys,
                [labels == lo_ref[...], labels == lf_ref[...]],
                [(sums_own, 0, docs), (sums_far, 0, docs)],
            )
        row = lax.broadcasted_iota(jnp.int32, (asked, asked), 0) // QLEN
        col = lax.broadcasted_iota(jnp.int32, (asked, asked), 1) // QLEN
        part(
            docs,
            asked,
            [(qkv_ref[1, docs:, :], qkv_ref[2, docs:, :])],
            [row == col],
            [(sums_own, docs, asked)],
        )
        own_ref[0] = sums_own[0] * c_ref[...] - turned(sums_own[0]) * s_ref[...]
        own_ref[1] = sums_own[1]
        give_ref[0] = (sums_far[0] * fc_ref[...] - turned(sums_far[0]) * fs_ref[...]).astype(BF)
        give_ref[1] = sums_far[1].astype(BF)

    whole = lambda shape: pl.BlockSpec(shape, lambda h: (0, 0))
    return pl.pallas_call(
        kernel,
        grid=(count,),
        in_specs=[
            pl.BlockSpec((3, rows, 128), lambda h: (0, 0, h + first)),
            pl.BlockSpec((2, docs, 128), lambda h: (0, 0, h + first)),
            pl.BlockSpec((rows, 128), lambda h: (0, h + first)),
            whole((rows, 128)),
            whole((rows, 128)),
            whole((docs, 128)),
            whole((docs, 128)),
            whole((docs, 1)),
            whole((1, docs)),
            whole((1, docs)),
        ],
        out_specs=[
            pl.BlockSpec((rows, 128), lambda h: (0, h)),
            pl.BlockSpec((2, rows, 128), lambda h: (0, 0, h)),
            pl.BlockSpec((2, docs, 128), lambda h: (0, 0, h)),
        ],
        out_shape=[
            jax.ShapeDtypeStruct((rows, width), BF),
            jax.ShapeDtypeStruct((2, rows, width), F32),
            jax.ShapeDtypeStruct((2, docs, width), BF),
        ],
        scratch_shapes=[pltpu.VMEM((2, rows, 128), F32), pltpu.VMEM((2, docs, 128), F32)],
        compiler_params=pltpu.CompilerParams(vmem_limit_bytes=40 << 20),
        name="attend_backward",
        cost_estimate=pl.CostEstimate(
            flops=100 * rows * 2 * docs * width,
            bytes_accessed=4 * (6 * rows + 4 * docs) * width,
            transcendentals=rows * 2 * docs * width // 64,
        ),
    )(
        qkv, far_kv, grad, cosine, sine, far_cosine, far_sine, col_labels, own_labels, far_labels
    )


def gather_kernel(x_doc, x_query, qkv, out, up, back, proj, bias, picks):
    chips, ways = 4, 4
    groups = 2 * chips
    weights = [qkv, out, up, back]
    feature_axis = [1, 1, 0, 1]
    tensor_axis = [2, 0, 1, 0]
    first_bits = [(2, 4), (4, 2), (2, 4), (4, 2)]
    count = len(weights)
    quarter, width = x_doc.shape[1:]
    asked = x_query.shape[1]
    docs = 2 * quarter
    slots = 32

    def place(j):
        return (j & 1) * chips + (j >> 1)

    def kernel(*refs):
        xd_ref, xq_ref = refs[:2]
        sources = refs[2 : 2 + count]
        proj_ref, bias_ref, picks_ref = refs[2 + count : 5 + count]
        x_out = refs[5 + count]
        outs = refs[6 + count : 6 + 2 * count]
        proj_out, bias_out, picks_out = refs[6 + 2 * count : 9 + 2 * count]
        send_sem, recv_sem, small_send, small_recv, x_send, x_recv, local_sem = refs[9 + 2 * count :]
        rank = lax.axis_index("dp")
        column = lax.axis_index("tensor")
        core = rank % 2
        base = rank - core

        def other(bit):
            return rank + bit - 2 * bit * ((rank // bit) % 2)

        barrier = pltpu.get_barrier_semaphore()
        for dc in range(2):
            for dt in range(4):
                if dc + dt > 0:
                    pl.semaphore_signal(
                        barrier,
                        inc=1,
                        device_id=(base + (core + dc) % 2, (column + dt) % 4),
                        device_id_type=MESH,
                    )
        for bit in (2, 4):
            pl.semaphore_signal(
                barrier, inc=1, device_id=(other(bit), column), device_id_type=MESH
            )
        pl.semaphore_wait(barrier, 9)

        local = []

        def keep(src, dst):
            copy = pltpu.make_async_copy(src, dst, local_sem.at[len(local)])
            copy.start()
            local.append(copy)

        lonely = 3 * core == column
        x_copies = []
        for m in range(2):
            mine = jnp.logical_and(lonely, column // 2 == m)
            q = column % 2
            for kind, (ref, size, begin) in enumerate(((xd_ref, quarter, 0), (xq_ref, asked, docs))):
                src = ref.at[m]
                dst = x_out.at[pl.ds(pl.multiple_of(begin + q * size, 32), size), :]
                away = pltpu.make_async_remote_copy(
                    src_ref=src,
                    dst_ref=dst,
                    send_sem=x_send.at[m, kind],
                    recv_sem=x_recv.at[q, kind],
                    device_id=(base + column // 2, 2 * m + core),
                    device_id_type=MESH,
                )
                here = pltpu.make_async_copy(src, dst, x_send.at[m, kind])

                @pl.when(mine)
                def _():
                    here.start()

                @pl.when(jnp.logical_not(mine))
                def _():
                    away.start()

                x_copies.append((mine, here, away))

        waits = []

        def remote(a, slot, src, dst, to):
            return pltpu.make_async_remote_copy(
                src_ref=src,
                dst_ref=dst,
                send_sem=send_sem.at[a, slot],
                recv_sem=recv_sem.at[a, slot],
                device_id=to,
                device_id_type=MESH,
            )

        def piece(a, j, source, at=None):
            at = column if at is None else at
            index = [slice(None)] * len(sources[a].shape)
            size = sources[a].shape[feature_axis[a]]
            index[feature_axis[a]] = pl.ds(place(j) * size, size)
            size = sources[a].shape[tensor_axis[a]]
            offset = pl.multiple_of(differing(at, source, 2) * size, size)
            index[tensor_axis[a]] = pl.ds(offset, size)
            return outs[a].at[tuple(index)]

        def line(a, j):
            index = [slice(None)] * len(sources[a].shape)
            size = sources[a].shape[feature_axis[a]]
            index[feature_axis[a]] = pl.ds(place(j) * size, size)
            return outs[a].at[tuple(index)]

        def go(copy, condition):
            if condition is None:
                copy.start()
            else:

                @pl.when(condition)
                def _():
                    copy.start()

            waits.append((condition, copy))

        def origin(kind):
            if kind == 0:
                return column, None
            if kind <= 3:
                return column - kind, column >= kind
            return column + (kind - 3), column + (kind - 3) <= 3

        def both(x, y):
            if x is None:
                return y
            return x if y is None else jnp.logical_and(x, y)

        def spread(a, kind):
            source, there = origin(kind)
            first, second = first_bits[a]
            src = sources[a] if kind == 0 else piece(a, 0, source)
            go(remote(a, 6 + kind, src, piece(a, first, source), (other(first), column)), there)
            go(remote(a, 13 + kind, src, piece(a, second, source), (other(second), column)), there)

        def along(a, kind):
            source, there = origin(kind)
            src = sources[a] if kind == 0 else piece(a, 0, source)
            hops = kind if kind <= 3 else kind - 3
            if kind <= 3 and hops < 3:
                dst = piece(a, 0, source, column + 1)
                go(remote(a, hops, src, dst, (rank, column + 1)), both(there, column < 3))
            if (kind == 0 or kind > 3) and hops < 3:
                dst = piece(a, 0, source, column - 1)
                go(remote(a, 3 + hops, src, dst, (rank, column - 1)), both(there, column > 0))

        def arrived(a, slot, dst, condition):
            copy = remote(a, slot, dst, dst, (rank, column))
            if condition is None:
                copy.wait_recv()
            else:

                @pl.when(condition)
                def _():
                    copy.wait_recv()

        def onward(a, kind):
            source, there = origin(kind)
            first, second = first_bits[a]
            src = piece(a, first, source)
            arrived(a, 6 + kind, src, there)
            dst = piece(a, first | second, source)
            go(remote(a, 20 + kind, src, dst, (other(second), column)), there)

        small = []

        def tiny(src, dst, to):
            at = len(small)
            copy = pltpu.make_async_remote_copy(
                src_ref=src,
                dst_ref=dst,
                send_sem=small_send.at[at],
                recv_sem=small_recv.at[at],
                device_id=to,
                device_id_type=MESH,
            )
            copy.start()
            small.append(copy)
            return copy

        for a in range(count):
            along(a, 0)
            spread(a, 0)
        for a in range(count):
            keep(sources[a], piece(a, 0, column))
        keep(bias_ref, bias_out.at[0])
        for dt in range(1, 4):
            to = differing(column, dt, 2)
            tiny(bias_ref, bias_out.at[dt], (rank, to))
        flat = []
        for ref, out_ref in ((proj_ref, proj_out), (picks_ref, picks_out)):
            keep(ref, out_ref.at[0])
            flat.append(
                (
                    tiny(ref, out_ref.at[place(2)], (other(2), column)),
                    tiny(ref, out_ref.at[place(4)], (other(4), column)),
                    tiny(ref, out_ref.at[place(1)], (other(1), column)),
                    out_ref,
                )
            )

        for hops in range(1, 4):
            for a in range(count):
                for kind in (hops, hops + 3):
                    source, there = origin(kind)
                    slot = hops - 1 if kind <= 3 else 2 + hops
                    arrived(a, slot, piece(a, 0, source), there)
                    along(a, kind)
                    spread(a, kind)
            kinds = (0,) if hops == 1 else (hops - 1, hops + 2)
            for a in range(count):
                for kind in kinds:
                    onward(a, kind)
        for copy in local:
            copy.wait()

        def sibling(a, slot, j):
            go(remote(a, slot, line(a, j), line(a, j | 1), (other(1), column)), None)

        for a in range(count):
            sibling(a, 27, 0)
        for by_two, by_four, _, out_ref in flat:
            by_two.wait_recv()
            tiny(out_ref.at[place(2)], out_ref.at[place(6)], (other(4), column))
            tiny(out_ref.at[place(2)], out_ref.at[place(3)], (other(1), column))
            by_four.wait_recv()
            tiny(out_ref.at[place(4)], out_ref.at[place(5)], (other(1), column))
        for a in range(count):
            for kind in (3, 6):
                onward(a, kind)
            sibling(a, 28, first_bits[a][0])
        for n, (_, _, _, out_ref) in enumerate(flat):
            small[9 + 3 * n].wait_recv()
            tiny(out_ref.at[place(6)], out_ref.at[place(7)], (other(1), column))
        for a in range(count):
            first, second = first_bits[a]
            for base_slot, j, slot in ((13, second, 29), (20, first | second, 30)):
                for kind in range(7):
                    source, there = origin(kind)
                    arrived(a, base_slot + kind, piece(a, j, source), there)
                sibling(a, slot, j)
        for n, copy in enumerate(small):
            if n not in (3, 4, 6, 7, 9, 12):
                copy.wait_recv()
            copy.wait_send()
        for q in range(2):
            mine = jnp.logical_and(lonely, column % 2 == q)
            for kind, (size, begin) in enumerate(((quarter, 0), (asked, docs))):
                dst = x_out.at[pl.ds(begin + q * size, size), :]
                copy = pltpu.make_async_remote_copy(
                    src_ref=dst,
                    dst_ref=dst,
                    send_sem=x_send.at[q, kind],
                    recv_sem=x_recv.at[q, kind],
                    device_id=(rank, column),
                    device_id_type=MESH,
                )

                @pl.when(jnp.logical_not(mine))
                def _():
                    copy.wait_recv()

        for mine, here, away in x_copies:

            @pl.when(mine)
            def _():
                here.wait()

            @pl.when(jnp.logical_not(mine))
            def _():
                away.wait_send()

        for a in range(count):
            for slot, j in ((27, 1), (28, first_bits[a][0] | 1), (29, first_bits[a][1] | 1), (30, 7)):
                arrived(a, slot, line(a, j), None)
        for condition, copy in waits:
            if condition is None:
                copy.wait_send()
            else:

                @pl.when(condition)
                def _():
                    copy.wait_send()

    out_shape = [jax.ShapeDtypeStruct((docs + 2 * asked, width), x_doc.dtype)]
    for w, f, t in zip(weights, feature_axis, tensor_axis):
        shape = list(w.shape)
        shape[f] *= groups
        shape[t] *= ways
        out_shape.append(jax.ShapeDtypeStruct(tuple(shape), w.dtype))
    out_shape += [
        jax.ShapeDtypeStruct((groups,) + proj.shape, proj.dtype),
        jax.ShapeDtypeStruct((ways,) + bias.shape, bias.dtype),
        jax.ShapeDtypeStruct((groups,) + picks.shape, picks.dtype),
    ]
    anywhere = pl.BlockSpec(memory_space=pl.ANY)
    dma = pltpu.SemaphoreType.DMA
    return pl.pallas_call(
        kernel,
        out_shape=out_shape,
        in_specs=[anywhere] * (5 + count),
        out_specs=[anywhere] * (4 + count),
        scratch_shapes=[
            dma((count, slots)),
            dma((count, slots)),
            dma((17,)),
            dma((17,)),
            dma((2, 2)),
            dma((2, 2)),
            dma((count + 3,)),
        ],
        compiler_params=pltpu.CompilerParams(collective_id=0, has_side_effects=True),
        name="gather_weights",
    )(x_doc, x_query, *weights, proj, bias, picks)


def loss_kernel(projection, labels, log_counts, picks, y):
    rows, columns = projection.shape
    width = y.shape[1]
    docs = labels.shape[0]
    own = rows - docs
    tokens = 16 * own
    units, segments = 8, 4
    chunk = 64

    def kernel(
        p_ref, lab_ref, cnt_ref, pick_ref, y_ref,
        grad_ref, loss_ref, yd_ref, yq_ref,
        asked_all, weight, sums, sums_all, coef_all, slope, part, part_low, got, tile, tile_got,
        send_sem, recv_sem, row_send, row_recv, tile_send, tile_recv,
    ):
        around = Around()
        rank, column, core, base = around.rank, around.column, around.core, around.base
        chip, side = rank // 2, column % 2
        mine = (chip * 2 + side) * 2 + core
        unit = chip * 2 + side

        def flip(value, bit, on):
            return value + bit - 2 * bit * ((value // bit) % 2) if on else value

        def peer(i):
            to = flip(flip(flip(rank, 1, i & 1), 2, i & 4), 4, i & 8)
            return (to, flip(column, 1, i & 2))

        def index_of(i):
            to, z = peer(i)
            return ((to // 2) * 2 + z % 2) * 2 + to % 2

        barrier = pltpu.get_barrier_semaphore()
        peers = [peer(i) for i in range(1, 16)]
        for dt in (2, 3):
            for dc in range(2):
                away, z = around.along(dt)
                peers.append((flip(rank, 1, dc), z))
        for to in peers:
            pl.semaphore_signal(barrier, inc=1, device_id=to, device_id_type=MESH)
        pl.semaphore_wait(barrier, len(peers))

        values = p_ref[...]
        rate = lax.rsqrt(jnp.sum(values * values, axis=-1, keepdims=True) + 1e-06)
        unit_wide = values * rate
        unit_low = unit_wide.astype(BF)
        own_at = pl.ds(pl.multiple_of(mine * own, own), own)
        asked_all[own_at, :] = unit_low[docs:]

        def all_to_all(kind, src, dst):
            copies = []
            for i in range(1, 16):
                copy = pltpu.make_async_remote_copy(
                    src_ref=src(i),
                    dst_ref=dst(i),
                    send_sem=send_sem.at[kind, i],
                    recv_sem=recv_sem.at[kind, i],
                    device_id=peer(i),
                    device_id_type=MESH,
                )
                copy.start()
                copies.append(copy)
            return copies

        first = all_to_all(0, lambda i: asked_all.at[own_at, :], lambda i: asked_all.at[own_at, :])
        home = RowMoves(around, False, yd_ref, yq_ref, y_ref, row_send, row_recv)
        doc_low = unit_low[:docs]
        seg_of = lab_ref[...]
        for copy in first:
            copy.wait_recv()
        queries = asked_all[...]
        sums[...] = jnp.zeros_like(sums)
        for at in range(0, docs, chunk):
            cosines = dot_nt(doc_low[at : at + chunk], queries)
            power = jnp.exp(TAU * (cosines - 1.0))
            weight[at : at + chunk, :] = power
            for s in range(segments):
                chosen = seg_of[at : at + chunk] == s
                sums[s : s + 1, :] += jnp.sum(
                    jnp.where(chosen, power, 0.0), axis=0, keepdims=True
                )
        second = all_to_all(1, lambda i: sums, lambda i: sums_all.at[mine])
        home.start()
        sums_all[mine] = sums[...]
        for copy in second:
            copy.wait_recv()
        row = lax.broadcasted_iota(jnp.int32, (8, tokens), 0)
        lane = lax.broadcasted_iota(jnp.int32, (8, tokens), 1)
        valid = row < segments
        totals, logits = [], []
        for n in range(units):
            total = jnp.where(valid, sums_all[2 * n] + sums_all[2 * n + 1], 1.0)
            best = (jnp.log(total) - cnt_ref[8 * n : 8 * n + 8, :]) / TAU + 1.0
            for step in (1, 2, 4, 8, 16):
                other = jnp.where(
                    (lane // step) % 2 == 1,
                    pltpu.roll(best, step, 1),
                    pltpu.roll(best, tokens - step, 1),
                )
                best = best + other
            totals.append(total)
            logits.append(jnp.where(valid, LOGIT_SCALE * best, MASKED))
        peak = functools.reduce(
            jnp.maximum, [jnp.max(x, axis=0, keepdims=True) for x in logits]
        )
        powers = [jnp.exp(x - peak) for x in logits]
        mass = functools.reduce(jnp.add, [jnp.sum(x, axis=0, keepdims=True) for x in powers])
        picked = jnp.zeros_like(peak)
        for n in range(units):
            hit = jnp.logical_and(valid, pick_ref[...] == n * segments + row)
            picked = picked + jnp.sum(jnp.where(hit, logits[n], 0.0), axis=0, keepdims=True)
            slope_n = LOGIT_SCALE * (powers[n] / mass - jnp.where(hit, 1.0, 0.0))
            coef_all[n] = slope_n / totals[n]
        losses = peak + jnp.log(mass) - picked
        tiles = []
        for q in range(2):
            at = mine * own + q * QLEN
            value = jnp.sum(
                jnp.where(lane[:1] == at, losses, 0.0), axis=1, keepdims=True
            )
            tile[q, 0] = jnp.broadcast_to(value, (8, 128))
            tile[q, 1] = jnp.zeros((8, 128), F32)
        lonely = 3 * core == column
        for q in range(2):
            here = jnp.logical_and(lonely, core == q)
            slot = column // 2
            away = pltpu.make_async_remote_copy(
                src_ref=tile.at[q],
                dst_ref=tile_got.at[slot],
                send_sem=tile_send.at[q],
                recv_sem=tile_recv.at[slot],
                device_id=(base + column % 2, 2 * core + q),
                device_id_type=MESH,
            )
            tiles.append((here, away))

            @pl.when(here)
            def _(q=q):
                tile_got[slot] = tile[q]

            @pl.when(jnp.logical_not(here))
            def _(away=away):
                away.start()

        coef = coef_all[unit]
        doc_grads = []
        part[...] = jnp.zeros_like(part)
        for at in range(0, docs, chunk):
            spread = jnp.zeros((chunk, tokens), F32)
            for s in range(segments):
                chosen = seg_of[at : at + chunk] == s
                spread = jnp.where(chosen, coef[s : s + 1, :], spread)
            low = (weight[at : at + chunk, :] * spread).astype(BF)
            slope[at : at + chunk, :] = low
            doc_grads.append(dot_nn(low, queries))
        part[...] = dot_tn(slope[...], doc_low)
        part_low[...] = part[...].astype(BF)

        def theirs(i):
            return part_low.at[pl.ds(pl.multiple_of(index_of(i) * own, own), own), :]

        third = all_to_all(2, theirs, lambda i: got.at[i])

        def pull(grad, begin, size):
            v, r = unit_wide[begin : begin + size], rate[begin : begin + size]
            inner = jnp.sum(v * grad, axis=-1, keepdims=True)
            return ((grad - v * inner) * r).astype(BF)

        for n, at in enumerate(range(0, docs, chunk)):
            grad_ref[at : at + chunk, :] = pull(doc_grads[n], at, chunk)
        total = part[own_at, :]
        for copy in third:
            copy.wait_recv()
        for i in range(1, 16):
            total = total + got[i].astype(F32)
        grad_ref[docs:, :] = pull(total, docs, own)
        for n in range(2):
            here = jnp.logical_and(lonely, column // 2 == n)
            came = pltpu.make_async_remote_copy(
                src_ref=tile.at[n],
                dst_ref=tile_got.at[n],
                send_sem=tile_send.at[n],
                recv_sem=tile_recv.at[n],
                device_id=peer(1),
                device_id_type=MESH,
            )

            @pl.when(jnp.logical_not(here))
            def _(came=came):
                came.wait_recv()

        loss_ref[...] = tile_got[:, 0]
        home.wait()
        for here, away in tiles:

            @pl.when(jnp.logical_not(here))
            def _(away=away):
                away.wait_send()

        for copy in first + second + third:
            copy.wait_send()

    def whole(shape):
        return pl.BlockSpec(shape, lambda: (0,) * len(shape))

    anywhere = pl.BlockSpec(memory_space=pl.ANY)
    vmem = pltpu.VMEM
    dma = pltpu.SemaphoreType.DMA
    return pl.pallas_call(
        kernel,
        in_specs=[
            whole(projection.shape),
            whole(labels.shape),
            whole(log_counts.shape),
            whole(picks.shape),
            anywhere,
        ],
        out_specs=[whole((rows, columns)), whole((2, 8, 128)), anywhere, anywhere],
        out_shape=[
            jax.ShapeDtypeStruct((rows, columns), BF),
            jax.ShapeDtypeStruct((2, 8, 128), F32),
            jax.ShapeDtypeStruct((2, docs // 2, width), BF),
            jax.ShapeDtypeStruct((2, own // 2, width), BF),
        ],
        scratch_shapes=[
            vmem((tokens, columns), BF),
            vmem((docs, tokens), F32),
            vmem((8, tokens), F32),
            vmem((16, 8, tokens), F32),
            vmem((units, 8, tokens), F32),
            vmem((docs, tokens), BF),
            vmem((tokens, columns), F32),
            vmem((tokens, columns), BF),
            vmem((16, own, columns), BF),
            vmem((2, 2, 8, 128), F32),
            vmem((2, 2, 8, 128), F32),
            dma((3, 16)),
            dma((3, 16)),
            dma((2, 2)),
            dma((2, 2)),
            dma((2,)),
            dma((2,)),
        ],
        compiler_params=pltpu.CompilerParams(
            collective_id=5, has_side_effects=True, vmem_limit_bytes=40 << 20
        ),
        name="loss",
        cost_estimate=pl.CostEstimate(
            flops=100 * docs * tokens * columns,
            bytes_accessed=2 * rows * width,
            transcendentals=docs * tokens,
        ),
    )(projection, labels, log_counts, picks, y)


class MatrixSum:
    def __init__(
        self, around, send, axis, across, own, got, next_, near, far, home, local_sems, pieces
    ):
        self.axis, self.own, self.got, self.next, self.near = axis, own, got, next_, near
        self.block = own.shape[axis] // 4
        first, second = (2, 4) if across else (4, 2)
        self.gone, self.later = ((1, 3), 2) if across else ((2, 3), 1)
        self.cores = [send(src, dst, around.other(1)) for src, dst in far]
        self.loads = [
            pltpu.make_async_copy(src, dst, sem) for (src, dst), sem in zip(home, local_sems)
        ]
        self.firsts = [
            send(self.at(own, n), self.at(next_, slot), around.other(first))
            for slot, n in enumerate(self.gone)
        ]
        self.second = send(self.at(own, self.later), near, around.other(second))
        self.pieces = [send(own.at[index], dst, around.along(dt)) for dt, index, dst in pieces]

    def at(self, ref, n):
        span = pl.ds(n * self.block, self.block)
        return ref.at[span, :] if self.axis == 0 else ref.at[:, span]

    def begin(self):
        for copy in self.cores + self.loads:
            copy.start()

    def add(self, n, ref, m):
        rows = self.block if self.axis == 0 else self.own.shape[0]
        step = 16 if self.axis == 0 else 128
        block = self.block

        @pl.loop(0, rows // step)
        def _(k):
            if self.axis == 0:
                to = (pl.ds(pl.multiple_of(n * block + k * step, step), step), slice(None))
                fr = (pl.ds(pl.multiple_of(m * block + k * step, step), step), slice(None))
            else:
                at = pl.ds(pl.multiple_of(k * step, step), step)
                to, fr = (at, pl.ds(n * block, block)), (at, pl.ds(m * block, block))
            self.own[to] = self.own[to] + ref[fr]

    def first_axis(self):
        for load in self.loads:
            load.wait()
        for copy in self.cores:
            copy.wait_recv()
        for n, copy in zip(self.gone, self.firsts):
            self.add(n, self.got, n)
            copy.start()
        for n in (self.later, 0):
            self.add(n, self.got, n)

    def second_axis(self):
        for copy in self.firsts:
            copy.wait_recv()
        self.add(self.later, self.next, 1)
        self.second.start()
        self.add(0, self.next, 0)

    def tensor(self):
        self.second.wait_recv()
        self.add(0, self.near, 0)
        for copy in self.pieces:
            copy.start()

    def settle(self):
        for copy in self.pieces:
            copy.wait_recv()


class SmallSum:
    def __init__(self, around, send, got, run, bits=(1, 4, 2), tensor=(1, 2)):
        self.got, self.run = got, run
        tos = [around.other(bit) for bit in bits] + [around.along(dt) for dt in tensor]
        self.copies = [send(run.at[n], got.at[n], to) for n, to in enumerate(tos)]

    def begin(self, value):
        self.run[0] = value
        self.copies[0].start()

    def hop(self, n):
        self.copies[n].wait_recv()
        self.run[n + 1] = self.run[n] + self.got[n]
        if n + 1 < len(self.copies):
            self.copies[n + 1].start()


class ProjSum:
    def __init__(self, around, send, ref, run, got):
        self.ref, self.run, self.got = ref, run, got
        rows = ref.shape[0]
        self.half = [rows // 2, rows // 4, rows // 8]
        starts = [0, rows // 2, 3 * rows // 4]
        self.starts = starts
        self.copies = [
            send(ref.at[self.half[0] :, :], got.at[pl.ds(starts[0], self.half[0]), :], around.other(1))
        ]
        for n, bit in ((1, 4), (2, 2)):
            self.copies.append(
                send(
                    run.at[pl.ds(self.half[n], self.half[n]), :],
                    got.at[pl.ds(starts[n], self.half[n]), :],
                    around.other(bit),
                )
            )
        last = self.half[2]
        self.last = last
        base = rows
        for n, dt in ((0, 1), (1, 2)):
            self.copies.append(
                send(
                    run.at[pl.ds(rows // 2 + n * last, last), :],
                    got.at[pl.ds(base + n * last, last), :],
                    around.along(dt),
                )
            )

    def begin(self):
        self.copies[0].start()

    def hop(self, n):
        self.copies[n].wait_recv()
        rows = self.ref.shape[0]
        last = self.last
        if n < 3:
            size = self.half[n]
            old = self.ref if n == 0 else self.run
            total = old[:size, :] + self.got[pl.ds(self.starts[n], size), :]
            if n < 2:
                self.run[:size, :] = total
            else:
                self.run[pl.ds(rows // 2, last), :] = total
        else:
            at = rows // 2 + (n - 3) * last
            got = self.got[pl.ds(rows + (n - 3) * last, last), :]
            self.run[pl.ds(at + last, last), :] = self.run[pl.ds(at, last), :] + got
        if n + 1 < len(self.copies):
            self.copies[n + 1].start()

    def result(self):
        return self.run[pl.ds(self.ref.shape[0] // 2 + 2 * self.last, self.last), :]


def finish_kernel(qkv, out, rows, tensor_sums):
    ways = 4
    width = qkv.shape[0]
    half, block = width // 2, width // 8
    share = width // ways
    docs = rows.shape[0] // 9 * 8
    quarter, asked = docs // 2, (rows.shape[0] - docs) // 2
    chunk = 16
    parts = 4
    part = 3 * share

    def kernel(
        qkv_ref, out_ref, rows_ref, ten_ref,
        qkv_o, out_o, doc_o, ask_o, ten_o,
        qa, q0, q1, q2, q3, oa, o0, o1, o2, o3, gd, ga, t_got, t_run, tz,
        send_sem, recv_sem, local_sem, row_send, row_recv,
    ):
        around = Around()
        around.meet()
        send = Sender(send_sem, recv_sem)
        small = SmallSum(around, send, t_got, t_run, tensor=())
        spread = [send(t_run.at[3, dt], tz.at[dt - 1], around.along(dt)) for dt in range(1, ways)]
        across = (True, False, False, True)
        heads, feats = [], []
        for n in range(parts):
            spans = [(pl.ds(j * width + n * share, share), pl.ds(j * share, share)) for j in range(3)]
            heads.append(
                MatrixSum(
                    around, send, 0, across[n], qa.at[n], q0.at[n], q1.at[n], q2.at[n],
                    [(qkv_ref.at[half:, fr], q0.at[n, :, to]) for fr, to in spans],
                    [(qkv_ref.at[:half, fr], qa.at[n, :, to]) for fr, to in spans],
                    [local_sem.at[3 * n + j] for j in range(3)],
                    [
                        (n, (slice(0, block), pl.ds(j * share, share)), q3.at[n - 1, j])
                        for j in range(3)
                        if n > 0
                    ],
                )
            )
        for n in range(2):
            span = pl.ds(n * half, half)
            feats.append(
                MatrixSum(
                    around, send, 1, n == 0, oa.at[n], o0.at[n], o1.at[n], o2.at[n],
                    [(out_ref.at[span, half:], o0.at[n])],
                    [(out_ref.at[span, :half], oa.at[n])],
                    [local_sem.at[3 * parts + n]],
                    [
                        (dt, (pl.ds((dt % 2) * share, share), slice(0, block)), o3.at[dt - 1])
                        for dt in (2 * n, 2 * n + 1)
                        if dt > 0
                    ],
                )
            )
        items = [heads[2], heads[3], feats[1], heads[0], heads[1], feats[0]]
        small.begin(ten_ref[...])
        for item in items:
            item.begin()

        home = RowMoves(around, False, gd, ga, rows_ref, row_send, row_recv)
        home.start()

        for n in range(0, len(items) + 4, 2):
            for item in items[n - 2 : n] if n >= 2 else []:
                item.second_axis()
            for item in items[n : n + 2]:
                item.first_axis()
            if n // 2 < 3:
                small.hop(n // 2)
            if n // 2 == 2:
                for copy in spread:
                    copy.start()
            for m in (n - 4, n - 3):
                if 0 <= m < len(items):
                    items[m].tensor()

        home.wait()
        for m in range(2):

            @pl.loop(0, quarter // chunk)
            def _(n):
                at = pl.ds(pl.multiple_of(n * chunk, chunk), chunk)
                doc_o[m, at, :] = gd[m, at, :].astype(F32)

        ask_o[...] = ga[...].astype(F32)
        for copy in spread:
            copy.wait_recv()
        ten_o[...] = t_run[3, 0] + tz[0] + tz[1] + tz[2]
        for item in items:
            item.settle()
        for j in range(3):
            total = qa[0, :block, pl.ds(j * share, share)].astype(F32)
            for dt in range(ways - 1):
                total = total + q3[dt, j].astype(F32)
            qkv_o[j] = total
        total = oa[0, :share, :block].astype(F32)
        for dt in range(ways - 1):
            total = total + o3[dt].astype(F32)
        out_o[...] = total
        send.drain()

    def whole(x):
        return pl.BlockSpec(x.shape, lambda: (0,) * len(x.shape))

    out_shape = [
        jax.ShapeDtypeStruct((3, block, share), F32),
        jax.ShapeDtypeStruct((share, block), F32),
        jax.ShapeDtypeStruct((2, quarter, width), F32),
        jax.ShapeDtypeStruct((2, asked, width), F32),
        jax.ShapeDtypeStruct(tensor_sums.shape[1:], F32),
    ]
    anywhere = pl.BlockSpec(memory_space=pl.ANY)
    vmem = pltpu.VMEM
    dma = pltpu.SemaphoreType.DMA
    count = 6 + parts * 6 + 9 + 2 * 4 + 3
    return pl.pallas_call(
        kernel,
        out_shape=out_shape,
        in_specs=[anywhere] * 3 + [whole(tensor_sums)],
        out_specs=[whole(x) for x in out_shape],
        scratch_shapes=[
            vmem((parts, half, part), BF),
            vmem((parts, half, part), BF),
            vmem((parts, 2 * block, part), BF),
            vmem((parts, block, part), BF),
            vmem((ways - 1, 3, block, share), BF),
            vmem((2, half, half), BF),
            vmem((2, half, half), BF),
            vmem((2, half, 2 * block), BF),
            vmem((2, half, block), BF),
            vmem((ways - 1, share, block), BF),
            vmem((2, quarter, width), BF),
            vmem((2, asked, width), BF),
            vmem((3,) + tensor_sums.shape, F32),
            vmem((4,) + tensor_sums.shape, F32),
            vmem((ways - 1,) + tensor_sums.shape[1:], F32),
            dma((count,)),
            dma((count,)),
            dma((3 * parts + 2,)),
            dma((2, 2)),
            dma((2, 2)),
        ],
        compiler_params=pltpu.CompilerParams(
            collective_id=1, has_side_effects=True, vmem_limit_bytes=48 << 20
        ),
        name="last_sums",
    )(qkv, out, rows, tensor_sums)


def attention_backward_kernel(
    qkv, far_kv, grad, cosine, sine, far_cosine, far_sine, col_labels, own_labels, far_labels,
    up, back, vectors, proj,
):
    rows, width = qkv.shape[1:]
    docs = far_kv.shape[1]
    pairs = width // 128
    block = 128
    asked = rows - docs
    ways = 4
    half, own_block = width // 2, width // 8
    share = up.shape[1] // ways
    count, piece = 2 * ways, share // 2
    assert pairs == 8

    def kernel(
        qkv_ref, far_ref, g_ref, c_ref, s_ref, fc_ref, fs_ref, lc_ref, lo_ref, lf_ref,
        up_ref, back_ref, vec_ref, proj_ref,
        pre_ref, bias_ref, up_o, back_o, vec_o, proj_o,
        sums_own, sums_far, give, kept, got_kv,
        ua, u0, u1, u2, u3, ba, b0, b1, b2, b3, v_got, v_run, p_run, p_got,
        send_sem, recv_sem, local_sem,
    ):
        h = pl.program_id(0)
        around = Around()
        send = Sender(send_sem, recv_sem)
        ups, backs = [], []
        for n in range(count):
            span = pl.ds(n * piece, piece)
            dt, side = n // 2, pl.ds(n % 2 * piece, piece)
            ups.append(
                MatrixSum(
                    around, send, 0, False, ua.at[n], u0.at[n], u1.at[n], u2.at[n],
                    [(up_ref.at[half:, span], u0.at[n])],
                    [(up_ref.at[:half, span], ua.at[n])],
                    [local_sem.at[n]],
                    [(dt, (slice(0, own_block), slice(None)), u3.at[dt - 1, :, side])] if dt else [],
                )
            )
            backs.append(
                MatrixSum(
                    around, send, 1, True, ba.at[n], b0.at[n], b1.at[n], b2.at[n],
                    [(back_ref.at[span, half:], b0.at[n])],
                    [(back_ref.at[span, :half], ba.at[n])],
                    [local_sem.at[count + n]],
                    [(dt, (slice(None), slice(0, own_block)), b3.at[dt - 1, side, :])] if dt else [],
                )
            )
        couples = [(ups[n], backs[n]) for n in (4, 5, 6, 7, 2, 3, 0, 1)]
        small = SmallSum(around, send, v_got, v_run)
        mean_proj = ProjSum(around, send, proj_ref, p_run, p_got)
        gives = [send(give.at[n], got_kv.at[n], around.other(1)) for n in range(pairs)]
        lane = lax.broadcasted_iota(jnp.int32, (1, 128), 1)

        def finish(n):
            gives[n].wait_recv()
            at = pl.ds(n * 128, 128)
            for i in range(2):
                low = (kept[n % 2, i, :docs, :] + got_kv[n, i].astype(F32)).astype(BF)
                tail = kept[n % 2, i, docs:, :].astype(BF)
                pre_ref[i + 1, :docs, at] = low
                pre_ref[i + 1, docs:, at] = tail
                total = jnp.sum(low.astype(F32), axis=0, keepdims=True)
                total = total + jnp.sum(tail.astype(F32), axis=0, keepdims=True)
                bias_ref[i + 1 : i + 2, at] = total

        for step in range(pairs):

            @pl.when(h == step)
            def _(step=step):
                if step == 0:
                    around.meet()
                    small.begin(vec_ref[...])
                    mean_proj.begin()
                    for couple in couples:
                        for item in couple:
                            item.begin()
                else:
                    if step >= 2:
                        for item in couples[step - 2]:
                            item.second_axis()
                    for couple in couples[:2] if step == 1 else [couples[step]]:
                        for item in couple:
                            item.first_axis()
                    if step <= 5:
                        small.hop(step - 1)
                        mean_proj.hop(step - 1)
                    if step >= 3:
                        for item in couples[step - 3]:
                            item.tensor()
                    finish(step - 1)

        sums_own[...] = jnp.zeros_like(sums_own)
        sums_far[...] = jnp.zeros_like(sums_far)

        def part(start, size, keys, sames, sums):
            q_block = qkv_ref[0, pl.ds(start, size), :]
            g_block = g_ref[pl.ds(start, size), :]
            grads = []
            for head in range(2):
                mask = (lane // HEAD_WIDTH) == head
                q_head = jnp.where(mask, q_block, jnp.zeros_like(q_block))
                g_head = jnp.where(mask, g_block, jnp.zeros_like(g_block))
                scores = [
                    jnp.where(same, dot_nt(q_head, key), MASKED)
                    for (key, _), same in zip(keys, sames)
                ]
                top = functools.reduce(
                    jnp.maximum, [jnp.max(s, axis=-1, keepdims=True) for s in scores]
                )
                powers = [jnp.exp(s - top) for s in scores]
                total = functools.reduce(
                    jnp.add, [jnp.sum(p, axis=-1, keepdims=True) for p in powers]
                )
                inverse = 1.0 / total
                g_head = (g_head.astype(F32) * inverse).astype(BF)
                pulls = [dot_nt(g_head, value) for _, value in keys]
                mean = functools.reduce(
                    jnp.add,
                    [jnp.sum(p * d, axis=-1, keepdims=True) for p, d in zip(powers, pulls)],
                ) * inverse
                slopes = [(p * (d - mean)).astype(BF) for p, d in zip(powers, pulls)]
                got = functools.reduce(
                    jnp.add, [dot_nn(s, key) for s, (key, _) in zip(slopes, keys)]
                )
                grads.append(got * 0.125)
                for (ref, begin, many), s, p in zip(sums, slopes, powers):
                    ref[0, pl.ds(begin, many), :] += dot_tn(s, q_head)
                    ref[1, pl.ds(begin, many), :] += dot_tn(p.astype(BF), g_head)
            total = jnp.where(lane < HEAD_WIDTH, grads[0], grads[1])
            at = pl.ds(start, size)
            low = (total * c_ref[at, :] - turned(total) * s_ref[at, :]).astype(BF)
            pre_ref[0, at, pl.ds(pl.multiple_of(h * 128, 128), 128)] = low
            return jnp.sum(low.astype(F32), axis=0, keepdims=True)

        doc_keys = [
            (qkv_ref[1, :docs, :], qkv_ref[2, :docs, :]),
            (far_ref[0], far_ref[1]),
        ]
        bias = jnp.zeros((1, 128), F32)
        for at in range(docs // block):
            labels = lc_ref[pl.ds(at * block, block), :]
            bias = bias + part(
                at * block,
                block,
                doc_keys,
                [labels == lo_ref[...], labels == lf_ref[...]],
                [(sums_own, 0, docs), (sums_far, 0, docs)],
            )
        row = lax.broadcasted_iota(jnp.int32, (asked, asked), 0) // QLEN
        col = lax.broadcasted_iota(jnp.int32, (asked, asked), 1) // QLEN
        bias = bias + part(
            docs,
            asked,
            [(qkv_ref[1, docs:, :], qkv_ref[2, docs:, :])],
            [row == col],
            [(sums_own, docs, asked)],
        )
        bias_ref[0:1, pl.ds(pl.multiple_of(h * 128, 128), 128)] = bias
        side = h % 2
        kept[side, 0] = sums_own[0] * c_ref[...] - turned(sums_own[0]) * s_ref[...]
        kept[side, 1] = sums_own[1]
        give[h, 0] = (sums_far[0] * fc_ref[...] - turned(sums_far[0]) * fs_ref[...]).astype(BF)
        give[h, 1] = sums_far[1].astype(BF)
        for step in range(pairs):

            @pl.when(h == step)
            def _(step=step):
                gives[step].start()

        @pl.when(h == pairs - 1)
        def _():
            finish(pairs - 1)
            for couple in couples[6:]:
                for item in couple:
                    item.second_axis()
            for couple in couples[5:]:
                for item in couple:
                    item.tensor()
            for couple in couples:
                for item in couple:
                    item.settle()
            for n in range(2):
                at = pl.ds(n * piece, piece)
                total = ua[n, :own_block, :].astype(F32)
                for dt in range(ways - 1):
                    total = total + u3[dt, :, at].astype(F32)
                up_o[:, at] = total
                total = ba[n, :, :own_block].astype(F32)
                for dt in range(ways - 1):
                    total = total + b3[dt, at, :].astype(F32)
                back_o[at, :] = total
            vec_o[...] = v_run[5]
            proj_o[...] = mean_proj.result()
            send.drain()

    def whole(shape):
        return pl.BlockSpec(shape, lambda h: (0,) * len(shape))

    anywhere = pl.BlockSpec(memory_space=pl.ANY)
    vmem = pltpu.VMEM
    dma = pltpu.SemaphoreType.DMA
    columns = proj.shape[1]
    out_shape = [
        jax.ShapeDtypeStruct((3, rows, width), BF),
        jax.ShapeDtypeStruct((8, width), F32),
        jax.ShapeDtypeStruct((own_block, share), F32),
        jax.ShapeDtypeStruct((share, own_block), F32),
        jax.ShapeDtypeStruct(vectors.shape, F32),
        jax.ShapeDtypeStruct((own_block, columns), F32),
    ]
    slots = 2 * (count * 4 + 6) + 5 + 5 + pairs
    return pl.pallas_call(
        kernel,
        grid=(pairs,),
        in_specs=[
            pl.BlockSpec((3, rows, 128), lambda h: (0, 0, h)),
            pl.BlockSpec((2, docs, 128), lambda h: (0, 0, h)),
            pl.BlockSpec((rows, 128), lambda h: (0, h)),
            whole((rows, 128)),
            whole((rows, 128)),
            whole((docs, 128)),
            whole((docs, 128)),
            whole((docs, 1)),
            whole((1, docs)),
            whole((1, docs)),
            anywhere,
            anywhere,
            whole(vectors.shape),
            whole(proj.shape),
        ],
        out_specs=[whole(x.shape) for x in out_shape],
        out_shape=out_shape,
        scratch_shapes=[
            vmem((2, rows, 128), F32),
            vmem((2, docs, 128), F32),
            vmem((pairs, 2, docs, 128), BF),
            vmem((2, 2, rows, 128), F32),
            vmem((pairs, 2, docs, 128), BF),
            vmem((count, half, piece), BF),
            vmem((count, half, piece), BF),
            vmem((count, 2 * own_block, piece), BF),
            vmem((count, own_block, piece), BF),
            vmem((ways - 1, own_block, share), BF),
            vmem((count, piece, half), BF),
            vmem((count, piece, half), BF),
            vmem((count, piece, 2 * own_block), BF),
            vmem((count, piece, own_block), BF),
            vmem((ways - 1, share, own_block), BF),
            vmem((5,) + vectors.shape, F32),
            vmem((6,) + vectors.shape, F32),
            vmem((width, columns), F32),
            vmem((width + 2 * own_block, columns), F32),
            dma((slots,)),
            dma((slots,)),
            dma((2 * count,)),
        ],
        compiler_params=pltpu.CompilerParams(
            collective_id=2, has_side_effects=True, vmem_limit_bytes=60 << 20
        ),
        name="attend_backward_and_sum",
        cost_estimate=pl.CostEstimate(
            flops=100 * rows * 2 * docs * width,
            bytes_accessed=4 * (6 * rows + 4 * docs) * width,
            transcendentals=rows * 2 * docs * width // 64,
        ),
    )(
        qkv, far_kv, grad, cosine, sine, far_cosine, far_sine, col_labels, own_labels, far_labels,
        up, back, vectors, proj,
    )


def body(
    x_doc,
    x_query,
    doc_cot,
    query_cot,
    lengths,
    positives,
    w_qkv,
    b_qkv,
    w_out,
    b_out,
    gain_one,
    shift_one,
    w_in,
    b_in,
    w_back,
    b_back,
    gain_two,
    shift_two,
    w_proj,
):
    ways = lax.axis_size("tensor")
    groups = lax.axis_size("dp")
    column = lax.axis_index("tensor")
    rank = lax.axis_index("dp")
    core = rank % 2
    chip = rank // 2
    chips = groups // 2
    micro, quarter, width = x_doc.shape
    asked = x_query.shape[1]
    segments = lengths.shape[2] - 1
    proj_width = w_proj.shape[1]
    heads_local = w_qkv.shape[2]
    units_local = w_in.shape[1]
    block = width // groups
    assert ways == 2 * micro and ways == 4

    def exchange(value, dr=0, dt=0):
        pairs = [
            (r * ways + t, (r ^ dr) * ways + (t ^ dt)) for r in range(groups) for t in range(ways)
        ]
        return lax.ppermute(value, AXES, pairs)

    chip_bits = []
    bit = 2
    while bit < groups:
        chip_bits.append(bit)
        bit *= 2

    def gather_weights(pack, reverse):
        pieces = [pack] + [exchange(pack, dt=j) for j in range(1, ways)]
        pieces = [(0, jnp.concatenate(pieces, axis=-1))]
        order = chip_bits[::-1] if reverse and len(chip_bits) == 2 else chip_bits
        for dr in order:
            pieces = pieces + [(j + dr // 2, exchange(p, dr=dr)) for j, p in pieces]
            if len(pieces) >= 4 or dr == order[-1]:
                pieces.sort(key=lambda item: item[0])
                pieces = [(0, jnp.concatenate([p for _, p in pieces], axis=-2))]
        (_, half), = pieces
        return jnp.concatenate([half, exchange(half, dr=1)], axis=-2)

    def gather_proj(pack):
        for dr in chip_bits + [1]:
            pack = jnp.concatenate([pack, exchange(pack, dr=dr)], axis=0)
        return pack

    unit_micro = column // 2
    unit_row = chip * 2 + column % 2

    def rows_in(docs, queries):
        blocks = jnp.concatenate([docs, queries], axis=1)
        got = []
        for j in range(2):
            send = jnp.where((column + j) % 2 == 0, blocks[0], blocks[1])
            pairs = []
            for r in range(groups):
                for t in range(ways):
                    m = (t + j) % 2
                    pairs.append(
                        (r * ways + t, ((r // 2) * 2 + t // 2) * ways + 2 * m + r % 2)
                    )
            got.append(lax.ppermute(send, AXES, pairs))
        first = jnp.where(unit_micro == 0, got[0], got[1])
        second = jnp.where(unit_micro == 0, got[1], got[0])
        return jnp.concatenate(
            [first[:quarter], second[:quarter], first[quarter:], second[quarter:]], axis=0
        )

    def quarters_out(first, second):
        got = []
        for j in range(2):
            send = jnp.where((unit_micro + j) % 2 == 0, first, second)
            pairs = []
            for r in range(groups):
                for t in range(ways):
                    m = t // 2
                    pairs.append(
                        (
                            r * ways + t,
                            ((r // 2) * 2 + t % 2) * ways + 2 * (r % 2) + (m + j) % 2,
                        )
                    )
            got.append(lax.ppermute(send, AXES, pairs))
        even = jnp.where(column % 2 == 0, got[0], got[1])
        odd = jnp.where(column % 2 == 0, got[1], got[0])
        return jnp.stack([even, odd])

    def rows_out(values):
        docs = 2 * quarter
        first = jnp.concatenate([values[:quarter], values[docs : docs + asked]], axis=0)
        second = jnp.concatenate([values[quarter:docs], values[docs + asked :]], axis=0)
        blocks = quarters_out(first, second)
        return blocks[:, :quarter], blocks[:, quarter:]

    place = jnp.arange(width, dtype=jnp.int32)
    step = place // block
    actual = (rank ^ (2 * (step % chips) + step // chips)) * block + place % block
    turn = (place[:, None] == actual[None, :]).astype(BF)

    bias_pack = jnp.concatenate([b_qkv.reshape(-1), b_in])
    own_picks = jnp.zeros((8, 128), jnp.int32).at[:micro, : positives.shape[1]].set(positives)
    if chips == 4:
        own_x, full_qkv, full_out, full_in, full_back, full_proj, biases, picks_rel = gather_kernel(
            x_doc, x_query, w_qkv, w_out, w_in, w_back, w_proj, bias_pack.reshape(-1, 128), own_picks
        )
        biases = [biases[j].reshape(-1) for j in range(ways)]
        full_proj = full_proj.reshape(width, proj_width)
    else:
        own_x = rows_in(x_doc, x_query)
        full_qkv = gather_weights(w_qkv, False)
        full_out = gather_weights(w_out.T, False).T
        full_in = gather_weights(w_in, False)
        full_back = gather_weights(w_back.T, False).T
        full_proj = gather_proj(w_proj)
        picks_rel = gather_proj(own_picks[None])
        biases = [bias_pack] + [exchange(bias_pack[None], dt=j)[0] for j in range(1, ways)]
    picks_rel = picks_rel[:, :micro, : positives.shape[1]].astype(F32)
    cots = (doc_cot.astype(BF), query_cot.astype(BF))
    if chips != 4:
        own_cot = rows_in(*cots)
    bias_qkv = jnp.concatenate(
        [b[: 3 * heads_local].reshape(3, heads_local) for b in biases], axis=1
    )
    bias_in = jnp.concatenate([b[3 * heads_local :] for b in biases])
    params = jnp.stack(
        [b_out, gain_one, shift_one, b_back, gain_two, shift_two, b_out, b_out]
    )
    params = jnp.dot(params, turn.astype(F32), precision=FULL_PRECISION)
    b_out, gain_one, shift_one, b_back, gain_two, shift_two = [params[i] for i in range(6)]

    docs = 2 * quarter
    queries = 2 * asked
    rows = docs + queries
    sizes_all = lengths[unit_micro]
    sizes = sizes_all[unit_row]
    ends = jnp.cumsum(sizes[:-1])
    starts = jnp.concatenate([jnp.zeros((1,), jnp.int32), ends])

    def layout(first):
        index = first + jnp.arange(docs, dtype=jnp.int32)
        segment = jnp.sum((index[:, None] >= ends[None, :]).astype(jnp.int32), axis=1)
        labels = jnp.arange(starts.shape[0], dtype=jnp.int32)
        begin = jnp.sum(
            jnp.where(segment[:, None] == labels[None, :], starts[None, :], 0), axis=1
        )
        return segment, index - begin

    own_labels, own_places = layout(core * docs)
    far_labels, far_places = layout((1 - core) * docs)
    own_places = jnp.concatenate([own_places, jnp.arange(queries, dtype=jnp.int32) % QLEN])
    half = HEAD_WIDTH // 2
    rates = 10000.0 ** (-(2.0 * jnp.arange(half, dtype=F32)) / HEAD_WIDTH)

    def rotation(places):
        angle = places.astype(F32)[:, None] * rates[None, :]
        sine = jnp.sin(angle)
        return jnp.tile(jnp.cos(angle), (1, 4)), jnp.concatenate([-sine, sine] * 2, axis=1)

    cosine, sine = rotation(own_places)
    far_cosine, far_sine = rotation(far_places)
    cosines_three = jnp.stack([cosine * 0.125, cosine, jnp.ones_like(cosine)])
    sines_three = jnp.stack([sine * 0.125, sine, jnp.zeros_like(sine)])

    x_low = dot_nn(own_x, turn).astype(BF)
    projected = project_heads(
        x_low, full_qkv, bias_qkv, cosines_three, sines_three, docs, chips == 4
    )
    qkv = projected[0]
    far_kv = projected[1] if chips == 4 else exchange(qkv[1:, :docs], dr=1)
    label_args = (own_labels[:, None], own_labels[None, :], far_labels[None, :])
    if chips == 4:
        mixed, own_cot = attention_forward(qkv, far_kv, *label_args, cots)
    else:
        (mixed,) = attention_forward(qkv, far_kv, *label_args)
    branch = dot_nn(mixed, full_out)
    resid_one = x_low.astype(F32) + branch + b_out
    normed, norm_one_pull = jax.vjp(layer_norm, resid_one, gain_one, shift_one)
    normed_low = normed.astype(BF)
    inner = dot_nn(normed_low, full_in) + bias_in
    active, gelu_pull = jax.vjp(gelu_exact, inner)
    active_low = active.astype(BF)
    resid_two = normed + dot_nn(active_low, full_back) + b_back
    output, norm_two_pull = jax.vjp(layer_norm, resid_two, gain_two, shift_two)
    output_low = output.astype(BF)
    y_low = dot_nt(output_low, turn).astype(BF)
    projection = dot_nn(output_low, full_proj)
    held = jnp.arange(groups, dtype=jnp.int32)
    held = rank ^ (2 * (held % chips) + held // chips)
    order = (jnp.arange(groups, dtype=jnp.int32)[:, None] == held[None, :]).astype(F32)
    picks = jnp.where(unit_micro == 0, picks_rel[:, 0], picks_rel[:, 1])
    picks = jnp.dot(order, picks, precision=FULL_PRECISION).astype(jnp.int32).reshape(-1)
    counts = sizes_all[:, :segments].reshape(-1).astype(F32)

    if chips == 4:
        log_counts = jnp.pad(
            jnp.log(counts).reshape(-1, segments), ((0, 0), (0, 8 - segments))
        ).reshape(-1, 1)
        proj_low, loss_out, y_doc, y_query = loss_kernel(
            projection, own_labels[:, None], log_counts, jnp.repeat(picks, QLEN)[None], y_low
        )
        loss_out = loss_out[:, : asked // QLEN, 0]
    else:
        y_doc, y_query = rows_out(y_low)
        unit, unit_pull = jax.vjp(normalize, projection)
        unit_low = unit.astype(BF)

        doc_unit = unit_low[:docs]
        query_unit = unit_low[docs:]

        def bit_of(dr, dt):
            return (rank // dr) % 2 == 1 if dr else (column // dt) % 2 == 1

        def join(value, dr, dt, axis=0):
            got = exchange(value, dr=dr, dt=dt)
            on = bit_of(dr, dt)
            low = jnp.where(on, got, value)
            high = jnp.where(on, value, got)
            return jnp.concatenate([low, high], axis=axis)

        def split_sum(value, dr, dt):
            on = bit_of(dr, dt)
            size = value.shape[0] // 2
            send = jnp.where(on, value[:size], value[size:])
            keep = jnp.where(on, value[size:], value[:size])
            return keep + exchange(send.astype(BF), dr=dr, dt=dt).astype(F32)

        steps = [(1, 0), (0, 1)] + [(dr, 0) for dr in chip_bits]
        all_queries = query_unit
        for dr, dt in steps:
            all_queries = join(all_queries, dr, dt)
        seg_labels = jnp.arange(segments, dtype=jnp.int32)
        member = (own_labels[:, None] == seg_labels[None, :]).astype(F32)
        cosines = dot_nt(doc_unit, all_queries)
        weight = jnp.exp(TAU * (cosines - 1.0))
        totals = jnp.einsum("js,ji->si", member, weight, precision=FULL_PRECISION)
        totals = totals + exchange(totals, dr=1)
        for dr, dt in steps[1:]:
            totals = join(totals, dr, dt)
        best = (jnp.log(totals) - jnp.log(counts)[:, None]) / TAU + 1.0
        score = jnp.sum(best.reshape(best.shape[0], -1, QLEN), axis=-1)
        logits = LOGIT_SCALE * score
        documents = jnp.arange(logits.shape[0], dtype=jnp.int32)
        chosen = (documents[:, None] == picks[None, :]).astype(F32)
        peak = jnp.max(logits, axis=0, keepdims=True)
        powers = jnp.exp(logits - peak)
        mass = jnp.sum(powers, axis=0, keepdims=True)
        losses = (peak + jnp.log(mass))[0] - jnp.sum(chosen * logits, axis=0)
        logit_grad = LOGIT_SCALE * (powers / mass - chosen)
        own_grad = lax.dynamic_slice_in_dim(logit_grad, unit_row * segments, segments, axis=0)
        own_total = lax.dynamic_slice_in_dim(totals, unit_row * segments, segments, axis=0)
        coef = jnp.repeat(own_grad, QLEN, axis=1) / own_total
        spread = jnp.einsum("js,si->ji", member, coef, precision=FULL_PRECISION)
        cosine_grad = (weight * spread).astype(BF)
        doc_grad = dot_nn(cosine_grad, all_queries)
        query_grad = dot_tn(cosine_grad, doc_unit)
        for dr, dt in steps[::-1]:
            query_grad = split_sum(query_grad, dr, dt)
        own_losses = lax.dynamic_slice_in_dim(losses, unit_row * (4 * asked // QLEN) + core * 2 * (asked // QLEN), 2 * (asked // QLEN))
        per = asked // QLEN
        loss_tiles = [
            jnp.broadcast_to(own_losses[i * per : (i + 1) * per, None], (per, 128)) for i in range(2)
        ]
        loss_out = quarters_out(loss_tiles[0], loss_tiles[1])[:, :, 0]

        unit_grad = jnp.concatenate([doc_grad, query_grad], axis=0)
        (proj_grad,) = unit_pull(unit_grad)
        proj_low = proj_grad.astype(BF)

    class Reduction:
        def __init__(self, half, axis, reverse, last):
            self.bits = chip_bits if reverse and len(chip_bits) == 2 else chip_bits[::-1]
            self.left = sorted(chip_bits)
            self.axis, self.last = axis, last
            self.sends = [half(1).astype(BF)]
            self.hops = [(1, 0)]
            self.kept = lambda: half(0)
            self.stage = 0

        def advance(self):
            total = self.kept()
            for s, (dr, dt) in zip(self.sends, self.hops):
                got = exchange(s, dr=dr, dt=dt).astype(F32)
                total = got if total is None else total + got
            if self.stage == len(self.bits) + 1:
                return total
            if self.stage < len(self.bits):
                dr = self.bits[self.stage]
                at = self.left.index(dr)
                self.left.remove(dr)
                size = block << at
                stay, send = [
                    jnp.concatenate(
                        [
                            lax.slice_in_dim(total, b, b + size, axis=self.axis)
                            for b in range(side * size, total.shape[self.axis], 2 * size)
                        ],
                        axis=self.axis,
                    )
                    for side in (0, 1)
                ]
                self.sends = [send.astype(BF)]
                self.hops = [(dr, 0)]
            else:
                stay, sends = self.last(total)
                self.sends = [piece.astype(BF) for _, piece in sends]
                self.hops = [(0, dt) for dt, _ in sends]
            self.kept = lambda: stay
            self.stage += 1
            return None

        def finish(self):
            total = None
            while total is None:
                total = self.advance()
            return total

    def weight_sum(left, right, axis, reverse):
        size = width // 2

        def half(n):
            if axis == 0:
                return dot_tn(left[:, n * size : (n + 1) * size], right)
            return dot_tn(left, right[:, n * size : (n + 1) * size])

        def last(total):
            size = total.shape[1 - axis] // ways
            pieces = [
                lax.slice_in_dim(total, j * size, (j + 1) * size, axis=1 - axis)
                for j in range(ways)
            ]
            return pieces[0], [(j, pieces[j]) for j in range(1, ways)]

        return Reduction(half, axis, reverse, last)

    def after(value, reductions):
        sends = [r.sends for r in reductions]
        value, sends = lax.optimization_barrier((value, sends))
        for r, s in zip(reductions, sends):
            r.sends = s
        return value

    out_grad = own_cot_turned = dot_nn(own_cot, turn) + dot_nt(proj_low, full_proj)
    resid_two_grad, gain_two_grad, shift_two_grad = norm_two_pull(out_grad)
    update_low = resid_two_grad.astype(BF)
    whole_path = chips == 4
    if whole_path:
        back_grad = dot_tn(active_low, update_low).astype(BF)
    else:
        sum_back = weight_sum(active_low, update_low, 1, True)
    active_grad = dot_nt(update_low, full_back)
    (inner_grad,) = gelu_pull(active_grad)
    inner_low = inner_grad.astype(BF)
    if whole_path:
        in_grad = dot_tn(normed_low, inner_low).astype(BF)
    else:
        sum_in = weight_sum(normed_low, inner_low, 0, False)
    normed_grad = dot_nt(inner_low, full_in) + resid_two_grad
    resid_one_grad, gain_one_grad, shift_one_grad = norm_one_pull(normed_grad)
    branch_low = resid_one_grad.astype(BF)
    mixed_grad = dot_nt(branch_low, full_out).astype(BF)
    grad_proj = dot_tn(output_low, proj_low)
    zero = jnp.zeros((width,), F32)
    vectors = jnp.stack(
        [
            jnp.sum(branch_low.astype(F32), axis=0),
            gain_one_grad,
            shift_one_grad,
            jnp.sum(update_low.astype(F32), axis=0),
            gain_two_grad,
            shift_two_grad,
            zero,
            zero,
        ]
    )
    vectors = lax.dot_general(
        vectors, turn.astype(F32), (((1,), (1,)), ((), ())), precision=FULL_PRECISION
    )

    def heads_sum(rights, first_block, blocks, reverse):
        size = width // 2
        many = rights.shape[1] // 3 // blocks

        def half(n):
            return dot_tn(x_low[:, n * size : (n + 1) * size], rights)

        def last(total):
            stay, sends = None, []
            for b in range(blocks):
                piece = jnp.stack(
                    [total[:, (j * blocks + b) * many : (j * blocks + b + 1) * many] for j in range(3)]
                )
                if first_block + b == 0:
                    stay = piece
                else:
                    sends.append((first_block + b, piece))
            return stay, sends

        return Reduction(half, 0, reverse, last)

    inner_bias = jnp.sum(inner_low.astype(F32), axis=0).reshape(ways, units_local)
    if whole_path:
        pre, head_bias, out_in, out_back, vectors, grad_proj = attention_backward_kernel(
            qkv,
            far_kv,
            mixed_grad,
            cosine,
            sine,
            far_cosine,
            far_sine,
            *label_args,
            in_grad,
            back_grad,
            vectors,
            grad_proj,
        )
        head_bias = head_bias[:3].reshape(3, ways, heads_local)
        pre = [pre[j] for j in range(3)]
    else:
        head_sums, head_rights = [], []
        running = [sum_back, sum_in]
        per_block = heads_local // 128
        sum_out = weight_sum(mixed, branch_low, 1, False)
        for first_block, blocks in ((0, 2), (2, 1), (3, 1)):
            for item in running:
                item.advance()
            mixed_grad = after(mixed_grad, running)
            dq, own_grads, give = attention_backward(
                first_block * per_block,
                blocks * per_block,
                qkv,
                far_kv,
                mixed_grad,
                cosine,
                sine,
                far_cosine,
                far_sine,
                *label_args,
            )
            got = exchange(give, dr=1).astype(F32)
            rights = [dq] + [
                jnp.concatenate(
                    [own_grads[i, :docs] + got[i], own_grads[i, docs:]], axis=0
                ).astype(BF)
                for i in range(2)
            ]
            head_rights.append(rights)
            head_sums.append(
                heads_sum(jnp.concatenate(rights, axis=1), first_block, blocks, first_block > 0)
            )
        out_back = sum_back.finish()
        out_in = sum_in.finish()
        pre = [jnp.concatenate([part[j] for part in head_rights], axis=1) for j in range(3)]
        head_bias = jnp.stack([jnp.sum(p.astype(F32), axis=0) for p in pre])
        head_bias = head_bias.reshape(3, ways, heads_local)
    x_grad = resid_one_grad
    for j in range(3):
        x_grad = x_grad + dot_nt(pre[j], full_qkv[j])
    x_grad = dot_nt(x_grad.astype(BF), turn).astype(BF)
    tensor_grads = jnp.concatenate(
        [jnp.swapaxes(head_bias, 0, 1).reshape(ways, 3 * heads_local), inner_bias], axis=1
    )
    if whole_path:
        out_qkv, out_out, gx_doc, gx_query, tensor_grads = finish_kernel(
            jnp.concatenate([dot_tn(x_low, p).astype(BF) for p in pre], axis=1),
            dot_tn(mixed, branch_low).astype(BF),
            x_grad,
            tensor_grads.reshape(ways, -1, 128),
        )
        tensor_grads = tensor_grads.reshape(-1)
    else:
        gx_doc, gx_query = rows_out(x_grad)
        gx_doc, gx_query = gx_doc.astype(F32), gx_query.astype(F32)
        out_out = sum_out.finish()
        out_qkv = functools.reduce(jnp.add, [item.finish() for item in head_sums])
        for dr in [1] + chip_bits[::-1]:
            size = grad_proj.shape[0] // 2
            got = exchange(grad_proj[size:].astype(BF), dr=dr)
            grad_proj = grad_proj[:size] + got.astype(F32)
        for dt in (1, 2):
            grad_proj = grad_proj + exchange(grad_proj, dt=dt)
        for dt in (2, 1):
            tensor_grads = tensor_grads[:dt] + exchange(tensor_grads[dt:], dt=dt)
            vectors = vectors + exchange(vectors, dt=dt)
        for dr in [1] + chip_bits:
            tensor_grads = tensor_grads + exchange(tensor_grads, dr=dr)
            vectors = vectors + exchange(vectors, dr=dr)
        tensor_grads = tensor_grads[0]
    return (
        y_doc,
        y_query,
        loss_out,
        gx_doc,
        gx_query,
        out_qkv,
        tensor_grads[: 3 * heads_local].reshape(3, heads_local),
        out_out,
        vectors[0],
        vectors[1],
        vectors[2],
        out_in,
        tensor_grads[3 * heads_local :],
        out_back,
        vectors[3],
        vectors[4],
        vectors[5],
        grad_proj,
    )


def solution(mesh):
    rows = P(None, ("dp", "tensor"), None)
    in_specs = (
        rows,
        rows,
        rows,
        rows,
        P(),
        P(None, "dp"),
        P(None, "dp", "tensor"),
        P(None, "tensor"),
        P("tensor", "dp"),
        P(),
        P(),
        P(),
        P("dp", "tensor"),
        P("tensor"),
        P("tensor", "dp"),
        P(),
        P(),
        P(),
        P("dp", None),
    )
    out_specs = (
        rows,
        rows,
        P(None, ("dp", "tensor")),
        rows,
        rows,
        P(None, "dp", "tensor"),
        P(None, "tensor"),
        P("tensor", "dp"),
        P(),
        P(),
        P(),
        P("dp", "tensor"),
        P("tensor"),
        P("tensor", "dp"),
        P(),
        P(),
        P(),
        P("dp", None),
    )
    return jax.shard_map(body, mesh=mesh, in_specs=in_specs, out_specs=out_specs, check_vma=False)
```

```python
import functools

import jax
import jax.numpy as jnp
from jax import lax
from jax.experimental import pallas as pl
from jax.experimental.pallas import tpu as pltpu
from jax.sharding import PartitionSpec as P

HEAD_WIDTH = 64
QLEN = 32
FULL_PRECISION = lax.Precision.HIGHEST
TAU = 20.0
EPS = 1e-05
LOGIT_SCALE = 2.0
MASKED = -1e30
AXES = ("dp", "tensor")
MESH = pl.DeviceIdType.MESH
BF = jnp.bfloat16
F32 = jnp.float32


def layer_norm(values, gain, shift):
    center = values - jnp.mean(values, axis=-1, keepdims=True)
    spread = jnp.mean(center * center, axis=-1, keepdims=True)
    return center * lax.rsqrt(spread + EPS) * gain + shift


def normalize(values):
    return values * lax.rsqrt(jnp.sum(values * values, axis=-1, keepdims=True) + 1e-06)


def gelu_exact(values):
    return jax.nn.gelu(values, approximate=False)


def dot_nn(a, b):
    return lax.dot_general(a, b, (((1,), (0,)), ((), ())), preferred_element_type=F32)


def dot_nt(a, b):
    return lax.dot_general(a, b, (((1,), (1,)), ((), ())), preferred_element_type=F32)


def dot_tn(a, b):
    return lax.dot_general(a, b, (((0,), (0,)), ((), ())), preferred_element_type=F32)


def differing(a, b, bits):
    total = 0
    for bit in range(bits):
        x, y = (a // 2**bit) % 2, (b // 2**bit) % 2
        total = total + 2**bit * (x + y - 2 * x * y)
    return total


class Around:
    def __init__(self):
        self.rank = lax.axis_index("dp")
        self.column = lax.axis_index("tensor")
        self.core = self.rank % 2
        self.base = self.rank - self.core

    def other(self, bit):
        rank = self.rank
        return (rank + bit - 2 * bit * ((rank // bit) % 2), self.column)

    def along(self, dt):
        return (self.rank, differing(self.column, dt, 2))

    def greet(self):
        barrier = pltpu.get_barrier_semaphore()
        for dc in range(2):
            for dt in range(4):
                if dc + dt > 0:
                    pl.semaphore_signal(
                        barrier,
                        inc=1,
                        device_id=(self.base + (self.core + dc) % 2, (self.column + dt) % 4),
                        device_id_type=MESH,
                    )
        for bit in (2, 4):
            pl.semaphore_signal(
                barrier, inc=1, device_id=self.other(bit), device_id_type=MESH
            )

    def await_all(self):
        pl.semaphore_wait(pltpu.get_barrier_semaphore(), 9)

    def meet(self):
        self.greet()
        self.await_all()


def feature_block(rank, p):
    return differing(rank, 2 * (p % 4) + p // 4, 3)


class Sender:
    def __init__(self, send_sem, recv_sem):
        self.send_sem, self.recv_sem = send_sem, recv_sem
        self.sent = []

    def __call__(self, src, dst, to):
        at = len(self.sent)
        copy = pltpu.make_async_remote_copy(
            src_ref=src,
            dst_ref=dst,
            send_sem=self.send_sem.at[at],
            recv_sem=self.recv_sem.at[at],
            device_id=to,
            device_id_type=MESH,
        )
        self.sent.append(copy)
        return copy

    def drain(self):
        for copy in self.sent:
            copy.wait_send()


class RowMoves:
    def __init__(self, around, inward, docs, asked, packed, send_sem, recv_sem):
        core, column, base = around.core, around.column, around.base
        lonely = 3 * core == column
        self.copies, self.arrivals = [], []
        size, few, width = docs.shape[1], asked.shape[1], docs.shape[2]
        block = width // 8
        for n in range(2):
            q, m = (column % 2, n) if inward else (n, column // 2)
            if inward:
                mine = jnp.logical_and(lonely, column // 2 == n)
                to = (base + column // 2, 2 * n + core)
                here = jnp.logical_and(lonely, column % 2 == n)
                holder = base + column // 2
            else:
                mine = jnp.logical_and(lonely, core == n)
                to = (base + column % 2, 2 * core + n)
                here = jnp.logical_and(lonely, column // 2 == n)
                holder = around.rank
            wheres = [
                pl.ds(pl.multiple_of(feature_block(holder, p) * block, block), block)
                for p in range(8)
            ]
            for kind, (ref, many, begin) in enumerate(((docs, size, 0), (asked, few, 2 * size))):
                span = pl.ds(pl.multiple_of(begin + q * many, few), many)
                aways, locals_ = [], []
                for p in list(range(8)) + [None]:
                    if p is None:
                        rows, flat = packed.at[span, :], ref.at[m]
                    else:
                        rows = packed.at[span, pl.ds(p * block, block)]
                        flat = ref.at[m, :, wheres[p]]
                    src, dst = (flat, rows) if inward else (rows, flat)
                    aways.append(
                        pltpu.make_async_remote_copy(
                            src_ref=src,
                            dst_ref=dst,
                            send_sem=send_sem.at[n, kind],
                            recv_sem=recv_sem.at[q if inward else m, kind],
                            device_id=to,
                            device_id_type=MESH,
                        )
                    )
                    locals_.append(pltpu.make_async_copy(src, dst, send_sem.at[n, kind]))
                self.copies.append((mine, locals_, aways))
                if inward:
                    land = packed.at[pl.ds(begin + n * many, many), :]
                else:
                    land = ref.at[n]
                came = pltpu.make_async_remote_copy(
                    src_ref=land,
                    dst_ref=land,
                    send_sem=send_sem.at[n, kind],
                    recv_sem=recv_sem.at[n, kind],
                    device_id=to,
                    device_id_type=MESH,
                )
                self.arrivals.append((here, came))

    def start(self):
        for mine, locals_, aways in self.copies:

            @pl.when(mine)
            def _(locals_=locals_):
                for copy in locals_[:8]:
                    copy.start()

            @pl.when(jnp.logical_not(mine))
            def _(aways=aways):
                for copy in aways[:8]:
                    copy.start()

    def wait(self):
        for here, came in self.arrivals:

            @pl.when(jnp.logical_not(here))
            def _(came=came):
                came.wait_recv()

        for mine, locals_, aways in self.copies:

            @pl.when(mine)
            def _(locals_=locals_):
                locals_[8].wait()

            @pl.when(jnp.logical_not(mine))
            def _(aways=aways):
                aways[8].wait_send()


class WeightGather:
    slots = 31

    def __init__(
        self, around, sources, outs, feature_axis, tensor_axis, bits, send_sem, recv_sem, local_sem
    ):
        self.around, self.sources, self.outs = around, sources, outs
        self.feature_axis, self.tensor_axis, self.bits = feature_axis, tensor_axis, bits
        self.send_sem, self.recv_sem, self.local_sem = send_sem, recv_sem, local_sem
        self.all = range(len(sources))

    def place(self, j):
        return (j & 1) * 4 + (j >> 1)

    def line(self, a, j):
        index = [slice(None)] * len(self.sources[a].shape)
        size = self.sources[a].shape[self.feature_axis[a]]
        index[self.feature_axis[a]] = pl.ds(self.place(j) * size, size)
        return self.outs[a].at[tuple(index)]

    def piece(self, a, j, source, column=None):
        column = self.around.column if column is None else column
        index = [slice(None)] * len(self.sources[a].shape)
        size = self.sources[a].shape[self.feature_axis[a]]
        index[self.feature_axis[a]] = pl.ds(self.place(j) * size, size)
        size = self.sources[a].shape[self.tensor_axis[a]]
        offset = pl.multiple_of(differing(column, source, 2) * size, size)
        index[self.tensor_axis[a]] = pl.ds(offset, size)
        return self.outs[a].at[tuple(index)]

    def origin(self, kind):
        column = self.around.column
        if kind == 0:
            return column, None
        if kind <= 3:
            return column - kind, column >= kind
        return column + (kind - 3), column + (kind - 3) <= 3

    def describe(self, a, slot):
        around, column = self.around, self.around.column
        first, second = self.bits[a]
        if slot >= 27:
            j = (0, first, second, first | second)[slot - 27]
            return None, self.line(a, j), self.line(a, j | 1), around.other(1)
        if slot < 6:
            kind = slot if slot < 3 else (0 if slot == 3 else slot)
            to = column + 1 if slot < 3 else column - 1
            edge = column < 3 if slot < 3 else column > 0
            source, there = self.origin(kind)
            there = edge if there is None else jnp.logical_and(there, edge)
            src = self.sources[a] if kind == 0 else self.piece(a, 0, source)
            return there, src, self.piece(a, 0, source, to), (around.rank, to)
        kind = (slot - 6) % 7
        source, there = self.origin(kind)
        if slot < 20:
            bit = first if slot < 13 else second
            src = self.sources[a] if kind == 0 else self.piece(a, 0, source)
            return there, src, self.piece(a, bit, source), around.other(bit)
        src, dst = self.piece(a, first, source), self.piece(a, first | second, source)
        return there, src, dst, around.other(second)

    def landing(self, a, slot):
        first, second = self.bits[a]
        if slot >= 27:
            return None, self.line(a, (0, first, second, first | second)[slot - 27] | 1)
        if slot < 6:
            kind, j = (slot + 1, 0)
        else:
            kind, j = (slot - 6) % 7, (first, second, first | second)[(slot - 6) // 7]
        source, there = self.origin(kind)
        return there, self.piece(a, j, source)

    def copy(self, a, slot, src, dst, to):
        return pltpu.make_async_remote_copy(
            src_ref=src,
            dst_ref=dst,
            send_sem=self.send_sem.at[a, slot],
            recv_sem=self.recv_sem.at[a, slot],
            device_id=to,
            device_id_type=MESH,
        )

    def when(self, condition, act):
        if condition is None:
            act()
        else:
            pl.when(condition)(act)

    def start(self, a, slot):
        condition, src, dst, to = self.describe(a, slot)
        self.when(condition, lambda: self.copy(a, slot, src, dst, to).start())

    def sent(self, a, slot):
        condition, src, dst, to = self.describe(a, slot)
        self.when(condition, lambda: self.copy(a, slot, src, dst, to).wait_send())

    def arrived(self, a, slot):
        condition, dst = self.landing(a, slot)
        to = self.around.other(1)
        self.when(condition, lambda: self.copy(a, slot, dst, dst, to).wait_recv())

    def home(self, a):
        return pltpu.make_async_copy(
            self.sources[a], self.piece(a, 0, self.around.column), self.local_sem.at[a]
        )

    def begin(self):
        for a in self.all:
            for slot in (0, 3, 6, 13):
                self.start(a, slot)
        for a in self.all:
            self.home(a).start()

    def onward(self, a, kind):
        self.arrived(a, 6 + kind)
        self.start(a, 20 + kind)

    def hop(self, n):
        for a in self.all:
            for kind, slot in ((n, n - 1), (n + 3, n + 2)):
                self.arrived(a, slot)
                if n < 3:
                    self.start(a, slot + 1)
                self.start(a, 6 + kind)
                self.start(a, 13 + kind)
        for a in self.all:
            for kind in (0,) if n == 1 else (n - 1, n + 2):
                self.onward(a, kind)

    def finish(self):
        for a in self.all:
            self.home(a).wait()
            self.start(a, 27)
        for a in self.all:
            for kind in (3, 6):
                self.onward(a, kind)
            self.start(a, 28)
        for begin, slot in ((13, 29), (20, 30)):
            for a in self.all:
                for kind in range(7):
                    self.arrived(a, begin + kind)
                self.start(a, slot)
        for a in self.all:
            for slot in range(27, 31):
                self.arrived(a, slot)
            for slot in range(31):
                self.sent(a, slot)


def gathered(weight, feature_axis, tensor_axis):
    shape = list(weight.shape)
    shape[feature_axis] *= 8
    shape[tensor_axis] *= 4
    return jax.ShapeDtypeStruct(tuple(shape), weight.dtype)


def gather_kernel(x_doc, x_query, qkv, out, proj, bias, picks):
    ways, groups = 4, 8
    quarter, width = x_doc.shape[1:]
    asked = x_query.shape[1]

    def kernel(
        xd_ref, xq_ref, qkv_ref, out_ref, proj_ref, bias_ref, picks_ref,
        x_o, qkv_o, out_o, proj_o, bias_o, picks_o,
        send_sem, recv_sem, small_send, small_recv, x_send, x_recv, local_sem,
    ):
        around = Around()
        around.meet()
        other, along = around.other, around.along
        gather = WeightGather(
            around,
            [qkv_ref.at[0:2], qkv_ref.at[2:3], out_ref],
            [qkv_o.at[0:2], qkv_o.at[2:3], out_o],
            [1, 1, 1],
            [2, 2, 0],
            [(2, 4), (4, 2), (4, 2)],
            send_sem,
            recv_sem,
            local_sem,
        )
        moves = RowMoves(around, True, xd_ref, xq_ref, x_o, x_send, x_recv)
        send = Sender(small_send, small_recv)
        gather.begin()
        place = gather.place
        small = [send(bias_ref, bias_o.at[dt], along(dt)) for dt in range(1, ways)]
        local = [pltpu.make_async_copy(bias_ref, bias_o.at[0], local_sem.at[3])]
        flat = []
        for n, (ref, o) in enumerate(((proj_ref, proj_o), (picks_ref, picks_o))):
            local.append(pltpu.make_async_copy(ref, o.at[0], local_sem.at[4 + n]))
            flat.append(
                (
                    send(ref, o.at[place(2)], other(2)),
                    send(ref, o.at[place(4)], other(4)),
                    send(ref, o.at[place(1)], other(1)),
                    send(o.at[place(2)], o.at[place(6)], other(4)),
                    send(o.at[place(2)], o.at[place(3)], other(1)),
                    send(o.at[place(4)], o.at[place(5)], other(1)),
                    send(o.at[place(6)], o.at[place(7)], other(1)),
                )
            )
        for copy in small + local + [c for f in flat for c in f[:3]]:
            copy.start()
        gather.hop(1)
        moves.start()
        for f in flat:
            f[0].wait_recv()
            f[3].start()
            f[4].start()
            f[1].wait_recv()
            f[5].start()
        gather.hop(2)
        gather.hop(3)
        for f in flat:
            f[3].wait_recv()
            f[6].start()
        gather.finish()
        for f in flat:
            for n in (2, 4, 5, 6):
                f[n].wait_recv()
        for copy in small:
            copy.wait_recv()
        for copy in local:
            copy.wait()
        moves.wait()
        send.drain()

    anywhere = pl.BlockSpec(memory_space=pl.ANY)
    dma = pltpu.SemaphoreType.DMA
    return pl.pallas_call(
        kernel,
        out_shape=[
            jax.ShapeDtypeStruct((2 * (quarter + asked), width), x_doc.dtype),
            gathered(qkv, 1, 2),
            gathered(out, 1, 0),
            jax.ShapeDtypeStruct((groups,) + proj.shape, proj.dtype),
            jax.ShapeDtypeStruct((ways,) + bias.shape, bias.dtype),
            jax.ShapeDtypeStruct((groups,) + picks.shape, picks.dtype),
        ],
        in_specs=[anywhere] * 7,
        out_specs=[anywhere] * 6,
        scratch_shapes=[
            dma((3, WeightGather.slots)),
            dma((3, WeightGather.slots)),
            dma((17,)),
            dma((17,)),
            dma((2, 2)),
            dma((2, 2)),
            dma((6,)),
        ],
        compiler_params=pltpu.CompilerParams(collective_id=0, has_side_effects=True),
        name="gather_weights",
    )(x_doc, x_query, qkv, out, proj, bias, picks)


def turned(values):
    lane = lax.broadcasted_iota(jnp.int32, (1, 128), 1)
    ahead = pltpu.roll(values, 96, 1)
    behind = pltpu.roll(values, 32, 1)
    return jnp.where(lane % HEAD_WIDTH < HEAD_WIDTH // 2, ahead, behind)


def project_heads(x, weights, bias, cosine, sine):
    rows, width = x.shape
    columns = 256
    steps = width // columns

    def kernel(x_ref, w_ref, b_ref, c_ref, s_ref, o_ref):
        got = dot_nn(x_ref[...], w_ref[0]) + b_ref[0]
        for at in range(0, columns, 128):
            piece = got[:, at : at + 128]
            o_ref[0, :, at : at + 128] = (piece * c_ref[0] + turned(piece) * s_ref[0]).astype(BF)

    return pl.pallas_call(
        kernel,
        grid=(3, steps),
        in_specs=[
            pl.BlockSpec((rows, width), lambda j, n: (0, 0)),
            pl.BlockSpec((1, width, columns), lambda j, n: (j, 0, n)),
            pl.BlockSpec((1, 1, columns), lambda j, n: (j, 0, n)),
            pl.BlockSpec((1, rows, 128), lambda j, n: (j, 0, 0)),
            pl.BlockSpec((1, rows, 128), lambda j, n: (j, 0, 0)),
        ],
        out_specs=pl.BlockSpec((1, rows, columns), lambda j, n: (j, 0, n)),
        out_shape=jax.ShapeDtypeStruct((3, rows, width), BF),
        compiler_params=pltpu.CompilerParams(vmem_limit_bytes=40 << 20),
        name="project_heads",
    )(x, weights, bias[:, None, :], cosine, sine)


def attention_forward(qkv, far_kv, col_labels, own_labels, far_labels):
    rows, width = qkv.shape[1:]
    docs = far_kv.shape[1]
    block = 128
    asked = rows - docs

    def kernel(qkv_ref, far_ref, lc_ref, lo_ref, lf_ref, o_ref):
        lane = lax.broadcasted_iota(jnp.int32, (1, 128), 1)

        def part(start, size, keys, sames):
            q_block = qkv_ref[0, pl.ds(start, size), :]
            outs = []
            for head in range(2):
                mask = (lane // HEAD_WIDTH) == head
                q_head = jnp.where(mask, q_block, jnp.zeros_like(q_block))
                scores = [
                    jnp.where(same, dot_nt(q_head, key), MASKED)
                    for (key, _), same in zip(keys, sames)
                ]
                top = functools.reduce(
                    jnp.maximum, [jnp.max(s, axis=-1, keepdims=True) for s in scores]
                )
                powers = [jnp.exp(s - top) for s in scores]
                total = functools.reduce(
                    jnp.add, [jnp.sum(p, axis=-1, keepdims=True) for p in powers]
                )
                mixed = functools.reduce(
                    jnp.add, [dot_nn(p.astype(BF), value) for p, (_, value) in zip(powers, keys)]
                )
                outs.append(mixed * (1.0 / total))
            o_ref[pl.ds(start, size), :] = jnp.where(lane < HEAD_WIDTH, outs[0], outs[1]).astype(BF)

        doc_keys = [
            (qkv_ref[1, :docs, :], qkv_ref[2, :docs, :]),
            (far_ref[0], far_ref[1]),
        ]
        for at in range(docs // block):
            labels = lc_ref[pl.ds(at * block, block), :]
            part(at * block, block, doc_keys, [labels == lo_ref[...], labels == lf_ref[...]])
        row = lax.broadcasted_iota(jnp.int32, (asked, asked), 0) // QLEN
        col = lax.broadcasted_iota(jnp.int32, (asked, asked), 1) // QLEN
        part(docs, asked, [(qkv_ref[1, docs:, :], qkv_ref[2, docs:, :])], [row == col])

    whole = lambda shape: pl.BlockSpec(shape, lambda h: (0, 0))
    return pl.pallas_call(
        kernel,
        grid=(width // 128,),
        in_specs=[
            pl.BlockSpec((3, rows, 128), lambda h: (0, 0, h)),
            pl.BlockSpec((2, docs, 128), lambda h: (0, 0, h)),
            whole((docs, 1)),
            whole((1, docs)),
            whole((1, docs)),
        ],
        out_specs=pl.BlockSpec((rows, 128), lambda h: (0, h)),
        out_shape=jax.ShapeDtypeStruct((rows, width), BF),
        compiler_params=pltpu.CompilerParams(vmem_limit_bytes=40 << 20),
        name="attend_forward",
        cost_estimate=pl.CostEstimate(
            flops=32 * rows * 2 * docs * width,
            bytes_accessed=2 * (4 * rows + 2 * docs) * width,
            transcendentals=rows * 2 * docs * width // 64,
        ),
    )(qkv, far_kv, col_labels, own_labels, far_labels)


def attention_backward(
    first, count, qkv, far_kv, grad, cosine, sine, far_cosine, far_sine,
    col_labels, own_labels, far_labels,
):
    rows = qkv.shape[1]
    docs = far_kv.shape[1]
    width = count * 128
    block = 128
    asked = rows - docs

    def kernel(
        qkv_ref, far_ref, g_ref, c_ref, s_ref, fc_ref, fs_ref, lc_ref, lo_ref, lf_ref,
        dq_ref, own_ref, give_ref, sums_own, sums_far,
    ):
        lane = lax.broadcasted_iota(jnp.int32, (1, 128), 1)
        sums_own[...] = jnp.zeros_like(sums_own)
        sums_far[...] = jnp.zeros_like(sums_far)

        def part(start, size, keys, sames, sums):
            q_block = qkv_ref[0, pl.ds(start, size), :]
            g_block = g_ref[pl.ds(start, size), :]
            grads = []
            for head in range(2):
                mask = (lane // HEAD_WIDTH) == head
                q_head = jnp.where(mask, q_block, jnp.zeros_like(q_block))
                g_head = jnp.where(mask, g_block, jnp.zeros_like(g_block))
                scores = [
                    jnp.where(same, dot_nt(q_head, key), MASKED)
                    for (key, _), same in zip(keys, sames)
                ]
                top = functools.reduce(
                    jnp.maximum, [jnp.max(s, axis=-1, keepdims=True) for s in scores]
                )
                powers = [jnp.exp(s - top) for s in scores]
                total = functools.reduce(
                    jnp.add, [jnp.sum(p, axis=-1, keepdims=True) for p in powers]
                )
                inverse = 1.0 / total
                g_head = (g_head.astype(F32) * inverse).astype(BF)
                pulls = [dot_nt(g_head, value) for _, value in keys]
                mean = functools.reduce(
                    jnp.add,
                    [jnp.sum(p * d, axis=-1, keepdims=True) for p, d in zip(powers, pulls)],
                ) * inverse
                slopes = [(p * (d - mean)).astype(BF) for p, d in zip(powers, pulls)]
                got = functools.reduce(
                    jnp.add, [dot_nn(s, key) for s, (key, _) in zip(slopes, keys)]
                )
                grads.append(got * 0.125)
                for (ref, begin, many), s, p in zip(sums, slopes, powers):
                    ref[0, pl.ds(begin, many), :] += dot_tn(s, q_head)
                    ref[1, pl.ds(begin, many), :] += dot_tn(p.astype(BF), g_head)
            whole = jnp.where(lane < HEAD_WIDTH, grads[0], grads[1])
            at = pl.ds(start, size)
            dq_ref[at, :] = (whole * c_ref[at, :] - turned(whole) * s_ref[at, :]).astype(BF)

        doc_keys = [
            (qkv_ref[1, :docs, :], qkv_ref[2, :docs, :]),
            (far_ref[0], far_ref[1]),
        ]
        for at in range(docs // block):
            labels = lc_ref[pl.ds(at * block, block), :]
            part(
                at * block,
                block,
                doc_keys,
                [labels == lo_ref[...], labels == lf_ref[...]],
                [(sums_own, 0, docs), (sums_far, 0, docs)],
            )
        row = lax.broadcasted_iota(jnp.int32, (asked, asked), 0) // QLEN
        col = lax.broadcasted_iota(jnp.int32, (asked, asked), 1) // QLEN
        part(
            docs,
            asked,
            [(qkv_ref[1, docs:, :], qkv_ref[2, docs:, :])],
            [row == col],
            [(sums_own, docs, asked)],
        )
        own_ref[0] = sums_own[0] * c_ref[...] - turned(sums_own[0]) * s_ref[...]
        own_ref[1] = sums_own[1]
        give_ref[0] = (sums_far[0] * fc_ref[...] - turned(sums_far[0]) * fs_ref[...]).astype(BF)
        give_ref[1] = sums_far[1].astype(BF)

    whole = lambda shape: pl.BlockSpec(shape, lambda h: (0, 0))
    return pl.pallas_call(
        kernel,
        grid=(count,),
        in_specs=[
            pl.BlockSpec((3, rows, 128), lambda h: (0, 0, h + first)),
            pl.BlockSpec((2, docs, 128), lambda h: (0, 0, h + first)),
            pl.BlockSpec((rows, 128), lambda h: (0, h + first)),
            whole((rows, 128)),
            whole((rows, 128)),
            whole((docs, 128)),
            whole((docs, 128)),
            whole((docs, 1)),
            whole((1, docs)),
            whole((1, docs)),
        ],
        out_specs=[
            pl.BlockSpec((rows, 128), lambda h: (0, h)),
            pl.BlockSpec((2, rows, 128), lambda h: (0, 0, h)),
            pl.BlockSpec((2, docs, 128), lambda h: (0, 0, h)),
        ],
        out_shape=[
            jax.ShapeDtypeStruct((rows, width), BF),
            jax.ShapeDtypeStruct((2, rows, width), F32),
            jax.ShapeDtypeStruct((2, docs, width), BF),
        ],
        scratch_shapes=[pltpu.VMEM((2, rows, 128), F32), pltpu.VMEM((2, docs, 128), F32)],
        compiler_params=pltpu.CompilerParams(vmem_limit_bytes=40 << 20),
        name="attend_backward",
        cost_estimate=pl.CostEstimate(
            flops=100 * rows * 2 * docs * width,
            bytes_accessed=4 * (6 * rows + 4 * docs) * width,
            transcendentals=rows * 2 * docs * width // 64,
        ),
    )(
        qkv, far_kv, grad, cosine, sine, far_cosine, far_sine, col_labels, own_labels, far_labels
    )


def project_and_attend(
    x, weights, bias, cosines, sines, col_labels, own_labels, far_labels,
    doc_cot, query_cot, up, back,
):
    rows, width = x.shape
    docs = col_labels.shape[0]
    asked = rows - docs
    pairs = width // 128
    block = 256
    columns = 256
    steps = width // columns
    assert pairs == 8

    def kernel(
        x_ref, w_ref, b_ref, c_ref, s_ref, lc_ref, lo_ref, lf_ref,
        cd_ref, cq_ref, up_ref, back_ref,
        qkv_o, far_o, o_ref, cot_o, up_o, back_o,
        held, far, load_sem, far_send, far_recv, row_send, row_recv, send_sem, recv_sem, local_sem,
    ):
        h = pl.program_id(0)

        def parts():
            around = Around()
            moves = RowMoves(around, True, cd_ref, cq_ref, cot_o, row_send, row_recv)
            gather = WeightGather(
                around,
                [up_ref, back_ref],
                [up_o, back_o],
                [0, 1],
                [1, 0],
                [(2, 4), (4, 2)],
                send_sem,
                recv_sem,
                local_sem,
            )
            return around, moves, gather

        @pl.when(h == 0)
        def _():
            loads = [pltpu.make_async_copy(w_ref.at[j], held.at[j], load_sem.at[j]) for j in range(3)]
            for j in (1, 2, 0):
                loads[j].start()
            around, _, gather = parts()
            around.meet()
            gather.begin()
            copies = []
            for j in (1, 2, 0):
                loads[j].wait()
                for n in range(steps):
                    at = pl.ds(n * columns, columns)
                    got = dot_nn(x_ref[...], held[j, :, at]) + b_ref[j : j + 1, at]
                    for m in range(columns // 128):
                        piece = got[:, m * 128 : (m + 1) * 128]
                        low = piece * c_ref[j] + turned(piece) * s_ref[j]
                        qkv_o[j, :, n * columns + m * 128 : n * columns + (m + 1) * 128] = low.astype(BF)
                    if j > 0:
                        copy = pltpu.make_async_remote_copy(
                            src_ref=qkv_o.at[j, pl.ds(0, docs), at],
                            dst_ref=far.at[j - 1, :, at],
                            send_sem=far_send.at[j - 1, n],
                            recv_sem=far_recv.at[j - 1, n],
                            device_id=around.other(1),
                            device_id_type=MESH,
                        )
                        copy.start()
                        copies.append(copy)
            for copy in copies:
                copy.wait()
            pltpu.make_async_copy(far, far_o, load_sem.at[3]).start()

        @pl.when(h == 1)
        def _():
            parts()[2].hop(1)

        @pl.when(h == 4)
        def _():
            _, moves, gather = parts()
            gather.hop(2)
            moves.start()

        @pl.when(h == 7)
        def _():
            parts()[2].hop(3)

        lane = lax.broadcasted_iota(jnp.int32, (1, 128), 1)
        pair = pl.ds(pl.multiple_of(h * 128, 128), 128)

        def part(start, size, keys, sames):
            q_block = qkv_o[0, pl.ds(start, size), pair]
            outs = []
            for head in range(2):
                mask = (lane // HEAD_WIDTH) == head
                q_head = jnp.where(mask, q_block, jnp.zeros_like(q_block))
                scores = [
                    jnp.where(same, dot_nt(q_head, key), MASKED)
                    for (key, _), same in zip(keys, sames)
                ]
                top = functools.reduce(
                    jnp.maximum, [jnp.max(s, axis=-1, keepdims=True) for s in scores]
                )
                powers = [jnp.exp(s - top) for s in scores]
                total = functools.reduce(
                    jnp.add, [jnp.sum(p, axis=-1, keepdims=True) for p in powers]
                )
                mixed = functools.reduce(
                    jnp.add, [dot_nn(p.astype(BF), value) for p, (_, value) in zip(powers, keys)]
                )
                outs.append(mixed * (1.0 / total))
            o_ref[pl.ds(start, size), :] = jnp.where(lane < HEAD_WIDTH, outs[0], outs[1]).astype(BF)

        doc_keys = [
            (qkv_o[1, :docs, pair], qkv_o[2, :docs, pair]),
            (far[0, :, pair], far[1, :, pair]),
        ]
        for at in range(docs // block):
            labels = lc_ref[pl.ds(at * block, block), :]
            part(at * block, block, doc_keys, [labels == lo_ref[...], labels == lf_ref[...]])
        row = lax.broadcasted_iota(jnp.int32, (asked, asked), 0) // QLEN
        col = lax.broadcasted_iota(jnp.int32, (asked, asked), 1) // QLEN
        part(docs, asked, [(qkv_o[1, docs:, pair], qkv_o[2, docs:, pair])], [row == col])

        @pl.when(h == pairs - 1)
        def _():
            _, moves, gather = parts()
            gather.finish()
            moves.wait()
            pltpu.make_async_copy(far, far_o, load_sem.at[3]).wait()

    def whole(shape):
        return pl.BlockSpec(shape, lambda h: (0,) * len(shape))

    anywhere = pl.BlockSpec(memory_space=pl.ANY)
    dma = pltpu.SemaphoreType.DMA
    return pl.pallas_call(
        kernel,
        grid=(pairs,),
        in_specs=[
            whole((rows, width)),
            anywhere,
            whole((3, width)),
            whole((3, rows, 128)),
            whole((3, rows, 128)),
            whole((docs, 1)),
            whole((1, docs)),
            whole((1, docs)),
        ]
        + [anywhere] * 4,
        out_specs=[
            whole((3, rows, width)),
            anywhere,
            pl.BlockSpec((rows, 128), lambda h: (0, h)),
        ]
        + [anywhere] * 3,
        out_shape=[
            jax.ShapeDtypeStruct((3, rows, width), BF),
            jax.ShapeDtypeStruct((2, docs, width), BF),
            jax.ShapeDtypeStruct((rows, width), BF),
            jax.ShapeDtypeStruct((rows, width), doc_cot.dtype),
            gathered(up, 0, 1),
            gathered(back, 1, 0),
        ],
        scratch_shapes=[
            pltpu.VMEM((3, width, width), BF),
            pltpu.VMEM((2, docs, width), BF),
            dma((4,)),
            dma((2, steps)),
            dma((2, steps)),
            dma((2, 2)),
            dma((2, 2)),
            dma((2, WeightGather.slots)),
            dma((2, WeightGather.slots)),
            dma((2,)),
        ],
        compiler_params=pltpu.CompilerParams(
            vmem_limit_bytes=56 << 20, collective_id=4, has_side_effects=True
        ),
        name="project_and_attend",
        cost_estimate=pl.CostEstimate(
            flops=64 * rows * 2 * docs * width,
            bytes_accessed=2 * (4 * rows + 2 * docs) * width,
            transcendentals=rows * 2 * docs * width // 64,
        ),
    )(
        x, weights, bias, cosines, sines, col_labels, own_labels, far_labels,
        doc_cot, query_cot, up, back,
    )


def feed_forward(hidden, up, bias, back):
    rows, width = hidden.shape
    units = up.shape[1]
    columns, piece = 512, 256

    def kernel(h_ref, u_ref, b_ref, w_ref, a_ref, d_ref, o_ref):
        @pl.when(pl.program_id(0) == 0)
        def _():
            o_ref[...] = jnp.zeros_like(o_ref)

        for at in range(0, columns, piece):
            z = dot_nn(h_ref[...], u_ref[:, at : at + piece]) + b_ref[:, at : at + piece]
            bell = jnp.exp(-0.5 * z * z)
            t = 1.0 / (1.0 + 0.23164189 * jnp.abs(z))
            tail = 0.5 * t * (
                0.254829592
                + t * (-0.284496736 + t * (1.421413741 + t * (-1.453152027 + t * 1.061405429)))
            ) * bell
            below = jnp.where(z < 0.0, tail, 1.0 - tail)
            low = (z * below).astype(BF)
            a_ref[:, at : at + piece] = low
            d_ref[:, at : at + piece] = (below + z * (bell * 0.3989422804014327)).astype(BF)
            o_ref[...] += dot_nn(low, w_ref[at : at + piece, :])

    return pl.pallas_call(
        kernel,
        grid=(units // columns,),
        in_specs=[
            pl.BlockSpec((rows, width), lambda n: (0, 0)),
            pl.BlockSpec((width, columns), lambda n: (0, n)),
            pl.BlockSpec((1, columns), lambda n: (0, n)),
            pl.BlockSpec((columns, width), lambda n: (n, 0)),
        ],
        out_specs=[
            pl.BlockSpec((rows, columns), lambda n: (0, n)),
            pl.BlockSpec((rows, columns), lambda n: (0, n)),
            pl.BlockSpec((rows, width), lambda n: (0, 0)),
        ],
        out_shape=[
            jax.ShapeDtypeStruct((rows, units), BF),
            jax.ShapeDtypeStruct((rows, units), BF),
            jax.ShapeDtypeStruct((rows, width), F32),
        ],
        compiler_params=pltpu.CompilerParams(vmem_limit_bytes=40 << 20),
        name="feed_forward",
    )(hidden, up, bias[None], back)


def feed_forward_backward(grad, back, slope, up, hidden, active):
    rows, width = grad.shape
    units = up.shape[1]
    columns = 512

    def kernel(g_ref, w_ref, d_ref, u_ref, h_ref, a_ref, o_ref, du_ref, dw_ref, db_ref):
        @pl.when(pl.program_id(0) == 0)
        def _():
            o_ref[...] = jnp.zeros_like(o_ref)

        g = g_ref[...]
        dw_ref[...] = dot_tn(a_ref[...], g).astype(BF)
        low = (dot_nt(g, w_ref[...]) * d_ref[...].astype(F32)).astype(BF)
        db_ref[...] = jnp.sum(low.astype(F32), axis=0, keepdims=True)
        o_ref[...] += dot_nt(low, u_ref[...])
        du_ref[...] = dot_tn(h_ref[...], low).astype(BF)

    return pl.pallas_call(
        kernel,
        grid=(units // columns,),
        in_specs=[
            pl.BlockSpec((rows, width), lambda n: (0, 0)),
            pl.BlockSpec((columns, width), lambda n: (n, 0)),
            pl.BlockSpec((rows, columns), lambda n: (0, n)),
            pl.BlockSpec((width, columns), lambda n: (0, n)),
            pl.BlockSpec((rows, width), lambda n: (0, 0)),
            pl.BlockSpec((rows, columns), lambda n: (0, n)),
        ],
        out_specs=[
            pl.BlockSpec((rows, width), lambda n: (0, 0)),
            pl.BlockSpec((width, columns), lambda n: (0, n)),
            pl.BlockSpec((columns, width), lambda n: (n, 0)),
            pl.BlockSpec((1, columns), lambda n: (0, n)),
        ],
        out_shape=[
            jax.ShapeDtypeStruct((rows, width), F32),
            jax.ShapeDtypeStruct((width, units), BF),
            jax.ShapeDtypeStruct((units, width), BF),
            jax.ShapeDtypeStruct((1, units), F32),
        ],
        compiler_params=pltpu.CompilerParams(vmem_limit_bytes=48 << 20),
        name="feed_forward_backward",
    )(grad, back, slope, up, hidden, active)


def loss_kernel(projection, labels, log_counts, picks):
    rows, columns = projection.shape
    docs = labels.shape[0]
    own = rows - docs
    tokens = 16 * own
    units, segments = 8, 4
    chunk = 64

    def kernel(
        p_ref, lab_ref, cnt_ref, pick_ref,
        grad_ref, loss_ref,
        asked_all, weight, sums, sums_all, coef_all, slope, part, part_low, got, tile, tile_got,
        send_sem, recv_sem, tile_send, tile_recv,
    ):
        around = Around()
        rank, column, core, base = around.rank, around.column, around.core, around.base
        chip, side = rank // 2, column % 2
        mine = (chip * 2 + side) * 2 + core
        unit = chip * 2 + side

        def flip(value, bit, on):
            return value + bit - 2 * bit * ((value // bit) % 2) if on else value

        def peer(i):
            to = flip(flip(flip(rank, 1, i & 1), 2, i & 4), 4, i & 8)
            return (to, flip(column, 1, i & 2))

        def index_of(i):
            to, z = peer(i)
            return ((to // 2) * 2 + z % 2) * 2 + to % 2

        barrier = pltpu.get_barrier_semaphore()
        peers = [peer(i) for i in range(1, 16)]
        for dt in (2, 3):
            for dc in range(2):
                away, z = around.along(dt)
                peers.append((flip(rank, 1, dc), z))
        for to in peers:
            pl.semaphore_signal(barrier, inc=1, device_id=to, device_id_type=MESH)
        pl.semaphore_wait(barrier, len(peers))

        values = p_ref[...]
        rate = lax.rsqrt(jnp.sum(values * values, axis=-1, keepdims=True) + 1e-06)
        unit_wide = values * rate
        unit_low = unit_wide.astype(BF)
        own_at = pl.ds(pl.multiple_of(mine * own, own), own)
        asked_all[own_at, :] = unit_low[docs:]

        def all_to_all(kind, src, dst):
            copies = []
            for i in range(1, 16):
                copy = pltpu.make_async_remote_copy(
                    src_ref=src(i),
                    dst_ref=dst(i),
                    send_sem=send_sem.at[kind, i],
                    recv_sem=recv_sem.at[kind, i],
                    device_id=peer(i),
                    device_id_type=MESH,
                )
                copy.start()
                copies.append(copy)
            return copies

        first = all_to_all(0, lambda i: asked_all.at[own_at, :], lambda i: asked_all.at[own_at, :])
        doc_low = unit_low[:docs]
        seg_of = lab_ref[...]
        for copy in first:
            copy.wait_recv()
        queries = asked_all[...]
        sums[...] = jnp.zeros_like(sums)
        for at in range(0, docs, chunk):
            cosines = dot_nt(doc_low[at : at + chunk], queries)
            power = jnp.exp(TAU * (cosines - 1.0))
            weight[at : at + chunk, :] = power
            for s in range(segments):
                chosen = seg_of[at : at + chunk] == s
                sums[s : s + 1, :] += jnp.sum(
                    jnp.where(chosen, power, 0.0), axis=0, keepdims=True
                )
        second = all_to_all(1, lambda i: sums, lambda i: sums_all.at[mine])
        sums_all[mine] = sums[...]
        for copy in second:
            copy.wait_recv()
        row = lax.broadcasted_iota(jnp.int32, (8, tokens), 0)
        lane = lax.broadcasted_iota(jnp.int32, (8, tokens), 1)
        valid = row < segments
        totals, logits = [], []
        for n in range(units):
            total = jnp.where(valid, sums_all[2 * n] + sums_all[2 * n + 1], 1.0)
            best = (jnp.log(total) - cnt_ref[8 * n : 8 * n + 8, :]) / TAU + 1.0
            for step in (1, 2, 4, 8, 16):
                other = jnp.where(
                    (lane // step) % 2 == 1,
                    pltpu.roll(best, step, 1),
                    pltpu.roll(best, tokens - step, 1),
                )
                best = best + other
            totals.append(total)
            logits.append(jnp.where(valid, LOGIT_SCALE * best, MASKED))
        peak = functools.reduce(
            jnp.maximum, [jnp.max(x, axis=0, keepdims=True) for x in logits]
        )
        powers = [jnp.exp(x - peak) for x in logits]
        mass = functools.reduce(jnp.add, [jnp.sum(x, axis=0, keepdims=True) for x in powers])
        picked = jnp.zeros_like(peak)
        for n in range(units):
            hit = jnp.logical_and(valid, pick_ref[...] == n * segments + row)
            picked = picked + jnp.sum(jnp.where(hit, logits[n], 0.0), axis=0, keepdims=True)
            slope_n = LOGIT_SCALE * (powers[n] / mass - jnp.where(hit, 1.0, 0.0))
            coef_all[n] = slope_n / totals[n]
        losses = peak + jnp.log(mass) - picked
        tiles = []
        for q in range(2):
            at = mine * own + q * QLEN
            value = jnp.sum(
                jnp.where(lane[:1] == at, losses, 0.0), axis=1, keepdims=True
            )
            tile[q, 0] = jnp.broadcast_to(value, (8, 128))
            tile[q, 1] = jnp.zeros((8, 128), F32)
        lonely = 3 * core == column
        for q in range(2):
            here = jnp.logical_and(lonely, core == q)
            slot = column // 2
            away = pltpu.make_async_remote_copy(
                src_ref=tile.at[q],
                dst_ref=tile_got.at[slot],
                send_sem=tile_send.at[q],
                recv_sem=tile_recv.at[slot],
                device_id=(base + column % 2, 2 * core + q),
                device_id_type=MESH,
            )
            tiles.append((here, away))

            @pl.when(here)
            def _(q=q):
                tile_got[slot] = tile[q]

            @pl.when(jnp.logical_not(here))
            def _(away=away):
                away.start()

        coef = coef_all[unit]
        doc_grads = []
        part[...] = jnp.zeros_like(part)
        for at in range(0, docs, chunk):
            spread = jnp.zeros((chunk, tokens), F32)
            for s in range(segments):
                chosen = seg_of[at : at + chunk] == s
                spread = jnp.where(chosen, coef[s : s + 1, :], spread)
            low = (weight[at : at + chunk, :] * spread).astype(BF)
            slope[at : at + chunk, :] = low
            doc_grads.append(dot_nn(low, queries))
        part[...] = dot_tn(slope[...], doc_low)
        part_low[...] = part[...].astype(BF)

        def theirs(i):
            return part_low.at[pl.ds(pl.multiple_of(index_of(i) * own, own), own), :]

        third = all_to_all(2, theirs, lambda i: got.at[i])

        def pull(grad, begin, size):
            v, r = unit_wide[begin : begin + size], rate[begin : begin + size]
            inner = jnp.sum(v * grad, axis=-1, keepdims=True)
            return ((grad - v * inner) * r).astype(BF)

        for n, at in enumerate(range(0, docs, chunk)):
            grad_ref[at : at + chunk, :] = pull(doc_grads[n], at, chunk)
        total = part[own_at, :]
        for copy in third:
            copy.wait_recv()
        for i in range(1, 16):
            total = total + got[i].astype(F32)
        grad_ref[docs:, :] = pull(total, docs, own)
        for n in range(2):
            here = jnp.logical_and(lonely, column // 2 == n)
            came = pltpu.make_async_remote_copy(
                src_ref=tile.at[n],
                dst_ref=tile_got.at[n],
                send_sem=tile_send.at[n],
                recv_sem=tile_recv.at[n],
                device_id=peer(1),
                device_id_type=MESH,
            )

            @pl.when(jnp.logical_not(here))
            def _(came=came):
                came.wait_recv()

        loss_ref[...] = tile_got[:, 0]
        for here, away in tiles:

            @pl.when(jnp.logical_not(here))
            def _(away=away):
                away.wait_send()

        for copy in first + second + third:
            copy.wait_send()

    def whole(shape):
        return pl.BlockSpec(shape, lambda: (0,) * len(shape))

    vmem = pltpu.VMEM
    dma = pltpu.SemaphoreType.DMA
    return pl.pallas_call(
        kernel,
        in_specs=[
            whole(projection.shape),
            whole(labels.shape),
            whole(log_counts.shape),
            whole(picks.shape),
        ],
        out_specs=[whole((rows, columns)), whole((2, 8, 128))],
        out_shape=[
            jax.ShapeDtypeStruct((rows, columns), BF),
            jax.ShapeDtypeStruct((2, 8, 128), F32),
        ],
        scratch_shapes=[
            vmem((tokens, columns), BF),
            vmem((docs, tokens), F32),
            vmem((8, tokens), F32),
            vmem((16, 8, tokens), F32),
            vmem((units, 8, tokens), F32),
            vmem((docs, tokens), BF),
            vmem((tokens, columns), F32),
            vmem((tokens, columns), BF),
            vmem((16, own, columns), BF),
            vmem((2, 2, 8, 128), F32),
            vmem((2, 2, 8, 128), F32),
            dma((3, 16)),
            dma((3, 16)),
            dma((2,)),
            dma((2,)),
        ],
        compiler_params=pltpu.CompilerParams(
            collective_id=5, has_side_effects=True, vmem_limit_bytes=40 << 20
        ),
        name="loss",
        cost_estimate=pl.CostEstimate(
            flops=100 * docs * tokens * columns,
            bytes_accessed=8 * rows * columns,
            transcendentals=docs * tokens,
        ),
    )(projection, labels, log_counts, picks)


class MatrixSum:
    def __init__(
        self, around, send, axis, across, own, got, next_, near, far, home, local_sems,
        away=None, extras=(),
    ):
        self.axis, self.own, self.got, self.next, self.near = axis, own, got, next_, near
        self.block = own.shape[axis] // 4
        first, second = (2, 4) if across else (4, 2)
        self.gone, self.later = ((1, 3), 2) if across else ((2, 3), 1)
        self.cores = [send(src, dst, around.other(1)) for src, dst in far]
        self.loads = [
            pltpu.make_async_copy(src, dst, sem) for (src, dst), sem in zip(home, local_sems)
        ]
        self.firsts = [
            send(self.at(own, n), self.at(next_, slot), around.other(first))
            for slot, n in enumerate(self.gone)
        ]
        self.second = send(self.at(own, self.later), near, around.other(second))
        self.extras = extras
        self.away = None
        if away is not None:
            self.away = send(self.at(own, 0), away[1], around.along(away[0]))

    def at(self, ref, n):
        span = pl.ds(n * self.block, self.block)
        return ref.at[span, :] if self.axis == 0 else ref.at[:, span]

    def begin(self):
        for copy in self.cores + self.loads:
            copy.start()

    def add(self, n, ref, m):
        rows = self.block if self.axis == 0 else self.own.shape[0]
        step = 16 if self.axis == 0 else 128
        block = self.block

        @pl.loop(0, rows // step)
        def _(k):
            if self.axis == 0:
                to = (pl.ds(pl.multiple_of(n * block + k * step, step), step), slice(None))
                fr = (pl.ds(pl.multiple_of(m * block + k * step, step), step), slice(None))
            else:
                at = pl.ds(pl.multiple_of(k * step, step), step)
                to, fr = (at, pl.ds(n * block, block)), (at, pl.ds(m * block, block))
            self.own[to] = self.own[to] + ref[fr]

    def first_axis(self):
        for load in self.loads:
            load.wait()
        for copy in self.cores:
            copy.wait_recv()
        for n, copy in zip(self.gone, self.firsts):
            self.add(n, self.got, n)
            copy.start()
        for n in (self.later, 0):
            self.add(n, self.got, n)

    def second_axis(self):
        for copy in self.firsts:
            copy.wait_recv()
        self.add(self.later, self.next, 1)
        self.second.start()
        self.add(0, self.next, 0)

    def tensor(self):
        self.second.wait_recv()
        self.add(0, self.near, 0)
        for buffer, copy in self.extras:
            copy.wait_recv()
            self.add(0, buffer, 0)
        if self.away is not None:
            self.away.start()


class SmallSum:
    def __init__(self, around, send, got, run, bits=(1, 4, 2), tensor=(1, 2)):
        self.got, self.run = got, run
        tos = [around.other(bit) for bit in bits] + [around.along(dt) for dt in tensor]
        self.copies = [send(run.at[n], got.at[n], to) for n, to in enumerate(tos)]

    def begin(self):
        self.copies[0].start()

    def hop(self, n):
        self.copies[n].wait_recv()
        self.run[n + 1] = self.run[n] + self.got[n]
        if n + 1 < len(self.copies):
            self.copies[n + 1].start()


class ProjSum:
    def __init__(self, around, send, ref, run, got):
        self.ref, self.run, self.got = ref, run, got
        rows = ref.shape[0]
        self.half = [rows // 2, rows // 4, rows // 8]
        starts = [0, rows // 2, 3 * rows // 4]
        self.starts = starts
        self.copies = [
            send(ref.at[self.half[0] :, :], got.at[pl.ds(starts[0], self.half[0]), :], around.other(1))
        ]
        for n, bit in ((1, 4), (2, 2)):
            self.copies.append(
                send(
                    run.at[pl.ds(self.half[n], self.half[n]), :],
                    got.at[pl.ds(starts[n], self.half[n]), :],
                    around.other(bit),
                )
            )
        last = self.half[2]
        self.last = last
        base = rows
        for n, dt in ((0, 1), (1, 2)):
            self.copies.append(
                send(
                    run.at[pl.ds(rows // 2 + n * last, last), :],
                    got.at[pl.ds(base + n * last, last), :],
                    around.along(dt),
                )
            )

    def begin(self):
        self.copies[0].start()

    def hop(self, n):
        self.copies[n].wait_recv()
        rows = self.ref.shape[0]
        last = self.last
        if n < 3:
            size = self.half[n]
            old = self.ref if n == 0 else self.run
            total = old[:size, :] + self.got[pl.ds(self.starts[n], size), :]
            if n < 2:
                self.run[:size, :] = total
            else:
                self.run[pl.ds(rows // 2, last), :] = total
        else:
            at = rows // 2 + (n - 3) * last
            got = self.got[pl.ds(rows + (n - 3) * last, last), :]
            self.run[pl.ds(at + last, last), :] = self.run[pl.ds(at, last), :] + got
        if n + 1 < len(self.copies):
            self.copies[n + 1].start()

    def result(self):
        return self.run[pl.ds(self.ref.shape[0] // 2 + 2 * self.last, self.last), :]


def finish_kernel(x, weights, pre, mixed, branch, resid, tensor_sums):
    ways = 4
    rows, width = x.shape
    half, block = width // 2, width // 8
    share = width // ways
    docs = rows // 9 * 8
    quarter, asked = docs // 2, (rows - docs) // 2
    part = 3 * share

    def kernel(
        x_ref, w_ref, p_ref, m_ref, g_ref, r_ref, ten_ref,
        qkv_o, out_o, doc_o, ask_o, ten_o,
        xs, ws, ps, ms, gs, rs, low, qf, qa, q0, q1, q2, q3, of, oa, o0, o1, o2, o3,
        t_got, t_run, tz, send_sem, recv_sem, local_sem, row_send, row_recv,
    ):
        around = Around()
        around.greet()
        loads = {}
        for n, (name, src, dst) in enumerate(
            [("p", p_ref, ps), ("r", r_ref, rs)]
            + [(j, w_ref.at[j], ws.at[j]) for j in range(3)]
            + [("x", x_ref, xs), ("m", m_ref, ms), ("g", g_ref, gs)]
        ):
            loads[name] = pltpu.make_async_copy(src, dst, local_sem.at[n])
            loads[name].start()
        send = Sender(send_sem, recv_sem)
        small = SmallSum(around, send, t_got, t_run, tensor=())
        spread = [send(t_run.at[3, dt], tz.at[dt - 1], around.along(dt)) for dt in range(1, ways)]
        heads, feats = [None] * ways, [None] * ways
        for n in (3, 2, 1, 0):
            step = {3: (1, 1), 2: (2, 2), 1: (1, 0), 0: None}[n]
            heads[n] = MatrixSum(
                around, send, 0, n % 2 == 0, qa.at[n], q0.at[n], q1.at[n], q2.at[n],
                [(qf.at[n], q0.at[n])], [], [],
                None if step is None else (step[0], q3.at[step[1]]),
                [(q3.at[1], heads[3].away)] if n == 2 else [],
            )
            feats[n] = MatrixSum(
                around, send, 1, n % 2 == 0, oa.at[n], o0.at[n], o1.at[n], o2.at[n],
                [(of.at[n], o0.at[n])], [], [],
                None if step is None else (step[0], o3.at[step[1]]),
                [(o3.at[1], feats[3].away)] if n == 2 else [],
            )
        names = [("h", 3), ("h", 2), ("f", 3), ("f", 2), ("h", 1), ("h", 0), ("f", 1), ("f", 0)]
        items = [(heads if kind == "h" else feats)[n] for kind, n in names]

        def compute(k):
            kind, n = names[k]
            at = pl.ds(n * share, share)
            for side, to in ((1, qf if kind == "h" else of), (0, qa if kind == "h" else oa)):
                span = pl.ds(side * half, half)
                if kind == "h":
                    for j in range(3):
                        to[n, :, j * share : (j + 1) * share] = dot_tn(
                            xs[:, span], ps[j, :, at]
                        ).astype(BF)
                else:
                    to[n] = dot_tn(ms[:, at], gs[:, span]).astype(BF)
                if side == 1:
                    items[k].begin()

        loads["p"].wait()
        loads["r"].wait()
        for j in range(3):
            loads[j].wait()
        for at in range(0, width, share):
            total = rs[:, at : at + share]
            for j in range(3):
                total = total + dot_nt(ps[j], ws[j, at : at + share, :])
            low[:, at : at + share] = total.astype(BF)
        around.await_all()
        t_run[0] = ten_ref[...]
        small.begin()
        home = RowMoves(around, False, doc_o, ask_o, low, row_send, row_recv)
        home.start()
        for name in ("x", "m", "g"):
            loads[name].wait()
        compute(0)
        compute(1)
        for n in range(0, len(items) + 4, 2):
            if 0 < n < 8:
                small.hop(n // 2 - 1)
            if n == 6:
                for copy in spread:
                    copy.start()
            for item in items[n - 2 : n] if n >= 2 else []:
                item.second_axis()
            for item in items[n : n + 2]:
                item.first_axis()
            for k in (n + 2, n + 3):
                if k < len(items):
                    compute(k)
            for m in (n - 4, n - 3):
                if 0 <= m < len(items):
                    items[m].tensor()

        home.wait()
        for copy in spread:
            copy.wait_recv()
        ten_o[...] = t_run[3, 0] + tz[0] + tz[1] + tz[2]
        for group in (heads, feats):
            group[1].away.wait_recv()
            group[2].away.wait_recv()
        for j in range(3):
            at = pl.ds(j * share, share)
            total = qa[0, :block, at].astype(F32) + q3[0, :, at].astype(F32)
            qkv_o[j] = total + q3[2, :, at].astype(F32)
        total = oa[0, :, :block].astype(F32) + o3[0].astype(F32)
        out_o[...] = total + o3[2].astype(F32)
        send.drain()

    def whole(x):
        return pl.BlockSpec(x.shape, lambda: (0,) * len(x.shape))

    out_shape = [
        jax.ShapeDtypeStruct((3, block, share), F32),
        jax.ShapeDtypeStruct((share, block), F32),
        jax.ShapeDtypeStruct((2, quarter, width), BF),
        jax.ShapeDtypeStruct((2, asked, width), BF),
        jax.ShapeDtypeStruct(tensor_sums.shape[1:], F32),
    ]
    anywhere = pl.BlockSpec(memory_space=pl.ANY)
    vmem = pltpu.VMEM
    dma = pltpu.SemaphoreType.DMA
    count = 6 + 2 * (ways * 4 + 3)
    return pl.pallas_call(
        kernel,
        out_shape=out_shape,
        in_specs=[anywhere] * 6 + [whole(tensor_sums)],
        out_specs=[
            whole(out_shape[0]),
            whole(out_shape[1]),
            anywhere,
            anywhere,
            whole(out_shape[4]),
        ],
        scratch_shapes=[
            vmem((rows, width), BF),
            vmem((3, width, width), BF),
            vmem((3, rows, width), BF),
            vmem((rows, width), BF),
            vmem((rows, width), BF),
            vmem((rows, width), F32),
            vmem((rows, width), BF),
            vmem((ways, half, part), BF),
            vmem((ways, half, part), BF),
            vmem((ways, half, part), BF),
            vmem((ways, 2 * block, part), BF),
            vmem((ways, block, part), BF),
            vmem((ways - 1, block, part), BF),
            vmem((ways, share, half), BF),
            vmem((ways, share, half), BF),
            vmem((ways, share, half), BF),
            vmem((ways, share, 2 * block), BF),
            vmem((ways, share, block), BF),
            vmem((ways - 1, share, block), BF),
            vmem((3,) + tensor_sums.shape, F32),
            vmem((4,) + tensor_sums.shape, F32),
            vmem((ways - 1,) + tensor_sums.shape[1:], F32),
            dma((count,)),
            dma((count,)),
            dma((8,)),
            dma((2, 2)),
            dma((2, 2)),
        ],
        compiler_params=pltpu.CompilerParams(
            collective_id=1, has_side_effects=True, vmem_limit_bytes=60 << 20
        ),
        name="last_sums",
    )(x, weights, pre, mixed, branch, resid, tensor_sums)


def attention_backward_kernel(
    qkv, far_kv, grad, cosines, sines, col_labels, own_labels, far_labels,
    up, back, vectors, proj, y,
):
    rows, width = qkv.shape[1:]
    docs = far_kv.shape[1]
    pairs = width // 128
    block = docs
    asked = rows - docs
    ways = 4
    half, own_block = width // 2, width // 8
    share = up.shape[1] // ways
    count, piece = 2 * ways, share // 2
    assert pairs == 8

    def kernel(
        qkv_ref, far_ref, g_ref, c_ref, s_ref, lc_ref, lo_ref, lf_ref,
        up_ref, back_ref, vec_ref, proj_ref, y_ref,
        pre_ref, bias_ref, up_o, back_o, vec_o, proj_o, yd_ref, yq_ref,
        sums_own, sums_far, give, kept, got_kv,
        ua, u0, u1, u2, u3, ba, b0, b1, b2, b3, v_got, v_run, p_run, p_got,
        send_sem, recv_sem, local_sem, row_send, row_recv,
    ):
        h = pl.program_id(0)
        around = Around()
        send = Sender(send_sem, recv_sem)
        ups, backs = [None] * count, [None] * count
        for n in range(count - 1, -1, -1):
            span = pl.ds(n * piece, piece)
            dt, side = n // 2, n % 2
            step = {3: (1, 1), 2: (2, 2), 1: (1, 0), 0: None}[dt]
            ups[n] = MatrixSum(
                around, send, 0, False, ua.at[n], u0.at[n], u1.at[n], u2.at[n],
                [(up_ref.at[half:, span], u0.at[n])],
                [(up_ref.at[:half, span], ua.at[n])],
                [local_sem.at[n]],
                None if step is None else (step[0], u3.at[step[1], side]),
                [(u3.at[1, side], ups[n + 2].away)] if dt == 2 else [],
            )
            backs[n] = MatrixSum(
                around, send, 1, True, ba.at[n], b0.at[n], b1.at[n], b2.at[n],
                [(back_ref.at[span, half:], b0.at[n])],
                [(back_ref.at[span, :half], ba.at[n])],
                [local_sem.at[count + n]],
                None if step is None else (step[0], b3.at[step[1], side]),
                [(b3.at[1, side], backs[n + 2].away)] if dt == 2 else [],
            )
        couples = [(ups[n], backs[n]) for n in (6, 7, 4, 5, 2, 3, 0, 1)]
        small = SmallSum(around, send, v_got, v_run)
        mean_proj = ProjSum(around, send, proj_ref, p_run, p_got)
        gives = [send(give.at[n], got_kv.at[n], around.other(1)) for n in range(pairs)]
        home = RowMoves(around, False, yd_ref, yq_ref, y_ref, row_send, row_recv)
        lane = lax.broadcasted_iota(jnp.int32, (1, 128), 1)

        def finish(n):
            gives[n].wait_recv()
            at = pl.ds(n * 128, 128)
            for i in range(2):
                head = kept[n % 2, i, :docs, :] + got_kv[n, i].astype(F32)
                tail = kept[n % 2, i, docs:, :]
                if i == 0:
                    head = head * c_ref[0, :docs, :] - turned(head) * s_ref[0, :docs, :]
                    tail = tail * c_ref[0, docs:, :] - turned(tail) * s_ref[0, docs:, :]
                head, tail = head.astype(BF), tail.astype(BF)
                pre_ref[i + 1, :docs, at] = head
                pre_ref[i + 1, docs:, at] = tail
                total = jnp.sum(head.astype(F32), axis=0, keepdims=True)
                total = total + jnp.sum(tail.astype(F32), axis=0, keepdims=True)
                bias_ref[i + 1 : i + 2, at] = total

        for step in range(pairs):

            @pl.when(h == step)
            def _(step=step):
                if step == 0:
                    around.meet()
                    for p in range(8):
                        to = feature_block(around.rank, p) * own_block
                        at = pl.ds(pl.multiple_of(to, own_block), own_block)
                        v_run[0, :, at] = vec_ref[:, p * own_block : (p + 1) * own_block]
                    small.begin()
                    mean_proj.begin()
                    for n, many in ((0, 2), (2, 4), (4, 8)):
                        for couple in couples[n:many]:
                            for item in couple:
                                item.begin()
                        if n < 4:
                            for item in couples[n // 2]:
                                item.first_axis()
                    home.start()
                else:
                    firsts = {1: (2,), 2: (3, 4), 3: (5,), 4: (6,), 5: (7,)}
                    seconds = {1: (0,), 2: (1,), 3: (2,), 4: (3, 4), 5: (5,), 6: (6,), 7: (7,)}
                    tensors = {3: (0, 1), 4: (2,), 5: (3,), 6: (4,), 7: (5, 6)}
                    if step <= 5:
                        small.hop(step - 1)
                        mean_proj.hop(step - 1)
                    for n in seconds.get(step, ()):
                        for item in couples[n]:
                            item.second_axis()
                    for n in firsts.get(step, ()):
                        for item in couples[n]:
                            item.first_axis()
                    for n in tensors.get(step, ()):
                        for item in couples[n]:
                            item.tensor()
                    finish(step - 1)

        sums_own[...] = jnp.zeros_like(sums_own)
        sums_far[...] = jnp.zeros_like(sums_far)

        def part(start, size, keys, sames, sums):
            q_block = qkv_ref[0, pl.ds(start, size), :]
            g_block = g_ref[pl.ds(start, size), :]
            grads = []
            for head in range(2):
                mask = (lane // HEAD_WIDTH) == head
                q_head = jnp.where(mask, q_block, jnp.zeros_like(q_block))
                g_head = jnp.where(mask, g_block, jnp.zeros_like(g_block))
                scores = [
                    jnp.where(same, dot_nt(q_head, key), MASKED)
                    for (key, _), same in zip(keys, sames)
                ]
                top = functools.reduce(
                    jnp.maximum, [jnp.max(s, axis=-1, keepdims=True) for s in scores]
                )
                powers = [jnp.exp(s - top) for s in scores]
                total = functools.reduce(
                    jnp.add, [jnp.sum(p, axis=-1, keepdims=True) for p in powers]
                )
                inverse = 1.0 / total
                g_head = (g_head.astype(F32) * inverse).astype(BF)
                pulls = [dot_nt(g_head, value) for _, value in keys]
                mean = functools.reduce(
                    jnp.add,
                    [jnp.sum(p * d, axis=-1, keepdims=True) for p, d in zip(powers, pulls)],
                ) * inverse
                slopes = [(p * (d - mean)).astype(BF) for p, d in zip(powers, pulls)]
                got = functools.reduce(
                    jnp.add, [dot_nn(s, key) for s, (key, _) in zip(slopes, keys)]
                )
                grads.append(got * 0.125)
                for (ref, begin, many), s, p in zip(sums, slopes, powers):
                    ref[0, pl.ds(begin, many), :] += dot_tn(s, q_head)
                    ref[1, pl.ds(begin, many), :] += dot_tn(p.astype(BF), g_head)
            total = jnp.where(lane < HEAD_WIDTH, grads[0], grads[1])
            at = pl.ds(start, size)
            low = (total * c_ref[0, at, :] - turned(total) * s_ref[0, at, :]).astype(BF)
            pre_ref[0, at, pl.ds(pl.multiple_of(h * 128, 128), 128)] = low
            return jnp.sum(low.astype(F32), axis=0, keepdims=True)

        doc_keys = [
            (qkv_ref[1, :docs, :], qkv_ref[2, :docs, :]),
            (far_ref[0], far_ref[1]),
        ]
        bias = jnp.zeros((1, 128), F32)
        for at in range(docs // block):
            labels = lc_ref[pl.ds(at * block, block), :]
            bias = bias + part(
                at * block,
                block,
                doc_keys,
                [labels == lo_ref[...], labels == lf_ref[...]],
                [(sums_own, 0, docs), (sums_far, 0, docs)],
            )
        row = lax.broadcasted_iota(jnp.int32, (asked, asked), 0) // QLEN
        col = lax.broadcasted_iota(jnp.int32, (asked, asked), 1) // QLEN
        bias = bias + part(
            docs,
            asked,
            [(qkv_ref[1, docs:, :], qkv_ref[2, docs:, :])],
            [row == col],
            [(sums_own, docs, asked)],
        )
        bias_ref[0:1, pl.ds(pl.multiple_of(h * 128, 128), 128)] = bias
        side = h % 2
        kept[side] = sums_own[...]
        give[h] = sums_far[...].astype(BF)
        for step in range(pairs):

            @pl.when(h == step)
            def _(step=step):
                gives[step].start()

        @pl.when(h == pairs - 1)
        def _():
            finish(pairs - 1)
            for couple in couples[7:]:
                for item in couple:
                    item.tensor()
            for group, acc, came, o in ((ups, ua, u3, up_o), (backs, ba, b3, back_o)):
                for n in range(2):
                    group[n + 2].away.wait_recv()
                    group[n + 4].away.wait_recv()
                    at = pl.ds(n * piece, piece)
                    if acc is ua:
                        total = acc[n, :own_block, :].astype(F32)
                    else:
                        total = acc[n, :, :own_block].astype(F32)
                    total = total + came[0, n].astype(F32) + came[2, n].astype(F32)
                    if acc is ua:
                        o[:, at] = total
                    else:
                        o[at, :] = total
            vec_o[...] = v_run[5]
            proj_o[...] = mean_proj.result()
            home.wait()
            send.drain()

    def whole(shape):
        return pl.BlockSpec(shape, lambda h: (0,) * len(shape))

    anywhere = pl.BlockSpec(memory_space=pl.ANY)
    vmem = pltpu.VMEM
    dma = pltpu.SemaphoreType.DMA
    columns = proj.shape[1]
    out_shape = [
        jax.ShapeDtypeStruct((3, rows, width), BF),
        jax.ShapeDtypeStruct((8, width), F32),
        jax.ShapeDtypeStruct((own_block, share), F32),
        jax.ShapeDtypeStruct((share, own_block), F32),
        jax.ShapeDtypeStruct(vectors.shape, F32),
        jax.ShapeDtypeStruct((own_block, columns), F32),
    ]
    slots = 2 * (count * 4 + 6) + 5 + 5 + pairs
    return pl.pallas_call(
        kernel,
        grid=(pairs,),
        in_specs=[
            pl.BlockSpec((3, rows, 128), lambda h: (0, 0, h)),
            pl.BlockSpec((2, docs, 128), lambda h: (0, 0, h)),
            pl.BlockSpec((rows, 128), lambda h: (0, h)),
            pl.BlockSpec((1, rows, 128), lambda h: (1, 0, 0)),
            pl.BlockSpec((1, rows, 128), lambda h: (1, 0, 0)),
            whole((docs, 1)),
            whole((1, docs)),
            whole((1, docs)),
            anywhere,
            anywhere,
            whole(vectors.shape),
            whole(proj.shape),
            anywhere,
        ],
        out_specs=[whole(x.shape) for x in out_shape] + [anywhere, anywhere],
        out_shape=out_shape
        + [
            jax.ShapeDtypeStruct((2, docs // 2, width), BF),
            jax.ShapeDtypeStruct((2, asked // 2, width), BF),
        ],
        scratch_shapes=[
            vmem((2, rows, 128), F32),
            vmem((2, docs, 128), F32),
            vmem((pairs, 2, docs, 128), BF),
            vmem((2, 2, rows, 128), F32),
            vmem((pairs, 2, docs, 128), BF),
            vmem((count, half, piece), BF),
            vmem((count, half, piece), BF),
            vmem((count, 2 * own_block, piece), BF),
            vmem((count, own_block, piece), BF),
            vmem((ways - 1, 2, own_block, piece), BF),
            vmem((count, piece, half), BF),
            vmem((count, piece, half), BF),
            vmem((count, piece, 2 * own_block), BF),
            vmem((count, piece, own_block), BF),
            vmem((ways - 1, 2, piece, own_block), BF),
            vmem((5,) + vectors.shape, F32),
            vmem((6,) + vectors.shape, F32),
            vmem((width, columns), F32),
            vmem((width + 2 * own_block, columns), F32),
            dma((slots,)),
            dma((slots,)),
            dma((2 * count,)),
            dma((2, 2)),
            dma((2, 2)),
        ],
        compiler_params=pltpu.CompilerParams(
            collective_id=2, has_side_effects=True, vmem_limit_bytes=60 << 20
        ),
        name="attend_backward_and_sum",
        cost_estimate=pl.CostEstimate(
            flops=100 * rows * 2 * docs * width,
            bytes_accessed=4 * (6 * rows + 4 * docs) * width,
            transcendentals=rows * 2 * docs * width // 64,
        ),
    )(
        qkv, far_kv, grad, cosines, sines, col_labels, own_labels, far_labels,
        up, back, vectors, proj, y,
    )


def body(
    x_doc,
    x_query,
    doc_cot,
    query_cot,
    lengths,
    positives,
    w_qkv,
    b_qkv,
    w_out,
    b_out,
    gain_one,
    shift_one,
    w_in,
    b_in,
    w_back,
    b_back,
    gain_two,
    shift_two,
    w_proj,
):
    ways = lax.axis_size("tensor")
    groups = lax.axis_size("dp")
    column = lax.axis_index("tensor")
    rank = lax.axis_index("dp")
    core = rank % 2
    chip = rank // 2
    chips = groups // 2
    micro, quarter, width = x_doc.shape
    asked = x_query.shape[1]
    segments = lengths.shape[2] - 1
    proj_width = w_proj.shape[1]
    heads_local = w_qkv.shape[2]
    units_local = w_in.shape[1]
    block = width // groups
    assert ways == 2 * micro and ways == 4

    def exchange(value, dr=0, dt=0):
        pairs = [
            (r * ways + t, (r ^ dr) * ways + (t ^ dt)) for r in range(groups) for t in range(ways)
        ]
        return lax.ppermute(value, AXES, pairs)

    chip_bits = []
    bit = 2
    while bit < groups:
        chip_bits.append(bit)
        bit *= 2

    def gather_weights(pack, reverse):
        pieces = [pack] + [exchange(pack, dt=j) for j in range(1, ways)]
        pieces = [(0, jnp.concatenate(pieces, axis=-1))]
        order = chip_bits[::-1] if reverse and len(chip_bits) == 2 else chip_bits
        for dr in order:
            pieces = pieces + [(j + dr // 2, exchange(p, dr=dr)) for j, p in pieces]
            if len(pieces) >= 4 or dr == order[-1]:
                pieces.sort(key=lambda item: item[0])
                pieces = [(0, jnp.concatenate([p for _, p in pieces], axis=-2))]
        (_, half), = pieces
        return jnp.concatenate([half, exchange(half, dr=1)], axis=-2)

    def gather_proj(pack):
        for dr in chip_bits + [1]:
            pack = jnp.concatenate([pack, exchange(pack, dr=dr)], axis=0)
        return pack

    unit_micro = column // 2
    unit_row = chip * 2 + column % 2

    def rows_in(docs, queries):
        blocks = jnp.concatenate([docs, queries], axis=1)
        got = []
        for j in range(2):
            send = jnp.where((column + j) % 2 == 0, blocks[0], blocks[1])
            pairs = []
            for r in range(groups):
                for t in range(ways):
                    m = (t + j) % 2
                    pairs.append(
                        (r * ways + t, ((r // 2) * 2 + t // 2) * ways + 2 * m + r % 2)
                    )
            got.append(lax.ppermute(send, AXES, pairs))
        first = jnp.where(unit_micro == 0, got[0], got[1])
        second = jnp.where(unit_micro == 0, got[1], got[0])
        return jnp.concatenate(
            [first[:quarter], second[:quarter], first[quarter:], second[quarter:]], axis=0
        )

    def quarters_out(first, second):
        got = []
        for j in range(2):
            send = jnp.where((unit_micro + j) % 2 == 0, first, second)
            pairs = []
            for r in range(groups):
                for t in range(ways):
                    m = t // 2
                    pairs.append(
                        (
                            r * ways + t,
                            ((r // 2) * 2 + t % 2) * ways + 2 * (r % 2) + (m + j) % 2,
                        )
                    )
            got.append(lax.ppermute(send, AXES, pairs))
        even = jnp.where(column % 2 == 0, got[0], got[1])
        odd = jnp.where(column % 2 == 0, got[1], got[0])
        return jnp.stack([even, odd])

    def rows_out(values):
        docs = 2 * quarter
        first = jnp.concatenate([values[:quarter], values[docs : docs + asked]], axis=0)
        second = jnp.concatenate([values[quarter:docs], values[docs + asked :]], axis=0)
        blocks = quarters_out(first, second)
        return blocks[:, :quarter], blocks[:, quarter:]

    place = jnp.arange(width, dtype=jnp.int32)
    step = place // block
    actual = (rank ^ (2 * (step % chips) + step // chips)) * block + place % block
    turn = (place[:, None] == actual[None, :]).astype(BF)

    bias_pack = jnp.concatenate([b_qkv.reshape(-1), b_in])
    own_picks = jnp.zeros((8, 128), jnp.int32).at[:micro, : positives.shape[1]].set(positives)
    if chips == 4:
        own_x, full_qkv, full_out, full_proj, biases, picks_rel = gather_kernel(
            x_doc, x_query, w_qkv, w_out, w_proj, bias_pack.reshape(-1, 128), own_picks
        )
        biases = [biases[j].reshape(-1) for j in range(ways)]
        full_proj = full_proj.reshape(width, proj_width)
    else:
        own_x = rows_in(x_doc, x_query)
        full_qkv = gather_weights(w_qkv, False)
        full_out = gather_weights(w_out.T, False).T
        full_in = gather_weights(w_in, False)
        full_back = gather_weights(w_back.T, False).T
        full_proj = gather_proj(w_proj)
        picks_rel = gather_proj(own_picks[None])
        biases = [bias_pack] + [exchange(bias_pack[None], dt=j)[0] for j in range(1, ways)]
    picks_rel = picks_rel[:, :micro, : positives.shape[1]].astype(F32)
    cots = (doc_cot.astype(BF), query_cot.astype(BF))
    if chips != 4:
        own_cot = rows_in(*cots)
    bias_qkv = jnp.concatenate(
        [b[: 3 * heads_local].reshape(3, heads_local) for b in biases], axis=1
    )
    bias_in = jnp.concatenate([b[3 * heads_local :] for b in biases])
    params = jnp.stack(
        [b_out, gain_one, shift_one, b_back, gain_two, shift_two, b_out, b_out]
    )
    params = jnp.dot(params, turn.astype(F32), precision=FULL_PRECISION)
    b_out, gain_one, shift_one, b_back, gain_two, shift_two = [params[i] for i in range(6)]

    docs = 2 * quarter
    queries = 2 * asked
    rows = docs + queries
    sizes_all = lengths[unit_micro]
    sizes = sizes_all[unit_row]
    ends = jnp.cumsum(sizes[:-1])
    starts = jnp.concatenate([jnp.zeros((1,), jnp.int32), ends])

    def layout(first):
        index = first + jnp.arange(docs, dtype=jnp.int32)
        segment = jnp.sum((index[:, None] >= ends[None, :]).astype(jnp.int32), axis=1)
        labels = jnp.arange(starts.shape[0], dtype=jnp.int32)
        begin = jnp.sum(
            jnp.where(segment[:, None] == labels[None, :], starts[None, :], 0), axis=1
        )
        return segment, index - begin

    own_labels, own_places = layout(core * docs)
    far_labels, far_places = layout((1 - core) * docs)
    own_places = jnp.concatenate([own_places, jnp.arange(queries, dtype=jnp.int32) % QLEN])
    half = HEAD_WIDTH // 2
    rates = 10000.0 ** (-(2.0 * jnp.arange(half, dtype=F32)) / HEAD_WIDTH)

    def rotation(places):
        angle = places.astype(F32)[:, None] * rates[None, :]
        sine = jnp.sin(angle)
        return jnp.tile(jnp.cos(angle), (1, 4)), jnp.concatenate([-sine, sine] * 2, axis=1)

    cosine, sine = rotation(own_places)
    far_cosine, far_sine = rotation(far_places)
    cosines_three = jnp.stack([cosine * 0.125, cosine, jnp.ones_like(cosine)])
    sines_three = jnp.stack([sine * 0.125, sine, jnp.zeros_like(sine)])

    label_args = (own_labels[:, None], own_labels[None, :], far_labels[None, :])
    if chips == 4:
        x_low = own_x
        qkv, far_kv, mixed, own_cot, full_in, full_back = project_and_attend(
            own_x, full_qkv, bias_qkv, cosines_three, sines_three, *label_args,
            *cots, w_in, w_back,
        )
    else:
        x_low = dot_nn(own_x, turn).astype(BF)
        qkv = project_heads(x_low, full_qkv, bias_qkv, cosines_three, sines_three)
        far_kv = exchange(qkv[1:, :docs], dr=1)
        mixed = attention_forward(qkv, far_kv, *label_args)
    branch = dot_nn(mixed, full_out)
    resid_one = x_low.astype(F32) + branch + b_out
    normed, norm_one_pull = jax.vjp(layer_norm, resid_one, gain_one, shift_one)
    normed_low = normed.astype(BF)
    if chips == 4:
        active_low, active_slope, update = feed_forward(normed_low, full_in, bias_in, full_back)
    else:
        inner = dot_nn(normed_low, full_in) + bias_in
        active, gelu_pull = jax.vjp(gelu_exact, inner)
        active_low = active.astype(BF)
        update = dot_nn(active_low, full_back)
    resid_two = normed + update + b_back
    output, norm_two_pull = jax.vjp(layer_norm, resid_two, gain_two, shift_two)
    output_low = output.astype(BF)
    y_low = output_low if chips == 4 else dot_nt(output_low, turn).astype(BF)
    projection = dot_nn(output_low, full_proj)
    held = jnp.arange(groups, dtype=jnp.int32)
    held = rank ^ (2 * (held % chips) + held // chips)
    order = (jnp.arange(groups, dtype=jnp.int32)[:, None] == held[None, :]).astype(F32)
    picks = jnp.where(unit_micro == 0, picks_rel[:, 0], picks_rel[:, 1])
    picks = jnp.dot(order, picks, precision=FULL_PRECISION).astype(jnp.int32).reshape(-1)
    counts = sizes_all[:, :segments].reshape(-1).astype(F32)

    if chips == 4:
        log_counts = jnp.pad(
            jnp.log(counts).reshape(-1, segments), ((0, 0), (0, 8 - segments))
        ).reshape(-1, 1)
        proj_low, loss_out = loss_kernel(
            projection, own_labels[:, None], log_counts, jnp.repeat(picks, QLEN)[None]
        )
        loss_out = loss_out[:, : asked // QLEN, 0]
    else:
        y_doc, y_query = rows_out(y_low)
        unit, unit_pull = jax.vjp(normalize, projection)
        unit_low = unit.astype(BF)

        doc_unit = unit_low[:docs]
        query_unit = unit_low[docs:]

        def bit_of(dr, dt):
            return (rank // dr) % 2 == 1 if dr else (column // dt) % 2 == 1

        def join(value, dr, dt, axis=0):
            got = exchange(value, dr=dr, dt=dt)
            on = bit_of(dr, dt)
            low = jnp.where(on, got, value)
            high = jnp.where(on, value, got)
            return jnp.concatenate([low, high], axis=axis)

        def split_sum(value, dr, dt):
            on = bit_of(dr, dt)
            size = value.shape[0] // 2
            send = jnp.where(on, value[:size], value[size:])
            keep = jnp.where(on, value[size:], value[:size])
            return keep + exchange(send.astype(BF), dr=dr, dt=dt).astype(F32)

        steps = [(1, 0), (0, 1)] + [(dr, 0) for dr in chip_bits]
        all_queries = query_unit
        for dr, dt in steps:
            all_queries = join(all_queries, dr, dt)
        seg_labels = jnp.arange(segments, dtype=jnp.int32)
        member = (own_labels[:, None] == seg_labels[None, :]).astype(F32)
        cosines = dot_nt(doc_unit, all_queries)
        weight = jnp.exp(TAU * (cosines - 1.0))
        totals = jnp.einsum("js,ji->si", member, weight, precision=FULL_PRECISION)
        totals = totals + exchange(totals, dr=1)
        for dr, dt in steps[1:]:
            totals = join(totals, dr, dt)
        best = (jnp.log(totals) - jnp.log(counts)[:, None]) / TAU + 1.0
        score = jnp.sum(best.reshape(best.shape[0], -1, QLEN), axis=-1)
        logits = LOGIT_SCALE * score
        documents = jnp.arange(logits.shape[0], dtype=jnp.int32)
        chosen = (documents[:, None] == picks[None, :]).astype(F32)
        peak = jnp.max(logits, axis=0, keepdims=True)
        powers = jnp.exp(logits - peak)
        mass = jnp.sum(powers, axis=0, keepdims=True)
        losses = (peak + jnp.log(mass))[0] - jnp.sum(chosen * logits, axis=0)
        logit_grad = LOGIT_SCALE * (powers / mass - chosen)
        own_grad = lax.dynamic_slice_in_dim(logit_grad, unit_row * segments, segments, axis=0)
        own_total = lax.dynamic_slice_in_dim(totals, unit_row * segments, segments, axis=0)
        coef = jnp.repeat(own_grad, QLEN, axis=1) / own_total
        spread = jnp.einsum("js,si->ji", member, coef, precision=FULL_PRECISION)
        cosine_grad = (weight * spread).astype(BF)
        doc_grad = dot_nn(cosine_grad, all_queries)
        query_grad = dot_tn(cosine_grad, doc_unit)
        for dr, dt in steps[::-1]:
            query_grad = split_sum(query_grad, dr, dt)
        own_losses = lax.dynamic_slice_in_dim(losses, unit_row * (4 * asked // QLEN) + core * 2 * (asked // QLEN), 2 * (asked // QLEN))
        per = asked // QLEN
        loss_tiles = [
            jnp.broadcast_to(own_losses[i * per : (i + 1) * per, None], (per, 128)) for i in range(2)
        ]
        loss_out = quarters_out(loss_tiles[0], loss_tiles[1])[:, :, 0]

        unit_grad = jnp.concatenate([doc_grad, query_grad], axis=0)
        (proj_grad,) = unit_pull(unit_grad)
        proj_low = proj_grad.astype(BF)

    class Reduction:
        def __init__(self, half, axis, reverse, last):
            self.bits = chip_bits if reverse and len(chip_bits) == 2 else chip_bits[::-1]
            self.left = sorted(chip_bits)
            self.axis, self.last = axis, last
            self.sends = [half(1).astype(BF)]
            self.hops = [(1, 0)]
            self.kept = lambda: half(0)
            self.stage = 0

        def advance(self):
            total = self.kept()
            for s, (dr, dt) in zip(self.sends, self.hops):
                got = exchange(s, dr=dr, dt=dt).astype(F32)
                total = got if total is None else total + got
            if self.stage == len(self.bits) + 1:
                return total
            if self.stage < len(self.bits):
                dr = self.bits[self.stage]
                at = self.left.index(dr)
                self.left.remove(dr)
                size = block << at
                stay, send = [
                    jnp.concatenate(
                        [
                            lax.slice_in_dim(total, b, b + size, axis=self.axis)
                            for b in range(side * size, total.shape[self.axis], 2 * size)
                        ],
                        axis=self.axis,
                    )
                    for side in (0, 1)
                ]
                self.sends = [send.astype(BF)]
                self.hops = [(dr, 0)]
            else:
                stay, sends = self.last(total)
                self.sends = [piece.astype(BF) for _, piece in sends]
                self.hops = [(0, dt) for dt, _ in sends]
            self.kept = lambda: stay
            self.stage += 1
            return None

        def finish(self):
            total = None
            while total is None:
                total = self.advance()
            return total

    def weight_sum(left, right, axis, reverse):
        size = width // 2

        def half(n):
            if axis == 0:
                return dot_tn(left[:, n * size : (n + 1) * size], right)
            return dot_tn(left, right[:, n * size : (n + 1) * size])

        def last(total):
            size = total.shape[1 - axis] // ways
            pieces = [
                lax.slice_in_dim(total, j * size, (j + 1) * size, axis=1 - axis)
                for j in range(ways)
            ]
            return pieces[0], [(j, pieces[j]) for j in range(1, ways)]

        return Reduction(half, axis, reverse, last)

    def after(value, reductions):
        sends = [r.sends for r in reductions]
        value, sends = lax.optimization_barrier((value, sends))
        for r, s in zip(reductions, sends):
            r.sends = s
        return value

    if chips == 4:
        out_cot = own_cot.astype(F32)
    else:
        out_cot = dot_nn(own_cot, turn)
    out_grad = out_cot + dot_nt(proj_low, full_proj)
    resid_two_grad, gain_two_grad, shift_two_grad = norm_two_pull(out_grad)
    update_low = resid_two_grad.astype(BF)
    whole_path = chips == 4
    if whole_path:
        hidden_grad, in_grad, back_grad, inner_bias = feed_forward_backward(
            update_low, full_back, active_slope, full_in, normed_low, active_low
        )
    else:
        sum_back = weight_sum(active_low, update_low, 1, True)
        (inner_grad,) = gelu_pull(dot_nt(update_low, full_back))
        inner_low = inner_grad.astype(BF)
        sum_in = weight_sum(normed_low, inner_low, 0, False)
        hidden_grad = dot_nt(inner_low, full_in)
        inner_bias = jnp.sum(inner_low.astype(F32), axis=0)
    normed_grad = hidden_grad + resid_two_grad
    resid_one_grad, gain_one_grad, shift_one_grad = norm_one_pull(normed_grad)
    branch_low = resid_one_grad.astype(BF)
    mixed_grad = dot_nt(branch_low, full_out).astype(BF)
    grad_proj = dot_tn(output_low, proj_low)
    zero = jnp.zeros((width,), F32)
    vectors = jnp.stack(
        [
            jnp.sum(branch_low.astype(F32), axis=0),
            gain_one_grad,
            shift_one_grad,
            jnp.sum(update_low.astype(F32), axis=0),
            gain_two_grad,
            shift_two_grad,
            zero,
            zero,
        ]
    )
    if not whole_path:
        vectors = lax.dot_general(
            vectors, turn.astype(F32), (((1,), (1,)), ((), ())), precision=FULL_PRECISION
        )

    def heads_sum(rights, first_block, blocks, reverse):
        size = width // 2
        many = rights.shape[1] // 3 // blocks

        def half(n):
            return dot_tn(x_low[:, n * size : (n + 1) * size], rights)

        def last(total):
            stay, sends = None, []
            for b in range(blocks):
                piece = jnp.stack(
                    [total[:, (j * blocks + b) * many : (j * blocks + b + 1) * many] for j in range(3)]
                )
                if first_block + b == 0:
                    stay = piece
                else:
                    sends.append((first_block + b, piece))
            return stay, sends

        return Reduction(half, 0, reverse, last)

    inner_bias = inner_bias.reshape(ways, units_local)
    if whole_path:
        pre, head_bias, out_in, out_back, vectors, grad_proj, y_doc, y_query = (
            attention_backward_kernel(
                qkv,
                far_kv,
                mixed_grad,
                cosines_three,
                sines_three,
                *label_args,
                in_grad,
                back_grad,
                vectors,
                grad_proj,
                y_low,
            )
        )
        head_bias = head_bias[:3].reshape(3, ways, heads_local)
    else:
        head_sums, head_rights = [], []
        running = [sum_back, sum_in]
        per_block = heads_local // 128
        sum_out = weight_sum(mixed, branch_low, 1, False)
        for first_block, blocks in ((0, 2), (2, 1), (3, 1)):
            for item in running:
                item.advance()
            mixed_grad = after(mixed_grad, running)
            dq, own_grads, give = attention_backward(
                first_block * per_block,
                blocks * per_block,
                qkv,
                far_kv,
                mixed_grad,
                cosine,
                sine,
                far_cosine,
                far_sine,
                *label_args,
            )
            got = exchange(give, dr=1).astype(F32)
            rights = [dq] + [
                jnp.concatenate(
                    [own_grads[i, :docs] + got[i], own_grads[i, docs:]], axis=0
                ).astype(BF)
                for i in range(2)
            ]
            head_rights.append(rights)
            head_sums.append(
                heads_sum(jnp.concatenate(rights, axis=1), first_block, blocks, first_block > 0)
            )
        out_back = sum_back.finish()
        out_in = sum_in.finish()
        pre = [jnp.concatenate([part[j] for part in head_rights], axis=1) for j in range(3)]
        head_bias = jnp.stack([jnp.sum(p.astype(F32), axis=0) for p in pre])
        head_bias = head_bias.reshape(3, ways, heads_local)
    tensor_grads = jnp.concatenate(
        [jnp.swapaxes(head_bias, 0, 1).reshape(ways, 3 * heads_local), inner_bias], axis=1
    )
    if whole_path:
        out_qkv, out_out, gx_doc, gx_query, tensor_grads = finish_kernel(
            x_low,
            full_qkv,
            pre,
            mixed,
            branch_low,
            resid_one_grad,
            tensor_grads.reshape(ways, -1, 128),
        )
        gx_doc, gx_query = gx_doc.astype(F32), gx_query.astype(F32)
        tensor_grads = tensor_grads.reshape(-1)
    else:
        x_grad = resid_one_grad
        for j in range(3):
            x_grad = x_grad + dot_nt(pre[j], full_qkv[j])
        x_grad = dot_nt(x_grad.astype(BF), turn).astype(BF)
        gx_doc, gx_query = rows_out(x_grad)
        gx_doc, gx_query = gx_doc.astype(F32), gx_query.astype(F32)
        out_out = sum_out.finish()
        out_qkv = functools.reduce(jnp.add, [item.finish() for item in head_sums])
        for dr in [1] + chip_bits[::-1]:
            size = grad_proj.shape[0] // 2
            got = exchange(grad_proj[size:].astype(BF), dr=dr)
            grad_proj = grad_proj[:size] + got.astype(F32)
        for dt in (1, 2):
            grad_proj = grad_proj + exchange(grad_proj, dt=dt)
        for dt in (2, 1):
            tensor_grads = tensor_grads[:dt] + exchange(tensor_grads[dt:], dt=dt)
            vectors = vectors + exchange(vectors, dt=dt)
        for dr in [1] + chip_bits:
            tensor_grads = tensor_grads + exchange(tensor_grads, dr=dr)
            vectors = vectors + exchange(vectors, dr=dr)
        tensor_grads = tensor_grads[0]
    return (
        y_doc,
        y_query,
        loss_out,
        gx_doc,
        gx_query,
        out_qkv,
        tensor_grads[: 3 * heads_local].reshape(3, heads_local),
        out_out,
        vectors[0],
        vectors[1],
        vectors[2],
        out_in,
        tensor_grads[3 * heads_local :],
        out_back,
        vectors[3],
        vectors[4],
        vectors[5],
        grad_proj,
    )


def solution(mesh):
    rows = P(None, ("dp", "tensor"), None)
    in_specs = (
        rows,
        rows,
        rows,
        rows,
        P(),
        P(None, "dp"),
        P(None, "dp", "tensor"),
        P(None, "tensor"),
        P("tensor", "dp"),
        P(),
        P(),
        P(),
        P("dp", "tensor"),
        P("tensor"),
        P("tensor", "dp"),
        P(),
        P(),
        P(),
        P("dp", None),
    )
    out_specs = (
        rows,
        rows,
        P(None, ("dp", "tensor")),
        rows,
        rows,
        P(None, "dp", "tensor"),
        P(None, "tensor"),
        P("tensor", "dp"),
        P(),
        P(),
        P(),
        P("dp", "tensor"),
        P("tensor"),
        P("tensor", "dp"),
        P(),
        P(),
        P(),
        P("dp", None),
    )
    return jax.shard_map(body, mesh=mesh, in_specs=in_specs, out_specs=out_specs, check_vma=False)
```

```python
import functools

import jax
import jax.numpy as jnp
from jax import lax
from jax.experimental import pallas as pl
from jax.experimental.pallas import tpu as pltpu
from jax.sharding import PartitionSpec as P

HEAD_WIDTH = 64
QLEN = 32
FULL_PRECISION = lax.Precision.HIGHEST
TAU = 20.0
EPS = 1e-05
LOGIT_SCALE = 2.0
MASKED = -1e30
AXES = ("dp", "tensor")
MESH = pl.DeviceIdType.MESH
BF = jnp.bfloat16
F32 = jnp.float32


def layer_norm(values, gain, shift):
    center = values - jnp.mean(values, axis=-1, keepdims=True)
    spread = jnp.mean(center * center, axis=-1, keepdims=True)
    return center * lax.rsqrt(spread + EPS) * gain + shift


def normalize(values):
    return values * lax.rsqrt(jnp.sum(values * values, axis=-1, keepdims=True) + 1e-06)


def gelu_exact(values):
    return jax.nn.gelu(values, approximate=False)


def dot_nn(a, b):
    return lax.dot_general(a, b, (((1,), (0,)), ((), ())), preferred_element_type=F32)


def dot_nt(a, b):
    return lax.dot_general(a, b, (((1,), (1,)), ((), ())), preferred_element_type=F32)


def dot_tn(a, b):
    return lax.dot_general(a, b, (((0,), (0,)), ((), ())), preferred_element_type=F32)


def differing(a, b, bits):
    total = 0
    for bit in range(bits):
        x, y = (a // 2**bit) % 2, (b // 2**bit) % 2
        total = total + 2**bit * (x + y - 2 * x * y)
    return total


class Around:
    def __init__(self):
        self.rank = lax.axis_index("dp")
        self.column = lax.axis_index("tensor")
        self.core = self.rank % 2
        self.base = self.rank - self.core

    def other(self, bit):
        rank = self.rank
        return (rank + bit - 2 * bit * ((rank // bit) % 2), self.column)

    def along(self, dt):
        return (self.rank, differing(self.column, dt, 2))

    def greet(self):
        barrier = pltpu.get_barrier_semaphore()
        for dc in range(2):
            for dt in range(4):
                if dc + dt > 0:
                    pl.semaphore_signal(
                        barrier,
                        inc=1,
                        device_id=(self.base + (self.core + dc) % 2, (self.column + dt) % 4),
                        device_id_type=MESH,
                    )
        for bit in (2, 4):
            pl.semaphore_signal(
                barrier, inc=1, device_id=self.other(bit), device_id_type=MESH
            )

    def await_all(self):
        pl.semaphore_wait(pltpu.get_barrier_semaphore(), 9)

    def meet(self):
        self.greet()
        self.await_all()


def feature_block(rank, p):
    return differing(rank, 2 * (p % 4) + p // 4, 3)


class Sender:
    def __init__(self, send_sem, recv_sem):
        self.send_sem, self.recv_sem = send_sem, recv_sem
        self.sent = []

    def __call__(self, src, dst, to):
        at = len(self.sent)
        copy = pltpu.make_async_remote_copy(
            src_ref=src,
            dst_ref=dst,
            send_sem=self.send_sem.at[at],
            recv_sem=self.recv_sem.at[at],
            device_id=to,
            device_id_type=MESH,
        )
        self.sent.append(copy)
        return copy

    def drain(self):
        for copy in self.sent:
            copy.wait_send()


class RowMoves:
    def __init__(self, around, inward, docs, asked, packed, send_sem, recv_sem):
        core, column, base = around.core, around.column, around.base
        lonely = 3 * core == column
        self.copies, self.arrivals = [], []
        size, few, width = docs.shape[1], asked.shape[1], docs.shape[2]
        block = width // 8
        for n in range(2):
            q, m = (column % 2, n) if inward else (n, column // 2)
            if inward:
                mine = jnp.logical_and(lonely, column // 2 == n)
                to = (base + column // 2, 2 * n + core)
                here = jnp.logical_and(lonely, column % 2 == n)
                holder = base + column // 2
            else:
                mine = jnp.logical_and(lonely, core == n)
                to = (base + column % 2, 2 * core + n)
                here = jnp.logical_and(lonely, column // 2 == n)
                holder = around.rank
            wheres = [
                pl.ds(pl.multiple_of(feature_block(holder, p) * block, block), block)
                for p in range(8)
            ]
            for kind, (ref, many, begin) in enumerate(((docs, size, 0), (asked, few, 2 * size))):
                span = pl.ds(pl.multiple_of(begin + q * many, few), many)
                aways, locals_ = [], []
                for p in list(range(8)) + [None]:
                    if p is None:
                        rows, flat = packed.at[span, :], ref.at[m]
                    else:
                        rows = packed.at[span, pl.ds(p * block, block)]
                        flat = ref.at[m, :, wheres[p]]
                    src, dst = (flat, rows) if inward else (rows, flat)
                    aways.append(
                        pltpu.make_async_remote_copy(
                            src_ref=src,
                            dst_ref=dst,
                            send_sem=send_sem.at[n, kind],
                            recv_sem=recv_sem.at[q if inward else m, kind],
                            device_id=to,
                            device_id_type=MESH,
                        )
                    )
                    locals_.append(pltpu.make_async_copy(src, dst, send_sem.at[n, kind]))
                self.copies.append((mine, locals_, aways))
                if inward:
                    land = packed.at[pl.ds(begin + n * many, many), :]
                else:
                    land = ref.at[n]
                came = pltpu.make_async_remote_copy(
                    src_ref=land,
                    dst_ref=land,
                    send_sem=send_sem.at[n, kind],
                    recv_sem=recv_sem.at[n, kind],
                    device_id=to,
                    device_id_type=MESH,
                )
                self.arrivals.append((here, came))

    def start(self):
        for mine, locals_, aways in self.copies:

            @pl.when(mine)
            def _(locals_=locals_):
                for copy in locals_[:8]:
                    copy.start()

            @pl.when(jnp.logical_not(mine))
            def _(aways=aways):
                for copy in aways[:8]:
                    copy.start()

    def wait(self):
        for here, came in self.arrivals:

            @pl.when(jnp.logical_not(here))
            def _(came=came):
                came.wait_recv()

        for mine, locals_, aways in self.copies:

            @pl.when(mine)
            def _(locals_=locals_):
                locals_[8].wait()

            @pl.when(jnp.logical_not(mine))
            def _(aways=aways):
                aways[8].wait_send()


class WeightGather:
    slots = 31

    def __init__(
        self, around, sources, outs, feature_axis, tensor_axis, bits, send_sem, recv_sem, local_sem
    ):
        self.around, self.sources, self.outs = around, sources, outs
        self.feature_axis, self.tensor_axis, self.bits = feature_axis, tensor_axis, bits
        self.send_sem, self.recv_sem, self.local_sem = send_sem, recv_sem, local_sem
        self.all = range(len(sources))

    def place(self, j):
        return (j & 1) * 4 + (j >> 1)

    def line(self, a, j):
        index = [slice(None)] * len(self.sources[a].shape)
        size = self.sources[a].shape[self.feature_axis[a]]
        index[self.feature_axis[a]] = pl.ds(self.place(j) * size, size)
        return self.outs[a].at[tuple(index)]

    def piece(self, a, j, source, column=None):
        column = self.around.column if column is None else column
        index = [slice(None)] * len(self.sources[a].shape)
        size = self.sources[a].shape[self.feature_axis[a]]
        index[self.feature_axis[a]] = pl.ds(self.place(j) * size, size)
        size = self.sources[a].shape[self.tensor_axis[a]]
        offset = pl.multiple_of(differing(column, source, 2) * size, size)
        index[self.tensor_axis[a]] = pl.ds(offset, size)
        return self.outs[a].at[tuple(index)]

    def origin(self, kind):
        column = self.around.column
        if kind == 0:
            return column, None
        if kind <= 3:
            return column - kind, column >= kind
        return column + (kind - 3), column + (kind - 3) <= 3

    def describe(self, a, slot):
        around, column = self.around, self.around.column
        first, second = self.bits[a]
        if slot >= 27:
            j = (0, first, second, first | second)[slot - 27]
            return None, self.line(a, j), self.line(a, j | 1), around.other(1)
        if slot < 6:
            kind = slot if slot < 3 else (0 if slot == 3 else slot)
            to = column + 1 if slot < 3 else column - 1
            edge = column < 3 if slot < 3 else column > 0
            source, there = self.origin(kind)
            there = edge if there is None else jnp.logical_and(there, edge)
            src = self.sources[a] if kind == 0 else self.piece(a, 0, source)
            return there, src, self.piece(a, 0, source, to), (around.rank, to)
        kind = (slot - 6) % 7
        source, there = self.origin(kind)
        if slot < 20:
            bit = first if slot < 13 else second
            src = self.sources[a] if kind == 0 else self.piece(a, 0, source)
            return there, src, self.piece(a, bit, source), around.other(bit)
        src, dst = self.piece(a, first, source), self.piece(a, first | second, source)
        return there, src, dst, around.other(second)

    def landing(self, a, slot):
        first, second = self.bits[a]
        if slot >= 27:
            return None, self.line(a, (0, first, second, first | second)[slot - 27] | 1)
        if slot < 6:
            kind, j = (slot + 1, 0)
        else:
            kind, j = (slot - 6) % 7, (first, second, first | second)[(slot - 6) // 7]
        source, there = self.origin(kind)
        return there, self.piece(a, j, source)

    def copy(self, a, slot, src, dst, to):
        return pltpu.make_async_remote_copy(
            src_ref=src,
            dst_ref=dst,
            send_sem=self.send_sem.at[a, slot],
            recv_sem=self.recv_sem.at[a, slot],
            device_id=to,
            device_id_type=MESH,
        )

    def when(self, condition, act):
        if condition is None:
            act()
        else:
            pl.when(condition)(act)

    def start(self, a, slot):
        condition, src, dst, to = self.describe(a, slot)
        self.when(condition, lambda: self.copy(a, slot, src, dst, to).start())

    def sent(self, a, slot):
        condition, src, dst, to = self.describe(a, slot)
        self.when(condition, lambda: self.copy(a, slot, src, dst, to).wait_send())

    def arrived(self, a, slot):
        condition, dst = self.landing(a, slot)
        to = self.around.other(1)
        self.when(condition, lambda: self.copy(a, slot, dst, dst, to).wait_recv())

    def home(self, a):
        return pltpu.make_async_copy(
            self.sources[a], self.piece(a, 0, self.around.column), self.local_sem.at[a]
        )

    def begin(self):
        for a in self.all:
            for slot in (0, 3, 6, 13):
                self.start(a, slot)
        for a in self.all:
            self.home(a).start()

    def onward(self, a, kind):
        self.arrived(a, 6 + kind)
        self.start(a, 20 + kind)

    def hop(self, n):
        for a in self.all:
            for kind, slot in ((n, n - 1), (n + 3, n + 2)):
                self.arrived(a, slot)
                if n < 3:
                    self.start(a, slot + 1)
                self.start(a, 6 + kind)
                self.start(a, 13 + kind)
        for a in self.all:
            for kind in (0,) if n == 1 else (n - 1, n + 2):
                self.onward(a, kind)

    def finish(self):
        for a in self.all:
            self.home(a).wait()
            self.start(a, 27)
        for a in self.all:
            for kind in (3, 6):
                self.onward(a, kind)
            self.start(a, 28)
        for begin, slot in ((13, 29), (20, 30)):
            for a in self.all:
                for kind in range(7):
                    self.arrived(a, begin + kind)
                self.start(a, slot)
        for a in self.all:
            for slot in range(27, 31):
                self.arrived(a, slot)
            for slot in range(31):
                self.sent(a, slot)


def gathered(weight, feature_axis, tensor_axis):
    shape = list(weight.shape)
    shape[feature_axis] *= 8
    shape[tensor_axis] *= 4
    return jax.ShapeDtypeStruct(tuple(shape), weight.dtype)


def gather_kernel(
    x_doc, x_query, qkv, out, proj, b_qkv, b_in, picks, doc_cot, query_cot, ends, rates, params
):
    ways, groups = 4, 8
    quarter, width = x_doc.shape[1:]
    asked = x_query.shape[1]
    docs, queries = 2 * quarter, 2 * asked
    rows = docs + queries
    share, units = b_qkv.shape[1], b_in.shape[1]
    block = width // groups
    marks = ends.shape[0]
    count = len(params)

    def kernel(*refs):
        xd_ref, xq_ref, qkv_ref, out_ref, proj_ref, bq_ref, bi_ref, picks_ref = refs[:8]
        cd_ref, cq_ref, ends_ref, rates_ref = refs[8:12]
        param_refs = refs[12 : 12 + count]
        x_o, qkv_o, out_o, proj_o, picks_o = refs[12 + count : 17 + count]
        bq_o, bi_o, cos_o, sin_o, col_o, row_o, cd_o, cq_o, param_o = refs[17 + count : 26 + count]
        (
            bq, bi, send_sem, recv_sem, small_send, small_recv, x_send, x_recv, local_sem,
        ) = refs[26 + count :]
        around = Around()
        around.meet()
        other, along = around.other, around.along
        gather = WeightGather(
            around,
            [qkv_ref.at[0:2], qkv_ref.at[2:3], out_ref],
            [qkv_o.at[0:2], qkv_o.at[2:3], out_o],
            [1, 1, 1],
            [2, 2, 0],
            [(2, 4), (4, 2), (4, 2)],
            send_sem,
            recv_sem,
            local_sem,
        )
        moves = RowMoves(around, True, xd_ref, xq_ref, x_o, x_send, x_recv)
        send = Sender(small_send, small_recv)
        gather.begin()
        place = gather.place
        small = [send(bq_ref, bq.at[dt], along(dt)) for dt in range(1, ways)]
        small += [send(bi_ref, bi.at[dt], along(dt)) for dt in range(1, ways)]
        local = []
        flat = []
        for n, (ref, o) in enumerate(((proj_ref, proj_o), (picks_ref, picks_o))):
            local.append(pltpu.make_async_copy(ref, o.at[0], local_sem.at[3 + n]))
            flat.append(
                (
                    send(ref, o.at[place(2)], other(2)),
                    send(ref, o.at[place(4)], other(4)),
                    send(ref, o.at[place(1)], other(1)),
                    send(o.at[place(2)], o.at[place(6)], other(4)),
                    send(o.at[place(2)], o.at[place(3)], other(1)),
                    send(o.at[place(4)], o.at[place(5)], other(1)),
                    send(o.at[place(6)], o.at[place(7)], other(1)),
                )
            )
        for copy in small + local + [c for f in flat for c in f[:3]]:
            copy.start()

        def layout(first, shape, axis):
            index = lax.broadcasted_iota(jnp.int32, shape, axis) + first
            segment = jnp.zeros(shape, jnp.int32)
            begin = jnp.zeros(shape, jnp.int32)
            for n in range(marks):
                after = index >= ends_ref[n]
                segment = segment + jnp.where(after, 1, 0)
                begin = jnp.where(after, ends_ref[n], begin)
            return segment, index - begin

        segment, places = layout(around.core * docs, (docs, 1), 0)
        col_o[...] = segment
        row_o[0:1, :] = layout(around.core * docs, (1, docs), 1)[0]
        row_o[1:2, :] = layout((1 - around.core) * docs, (1, docs), 1)[0]
        lane = lax.broadcasted_iota(jnp.int32, (1, 128), 1)
        first_half = lane % HEAD_WIDTH < HEAD_WIDTH // 2
        asked_places = lax.broadcasted_iota(jnp.int32, (queries, 1), 0) % QLEN
        for begin, at in ((0, places), (docs, asked_places)):
            span = pl.ds(begin, at.shape[0])
            angle = at.astype(F32) * rates_ref[...]
            sine = jnp.sin(angle)
            cos_o[span, :] = jnp.cos(angle)
            sin_o[span, :] = jnp.where(first_half, -sine, sine)
        gather.hop(1)
        for m in range(2):
            cd_o[m] = cd_ref[m].astype(BF)
            cq_o[m] = cq_ref[m].astype(BF)
        for f in flat:
            f[0].wait_recv()
            f[3].start()
            f[4].start()
            f[1].wait_recv()
            f[5].start()
        gather.hop(2)
        moves.start()
        for p in range(groups):
            fr = pl.ds(pl.multiple_of(feature_block(around.rank, p) * block, block), block)
            for n in range(count):
                param_o[n : n + 1, p * block : (p + 1) * block] = param_refs[n][:, fr]
        bq[0] = bq_ref[...]
        bi[0] = bi_ref[...]
        gather.hop(3)
        for f in flat:
            f[3].wait_recv()
            f[6].start()
        for copy in small:
            copy.wait_recv()
        for dt in range(ways):
            bq_o[:, dt * share : (dt + 1) * share] = bq[dt]
            bi_o[:, dt * units : (dt + 1) * units] = bi[dt]
        gather.finish()
        for f in flat:
            for n in (2, 4, 5, 6):
                f[n].wait_recv()
        for copy in local:
            copy.wait()
        moves.wait()
        send.drain()

    def whole(shape):
        return pl.BlockSpec(shape, lambda: (0,) * len(shape))

    anywhere = pl.BlockSpec(memory_space=pl.ANY)
    dma = pltpu.SemaphoreType.DMA
    tables = [
        jax.ShapeDtypeStruct((3, ways * share), F32),
        jax.ShapeDtypeStruct((1, ways * units), F32),
        jax.ShapeDtypeStruct((rows, 128), F32),
        jax.ShapeDtypeStruct((rows, 128), F32),
        jax.ShapeDtypeStruct((docs, 1), jnp.int32),
        jax.ShapeDtypeStruct((2, docs), jnp.int32),
        jax.ShapeDtypeStruct(doc_cot.shape, BF),
        jax.ShapeDtypeStruct(query_cot.shape, BF),
        jax.ShapeDtypeStruct((8, width), F32),
    ]
    return pl.pallas_call(
        kernel,
        out_shape=[
            jax.ShapeDtypeStruct((rows, width), x_doc.dtype),
            gathered(qkv, 1, 2),
            gathered(out, 1, 0),
            jax.ShapeDtypeStruct((groups,) + proj.shape, proj.dtype),
            jax.ShapeDtypeStruct((groups,) + picks.shape, picks.dtype),
        ]
        + tables,
        in_specs=[anywhere] * 5
        + [whole(b_qkv.shape), whole(b_in.shape), anywhere]
        + [whole(doc_cot.shape), whole(query_cot.shape)]
        + [pl.BlockSpec(memory_space=pltpu.SMEM), whole(rates.shape)]
        + [whole((1, width))] * count,
        out_specs=[anywhere] * 5 + [whole(x.shape) for x in tables],
        scratch_shapes=[
            pltpu.VMEM((ways,) + b_qkv.shape, F32),
            pltpu.VMEM((ways,) + b_in.shape, F32),
            dma((3, WeightGather.slots)),
            dma((3, WeightGather.slots)),
            dma((20,)),
            dma((20,)),
            dma((2, 2)),
            dma((2, 2)),
            dma((5,)),
        ],
        compiler_params=pltpu.CompilerParams(
            collective_id=0, has_side_effects=True, vmem_limit_bytes=60 << 20
        ),
        name="gather_weights",
    )(
        x_doc, x_query, qkv, out, proj, b_qkv, b_in, picks, doc_cot, query_cot, ends, rates,
        *[p[None] for p in params],
    )


def turned(values):
    lane = lax.broadcasted_iota(jnp.int32, (1, 128), 1)
    ahead = pltpu.roll(values, 96, 1)
    behind = pltpu.roll(values, 32, 1)
    return jnp.where(lane % HEAD_WIDTH < HEAD_WIDTH // 2, ahead, behind)


def project_heads(x, weights, bias, cosine, sine):
    rows, width = x.shape
    columns = 256
    steps = width // columns

    def kernel(x_ref, w_ref, b_ref, c_ref, s_ref, o_ref):
        got = dot_nn(x_ref[...], w_ref[0]) + b_ref[0]
        for at in range(0, columns, 128):
            piece = got[:, at : at + 128]
            o_ref[0, :, at : at + 128] = (piece * c_ref[0] + turned(piece) * s_ref[0]).astype(BF)

    return pl.pallas_call(
        kernel,
        grid=(3, steps),
        in_specs=[
            pl.BlockSpec((rows, width), lambda j, n: (0, 0)),
            pl.BlockSpec((1, width, columns), lambda j, n: (j, 0, n)),
            pl.BlockSpec((1, 1, columns), lambda j, n: (j, 0, n)),
            pl.BlockSpec((1, rows, 128), lambda j, n: (j, 0, 0)),
            pl.BlockSpec((1, rows, 128), lambda j, n: (j, 0, 0)),
        ],
        out_specs=pl.BlockSpec((1, rows, columns), lambda j, n: (j, 0, n)),
        out_shape=jax.ShapeDtypeStruct((3, rows, width), BF),
        compiler_params=pltpu.CompilerParams(vmem_limit_bytes=40 << 20),
        name="project_heads",
    )(x, weights, bias[:, None, :], cosine, sine)


def attention_forward(qkv, far_kv, col_labels, own_labels, far_labels):
    rows, width = qkv.shape[1:]
    docs = far_kv.shape[1]
    block = 128
    asked = rows - docs

    def kernel(qkv_ref, far_ref, lc_ref, lo_ref, lf_ref, o_ref):
        lane = lax.broadcasted_iota(jnp.int32, (1, 128), 1)

        def part(start, size, keys, sames):
            q_block = qkv_ref[0, pl.ds(start, size), :]
            outs = []
            for head in range(2):
                mask = (lane // HEAD_WIDTH) == head
                q_head = jnp.where(mask, q_block, jnp.zeros_like(q_block))
                scores = [
                    jnp.where(same, dot_nt(q_head, key), MASKED)
                    for (key, _), same in zip(keys, sames)
                ]
                top = functools.reduce(
                    jnp.maximum, [jnp.max(s, axis=-1, keepdims=True) for s in scores]
                )
                powers = [jnp.exp(s - top) for s in scores]
                total = functools.reduce(
                    jnp.add, [jnp.sum(p, axis=-1, keepdims=True) for p in powers]
                )
                mixed = functools.reduce(
                    jnp.add, [dot_nn(p.astype(BF), value) for p, (_, value) in zip(powers, keys)]
                )
                outs.append(mixed * (1.0 / total))
            o_ref[pl.ds(start, size), :] = jnp.where(lane < HEAD_WIDTH, outs[0], outs[1]).astype(BF)

        doc_keys = [
            (qkv_ref[1, :docs, :], qkv_ref[2, :docs, :]),
            (far_ref[0], far_ref[1]),
        ]
        for at in range(docs // block):
            labels = lc_ref[pl.ds(at * block, block), :]
            part(at * block, block, doc_keys, [labels == lo_ref[...], labels == lf_ref[...]])
        row = lax.broadcasted_iota(jnp.int32, (asked, asked), 0) // QLEN
        col = lax.broadcasted_iota(jnp.int32, (asked, asked), 1) // QLEN
        part(docs, asked, [(qkv_ref[1, docs:, :], qkv_ref[2, docs:, :])], [row == col])

    whole = lambda shape: pl.BlockSpec(shape, lambda h: (0, 0))
    return pl.pallas_call(
        kernel,
        grid=(width // 128,),
        in_specs=[
            pl.BlockSpec((3, rows, 128), lambda h: (0, 0, h)),
            pl.BlockSpec((2, docs, 128), lambda h: (0, 0, h)),
            whole((docs, 1)),
            whole((1, docs)),
            whole((1, docs)),
        ],
        out_specs=pl.BlockSpec((rows, 128), lambda h: (0, h)),
        out_shape=jax.ShapeDtypeStruct((rows, width), BF),
        compiler_params=pltpu.CompilerParams(vmem_limit_bytes=40 << 20),
        name="attend_forward",
        cost_estimate=pl.CostEstimate(
            flops=32 * rows * 2 * docs * width,
            bytes_accessed=2 * (4 * rows + 2 * docs) * width,
            transcendentals=rows * 2 * docs * width // 64,
        ),
    )(qkv, far_kv, col_labels, own_labels, far_labels)


def attention_backward(
    first, count, qkv, far_kv, grad, cosine, sine, far_cosine, far_sine,
    col_labels, own_labels, far_labels,
):
    rows = qkv.shape[1]
    docs = far_kv.shape[1]
    width = count * 128
    block = 128
    asked = rows - docs

    def kernel(
        qkv_ref, far_ref, g_ref, c_ref, s_ref, fc_ref, fs_ref, lc_ref, lo_ref, lf_ref,
        dq_ref, own_ref, give_ref, sums_own, sums_far,
    ):
        lane = lax.broadcasted_iota(jnp.int32, (1, 128), 1)
        sums_own[...] = jnp.zeros_like(sums_own)
        sums_far[...] = jnp.zeros_like(sums_far)

        def part(start, size, keys, sames, sums):
            q_block = qkv_ref[0, pl.ds(start, size), :]
            g_block = g_ref[pl.ds(start, size), :]
            grads = []
            for head in range(2):
                mask = (lane // HEAD_WIDTH) == head
                q_head = jnp.where(mask, q_block, jnp.zeros_like(q_block))
                g_head = jnp.where(mask, g_block, jnp.zeros_like(g_block))
                scores = [
                    jnp.where(same, dot_nt(q_head, key), MASKED)
                    for (key, _), same in zip(keys, sames)
                ]
                top = functools.reduce(
                    jnp.maximum, [jnp.max(s, axis=-1, keepdims=True) for s in scores]
                )
                powers = [jnp.exp(s - top) for s in scores]
                total = functools.reduce(
                    jnp.add, [jnp.sum(p, axis=-1, keepdims=True) for p in powers]
                )
                inverse = 1.0 / total
                g_head = (g_head.astype(F32) * inverse).astype(BF)
                pulls = [dot_nt(g_head, value) for _, value in keys]
                mean = functools.reduce(
                    jnp.add,
                    [jnp.sum(p * d, axis=-1, keepdims=True) for p, d in zip(powers, pulls)],
                ) * inverse
                slopes = [(p * (d - mean)).astype(BF) for p, d in zip(powers, pulls)]
                got = functools.reduce(
                    jnp.add, [dot_nn(s, key) for s, (key, _) in zip(slopes, keys)]
                )
                grads.append(got * 0.125)
                for (ref, begin, many), s, p in zip(sums, slopes, powers):
                    ref[0, pl.ds(begin, many), :] += dot_tn(s, q_head)
                    ref[1, pl.ds(begin, many), :] += dot_tn(p.astype(BF), g_head)
            whole = jnp.where(lane < HEAD_WIDTH, grads[0], grads[1])
            at = pl.ds(start, size)
            dq_ref[at, :] = (whole * c_ref[at, :] - turned(whole) * s_ref[at, :]).astype(BF)

        doc_keys = [
            (qkv_ref[1, :docs, :], qkv_ref[2, :docs, :]),
            (far_ref[0], far_ref[1]),
        ]
        for at in range(docs // block):
            labels = lc_ref[pl.ds(at * block, block), :]
            part(
                at * block,
                block,
                doc_keys,
                [labels == lo_ref[...], labels == lf_ref[...]],
                [(sums_own, 0, docs), (sums_far, 0, docs)],
            )
        row = lax.broadcasted_iota(jnp.int32, (asked, asked), 0) // QLEN
        col = lax.broadcasted_iota(jnp.int32, (asked, asked), 1) // QLEN
        part(
            docs,
            asked,
            [(qkv_ref[1, docs:, :], qkv_ref[2, docs:, :])],
            [row == col],
            [(sums_own, docs, asked)],
        )
        own_ref[0] = sums_own[0] * c_ref[...] - turned(sums_own[0]) * s_ref[...]
        own_ref[1] = sums_own[1]
        give_ref[0] = (sums_far[0] * fc_ref[...] - turned(sums_far[0]) * fs_ref[...]).astype(BF)
        give_ref[1] = sums_far[1].astype(BF)

    whole = lambda shape: pl.BlockSpec(shape, lambda h: (0, 0))
    return pl.pallas_call(
        kernel,
        grid=(count,),
        in_specs=[
            pl.BlockSpec((3, rows, 128), lambda h: (0, 0, h + first)),
            pl.BlockSpec((2, docs, 128), lambda h: (0, 0, h + first)),
            pl.BlockSpec((rows, 128), lambda h: (0, h + first)),
            whole((rows, 128)),
            whole((rows, 128)),
            whole((docs, 128)),
            whole((docs, 128)),
            whole((docs, 1)),
            whole((1, docs)),
            whole((1, docs)),
        ],
        out_specs=[
            pl.BlockSpec((rows, 128), lambda h: (0, h)),
            pl.BlockSpec((2, rows, 128), lambda h: (0, 0, h)),
            pl.BlockSpec((2, docs, 128), lambda h: (0, 0, h)),
        ],
        out_shape=[
            jax.ShapeDtypeStruct((rows, width), BF),
            jax.ShapeDtypeStruct((2, rows, width), F32),
            jax.ShapeDtypeStruct((2, docs, width), BF),
        ],
        scratch_shapes=[pltpu.VMEM((2, rows, 128), F32), pltpu.VMEM((2, docs, 128), F32)],
        compiler_params=pltpu.CompilerParams(vmem_limit_bytes=40 << 20),
        name="attend_backward",
        cost_estimate=pl.CostEstimate(
            flops=100 * rows * 2 * docs * width,
            bytes_accessed=4 * (6 * rows + 4 * docs) * width,
            transcendentals=rows * 2 * docs * width // 64,
        ),
    )(
        qkv, far_kv, grad, cosine, sine, far_cosine, far_sine, col_labels, own_labels, far_labels
    )


def project_and_attend(
    x, weights, bias, cosine, sine, col_labels, row_labels, out, params,
    doc_cot, query_cot, up, back,
):
    rows, width = x.shape
    docs = col_labels.shape[0]
    asked = rows - docs
    pairs = width // 128
    block = 256
    columns = 256
    steps = width // columns
    assert pairs == 8

    def kernel(
        x_ref, w_ref, b_ref, c_ref, s_ref, lc_ref, lr_ref, ow_ref, par_ref,
        cd_ref, cq_ref, up_ref, back_ref,
        qkv_o, far_o, mixed_o, resid_o, norm_o, low_o, cot_o, up_o, back_o,
        held, far, qkv, mixed, out_w, resid, norm, low, load_sem, far_send, far_recv, row_send, row_recv, send_sem, recv_sem, local_sem,
    ):
        h = pl.program_id(0)

        def parts():
            around = Around()
            moves = RowMoves(around, True, cd_ref, cq_ref, cot_o, row_send, row_recv)
            gather = WeightGather(
                around,
                [up_ref, back_ref],
                [up_o, back_o],
                [0, 1],
                [1, 0],
                [(2, 4), (4, 2)],
                send_sem,
                recv_sem,
                local_sem,
            )
            return around, moves, gather

        @pl.when(h == 0)
        def _():
            loads = [pltpu.make_async_copy(w_ref.at[j], held.at[j], load_sem.at[j]) for j in range(3)]
            for j in (1, 2, 0):
                loads[j].start()
            pltpu.make_async_copy(ow_ref, out_w, load_sem.at[4]).start()
            around, _, gather = parts()
            around.meet()
            gather.begin()
            copies = []
            for j in (1, 2, 0):
                loads[j].wait()
                for n in range(steps):
                    at = pl.ds(n * columns, columns)
                    got = dot_nn(x_ref[...], held[j, :, at]) + b_ref[j : j + 1, at]
                    for m in range(columns // 128):
                        piece = got[:, m * 128 : (m + 1) * 128]
                        if j < 2:
                            piece = piece * c_ref[...] + turned(piece) * s_ref[...]
                        if j == 0:
                            piece = piece * 0.125
                        qkv[j, :, n * columns + m * 128 : n * columns + (m + 1) * 128] = piece.astype(BF)
                    if j > 0:
                        copy = pltpu.make_async_remote_copy(
                            src_ref=qkv.at[j, pl.ds(0, docs), at],
                            dst_ref=far.at[j - 1, :, at],
                            send_sem=far_send.at[j - 1, n],
                            recv_sem=far_recv.at[j - 1, n],
                            device_id=around.other(1),
                            device_id_type=MESH,
                        )
                        copy.start()
                        copies.append(copy)
            for copy in copies:
                copy.wait()
            pltpu.make_async_copy(far, far_o, load_sem.at[3]).start()
            pltpu.make_async_copy(qkv, qkv_o, load_sem.at[5]).start()

        @pl.when(h == 1)
        def _():
            parts()[2].hop(1)

        @pl.when(h == 4)
        def _():
            _, moves, gather = parts()
            gather.hop(2)
            moves.start()

        @pl.when(h == 7)
        def _():
            parts()[2].hop(3)

        lane = lax.broadcasted_iota(jnp.int32, (1, 128), 1)
        pair = pl.ds(pl.multiple_of(h * 128, 128), 128)

        def part(start, size, keys, sames):
            q_block = qkv[0, pl.ds(start, size), pair]
            outs = []
            for head in range(2):
                mask = (lane // HEAD_WIDTH) == head
                q_head = jnp.where(mask, q_block, jnp.zeros_like(q_block))
                scores = [
                    jnp.where(same, dot_nt(q_head, key), MASKED)
                    for (key, _), same in zip(keys, sames)
                ]
                top = functools.reduce(
                    jnp.maximum, [jnp.max(s, axis=-1, keepdims=True) for s in scores]
                )
                powers = [jnp.exp(s - top) for s in scores]
                total = functools.reduce(
                    jnp.add, [jnp.sum(p, axis=-1, keepdims=True) for p in powers]
                )
                blend = functools.reduce(
                    jnp.add, [dot_nn(p.astype(BF), value) for p, (_, value) in zip(powers, keys)]
                )
                outs.append(blend * (1.0 / total))
            both = jnp.where(lane < HEAD_WIDTH, outs[0], outs[1]).astype(BF)
            mixed[pl.ds(start, size), pair] = both

        doc_keys = [
            (qkv[1, :docs, pair], qkv[2, :docs, pair]),
            (far[0, :, pair], far[1, :, pair]),
        ]
        for at in range(docs // block):
            labels = lc_ref[pl.ds(at * block, block), :]
            part(at * block, block, doc_keys, [labels == lr_ref[0:1, :], labels == lr_ref[1:2, :]])
        row = lax.broadcasted_iota(jnp.int32, (asked, asked), 0) // QLEN
        col = lax.broadcasted_iota(jnp.int32, (asked, asked), 1) // QLEN
        part(docs, asked, [(qkv[1, docs:, pair], qkv[2, docs:, pair])], [row == col])

        @pl.when(h == pairs - 1)
        def _():
            _, moves, gather = parts()
            pltpu.make_async_copy(ow_ref, out_w, load_sem.at[4]).wait()
            for at in range(0, rows, rows // 4):
                span = pl.ds(at, rows // 4)
                total = x_ref[span, :].astype(F32) + dot_nn(mixed[span, :], out_w[...])
                total = total + par_ref[0:1, :]
                resid[span, :] = total
                total = layer_norm(total, par_ref[1:2, :], par_ref[2:3, :])
                norm[span, :] = total
                low[span, :] = total.astype(BF)
            stores = [
                pltpu.make_async_copy(src, dst, load_sem.at[6 + n])
                for n, (src, dst) in enumerate(
                    ((mixed, mixed_o), (resid, resid_o), (norm, norm_o), (low, low_o))
                )
            ]
            for store in stores:
                store.start()
            gather.finish()
            moves.wait()
            pltpu.make_async_copy(far, far_o, load_sem.at[3]).wait()
            pltpu.make_async_copy(qkv, qkv_o, load_sem.at[5]).wait()
            for store in stores:
                store.wait()

    def whole(shape):
        return pl.BlockSpec(shape, lambda h: (0,) * len(shape))

    anywhere = pl.BlockSpec(memory_space=pl.ANY)
    dma = pltpu.SemaphoreType.DMA
    return pl.pallas_call(
        kernel,
        grid=(pairs,),
        in_specs=[
            whole((rows, width)),
            anywhere,
            whole((3, width)),
            whole((rows, 128)),
            whole((rows, 128)),
            whole((docs, 1)),
            whole((2, docs)),
            anywhere,
            whole(params.shape),
        ]
        + [anywhere] * 4,
        out_specs=[anywhere] * 9,
        out_shape=[
            jax.ShapeDtypeStruct((3, rows, width), BF),
            jax.ShapeDtypeStruct((2, docs, width), BF),
            jax.ShapeDtypeStruct((rows, width), BF),
            jax.ShapeDtypeStruct((rows, width), F32),
            jax.ShapeDtypeStruct((rows, width), F32),
            jax.ShapeDtypeStruct((rows, width), BF),
            jax.ShapeDtypeStruct((rows, width), doc_cot.dtype),
            gathered(up, 0, 1),
            gathered(back, 1, 0),
        ],
        scratch_shapes=[
            pltpu.VMEM((3, width, width), BF),
            pltpu.VMEM((2, docs, width), BF),
            pltpu.VMEM((3, rows, width), BF),
            pltpu.VMEM((rows, width), BF),
            pltpu.VMEM((width, width), BF),
            pltpu.VMEM((rows, width), F32),
            pltpu.VMEM((rows, width), F32),
            pltpu.VMEM((rows, width), BF),
            dma((10,)),
            dma((2, steps)),
            dma((2, steps)),
            dma((2, 2)),
            dma((2, 2)),
            dma((2, WeightGather.slots)),
            dma((2, WeightGather.slots)),
            dma((2,)),
        ],
        compiler_params=pltpu.CompilerParams(
            vmem_limit_bytes=60 << 20, collective_id=4, has_side_effects=True
        ),
        name="project_and_attend",
        cost_estimate=pl.CostEstimate(
            flops=64 * rows * 2 * docs * width,
            bytes_accessed=2 * (4 * rows + 2 * docs) * width,
            transcendentals=rows * 2 * docs * width // 64,
        ),
    )(
        x, weights, bias, cosine, sine, col_labels, row_labels, out, params,
        doc_cot, query_cot, up, back,
    )


def feed_forward(hidden, up, bias, back, normed, params, proj):
    rows, width = hidden.shape
    units = up.shape[1]
    columns, piece = 512, 256

    def kernel(
        h_ref, u_ref, b_ref, w_ref, n_ref, par_ref, p_ref, a_ref, d_ref, o_ref, y_ref, q_ref
    ):
        @pl.when(pl.program_id(0) == 0)
        def _():
            o_ref[...] = jnp.zeros_like(o_ref)

        for at in range(0, columns, piece):
            z = dot_nn(h_ref[...], u_ref[:, at : at + piece]) + b_ref[:, at : at + piece]
            bell = jnp.exp(-0.5 * z * z)
            t = 1.0 / (1.0 + 0.23164189 * jnp.abs(z))
            tail = 0.5 * t * (
                0.254829592
                + t * (-0.284496736 + t * (1.421413741 + t * (-1.453152027 + t * 1.061405429)))
            ) * bell
            below = jnp.where(z < 0.0, tail, 1.0 - tail)
            low = (z * below).astype(BF)
            a_ref[:, at : at + piece] = low
            d_ref[:, at : at + piece] = (below + z * (bell * 0.3989422804014327)).astype(BF)
            o_ref[...] += dot_nn(low, w_ref[at : at + piece, :])

        @pl.when(pl.program_id(0) == units // columns - 1)
        def _():
            for at in range(0, rows, rows // 4):
                span = pl.ds(at, rows // 4)
                total = n_ref[span, :] + o_ref[span, :] + par_ref[3:4, :]
                o_ref[span, :] = total
                low = layer_norm(total, par_ref[4:5, :], par_ref[5:6, :]).astype(BF)
                y_ref[span, :] = low
                q_ref[span, :] = dot_nn(low, p_ref[...])

    return pl.pallas_call(
        kernel,
        grid=(units // columns,),
        in_specs=[
            pl.BlockSpec((rows, width), lambda n: (0, 0)),
            pl.BlockSpec((width, columns), lambda n: (0, n)),
            pl.BlockSpec((1, columns), lambda n: (0, n)),
            pl.BlockSpec((columns, width), lambda n: (n, 0)),
            pl.BlockSpec((rows, width), lambda n: (0, 0)),
            pl.BlockSpec(params.shape, lambda n: (0, 0)),
            pl.BlockSpec(proj.shape, lambda n: (0, 0)),
        ],
        out_specs=[
            pl.BlockSpec((rows, columns), lambda n: (0, n)),
            pl.BlockSpec((rows, columns), lambda n: (0, n)),
            pl.BlockSpec((rows, width), lambda n: (0, 0)),
            pl.BlockSpec((rows, width), lambda n: (0, 0)),
            pl.BlockSpec((rows, proj.shape[1]), lambda n: (0, 0)),
        ],
        out_shape=[
            jax.ShapeDtypeStruct((rows, units), BF),
            jax.ShapeDtypeStruct((rows, units), BF),
            jax.ShapeDtypeStruct((rows, width), F32),
            jax.ShapeDtypeStruct((rows, width), BF),
            jax.ShapeDtypeStruct((rows, proj.shape[1]), F32),
        ],
        compiler_params=pltpu.CompilerParams(vmem_limit_bytes=60 << 20),
        name="feed_forward",
    )(hidden, up, bias, back, normed, params, proj)


def norm_backward(values, gain, grad):
    center = values - jnp.mean(values, axis=-1, keepdims=True)
    rate = lax.rsqrt(jnp.mean(center * center, axis=-1, keepdims=True) + EPS)
    unit = center * rate
    inner = grad * gain
    pull = inner - jnp.mean(inner, axis=-1, keepdims=True)
    pull = pull - unit * jnp.mean(inner * unit, axis=-1, keepdims=True)
    return (
        pull * rate,
        jnp.sum(grad * unit, axis=0, keepdims=True),
        jnp.sum(grad, axis=0, keepdims=True),
    )


def feed_forward_backward(
    cot, proj_low, proj, resid_two, output_low, params, back, slope, up, hidden, active,
    resid_one, out,
):
    rows, width = cot.shape
    units = up.shape[1]
    columns = 512
    steps = units // columns
    piece = rows // 4

    def kernel(
        c_ref, pl_ref, p_ref, r2_ref, y_ref, par_ref, w_ref, d_ref, u_ref, h_ref, a_ref,
        r1_ref, out_ref,
        one_ref, low_ref, mix_ref, du_ref, dw_ref, db_ref, dp_ref, vec_ref,
        two, g, total, r1, out_w, sem,
    ):
        step = pl.program_id(0)

        @pl.when(step == 0)
        def _():
            pltpu.make_async_copy(r1_ref, r1, sem.at[0]).start()
            pltpu.make_async_copy(out_ref, out_w, sem.at[1]).start()
            total[...] = jnp.zeros_like(total)
            vec_ref[...] = jnp.zeros_like(vec_ref)
            for at in range(0, rows, piece):
                span = pl.ds(at, piece)
                grad = c_ref[span, :].astype(F32) + dot_nt(pl_ref[span, :], p_ref[...])
                pull, gain, shift = norm_backward(r2_ref[span, :], par_ref[4:5, :], grad)
                two[span, :] = pull
                low = pull.astype(BF)
                g[span, :] = low
                vec_ref[3:4, :] += jnp.sum(low.astype(F32), axis=0, keepdims=True)
                vec_ref[4:5, :] += gain
                vec_ref[5:6, :] += shift
            dp_ref[...] = dot_tn(y_ref[...], pl_ref[...])

        dw_ref[...] = dot_tn(a_ref[...], g[...]).astype(BF)
        low = (dot_nt(g[...], w_ref[...]) * d_ref[...].astype(F32)).astype(BF)
        db_ref[...] = jnp.sum(low.astype(F32), axis=0, keepdims=True)
        total[...] += dot_nt(low, u_ref[...])
        du_ref[...] = dot_tn(h_ref[...], low).astype(BF)

        @pl.when(step == steps - 1)
        def _():
            pltpu.make_async_copy(r1_ref, r1, sem.at[0]).wait()
            pltpu.make_async_copy(out_ref, out_w, sem.at[1]).wait()
            for at in range(0, rows, piece):
                span = pl.ds(at, piece)
                grad = total[span, :] + two[span, :]
                pull, gain, shift = norm_backward(r1[span, :], par_ref[1:2, :], grad)
                one_ref[span, :] = pull
                low = pull.astype(BF)
                low_ref[span, :] = low
                vec_ref[0:1, :] += jnp.sum(low.astype(F32), axis=0, keepdims=True)
                vec_ref[1:2, :] += gain
                vec_ref[2:3, :] += shift
                mix_ref[span, :] = dot_nt(low, out_w[...]).astype(BF)

    def whole(shape):
        return pl.BlockSpec(shape, lambda n: (0,) * len(shape))

    anywhere = pl.BlockSpec(memory_space=pl.ANY)
    vmem = pltpu.VMEM
    return pl.pallas_call(
        kernel,
        grid=(steps,),
        in_specs=[
            whole((rows, width)),
            whole(proj_low.shape),
            whole(proj.shape),
            whole((rows, width)),
            whole((rows, width)),
            whole(params.shape),
            pl.BlockSpec((columns, width), lambda n: (n, 0)),
            pl.BlockSpec((rows, columns), lambda n: (0, n)),
            pl.BlockSpec((width, columns), lambda n: (0, n)),
            whole((rows, width)),
            pl.BlockSpec((rows, columns), lambda n: (0, n)),
            anywhere,
            anywhere,
        ],
        out_specs=[
            whole((rows, width)),
            whole((rows, width)),
            whole((rows, width)),
            pl.BlockSpec((width, columns), lambda n: (0, n)),
            pl.BlockSpec((columns, width), lambda n: (n, 0)),
            pl.BlockSpec((1, columns), lambda n: (0, n)),
            whole(proj.shape),
            whole((8, width)),
        ],
        out_shape=[
            jax.ShapeDtypeStruct((rows, width), F32),
            jax.ShapeDtypeStruct((rows, width), BF),
            jax.ShapeDtypeStruct((rows, width), BF),
            jax.ShapeDtypeStruct((width, units), BF),
            jax.ShapeDtypeStruct((units, width), BF),
            jax.ShapeDtypeStruct((1, units), F32),
            jax.ShapeDtypeStruct(proj.shape, F32),
            jax.ShapeDtypeStruct((8, width), F32),
        ],
        scratch_shapes=[
            vmem((rows, width), F32),
            vmem((rows, width), BF),
            vmem((rows, width), F32),
            vmem((rows, width), F32),
            vmem((width, width), BF),
            pltpu.SemaphoreType.DMA((2,)),
        ],
        compiler_params=pltpu.CompilerParams(vmem_limit_bytes=60 << 20),
        name="feed_forward_backward",
    )(
        cot, proj_low, proj, resid_two, output_low, params, back, slope, up, hidden, active,
        resid_one, out,
    )


def emit_kernel(arrays, dtypes):
    def kernel(*refs):
        for src, dst in zip(refs[: len(arrays)], refs[len(arrays) :]):
            dst[...] = src[...].astype(dst.dtype)

    def whole(x):
        return pl.BlockSpec(x.shape, lambda: (0,) * len(x.shape))

    return pl.pallas_call(
        kernel,
        in_specs=[whole(x) for x in arrays],
        out_specs=[whole(x) for x in arrays],
        out_shape=[jax.ShapeDtypeStruct(x.shape, t) for x, t in zip(arrays, dtypes)],
        compiler_params=pltpu.CompilerParams(vmem_limit_bytes=60 << 20),
        name="emit",
    )(*arrays)


def loss_kernel(projection, labels, log_counts, picks):
    rows, columns = projection.shape
    docs = labels.shape[0]
    own = rows - docs
    tokens = 16 * own
    units, segments = 8, 4
    chunk = 64

    def kernel(
        p_ref, lab_ref, cnt_ref, pick_ref,
        grad_ref, loss_ref,
        asked_all, weight, sums, sums_all, coef_all, slope, part, part_low, got, tile, tile_got,
        send_sem, recv_sem, tile_send, tile_recv,
    ):
        around = Around()
        rank, column, core, base = around.rank, around.column, around.core, around.base
        chip, side = rank // 2, column % 2
        mine = (chip * 2 + side) * 2 + core
        unit = chip * 2 + side

        def flip(value, bit, on):
            return value + bit - 2 * bit * ((value // bit) % 2) if on else value

        def peer(i):
            to = flip(flip(flip(rank, 1, i & 1), 2, i & 4), 4, i & 8)
            return (to, flip(column, 1, i & 2))

        def index_of(i):
            to, z = peer(i)
            return ((to // 2) * 2 + z % 2) * 2 + to % 2

        barrier = pltpu.get_barrier_semaphore()
        peers = [peer(i) for i in range(1, 16)]
        for dt in (2, 3):
            for dc in range(2):
                away, z = around.along(dt)
                peers.append((flip(rank, 1, dc), z))
        for to in peers:
            pl.semaphore_signal(barrier, inc=1, device_id=to, device_id_type=MESH)
        pl.semaphore_wait(barrier, len(peers))

        values = p_ref[...]
        rate = lax.rsqrt(jnp.sum(values * values, axis=-1, keepdims=True) + 1e-06)
        unit_wide = values * rate
        unit_low = unit_wide.astype(BF)
        own_at = pl.ds(pl.multiple_of(mine * own, own), own)
        asked_all[own_at, :] = unit_low[docs:]

        def all_to_all(kind, src, dst):
            copies = []
            for i in range(1, 16):
                copy = pltpu.make_async_remote_copy(
                    src_ref=src(i),
                    dst_ref=dst(i),
                    send_sem=send_sem.at[kind, i],
                    recv_sem=recv_sem.at[kind, i],
                    device_id=peer(i),
                    device_id_type=MESH,
                )
                copy.start()
                copies.append(copy)
            return copies

        first = all_to_all(0, lambda i: asked_all.at[own_at, :], lambda i: asked_all.at[own_at, :])
        doc_low = unit_low[:docs]
        seg_of = lab_ref[...]
        for copy in first:
            copy.wait_recv()
        queries = asked_all[...]
        sums[...] = jnp.zeros_like(sums)
        for at in range(0, docs, chunk):
            cosines = dot_nt(doc_low[at : at + chunk], queries)
            power = jnp.exp(TAU * (cosines - 1.0))
            weight[at : at + chunk, :] = power
            for s in range(segments):
                chosen = seg_of[at : at + chunk] == s
                sums[s : s + 1, :] += jnp.sum(
                    jnp.where(chosen, power, 0.0), axis=0, keepdims=True
                )
        second = all_to_all(1, lambda i: sums, lambda i: sums_all.at[mine])
        sums_all[mine] = sums[...]
        for copy in second:
            copy.wait_recv()
        row = lax.broadcasted_iota(jnp.int32, (8, tokens), 0)
        lane = lax.broadcasted_iota(jnp.int32, (8, tokens), 1)
        valid = row < segments
        totals, logits = [], []
        for n in range(units):
            total = jnp.where(valid, sums_all[2 * n] + sums_all[2 * n + 1], 1.0)
            best = (jnp.log(total) - cnt_ref[8 * n : 8 * n + 8, :]) / TAU + 1.0
            for step in (1, 2, 4, 8, 16):
                other = jnp.where(
                    (lane // step) % 2 == 1,
                    pltpu.roll(best, step, 1),
                    pltpu.roll(best, tokens - step, 1),
                )
                best = best + other
            totals.append(total)
            logits.append(jnp.where(valid, LOGIT_SCALE * best, MASKED))
        peak = functools.reduce(
            jnp.maximum, [jnp.max(x, axis=0, keepdims=True) for x in logits]
        )
        powers = [jnp.exp(x - peak) for x in logits]
        mass = functools.reduce(jnp.add, [jnp.sum(x, axis=0, keepdims=True) for x in powers])
        picked = jnp.zeros_like(peak)
        for n in range(units):
            hit = jnp.logical_and(valid, pick_ref[...] == n * segments + row)
            picked = picked + jnp.sum(jnp.where(hit, logits[n], 0.0), axis=0, keepdims=True)
            slope_n = LOGIT_SCALE * (powers[n] / mass - jnp.where(hit, 1.0, 0.0))
            coef_all[n] = slope_n / totals[n]
        losses = peak + jnp.log(mass) - picked
        tiles = []
        for q in range(2):
            at = mine * own + q * QLEN
            value = jnp.sum(
                jnp.where(lane[:1] == at, losses, 0.0), axis=1, keepdims=True
            )
            tile[q, 0] = jnp.broadcast_to(value, (8, 128))
            tile[q, 1] = jnp.zeros((8, 128), F32)
        lonely = 3 * core == column
        for q in range(2):
            here = jnp.logical_and(lonely, core == q)
            slot = column // 2
            away = pltpu.make_async_remote_copy(
                src_ref=tile.at[q],
                dst_ref=tile_got.at[slot],
                send_sem=tile_send.at[q],
                recv_sem=tile_recv.at[slot],
                device_id=(base + column % 2, 2 * core + q),
                device_id_type=MESH,
            )
            tiles.append((here, away))

            @pl.when(here)
            def _(q=q):
                tile_got[slot] = tile[q]

            @pl.when(jnp.logical_not(here))
            def _(away=away):
                away.start()

        coef = coef_all[unit]
        doc_grads = []
        part[...] = jnp.zeros_like(part)
        for at in range(0, docs, chunk):
            spread = jnp.zeros((chunk, tokens), F32)
            for s in range(segments):
                chosen = seg_of[at : at + chunk] == s
                spread = jnp.where(chosen, coef[s : s + 1, :], spread)
            low = (weight[at : at + chunk, :] * spread).astype(BF)
            slope[at : at + chunk, :] = low
            doc_grads.append(dot_nn(low, queries))
        part[...] = dot_tn(slope[...], doc_low)
        part_low[...] = part[...].astype(BF)

        def theirs(i):
            return part_low.at[pl.ds(pl.multiple_of(index_of(i) * own, own), own), :]

        third = all_to_all(2, theirs, lambda i: got.at[i])

        def pull(grad, begin, size):
            v, r = unit_wide[begin : begin + size], rate[begin : begin + size]
            inner = jnp.sum(v * grad, axis=-1, keepdims=True)
            return ((grad - v * inner) * r).astype(BF)

        for n, at in enumerate(range(0, docs, chunk)):
            grad_ref[at : at + chunk, :] = pull(doc_grads[n], at, chunk)
        total = part[own_at, :]
        for copy in third:
            copy.wait_recv()
        for i in range(1, 16):
            total = total + got[i].astype(F32)
        grad_ref[docs:, :] = pull(total, docs, own)
        for n in range(2):
            here = jnp.logical_and(lonely, column // 2 == n)
            came = pltpu.make_async_remote_copy(
                src_ref=tile.at[n],
                dst_ref=tile_got.at[n],
                send_sem=tile_send.at[n],
                recv_sem=tile_recv.at[n],
                device_id=peer(1),
                device_id_type=MESH,
            )

            @pl.when(jnp.logical_not(here))
            def _(came=came):
                came.wait_recv()

        loss_ref[...] = tile_got[:, 0]
        for here, away in tiles:

            @pl.when(jnp.logical_not(here))
            def _(away=away):
                away.wait_send()

        for copy in first + second + third:
            copy.wait_send()

    def whole(shape):
        return pl.BlockSpec(shape, lambda: (0,) * len(shape))

    vmem = pltpu.VMEM
    dma = pltpu.SemaphoreType.DMA
    return pl.pallas_call(
        kernel,
        in_specs=[
            whole(projection.shape),
            whole(labels.shape),
            whole(log_counts.shape),
            whole(picks.shape),
        ],
        out_specs=[whole((rows, columns)), whole((2, 8, 128))],
        out_shape=[
            jax.ShapeDtypeStruct((rows, columns), BF),
            jax.ShapeDtypeStruct((2, 8, 128), F32),
        ],
        scratch_shapes=[
            vmem((tokens, columns), BF),
            vmem((docs, tokens), F32),
            vmem((8, tokens), F32),
            vmem((16, 8, tokens), F32),
            vmem((units, 8, tokens), F32),
            vmem((docs, tokens), BF),
            vmem((tokens, columns), F32),
            vmem((tokens, columns), BF),
            vmem((16, own, columns), BF),
            vmem((2, 2, 8, 128), F32),
            vmem((2, 2, 8, 128), F32),
            dma((3, 16)),
            dma((3, 16)),
            dma((2,)),
            dma((2,)),
        ],
        compiler_params=pltpu.CompilerParams(
            collective_id=5, has_side_effects=True, vmem_limit_bytes=60 << 20
        ),
        name="loss",
        cost_estimate=pl.CostEstimate(
            flops=100 * docs * tokens * columns,
            bytes_accessed=8 * rows * columns,
            transcendentals=docs * tokens,
        ),
    )(projection, labels, log_counts, picks)


class MatrixSum:
    def __init__(
        self, around, send, axis, across, own, got, next_, near, far, home, local_sems,
        away=None, extras=(),
    ):
        self.axis, self.own, self.got, self.next, self.near = axis, own, got, next_, near
        self.block = own.shape[axis] // 4
        first, second = (2, 4) if across else (4, 2)
        self.gone, self.later = ((1, 3), 2) if across else ((2, 3), 1)
        self.cores = [send(src, dst, around.other(1)) for src, dst in far]
        self.loads = [
            pltpu.make_async_copy(src, dst, sem) for (src, dst), sem in zip(home, local_sems)
        ]
        self.firsts = [
            send(self.at(own, n), self.at(next_, slot), around.other(first))
            for slot, n in enumerate(self.gone)
        ]
        self.second = send(self.at(own, self.later), near, around.other(second))
        self.extras = extras
        self.away = None
        if away is not None:
            self.away = send(self.at(own, 0), away[1], around.along(away[0]))

    def at(self, ref, n):
        span = pl.ds(n * self.block, self.block)
        return ref.at[span, :] if self.axis == 0 else ref.at[:, span]

    def begin(self):
        for copy in self.cores + self.loads:
            copy.start()

    def add(self, n, ref, m):
        rows = self.block if self.axis == 0 else self.own.shape[0]
        step = 16 if self.axis == 0 else 128
        block = self.block

        @pl.loop(0, rows // step)
        def _(k):
            if self.axis == 0:
                to = (pl.ds(pl.multiple_of(n * block + k * step, step), step), slice(None))
                fr = (pl.ds(pl.multiple_of(m * block + k * step, step), step), slice(None))
            else:
                at = pl.ds(pl.multiple_of(k * step, step), step)
                to, fr = (at, pl.ds(n * block, block)), (at, pl.ds(m * block, block))
            self.own[to] = self.own[to] + ref[fr]

    def first_axis(self):
        for load in self.loads:
            load.wait()
        for copy in self.cores:
            copy.wait_recv()
        for n, copy in zip(self.gone, self.firsts):
            self.add(n, self.got, n)
            copy.start()
        for n in (self.later, 0):
            self.add(n, self.got, n)

    def second_axis(self):
        for copy in self.firsts:
            copy.wait_recv()
        self.add(self.later, self.next, 1)
        self.second.start()
        self.add(0, self.next, 0)

    def tensor(self):
        self.second.wait_recv()
        self.add(0, self.near, 0)
        for buffer, copy in self.extras:
            copy.wait_recv()
            self.add(0, buffer, 0)
        if self.away is not None:
            self.away.start()


class SmallSum:
    def __init__(self, around, send, got, run, bits=(1, 4, 2), tensor=(1, 2)):
        self.got, self.run = got, run
        tos = [around.other(bit) for bit in bits] + [around.along(dt) for dt in tensor]
        self.copies = [send(run.at[n], got.at[n], to) for n, to in enumerate(tos)]

    def begin(self):
        self.copies[0].start()

    def hop(self, n):
        self.copies[n].wait_recv()
        self.run[n + 1] = self.run[n] + self.got[n]
        if n + 1 < len(self.copies):
            self.copies[n + 1].start()


class ProjSum:
    def __init__(self, around, send, ref, run, got):
        self.ref, self.run, self.got = ref, run, got
        rows = ref.shape[0]
        self.half = [rows // 2, rows // 4, rows // 8]
        starts = [0, rows // 2, 3 * rows // 4]
        self.starts = starts
        self.copies = [
            send(ref.at[self.half[0] :, :], got.at[pl.ds(starts[0], self.half[0]), :], around.other(1))
        ]
        for n, bit in ((1, 4), (2, 2)):
            self.copies.append(
                send(
                    run.at[pl.ds(self.half[n], self.half[n]), :],
                    got.at[pl.ds(starts[n], self.half[n]), :],
                    around.other(bit),
                )
            )
        last = self.half[2]
        self.last = last
        base = rows
        for n, dt in ((0, 1), (1, 2)):
            self.copies.append(
                send(
                    run.at[pl.ds(rows // 2 + n * last, last), :],
                    got.at[pl.ds(base + n * last, last), :],
                    around.along(dt),
                )
            )

    def begin(self):
        self.copies[0].start()

    def hop(self, n):
        self.copies[n].wait_recv()
        rows = self.ref.shape[0]
        last = self.last
        if n < 3:
            size = self.half[n]
            old = self.ref if n == 0 else self.run
            total = old[:size, :] + self.got[pl.ds(self.starts[n], size), :]
            if n < 2:
                self.run[:size, :] = total
            else:
                self.run[pl.ds(rows // 2, last), :] = total
        else:
            at = rows // 2 + (n - 3) * last
            got = self.got[pl.ds(rows + (n - 3) * last, last), :]
            self.run[pl.ds(at + last, last), :] = self.run[pl.ds(at, last), :] + got
        if n + 1 < len(self.copies):
            self.copies[n + 1].start()

    def result(self):
        return self.run[pl.ds(self.ref.shape[0] // 2 + 2 * self.last, self.last), :]


def finish_kernel(x, weights, pre, mixed, branch, resid, tensor_sums):
    ways = 4
    rows, width = x.shape
    half, block = width // 2, width // 8
    share = width // ways
    docs = rows // 9 * 8
    quarter, asked = docs // 2, (rows - docs) // 2
    part = 3 * share

    def kernel(
        x_ref, w_ref, p_ref, m_ref, g_ref, r_ref, ten_ref,
        qkv_o, out_o, doc_o, ask_o, ten_o,
        xs, ws, ps, ms, gs, rs, low, qf, qa, q0, q1, q2, q3, of, oa, o0, o1, o2, o3,
        t_got, t_run, tz, send_sem, recv_sem, local_sem, row_send, row_recv,
    ):
        around = Around()
        around.greet()
        loads = {}
        for n, (name, src, dst) in enumerate(
            [("p", p_ref, ps), ("r", r_ref, rs)]
            + [(j, w_ref.at[j], ws.at[j]) for j in range(3)]
            + [("x", x_ref, xs), ("m", m_ref, ms), ("g", g_ref, gs)]
        ):
            loads[name] = pltpu.make_async_copy(src, dst, local_sem.at[n])
            loads[name].start()
        send = Sender(send_sem, recv_sem)
        small = SmallSum(around, send, t_got, t_run, tensor=())
        spread = [send(t_run.at[3, dt], tz.at[dt - 1], around.along(dt)) for dt in range(1, ways)]
        heads, feats = [None] * ways, [None] * ways
        for n in (3, 2, 1, 0):
            step = {3: (1, 1), 2: (2, 2), 1: (1, 0), 0: None}[n]
            heads[n] = MatrixSum(
                around, send, 0, n % 2 == 0, qa.at[n], q0.at[n], q1.at[n], q2.at[n],
                [(qf.at[n], q0.at[n])], [], [],
                None if step is None else (step[0], q3.at[step[1]]),
                [(q3.at[1], heads[3].away)] if n == 2 else [],
            )
            feats[n] = MatrixSum(
                around, send, 1, n % 2 == 0, oa.at[n], o0.at[n], o1.at[n], o2.at[n],
                [(of.at[n], o0.at[n])], [], [],
                None if step is None else (step[0], o3.at[step[1]]),
                [(o3.at[1], feats[3].away)] if n == 2 else [],
            )
        names = [("h", 3), ("h", 2), ("f", 3), ("f", 2), ("h", 1), ("h", 0), ("f", 1), ("f", 0)]
        items = [(heads if kind == "h" else feats)[n] for kind, n in names]

        def compute(k):
            kind, n = names[k]
            at = pl.ds(n * share, share)
            for side, to in ((1, qf if kind == "h" else of), (0, qa if kind == "h" else oa)):
                span = pl.ds(side * half, half)
                if kind == "h":
                    for j in range(3):
                        to[n, :, j * share : (j + 1) * share] = dot_tn(
                            xs[:, span], ps[j, :, at]
                        ).astype(BF)
                else:
                    to[n] = dot_tn(ms[:, at], gs[:, span]).astype(BF)
                if side == 1:
                    items[k].begin()

        loads["p"].wait()
        loads["r"].wait()
        for j in range(3):
            loads[j].wait()
        for at in range(0, width, share):
            total = rs[:, at : at + share]
            for j in range(3):
                total = total + dot_nt(ps[j], ws[j, at : at + share, :])
            low[:, at : at + share] = total.astype(BF)
        around.await_all()
        t_run[0] = ten_ref[...]
        small.begin()
        home = RowMoves(around, False, doc_o, ask_o, low, row_send, row_recv)
        home.start()
        for name in ("x", "m", "g"):
            loads[name].wait()
        compute(0)
        compute(1)
        for n in range(0, len(items) + 4, 2):
            if 0 < n < 8:
                small.hop(n // 2 - 1)
            if n == 6:
                for copy in spread:
                    copy.start()
            for item in items[n - 2 : n] if n >= 2 else []:
                item.second_axis()
            for item in items[n : n + 2]:
                item.first_axis()
            for k in (n + 2, n + 3):
                if k < len(items):
                    compute(k)
            for m in (n - 4, n - 3):
                if 0 <= m < len(items):
                    items[m].tensor()

        home.wait()
        for copy in spread:
            copy.wait_recv()
        ten_o[...] = t_run[3, 0] + tz[0] + tz[1] + tz[2]
        for group in (heads, feats):
            group[1].away.wait_recv()
            group[2].away.wait_recv()
        for j in range(3):
            at = pl.ds(j * share, share)
            total = qa[0, :block, at].astype(F32) + q3[0, :, at].astype(F32)
            qkv_o[j] = total + q3[2, :, at].astype(F32)
        total = oa[0, :, :block].astype(F32) + o3[0].astype(F32)
        out_o[...] = total + o3[2].astype(F32)
        send.drain()

    def whole(x):
        return pl.BlockSpec(x.shape, lambda: (0,) * len(x.shape))

    out_shape = [
        jax.ShapeDtypeStruct((3, block, share), F32),
        jax.ShapeDtypeStruct((share, block), F32),
        jax.ShapeDtypeStruct((2, quarter, width), BF),
        jax.ShapeDtypeStruct((2, asked, width), BF),
        jax.ShapeDtypeStruct(tensor_sums.shape[1:], F32),
    ]
    anywhere = pl.BlockSpec(memory_space=pl.ANY)
    vmem = pltpu.VMEM
    dma = pltpu.SemaphoreType.DMA
    count = 6 + 2 * (ways * 4 + 3)
    return pl.pallas_call(
        kernel,
        out_shape=out_shape,
        in_specs=[anywhere] * 6 + [whole(tensor_sums)],
        out_specs=[
            whole(out_shape[0]),
            whole(out_shape[1]),
            anywhere,
            anywhere,
            whole(out_shape[4]),
        ],
        scratch_shapes=[
            vmem((rows, width), BF),
            vmem((3, width, width), BF),
            vmem((3, rows, width), BF),
            vmem((rows, width), BF),
            vmem((rows, width), BF),
            vmem((rows, width), F32),
            vmem((rows, width), BF),
            vmem((ways, half, part), BF),
            vmem((ways, half, part), BF),
            vmem((ways, half, part), BF),
            vmem((ways, 2 * block, part), BF),
            vmem((ways, block, part), BF),
            vmem((ways - 1, block, part), BF),
            vmem((ways, share, half), BF),
            vmem((ways, share, half), BF),
            vmem((ways, share, half), BF),
            vmem((ways, share, 2 * block), BF),
            vmem((ways, share, block), BF),
            vmem((ways - 1, share, block), BF),
            vmem((3,) + tensor_sums.shape, F32),
            vmem((4,) + tensor_sums.shape, F32),
            vmem((ways - 1,) + tensor_sums.shape[1:], F32),
            dma((count,)),
            dma((count,)),
            dma((8,)),
            dma((2, 2)),
            dma((2, 2)),
        ],
        compiler_params=pltpu.CompilerParams(
            collective_id=1, has_side_effects=True, vmem_limit_bytes=60 << 20
        ),
        name="last_sums",
    )(x, weights, pre, mixed, branch, resid, tensor_sums)


def attention_backward_kernel(
    qkv, far_kv, grad, cosine, sine, col_labels, row_labels,
    up, back, vectors, proj, y,
):
    rows, width = qkv.shape[1:]
    docs = far_kv.shape[1]
    pairs = width // 128
    block = docs
    asked = rows - docs
    ways = 4
    half, own_block = width // 2, width // 8
    share = up.shape[1] // ways
    count, piece = 2 * ways, share // 2
    assert pairs == 8

    def kernel(
        qkv_ref, far_ref, g_ref, c_ref, s_ref, lc_ref, lr_ref,
        up_ref, back_ref, vec_ref, proj_ref, y_ref,
        pre_ref, bias_ref, up_o, back_o, vec_o, proj_o, yd_ref, yq_ref,
        sums_own, sums_far, give, kept, got_kv,
        ua, u0, u1, u2, u3, ba, b0, b1, b2, b3, v_got, v_run, p_run, p_got,
        send_sem, recv_sem, local_sem, row_send, row_recv,
    ):
        h = pl.program_id(0)
        around = Around()
        send = Sender(send_sem, recv_sem)
        ups, backs = [None] * count, [None] * count
        for n in range(count - 1, -1, -1):
            span = pl.ds(n * piece, piece)
            dt, side = n // 2, n % 2
            step = {3: (1, 1), 2: (2, 2), 1: (1, 0), 0: None}[dt]
            ups[n] = MatrixSum(
                around, send, 0, False, ua.at[n], u0.at[n], u1.at[n], u2.at[n],
                [(up_ref.at[half:, span], u0.at[n])],
                [(up_ref.at[:half, span], ua.at[n])],
                [local_sem.at[n]],
                None if step is None else (step[0], u3.at[step[1], side]),
                [(u3.at[1, side], ups[n + 2].away)] if dt == 2 else [],
            )
            backs[n] = MatrixSum(
                around, send, 1, True, ba.at[n], b0.at[n], b1.at[n], b2.at[n],
                [(back_ref.at[span, half:], b0.at[n])],
                [(back_ref.at[span, :half], ba.at[n])],
                [local_sem.at[count + n]],
                None if step is None else (step[0], b3.at[step[1], side]),
                [(b3.at[1, side], backs[n + 2].away)] if dt == 2 else [],
            )
        couples = [(ups[n], backs[n]) for n in (6, 7, 4, 5, 2, 3, 0, 1)]
        small = SmallSum(around, send, v_got, v_run)
        mean_proj = ProjSum(around, send, proj_ref, p_run, p_got)
        gives = [send(give.at[n], got_kv.at[n], around.other(1)) for n in range(pairs)]
        home = RowMoves(around, False, yd_ref, yq_ref, y_ref, row_send, row_recv)
        lane = lax.broadcasted_iota(jnp.int32, (1, 128), 1)

        def finish(n):
            gives[n].wait_recv()
            at = pl.ds(n * 128, 128)
            for i in range(2):
                head = kept[n % 2, i, :docs, :] + got_kv[n, i].astype(F32)
                tail = kept[n % 2, i, docs:, :]
                if i == 0:
                    head = head * c_ref[:docs, :] - turned(head) * s_ref[:docs, :]
                    tail = tail * c_ref[docs:, :] - turned(tail) * s_ref[docs:, :]
                head, tail = head.astype(BF), tail.astype(BF)
                pre_ref[i + 1, :docs, at] = head
                pre_ref[i + 1, docs:, at] = tail
                total = jnp.sum(head.astype(F32), axis=0, keepdims=True)
                total = total + jnp.sum(tail.astype(F32), axis=0, keepdims=True)
                bias_ref[i + 1 : i + 2, at] = total

        for step in range(pairs):

            @pl.when(h == step)
            def _(step=step):
                if step == 0:
                    around.meet()
                    for p in range(8):
                        to = feature_block(around.rank, p) * own_block
                        at = pl.ds(pl.multiple_of(to, own_block), own_block)
                        v_run[0, :, at] = vec_ref[:, p * own_block : (p + 1) * own_block]
                    small.begin()
                    mean_proj.begin()
                    for n, many in ((0, 2), (2, 4), (4, 8)):
                        for couple in couples[n:many]:
                            for item in couple:
                                item.begin()
                        if n < 4:
                            for item in couples[n // 2]:
                                item.first_axis()
                    home.start()
                else:
                    firsts = {1: (2,), 2: (3, 4), 3: (5,), 4: (6,), 5: (7,)}
                    seconds = {1: (0,), 2: (1,), 3: (2,), 4: (3, 4), 5: (5,), 6: (6,), 7: (7,)}
                    tensors = {3: (0, 1), 4: (2,), 5: (3,), 6: (4,), 7: (5, 6)}
                    if step <= 5:
                        small.hop(step - 1)
                        mean_proj.hop(step - 1)
                    for n in seconds.get(step, ()):
                        for item in couples[n]:
                            item.second_axis()
                    for n in firsts.get(step, ()):
                        for item in couples[n]:
                            item.first_axis()
                    for n in tensors.get(step, ()):
                        for item in couples[n]:
                            item.tensor()
                    finish(step - 1)

        sums_own[...] = jnp.zeros_like(sums_own)
        sums_far[...] = jnp.zeros_like(sums_far)

        def part(start, size, keys, sames, sums):
            q_block = qkv_ref[0, pl.ds(start, size), :]
            g_block = g_ref[pl.ds(start, size), :]
            grads = []
            for head in range(2):
                mask = (lane // HEAD_WIDTH) == head
                q_head = jnp.where(mask, q_block, jnp.zeros_like(q_block))
                g_head = jnp.where(mask, g_block, jnp.zeros_like(g_block))
                scores = [
                    jnp.where(same, dot_nt(q_head, key), MASKED)
                    for (key, _), same in zip(keys, sames)
                ]
                top = functools.reduce(
                    jnp.maximum, [jnp.max(s, axis=-1, keepdims=True) for s in scores]
                )
                powers = [jnp.exp(s - top) for s in scores]
                total = functools.reduce(
                    jnp.add, [jnp.sum(p, axis=-1, keepdims=True) for p in powers]
                )
                inverse = 1.0 / total
                g_head = (g_head.astype(F32) * inverse).astype(BF)
                pulls = [dot_nt(g_head, value) for _, value in keys]
                mean = functools.reduce(
                    jnp.add,
                    [jnp.sum(p * d, axis=-1, keepdims=True) for p, d in zip(powers, pulls)],
                ) * inverse
                slopes = [(p * (d - mean)).astype(BF) for p, d in zip(powers, pulls)]
                got = functools.reduce(
                    jnp.add, [dot_nn(s, key) for s, (key, _) in zip(slopes, keys)]
                )
                grads.append(got * 0.125)
                for (ref, begin, many), s, p in zip(sums, slopes, powers):
                    ref[0, pl.ds(begin, many), :] += dot_tn(s, q_head)
                    ref[1, pl.ds(begin, many), :] += dot_tn(p.astype(BF), g_head)
            total = jnp.where(lane < HEAD_WIDTH, grads[0], grads[1])
            at = pl.ds(start, size)
            low = (total * c_ref[at, :] - turned(total) * s_ref[at, :]).astype(BF)
            pre_ref[0, at, pl.ds(pl.multiple_of(h * 128, 128), 128)] = low
            return jnp.sum(low.astype(F32), axis=0, keepdims=True)

        doc_keys = [
            (qkv_ref[1, :docs, :], qkv_ref[2, :docs, :]),
            (far_ref[0], far_ref[1]),
        ]
        bias = jnp.zeros((1, 128), F32)
        for at in range(docs // block):
            labels = lc_ref[pl.ds(at * block, block), :]
            bias = bias + part(
                at * block,
                block,
                doc_keys,
                [labels == lr_ref[0:1, :], labels == lr_ref[1:2, :]],
                [(sums_own, 0, docs), (sums_far, 0, docs)],
            )
        row = lax.broadcasted_iota(jnp.int32, (asked, asked), 0) // QLEN
        col = lax.broadcasted_iota(jnp.int32, (asked, asked), 1) // QLEN
        bias = bias + part(
            docs,
            asked,
            [(qkv_ref[1, docs:, :], qkv_ref[2, docs:, :])],
            [row == col],
            [(sums_own, docs, asked)],
        )
        bias_ref[0:1, pl.ds(pl.multiple_of(h * 128, 128), 128)] = bias
        side = h % 2
        kept[side] = sums_own[...]
        give[h] = sums_far[...].astype(BF)
        for step in range(pairs):

            @pl.when(h == step)
            def _(step=step):
                gives[step].start()

        @pl.when(h == pairs - 1)
        def _():
            finish(pairs - 1)
            for couple in couples[7:]:
                for item in couple:
                    item.tensor()
            for group, acc, came, o in ((ups, ua, u3, up_o), (backs, ba, b3, back_o)):
                for n in range(2):
                    group[n + 2].away.wait_recv()
                    group[n + 4].away.wait_recv()
                    at = pl.ds(n * piece, piece)
                    if acc is ua:
                        total = acc[n, :own_block, :].astype(F32)
                    else:
                        total = acc[n, :, :own_block].astype(F32)
                    total = total + came[0, n].astype(F32) + came[2, n].astype(F32)
                    if acc is ua:
                        o[:, at] = total
                    else:
                        o[at, :] = total
            vec_o[...] = v_run[5]
            proj_o[...] = mean_proj.result()
            home.wait()
            send.drain()

    def whole(shape):
        return pl.BlockSpec(shape, lambda h: (0,) * len(shape))

    anywhere = pl.BlockSpec(memory_space=pl.ANY)
    vmem = pltpu.VMEM
    dma = pltpu.SemaphoreType.DMA
    columns = proj.shape[1]
    out_shape = [
        jax.ShapeDtypeStruct((3, rows, width), BF),
        jax.ShapeDtypeStruct((8, width), F32),
        jax.ShapeDtypeStruct((own_block, share), F32),
        jax.ShapeDtypeStruct((share, own_block), F32),
        jax.ShapeDtypeStruct(vectors.shape, F32),
        jax.ShapeDtypeStruct((own_block, columns), F32),
    ]
    slots = 2 * (count * 4 + 6) + 5 + 5 + pairs
    return pl.pallas_call(
        kernel,
        grid=(pairs,),
        in_specs=[
            pl.BlockSpec((3, rows, 128), lambda h: (0, 0, h)),
            pl.BlockSpec((2, docs, 128), lambda h: (0, 0, h)),
            pl.BlockSpec((rows, 128), lambda h: (0, h)),
            whole((rows, 128)),
            whole((rows, 128)),
            whole((docs, 1)),
            whole((2, docs)),
            anywhere,
            anywhere,
            whole(vectors.shape),
            whole(proj.shape),
            anywhere,
        ],
        out_specs=[whole(x.shape) for x in out_shape] + [anywhere, anywhere],
        out_shape=out_shape
        + [
            jax.ShapeDtypeStruct((2, docs // 2, width), BF),
            jax.ShapeDtypeStruct((2, asked // 2, width), BF),
        ],
        scratch_shapes=[
            vmem((2, rows, 128), F32),
            vmem((2, docs, 128), F32),
            vmem((pairs, 2, docs, 128), BF),
            vmem((2, 2, rows, 128), F32),
            vmem((pairs, 2, docs, 128), BF),
            vmem((count, half, piece), BF),
            vmem((count, half, piece), BF),
            vmem((count, 2 * own_block, piece), BF),
            vmem((count, own_block, piece), BF),
            vmem((ways - 1, 2, own_block, piece), BF),
            vmem((count, piece, half), BF),
            vmem((count, piece, half), BF),
            vmem((count, piece, 2 * own_block), BF),
            vmem((count, piece, own_block), BF),
            vmem((ways - 1, 2, piece, own_block), BF),
            vmem((5,) + vectors.shape, F32),
            vmem((6,) + vectors.shape, F32),
            vmem((width, columns), F32),
            vmem((width + 2 * own_block, columns), F32),
            dma((slots,)),
            dma((slots,)),
            dma((2 * count,)),
            dma((2, 2)),
            dma((2, 2)),
        ],
        compiler_params=pltpu.CompilerParams(
            collective_id=2, has_side_effects=True, vmem_limit_bytes=60 << 20
        ),
        name="attend_backward_and_sum",
        cost_estimate=pl.CostEstimate(
            flops=100 * rows * 2 * docs * width,
            bytes_accessed=4 * (6 * rows + 4 * docs) * width,
            transcendentals=rows * 2 * docs * width // 64,
        ),
    )(
        qkv, far_kv, grad, cosine, sine, col_labels, row_labels,
        up, back, vectors, proj, y,
    )


def body(
    x_doc,
    x_query,
    doc_cot,
    query_cot,
    lengths,
    positives,
    w_qkv,
    b_qkv,
    w_out,
    b_out,
    gain_one,
    shift_one,
    w_in,
    b_in,
    w_back,
    b_back,
    gain_two,
    shift_two,
    w_proj,
):
    ways = lax.axis_size("tensor")
    groups = lax.axis_size("dp")
    column = lax.axis_index("tensor")
    rank = lax.axis_index("dp")
    core = rank % 2
    chip = rank // 2
    chips = groups // 2
    micro, quarter, width = x_doc.shape
    asked = x_query.shape[1]
    segments = lengths.shape[2] - 1
    proj_width = w_proj.shape[1]
    heads_local = w_qkv.shape[2]
    units_local = w_in.shape[1]
    block = width // groups
    assert ways == 2 * micro and ways == 4

    def exchange(value, dr=0, dt=0):
        pairs = [
            (r * ways + t, (r ^ dr) * ways + (t ^ dt)) for r in range(groups) for t in range(ways)
        ]
        return lax.ppermute(value, AXES, pairs)

    chip_bits = []
    bit = 2
    while bit < groups:
        chip_bits.append(bit)
        bit *= 2

    def gather_weights(pack, reverse):
        pieces = [pack] + [exchange(pack, dt=j) for j in range(1, ways)]
        pieces = [(0, jnp.concatenate(pieces, axis=-1))]
        order = chip_bits[::-1] if reverse and len(chip_bits) == 2 else chip_bits
        for dr in order:
            pieces = pieces + [(j + dr // 2, exchange(p, dr=dr)) for j, p in pieces]
            if len(pieces) >= 4 or dr == order[-1]:
                pieces.sort(key=lambda item: item[0])
                pieces = [(0, jnp.concatenate([p for _, p in pieces], axis=-2))]
        (_, half), = pieces
        return jnp.concatenate([half, exchange(half, dr=1)], axis=-2)

    def gather_proj(pack):
        for dr in chip_bits + [1]:
            pack = jnp.concatenate([pack, exchange(pack, dr=dr)], axis=0)
        return pack

    unit_micro = column // 2
    unit_row = chip * 2 + column % 2

    def rows_in(docs, queries):
        blocks = jnp.concatenate([docs, queries], axis=1)
        got = []
        for j in range(2):
            send = jnp.where((column + j) % 2 == 0, blocks[0], blocks[1])
            pairs = []
            for r in range(groups):
                for t in range(ways):
                    m = (t + j) % 2
                    pairs.append(
                        (r * ways + t, ((r // 2) * 2 + t // 2) * ways + 2 * m + r % 2)
                    )
            got.append(lax.ppermute(send, AXES, pairs))
        first = jnp.where(unit_micro == 0, got[0], got[1])
        second = jnp.where(unit_micro == 0, got[1], got[0])
        return jnp.concatenate(
            [first[:quarter], second[:quarter], first[quarter:], second[quarter:]], axis=0
        )

    def quarters_out(first, second):
        got = []
        for j in range(2):
            send = jnp.where((unit_micro + j) % 2 == 0, first, second)
            pairs = []
            for r in range(groups):
                for t in range(ways):
                    m = t // 2
                    pairs.append(
                        (
                            r * ways + t,
                            ((r // 2) * 2 + t % 2) * ways + 2 * (r % 2) + (m + j) % 2,
                        )
                    )
            got.append(lax.ppermute(send, AXES, pairs))
        even = jnp.where(column % 2 == 0, got[0], got[1])
        odd = jnp.where(column % 2 == 0, got[1], got[0])
        return jnp.stack([even, odd])

    def rows_out(values):
        docs = 2 * quarter
        first = jnp.concatenate([values[:quarter], values[docs : docs + asked]], axis=0)
        second = jnp.concatenate([values[quarter:docs], values[docs + asked :]], axis=0)
        blocks = quarters_out(first, second)
        return blocks[:, :quarter], blocks[:, quarter:]

    place = jnp.arange(width, dtype=jnp.int32)
    step = place // block
    actual = (rank ^ (2 * (step % chips) + step // chips)) * block + place % block
    turn = (place[:, None] == actual[None, :]).astype(BF)

    docs = 2 * quarter
    queries = 2 * asked
    rows = docs + queries
    sizes_all = lengths[unit_micro]
    sizes = sizes_all[unit_row]
    ends = jnp.cumsum(sizes[:-1])
    half = HEAD_WIDTH // 2
    rates = 10000.0 ** (-(2.0 * jnp.arange(half, dtype=F32)) / HEAD_WIDTH)
    own_picks = jnp.zeros((8, 128), jnp.int32).at[:micro, : positives.shape[1]].set(positives)
    params = [b_out, gain_one, shift_one, b_back, gain_two, shift_two]
    if chips == 4:
        (
            own_x, full_qkv, full_out, full_proj, picks_rel,
            bias_qkv, bias_in, cosine, sine, col_labels, row_labels, *cots, params,
        ) = gather_kernel(
            x_doc, x_query, w_qkv, w_out, w_proj, b_qkv, b_in[None], own_picks,
            doc_cot, query_cot, ends, jnp.tile(rates, 4)[None], params,
        )
        full_proj = full_proj.reshape(width, proj_width)
    else:
        own_x = rows_in(x_doc, x_query)
        own_cot = rows_in(doc_cot.astype(BF), query_cot.astype(BF))
        full_qkv = gather_weights(w_qkv, False)
        full_out = gather_weights(w_out.T, False).T
        full_in = gather_weights(w_in, False)
        full_back = gather_weights(w_back.T, False).T
        full_proj = gather_proj(w_proj)
        picks_rel = gather_proj(own_picks[None])
        bias_pack = jnp.concatenate([b_qkv.reshape(-1), b_in])
        biases = [bias_pack] + [exchange(bias_pack[None], dt=j)[0] for j in range(1, ways)]
        bias_qkv = jnp.concatenate(
            [b[: 3 * heads_local].reshape(3, heads_local) for b in biases], axis=1
        )
        bias_in = jnp.concatenate([b[3 * heads_local :] for b in biases])
        params = jnp.dot(
            jnp.stack(params + [b_out, b_out]), turn.astype(F32), precision=FULL_PRECISION
        )
        starts = jnp.concatenate([jnp.zeros((1,), jnp.int32), ends])

        def layout(first):
            index = first + jnp.arange(docs, dtype=jnp.int32)
            segment = jnp.sum((index[:, None] >= ends[None, :]).astype(jnp.int32), axis=1)
            labels = jnp.arange(starts.shape[0], dtype=jnp.int32)
            begin = jnp.sum(
                jnp.where(segment[:, None] == labels[None, :], starts[None, :], 0), axis=1
            )
            return segment, index - begin

        def rotation(places):
            angle = places.astype(F32)[:, None] * rates[None, :]
            turned_sine = jnp.sin(angle)
            return (
                jnp.tile(jnp.cos(angle), (1, 4)),
                jnp.concatenate([-turned_sine, turned_sine] * 2, axis=1),
            )

        own_labels, own_places = layout(core * docs)
        far_labels, far_places = layout((1 - core) * docs)
        own_places = jnp.concatenate([own_places, jnp.arange(queries, dtype=jnp.int32) % QLEN])
        cosine, sine = rotation(own_places)
        far_cosine, far_sine = rotation(far_places)
        label_args = (own_labels[:, None], own_labels[None, :], far_labels[None, :])
    picks_rel = picks_rel[:, :micro, : positives.shape[1]].astype(F32)
    b_out, gain_one, shift_one, b_back, gain_two, shift_two = [params[n] for n in range(6)]

    if chips == 4:
        x_low = own_x
        qkv, far_kv, mixed, resid_one, normed, normed_low, own_cot, full_in, full_back = (
            project_and_attend(
                own_x, full_qkv, bias_qkv, cosine, sine, col_labels, row_labels, full_out, params,
                *cots, w_in, w_back,
            )
        )
        active_low, active_slope, resid_two, output_low, projection = feed_forward(
            normed_low, full_in, bias_in, full_back, normed, params, full_proj
        )
        y_low = output_low
    else:
        x_low = dot_nn(own_x, turn).astype(BF)
        qkv = project_heads(
            x_low,
            full_qkv,
            bias_qkv,
            jnp.stack([cosine * 0.125, cosine, jnp.ones_like(cosine)]),
            jnp.stack([sine * 0.125, sine, jnp.zeros_like(sine)]),
        )
        far_kv = exchange(qkv[1:, :docs], dr=1)
        mixed = attention_forward(qkv, far_kv, *label_args)
        resid_one = x_low.astype(F32) + dot_nn(mixed, full_out) + b_out
        normed, norm_one_pull = jax.vjp(layer_norm, resid_one, gain_one, shift_one)
        normed_low = normed.astype(BF)
        inner = dot_nn(normed_low, full_in) + bias_in
        active, gelu_pull = jax.vjp(gelu_exact, inner)
        active_low = active.astype(BF)
        resid_two = normed + dot_nn(active_low, full_back) + b_back
        output, norm_two_pull = jax.vjp(layer_norm, resid_two, gain_two, shift_two)
        output_low = output.astype(BF)
        y_low = dot_nt(output_low, turn).astype(BF)
        projection = dot_nn(output_low, full_proj)
    held = jnp.arange(groups, dtype=jnp.int32)
    held = rank ^ (2 * (held % chips) + held // chips)
    order = (jnp.arange(groups, dtype=jnp.int32)[:, None] == held[None, :]).astype(F32)
    picks = jnp.where(unit_micro == 0, picks_rel[:, 0], picks_rel[:, 1])
    picks = jnp.dot(order, picks, precision=FULL_PRECISION).astype(jnp.int32).reshape(-1)
    counts = sizes_all[:, :segments].reshape(-1).astype(F32)

    if chips == 4:
        log_counts = jnp.pad(
            jnp.log(counts).reshape(-1, segments), ((0, 0), (0, 8 - segments))
        ).reshape(-1, 1)
        proj_low, loss_out = loss_kernel(
            projection, col_labels, log_counts, jnp.repeat(picks, QLEN)[None]
        )
        loss_out = loss_out[:, : asked // QLEN, 0]
    else:
        y_doc, y_query = rows_out(y_low)
        unit, unit_pull = jax.vjp(normalize, projection)
        unit_low = unit.astype(BF)

        doc_unit = unit_low[:docs]
        query_unit = unit_low[docs:]

        def bit_of(dr, dt):
            return (rank // dr) % 2 == 1 if dr else (column // dt) % 2 == 1

        def join(value, dr, dt, axis=0):
            got = exchange(value, dr=dr, dt=dt)
            on = bit_of(dr, dt)
            low = jnp.where(on, got, value)
            high = jnp.where(on, value, got)
            return jnp.concatenate([low, high], axis=axis)

        def split_sum(value, dr, dt):
            on = bit_of(dr, dt)
            size = value.shape[0] // 2
            send = jnp.where(on, value[:size], value[size:])
            keep = jnp.where(on, value[size:], value[:size])
            return keep + exchange(send.astype(BF), dr=dr, dt=dt).astype(F32)

        steps = [(1, 0), (0, 1)] + [(dr, 0) for dr in chip_bits]
        all_queries = query_unit
        for dr, dt in steps:
            all_queries = join(all_queries, dr, dt)
        seg_labels = jnp.arange(segments, dtype=jnp.int32)
        member = (own_labels[:, None] == seg_labels[None, :]).astype(F32)
        cosines = dot_nt(doc_unit, all_queries)
        weight = jnp.exp(TAU * (cosines - 1.0))
        totals = jnp.einsum("js,ji->si", member, weight, precision=FULL_PRECISION)
        totals = totals + exchange(totals, dr=1)
        for dr, dt in steps[1:]:
            totals = join(totals, dr, dt)
        best = (jnp.log(totals) - jnp.log(counts)[:, None]) / TAU + 1.0
        score = jnp.sum(best.reshape(best.shape[0], -1, QLEN), axis=-1)
        logits = LOGIT_SCALE * score
        documents = jnp.arange(logits.shape[0], dtype=jnp.int32)
        chosen = (documents[:, None] == picks[None, :]).astype(F32)
        peak = jnp.max(logits, axis=0, keepdims=True)
        powers = jnp.exp(logits - peak)
        mass = jnp.sum(powers, axis=0, keepdims=True)
        losses = (peak + jnp.log(mass))[0] - jnp.sum(chosen * logits, axis=0)
        logit_grad = LOGIT_SCALE * (powers / mass - chosen)
        own_grad = lax.dynamic_slice_in_dim(logit_grad, unit_row * segments, segments, axis=0)
        own_total = lax.dynamic_slice_in_dim(totals, unit_row * segments, segments, axis=0)
        coef = jnp.repeat(own_grad, QLEN, axis=1) / own_total
        spread = jnp.einsum("js,si->ji", member, coef, precision=FULL_PRECISION)
        cosine_grad = (weight * spread).astype(BF)
        doc_grad = dot_nn(cosine_grad, all_queries)
        query_grad = dot_tn(cosine_grad, doc_unit)
        for dr, dt in steps[::-1]:
            query_grad = split_sum(query_grad, dr, dt)
        own_losses = lax.dynamic_slice_in_dim(losses, unit_row * (4 * asked // QLEN) + core * 2 * (asked // QLEN), 2 * (asked // QLEN))
        per = asked // QLEN
        loss_tiles = [
            jnp.broadcast_to(own_losses[i * per : (i + 1) * per, None], (per, 128)) for i in range(2)
        ]
        loss_out = quarters_out(loss_tiles[0], loss_tiles[1])[:, :, 0]

        unit_grad = jnp.concatenate([doc_grad, query_grad], axis=0)
        (proj_grad,) = unit_pull(unit_grad)
        proj_low = proj_grad.astype(BF)

    class Reduction:
        def __init__(self, half, axis, reverse, last):
            self.bits = chip_bits if reverse and len(chip_bits) == 2 else chip_bits[::-1]
            self.left = sorted(chip_bits)
            self.axis, self.last = axis, last
            self.sends = [half(1).astype(BF)]
            self.hops = [(1, 0)]
            self.kept = lambda: half(0)
            self.stage = 0

        def advance(self):
            total = self.kept()
            for s, (dr, dt) in zip(self.sends, self.hops):
                got = exchange(s, dr=dr, dt=dt).astype(F32)
                total = got if total is None else total + got
            if self.stage == len(self.bits) + 1:
                return total
            if self.stage < len(self.bits):
                dr = self.bits[self.stage]
                at = self.left.index(dr)
                self.left.remove(dr)
                size = block << at
                stay, send = [
                    jnp.concatenate(
                        [
                            lax.slice_in_dim(total, b, b + size, axis=self.axis)
                            for b in range(side * size, total.shape[self.axis], 2 * size)
                        ],
                        axis=self.axis,
                    )
                    for side in (0, 1)
                ]
                self.sends = [send.astype(BF)]
                self.hops = [(dr, 0)]
            else:
                stay, sends = self.last(total)
                self.sends = [piece.astype(BF) for _, piece in sends]
                self.hops = [(0, dt) for dt, _ in sends]
            self.kept = lambda: stay
            self.stage += 1
            return None

        def finish(self):
            total = None
            while total is None:
                total = self.advance()
            return total

    def weight_sum(left, right, axis, reverse):
        size = width // 2

        def half(n):
            if axis == 0:
                return dot_tn(left[:, n * size : (n + 1) * size], right)
            return dot_tn(left, right[:, n * size : (n + 1) * size])

        def last(total):
            size = total.shape[1 - axis] // ways
            pieces = [
                lax.slice_in_dim(total, j * size, (j + 1) * size, axis=1 - axis)
                for j in range(ways)
            ]
            return pieces[0], [(j, pieces[j]) for j in range(1, ways)]

        return Reduction(half, axis, reverse, last)

    def after(value, reductions):
        sends = [r.sends for r in reductions]
        value, sends = lax.optimization_barrier((value, sends))
        for r, s in zip(reductions, sends):
            r.sends = s
        return value

    whole_path = chips == 4
    if whole_path:
        (
            resid_one_grad, branch_low, mixed_grad, in_grad, back_grad, inner_bias, grad_proj, vectors,
        ) = feed_forward_backward(
            own_cot, proj_low, full_proj, resid_two, output_low, params, full_back, active_slope,
            full_in, normed_low, active_low, resid_one, full_out,
        )
    else:
        out_grad = dot_nn(own_cot, turn) + dot_nt(proj_low, full_proj)
        resid_two_grad, gain_two_grad, shift_two_grad = norm_two_pull(out_grad)
        update_low = resid_two_grad.astype(BF)
        sum_back = weight_sum(active_low, update_low, 1, True)
        (inner_grad,) = gelu_pull(dot_nt(update_low, full_back))
        inner_low = inner_grad.astype(BF)
        sum_in = weight_sum(normed_low, inner_low, 0, False)
        inner_bias = jnp.sum(inner_low.astype(F32), axis=0)
        normed_grad = dot_nt(inner_low, full_in) + resid_two_grad
        resid_one_grad, gain_one_grad, shift_one_grad = norm_one_pull(normed_grad)
        branch_low = resid_one_grad.astype(BF)
        mixed_grad = dot_nt(branch_low, full_out).astype(BF)
        grad_proj = dot_tn(output_low, proj_low)
        zero = jnp.zeros((width,), F32)
        vectors = jnp.stack(
            [
                jnp.sum(branch_low.astype(F32), axis=0),
                gain_one_grad,
                shift_one_grad,
                jnp.sum(update_low.astype(F32), axis=0),
                gain_two_grad,
                shift_two_grad,
                zero,
                zero,
            ]
        )
        vectors = lax.dot_general(
            vectors, turn.astype(F32), (((1,), (1,)), ((), ())), precision=FULL_PRECISION
        )

    def heads_sum(rights, first_block, blocks, reverse):
        size = width // 2
        many = rights.shape[1] // 3 // blocks

        def half(n):
            return dot_tn(x_low[:, n * size : (n + 1) * size], rights)

        def last(total):
            stay, sends = None, []
            for b in range(blocks):
                piece = jnp.stack(
                    [total[:, (j * blocks + b) * many : (j * blocks + b + 1) * many] for j in range(3)]
                )
                if first_block + b == 0:
                    stay = piece
                else:
                    sends.append((first_block + b, piece))
            return stay, sends

        return Reduction(half, 0, reverse, last)

    inner_bias = inner_bias.reshape(ways, units_local)
    if whole_path:
        pre, head_bias, out_in, out_back, vectors, grad_proj, y_doc, y_query = (
            attention_backward_kernel(
                qkv,
                far_kv,
                mixed_grad,
                cosine,
                sine,
                col_labels,
                row_labels,
                in_grad,
                back_grad,
                vectors,
                grad_proj,
                y_low,
            )
        )
        head_bias = head_bias[:3].reshape(3, ways, heads_local)
    else:
        head_sums, head_rights = [], []
        running = [sum_back, sum_in]
        per_block = heads_local // 128
        sum_out = weight_sum(mixed, branch_low, 1, False)
        for first_block, blocks in ((0, 2), (2, 1), (3, 1)):
            for item in running:
                item.advance()
            mixed_grad = after(mixed_grad, running)
            dq, own_grads, give = attention_backward(
                first_block * per_block,
                blocks * per_block,
                qkv,
                far_kv,
                mixed_grad,
                cosine,
                sine,
                far_cosine,
                far_sine,
                *label_args,
            )
            got = exchange(give, dr=1).astype(F32)
            rights = [dq] + [
                jnp.concatenate(
                    [own_grads[i, :docs] + got[i], own_grads[i, docs:]], axis=0
                ).astype(BF)
                for i in range(2)
            ]
            head_rights.append(rights)
            head_sums.append(
                heads_sum(jnp.concatenate(rights, axis=1), first_block, blocks, first_block > 0)
            )
        out_back = sum_back.finish()
        out_in = sum_in.finish()
        pre = [jnp.concatenate([part[j] for part in head_rights], axis=1) for j in range(3)]
        head_bias = jnp.stack([jnp.sum(p.astype(F32), axis=0) for p in pre])
        head_bias = head_bias.reshape(3, ways, heads_local)
    tensor_grads = jnp.concatenate(
        [jnp.swapaxes(head_bias, 0, 1).reshape(ways, 3 * heads_local), inner_bias], axis=1
    )
    if whole_path:
        out_qkv, out_out, gx_doc, gx_query, tensor_grads = finish_kernel(
            x_low,
            full_qkv,
            pre,
            mixed,
            branch_low,
            resid_one_grad,
            tensor_grads.reshape(ways, -1, 128),
        )
        y_doc, y_query, gx_doc, gx_query, out_qkv, out_out, out_in, out_back, grad_proj = emit_kernel(
            [y_doc, y_query, gx_doc, gx_query, out_qkv, out_out, out_in, out_back, grad_proj],
            [BF, BF] + [F32] * 7,
        )
        tensor_grads = tensor_grads.reshape(-1)
    else:
        x_grad = resid_one_grad
        for j in range(3):
            x_grad = x_grad + dot_nt(pre[j], full_qkv[j])
        x_grad = dot_nt(x_grad.astype(BF), turn).astype(BF)
        gx_doc, gx_query = rows_out(x_grad)
        gx_doc, gx_query = gx_doc.astype(F32), gx_query.astype(F32)
        out_out = sum_out.finish()
        out_qkv = functools.reduce(jnp.add, [item.finish() for item in head_sums])
        for dr in [1] + chip_bits[::-1]:
            size = grad_proj.shape[0] // 2
            got = exchange(grad_proj[size:].astype(BF), dr=dr)
            grad_proj = grad_proj[:size] + got.astype(F32)
        for dt in (1, 2):
            grad_proj = grad_proj + exchange(grad_proj, dt=dt)
        for dt in (2, 1):
            tensor_grads = tensor_grads[:dt] + exchange(tensor_grads[dt:], dt=dt)
            vectors = vectors + exchange(vectors, dt=dt)
        for dr in [1] + chip_bits:
            tensor_grads = tensor_grads + exchange(tensor_grads, dr=dr)
            vectors = vectors + exchange(vectors, dr=dr)
        tensor_grads = tensor_grads[0]
    return (
        y_doc,
        y_query,
        loss_out,
        gx_doc,
        gx_query,
        out_qkv,
        tensor_grads[: 3 * heads_local].reshape(3, heads_local),
        out_out,
        vectors[0],
        vectors[1],
        vectors[2],
        out_in,
        tensor_grads[3 * heads_local :],
        out_back,
        vectors[3],
        vectors[4],
        vectors[5],
        grad_proj,
    )


def solution(mesh):
    rows = P(None, ("dp", "tensor"), None)
    in_specs = (
        rows,
        rows,
        rows,
        rows,
        P(),
        P(None, "dp"),
        P(None, "dp", "tensor"),
        P(None, "tensor"),
        P("tensor", "dp"),
        P(),
        P(),
        P(),
        P("dp", "tensor"),
        P("tensor"),
        P("tensor", "dp"),
        P(),
        P(),
        P(),
        P("dp", None),
    )
    out_specs = (
        rows,
        rows,
        P(None, ("dp", "tensor")),
        rows,
        rows,
        P(None, "dp", "tensor"),
        P(None, "tensor"),
        P("tensor", "dp"),
        P(),
        P(),
        P(),
        P("dp", "tensor"),
        P("tensor"),
        P("tensor", "dp"),
        P(),
        P(),
        P(),
        P("dp", None),
    )
    return jax.shard_map(body, mesh=mesh, in_specs=in_specs, out_specs=out_specs, check_vma=False)
```

```python
import functools

import jax
import jax.numpy as jnp
from jax import lax
from jax.experimental import pallas as pl
from jax.experimental.pallas import tpu as pltpu
from jax.sharding import PartitionSpec as P

HEAD_WIDTH = 64
QLEN = 32
FULL_PRECISION = lax.Precision.HIGHEST
TAU = 20.0
EPS = 1e-05
LOGIT_SCALE = 2.0
MASKED = -1e30
AXES = ("dp", "tensor")
MESH = pl.DeviceIdType.MESH
BF = jnp.bfloat16
F32 = jnp.float32


def layer_norm(values, gain, shift):
    center = values - jnp.mean(values, axis=-1, keepdims=True)
    spread = jnp.mean(center * center, axis=-1, keepdims=True)
    return center * lax.rsqrt(spread + EPS) * gain + shift


def normalize(values):
    return values * lax.rsqrt(jnp.sum(values * values, axis=-1, keepdims=True) + 1e-06)


def gelu_exact(values):
    return jax.nn.gelu(values, approximate=False)


def dot_nn(a, b):
    return lax.dot_general(a, b, (((1,), (0,)), ((), ())), preferred_element_type=F32)


def dot_nt(a, b):
    return lax.dot_general(a, b, (((1,), (1,)), ((), ())), preferred_element_type=F32)


def dot_tn(a, b):
    return lax.dot_general(a, b, (((0,), (0,)), ((), ())), preferred_element_type=F32)


def differing(a, b, bits):
    total = 0
    for bit in range(bits):
        x, y = (a // 2**bit) % 2, (b // 2**bit) % 2
        total = total + 2**bit * (x + y - 2 * x * y)
    return total


class Around:
    def __init__(self):
        self.rank = lax.axis_index("dp")
        self.column = lax.axis_index("tensor")
        self.core = self.rank % 2
        self.base = self.rank - self.core

    def other(self, bit):
        rank = self.rank
        return (rank + bit - 2 * bit * ((rank // bit) % 2), self.column)

    def along(self, dt):
        return (self.rank, differing(self.column, dt, 2))

    def greet(self):
        barrier = pltpu.get_barrier_semaphore()
        for dc in range(2):
            for dt in range(4):
                if dc + dt > 0:
                    pl.semaphore_signal(
                        barrier,
                        inc=1,
                        device_id=(self.base + (self.core + dc) % 2, (self.column + dt) % 4),
                        device_id_type=MESH,
                    )
        for bit in (2, 4):
            pl.semaphore_signal(
                barrier, inc=1, device_id=self.other(bit), device_id_type=MESH
            )

    def await_all(self):
        pl.semaphore_wait(pltpu.get_barrier_semaphore(), 9)

    def meet(self):
        self.greet()
        self.await_all()


def feature_block(rank, p):
    return differing(rank, 2 * (p % 4) + p // 4, 3)


class Sender:
    def __init__(self, send_sem, recv_sem):
        self.send_sem, self.recv_sem = send_sem, recv_sem
        self.sent = []

    def __call__(self, src, dst, to):
        at = len(self.sent)
        copy = pltpu.make_async_remote_copy(
            src_ref=src,
            dst_ref=dst,
            send_sem=self.send_sem.at[at],
            recv_sem=self.recv_sem.at[at],
            device_id=to,
            device_id_type=MESH,
        )
        self.sent.append(copy)
        return copy

    def drain(self):
        for copy in self.sent:
            copy.wait_send()


class RowMoves:
    def __init__(self, around, inward, docs, asked, packed, send_sem, recv_sem):
        core, column, base = around.core, around.column, around.base
        lonely = 3 * core == column
        self.copies, self.arrivals = [], []
        size, few, width = docs.shape[1], asked.shape[1], docs.shape[2]
        block = width // 8
        for n in range(2):
            q, m = (column % 2, n) if inward else (n, column // 2)
            if inward:
                mine = jnp.logical_and(lonely, column // 2 == n)
                to = (base + column // 2, 2 * n + core)
                here = jnp.logical_and(lonely, column % 2 == n)
                holder = base + column // 2
            else:
                mine = jnp.logical_and(lonely, core == n)
                to = (base + column % 2, 2 * core + n)
                here = jnp.logical_and(lonely, column // 2 == n)
                holder = around.rank
            wheres = [
                pl.ds(pl.multiple_of(feature_block(holder, p) * block, block), block)
                for p in range(8)
            ]
            for kind, (ref, many, begin) in enumerate(((docs, size, 0), (asked, few, 2 * size))):
                span = pl.ds(pl.multiple_of(begin + q * many, few), many)
                aways, locals_ = [], []
                for p in list(range(8)) + [None]:
                    if p is None:
                        rows, flat = packed.at[span, :], ref.at[m]
                    else:
                        rows = packed.at[span, pl.ds(p * block, block)]
                        flat = ref.at[m, :, wheres[p]]
                    src, dst = (flat, rows) if inward else (rows, flat)
                    aways.append(
                        pltpu.make_async_remote_copy(
                            src_ref=src,
                            dst_ref=dst,
                            send_sem=send_sem.at[n, kind],
                            recv_sem=recv_sem.at[q if inward else m, kind],
                            device_id=to,
                            device_id_type=MESH,
                        )
                    )
                    locals_.append(pltpu.make_async_copy(src, dst, send_sem.at[n, kind]))
                self.copies.append((mine, locals_, aways))
                if inward:
                    land = packed.at[pl.ds(begin + n * many, many), :]
                else:
                    land = ref.at[n]
                came = pltpu.make_async_remote_copy(
                    src_ref=land,
                    dst_ref=land,
                    send_sem=send_sem.at[n, kind],
                    recv_sem=recv_sem.at[n, kind],
                    device_id=to,
                    device_id_type=MESH,
                )
                self.arrivals.append((here, came))

    def start(self, n=None):
        for mine, locals_, aways in self.copies if n is None else self.copies[2 * n : 2 * n + 2]:

            @pl.when(mine)
            def _(locals_=locals_):
                for copy in locals_[:8]:
                    copy.start()

            @pl.when(jnp.logical_not(mine))
            def _(aways=aways):
                for copy in aways[:8]:
                    copy.start()

    def wait(self):
        for here, came in self.arrivals:

            @pl.when(jnp.logical_not(here))
            def _(came=came):
                came.wait_recv()

        for mine, locals_, aways in self.copies:

            @pl.when(mine)
            def _(locals_=locals_):
                locals_[8].wait()

            @pl.when(jnp.logical_not(mine))
            def _(aways=aways):
                aways[8].wait_send()


class WeightGather:
    slots = 31

    def __init__(
        self, around, sources, outs, feature_axis, tensor_axis, bits, send_sem, recv_sem, local_sem
    ):
        self.around, self.sources, self.outs = around, sources, outs
        self.feature_axis, self.tensor_axis, self.bits = feature_axis, tensor_axis, bits
        self.send_sem, self.recv_sem, self.local_sem = send_sem, recv_sem, local_sem
        self.all = range(len(sources))

    def place(self, j):
        return (j & 1) * 4 + (j >> 1)

    def line(self, a, j):
        index = [slice(None)] * len(self.sources[a].shape)
        size = self.sources[a].shape[self.feature_axis[a]]
        index[self.feature_axis[a]] = pl.ds(self.place(j) * size, size)
        return self.outs[a].at[tuple(index)]

    def piece(self, a, j, source, column=None):
        column = self.around.column if column is None else column
        index = [slice(None)] * len(self.sources[a].shape)
        size = self.sources[a].shape[self.feature_axis[a]]
        index[self.feature_axis[a]] = pl.ds(self.place(j) * size, size)
        size = self.sources[a].shape[self.tensor_axis[a]]
        offset = pl.multiple_of(differing(column, source, 2) * size, size)
        index[self.tensor_axis[a]] = pl.ds(offset, size)
        return self.outs[a].at[tuple(index)]

    def origin(self, kind):
        column = self.around.column
        if kind == 0:
            return column, None
        if kind <= 3:
            return column - kind, column >= kind
        return column + (kind - 3), column + (kind - 3) <= 3

    def describe(self, a, slot):
        around, column = self.around, self.around.column
        first, second = self.bits[a]
        if slot >= 27:
            j = (0, first, second, first | second)[slot - 27]
            return None, self.line(a, j), self.line(a, j | 1), around.other(1)
        if slot < 6:
            kind = slot if slot < 3 else (0 if slot == 3 else slot)
            to = column + 1 if slot < 3 else column - 1
            edge = column < 3 if slot < 3 else column > 0
            source, there = self.origin(kind)
            there = edge if there is None else jnp.logical_and(there, edge)
            src = self.sources[a] if kind == 0 else self.piece(a, 0, source)
            return there, src, self.piece(a, 0, source, to), (around.rank, to)
        kind = (slot - 6) % 7
        source, there = self.origin(kind)
        if slot < 20:
            bit = first if slot < 13 else second
            src = self.sources[a] if kind == 0 else self.piece(a, 0, source)
            return there, src, self.piece(a, bit, source), around.other(bit)
        src, dst = self.piece(a, first, source), self.piece(a, first | second, source)
        return there, src, dst, around.other(second)

    def landing(self, a, slot):
        first, second = self.bits[a]
        if slot >= 27:
            return None, self.line(a, (0, first, second, first | second)[slot - 27] | 1)
        if slot < 6:
            kind, j = (slot + 1, 0)
        else:
            kind, j = (slot - 6) % 7, (first, second, first | second)[(slot - 6) // 7]
        source, there = self.origin(kind)
        return there, self.piece(a, j, source)

    def copy(self, a, slot, src, dst, to):
        return pltpu.make_async_remote_copy(
            src_ref=src,
            dst_ref=dst,
            send_sem=self.send_sem.at[a, slot],
            recv_sem=self.recv_sem.at[a, slot],
            device_id=to,
            device_id_type=MESH,
        )

    def when(self, condition, act):
        if condition is None:
            act()
        else:
            pl.when(condition)(act)

    def start(self, a, slot):
        condition, src, dst, to = self.describe(a, slot)
        self.when(condition, lambda: self.copy(a, slot, src, dst, to).start())

    def sent(self, a, slot):
        condition, src, dst, to = self.describe(a, slot)
        self.when(condition, lambda: self.copy(a, slot, src, dst, to).wait_send())

    def arrived(self, a, slot):
        condition, dst = self.landing(a, slot)
        to = self.around.other(1)
        self.when(condition, lambda: self.copy(a, slot, dst, dst, to).wait_recv())

    def home(self, a):
        return pltpu.make_async_copy(
            self.sources[a], self.piece(a, 0, self.around.column), self.local_sem.at[a]
        )

    def begin(self):
        for a in self.all:
            for slot in (0, 3, 6, 13):
                self.start(a, slot)
        for a in self.all:
            self.home(a).start()

    def onward(self, a, kind):
        self.arrived(a, 6 + kind)
        self.start(a, 20 + kind)

    def hop(self, n):
        for a in self.all:
            for kind, slot in ((n, n - 1), (n + 3, n + 2)):
                self.arrived(a, slot)
                if n < 3:
                    self.start(a, slot + 1)
                self.start(a, 6 + kind)
                self.start(a, 13 + kind)
        for a in self.all:
            for kind in (0,) if n == 1 else (n - 1, n + 2):
                self.onward(a, kind)

    def finish(self):
        for a in self.all:
            self.home(a).wait()
            self.start(a, 27)
        for a in self.all:
            for kind in (3, 6):
                self.onward(a, kind)
            self.start(a, 28)
        for begin, slot in ((13, 29), (20, 30)):
            for a in self.all:
                for kind in range(7):
                    self.arrived(a, begin + kind)
                self.start(a, slot)
        for a in self.all:
            for slot in range(27, 31):
                self.arrived(a, slot)
            for slot in range(31):
                self.sent(a, slot)


def gathered(weight, feature_axis, tensor_axis):
    shape = list(weight.shape)
    shape[feature_axis] *= 8
    shape[tensor_axis] *= 4
    return jax.ShapeDtypeStruct(tuple(shape), weight.dtype)


def gather_kernel(
    x_doc, x_query, qkv, out, proj, b_qkv, b_in, picks, doc_cot, query_cot, ends, rates, params
):
    ways, groups = 4, 8
    quarter, width = x_doc.shape[1:]
    asked = x_query.shape[1]
    docs, queries = 2 * quarter, 2 * asked
    rows = docs + queries
    share, units = b_qkv.shape[1], b_in.shape[1]
    block = width // groups
    marks = ends.shape[0]
    count = len(params)

    def kernel(*refs):
        xd_ref, xq_ref, qkv_ref, out_ref, proj_ref, bq_ref, bi_ref, picks_ref = refs[:8]
        cd_ref, cq_ref, ends_ref, rates_ref = refs[8:12]
        param_refs = refs[12 : 12 + count]
        x_o, qkv_o, out_o, proj_o, picks_o = refs[12 + count : 17 + count]
        bq_o, bi_o, cos_o, sin_o, col_o, row_o, cd_o, cq_o, param_o = refs[17 + count : 26 + count]
        (
            bq, bi, send_sem, recv_sem, small_send, small_recv, x_send, x_recv, local_sem,
        ) = refs[26 + count :]
        around = Around()
        around.meet()
        other, along = around.other, around.along
        gather = WeightGather(
            around,
            [qkv_ref.at[0:2], qkv_ref.at[2:3], out_ref],
            [qkv_o.at[0:2], qkv_o.at[2:3], out_o],
            [1, 1, 1],
            [2, 2, 0],
            [(2, 4), (4, 2), (4, 2)],
            send_sem,
            recv_sem,
            local_sem,
        )
        moves = RowMoves(around, True, xd_ref, xq_ref, x_o, x_send, x_recv)
        send = Sender(small_send, small_recv)
        gather.begin()
        place = gather.place
        small = [send(bq_ref, bq.at[dt], along(dt)) for dt in range(1, ways)]
        small += [send(bi_ref, bi.at[dt], along(dt)) for dt in range(1, ways)]
        local = []
        flat = []
        for n, (ref, o) in enumerate(((proj_ref, proj_o), (picks_ref, picks_o))):
            local.append(pltpu.make_async_copy(ref, o.at[0], local_sem.at[3 + n]))
            flat.append(
                (
                    send(ref, o.at[place(2)], other(2)),
                    send(ref, o.at[place(4)], other(4)),
                    send(ref, o.at[place(1)], other(1)),
                    send(o.at[place(2)], o.at[place(6)], other(4)),
                    send(o.at[place(2)], o.at[place(3)], other(1)),
                    send(o.at[place(4)], o.at[place(5)], other(1)),
                    send(o.at[place(6)], o.at[place(7)], other(1)),
                )
            )
        for copy in small + local + [c for f in flat for c in f[:3]]:
            copy.start()

        def layout(first, shape, axis):
            index = lax.broadcasted_iota(jnp.int32, shape, axis) + first
            segment = jnp.zeros(shape, jnp.int32)
            begin = jnp.zeros(shape, jnp.int32)
            for n in range(marks):
                after = index >= ends_ref[n]
                segment = segment + jnp.where(after, 1, 0)
                begin = jnp.where(after, ends_ref[n], begin)
            return segment, index - begin

        segment, places = layout(around.core * docs, (docs, 1), 0)
        col_o[...] = segment
        row_o[0:1, :] = layout(around.core * docs, (1, docs), 1)[0]
        row_o[1:2, :] = layout((1 - around.core) * docs, (1, docs), 1)[0]
        lane = lax.broadcasted_iota(jnp.int32, (1, 128), 1)
        first_half = lane % HEAD_WIDTH < HEAD_WIDTH // 2
        asked_places = lax.broadcasted_iota(jnp.int32, (queries, 1), 0) % QLEN
        for begin, at in ((0, places), (docs, asked_places)):
            span = pl.ds(begin, at.shape[0])
            angle = at.astype(F32) * rates_ref[...]
            sine = jnp.sin(angle)
            cos_o[span, :] = jnp.cos(angle)
            sin_o[span, :] = jnp.where(first_half, -sine, sine)
        gather.hop(1)
        for m in range(2):
            cd_o[m] = cd_ref[m].astype(BF)
            cq_o[m] = cq_ref[m].astype(BF)
        for f in flat:
            f[0].wait_recv()
            f[3].start()
            f[4].start()
            f[1].wait_recv()
            f[5].start()
        gather.hop(2)
        moves.start()
        for p in range(groups):
            fr = pl.ds(pl.multiple_of(feature_block(around.rank, p) * block, block), block)
            for n in range(count):
                param_o[n : n + 1, p * block : (p + 1) * block] = param_refs[n][:, fr]
        bq[0] = bq_ref[...]
        bi[0] = bi_ref[...]
        gather.hop(3)
        for f in flat:
            f[3].wait_recv()
            f[6].start()
        for copy in small:
            copy.wait_recv()
        for dt in range(ways):
            bq_o[:, dt * share : (dt + 1) * share] = bq[dt]
            bi_o[:, dt * units : (dt + 1) * units] = bi[dt]
        gather.finish()
        for f in flat:
            for n in (2, 4, 5, 6):
                f[n].wait_recv()
        for copy in local:
            copy.wait()
        moves.wait()
        send.drain()

    def whole(shape):
        return pl.BlockSpec(shape, lambda: (0,) * len(shape))

    anywhere = pl.BlockSpec(memory_space=pl.ANY)
    dma = pltpu.SemaphoreType.DMA
    tables = [
        jax.ShapeDtypeStruct((3, ways * share), F32),
        jax.ShapeDtypeStruct((1, ways * units), F32),
        jax.ShapeDtypeStruct((rows, 128), F32),
        jax.ShapeDtypeStruct((rows, 128), F32),
        jax.ShapeDtypeStruct((docs, 1), jnp.int32),
        jax.ShapeDtypeStruct((2, docs), jnp.int32),
        jax.ShapeDtypeStruct(doc_cot.shape, BF),
        jax.ShapeDtypeStruct(query_cot.shape, BF),
        jax.ShapeDtypeStruct((8, width), F32),
    ]
    return pl.pallas_call(
        kernel,
        out_shape=[
            jax.ShapeDtypeStruct((rows, width), x_doc.dtype),
            gathered(qkv, 1, 2),
            gathered(out, 1, 0),
            jax.ShapeDtypeStruct((groups,) + proj.shape, proj.dtype),
            jax.ShapeDtypeStruct((groups,) + picks.shape, picks.dtype),
        ]
        + tables,
        in_specs=[anywhere] * 5
        + [whole(b_qkv.shape), whole(b_in.shape), anywhere]
        + [whole(doc_cot.shape), whole(query_cot.shape)]
        + [pl.BlockSpec(memory_space=pltpu.SMEM), whole(rates.shape)]
        + [whole((1, width))] * count,
        out_specs=[anywhere] * 5 + [whole(x.shape) for x in tables],
        scratch_shapes=[
            pltpu.VMEM((ways,) + b_qkv.shape, F32),
            pltpu.VMEM((ways,) + b_in.shape, F32),
            dma((3, WeightGather.slots)),
            dma((3, WeightGather.slots)),
            dma((20,)),
            dma((20,)),
            dma((2, 2)),
            dma((2, 2)),
            dma((5,)),
        ],
        compiler_params=pltpu.CompilerParams(
            collective_id=0, has_side_effects=True, vmem_limit_bytes=60 << 20
        ),
        name="gather_weights",
    )(
        x_doc, x_query, qkv, out, proj, b_qkv, b_in, picks, doc_cot, query_cot, ends, rates,
        *[p[None] for p in params],
    )


def turned(values):
    lane = lax.broadcasted_iota(jnp.int32, (1, 128), 1)
    ahead = pltpu.roll(values, 96, 1)
    behind = pltpu.roll(values, 32, 1)
    return jnp.where(lane % HEAD_WIDTH < HEAD_WIDTH // 2, ahead, behind)


def project_heads(x, weights, bias, cosine, sine):
    rows, width = x.shape
    columns = 256
    steps = width // columns

    def kernel(x_ref, w_ref, b_ref, c_ref, s_ref, o_ref):
        got = dot_nn(x_ref[...], w_ref[0]) + b_ref[0]
        for at in range(0, columns, 128):
            piece = got[:, at : at + 128]
            o_ref[0, :, at : at + 128] = (piece * c_ref[0] + turned(piece) * s_ref[0]).astype(BF)

    return pl.pallas_call(
        kernel,
        grid=(3, steps),
        in_specs=[
            pl.BlockSpec((rows, width), lambda j, n: (0, 0)),
            pl.BlockSpec((1, width, columns), lambda j, n: (j, 0, n)),
            pl.BlockSpec((1, 1, columns), lambda j, n: (j, 0, n)),
            pl.BlockSpec((1, rows, 128), lambda j, n: (j, 0, 0)),
            pl.BlockSpec((1, rows, 128), lambda j, n: (j, 0, 0)),
        ],
        out_specs=pl.BlockSpec((1, rows, columns), lambda j, n: (j, 0, n)),
        out_shape=jax.ShapeDtypeStruct((3, rows, width), BF),
        compiler_params=pltpu.CompilerParams(vmem_limit_bytes=40 << 20),
        name="project_heads",
    )(x, weights, bias[:, None, :], cosine, sine)


def attention_forward(qkv, far_kv, col_labels, own_labels, far_labels):
    rows, width = qkv.shape[1:]
    docs = far_kv.shape[1]
    block = 128
    asked = rows - docs

    def kernel(qkv_ref, far_ref, lc_ref, lo_ref, lf_ref, o_ref):
        lane = lax.broadcasted_iota(jnp.int32, (1, 128), 1)

        def part(start, size, keys, sames):
            q_block = qkv_ref[0, pl.ds(start, size), :]
            outs = []
            for head in range(2):
                mask = (lane // HEAD_WIDTH) == head
                q_head = jnp.where(mask, q_block, jnp.zeros_like(q_block))
                scores = [
                    jnp.where(same, dot_nt(q_head, key), MASKED)
                    for (key, _), same in zip(keys, sames)
                ]
                top = functools.reduce(
                    jnp.maximum, [jnp.max(s, axis=-1, keepdims=True) for s in scores]
                )
                powers = [jnp.exp(s - top) for s in scores]
                total = functools.reduce(
                    jnp.add, [jnp.sum(p, axis=-1, keepdims=True) for p in powers]
                )
                mixed = functools.reduce(
                    jnp.add, [dot_nn(p.astype(BF), value) for p, (_, value) in zip(powers, keys)]
                )
                outs.append(mixed * (1.0 / total))
            o_ref[pl.ds(start, size), :] = jnp.where(lane < HEAD_WIDTH, outs[0], outs[1]).astype(BF)

        doc_keys = [
            (qkv_ref[1, :docs, :], qkv_ref[2, :docs, :]),
            (far_ref[0], far_ref[1]),
        ]
        for at in range(docs // block):
            labels = lc_ref[pl.ds(at * block, block), :]
            part(at * block, block, doc_keys, [labels == lo_ref[...], labels == lf_ref[...]])
        row = lax.broadcasted_iota(jnp.int32, (asked, asked), 0) // QLEN
        col = lax.broadcasted_iota(jnp.int32, (asked, asked), 1) // QLEN
        part(docs, asked, [(qkv_ref[1, docs:, :], qkv_ref[2, docs:, :])], [row == col])

    whole = lambda shape: pl.BlockSpec(shape, lambda h: (0, 0))
    return pl.pallas_call(
        kernel,
        grid=(width // 128,),
        in_specs=[
            pl.BlockSpec((3, rows, 128), lambda h: (0, 0, h)),
            pl.BlockSpec((2, docs, 128), lambda h: (0, 0, h)),
            whole((docs, 1)),
            whole((1, docs)),
            whole((1, docs)),
        ],
        out_specs=pl.BlockSpec((rows, 128), lambda h: (0, h)),
        out_shape=jax.ShapeDtypeStruct((rows, width), BF),
        compiler_params=pltpu.CompilerParams(vmem_limit_bytes=40 << 20),
        name="attend_forward",
        cost_estimate=pl.CostEstimate(
            flops=32 * rows * 2 * docs * width,
            bytes_accessed=2 * (4 * rows + 2 * docs) * width,
            transcendentals=rows * 2 * docs * width // 64,
        ),
    )(qkv, far_kv, col_labels, own_labels, far_labels)


def attention_backward(
    first, count, qkv, far_kv, grad, cosine, sine, far_cosine, far_sine,
    col_labels, own_labels, far_labels,
):
    rows = qkv.shape[1]
    docs = far_kv.shape[1]
    width = count * 128
    block = 128
    asked = rows - docs

    def kernel(
        qkv_ref, far_ref, g_ref, c_ref, s_ref, fc_ref, fs_ref, lc_ref, lo_ref, lf_ref,
        dq_ref, own_ref, give_ref, sums_own, sums_far,
    ):
        lane = lax.broadcasted_iota(jnp.int32, (1, 128), 1)
        sums_own[...] = jnp.zeros_like(sums_own)
        sums_far[...] = jnp.zeros_like(sums_far)

        def part(start, size, keys, sames, sums):
            q_block = qkv_ref[0, pl.ds(start, size), :]
            g_block = g_ref[pl.ds(start, size), :]
            grads = []
            for head in range(2):
                mask = (lane // HEAD_WIDTH) == head
                q_head = jnp.where(mask, q_block, jnp.zeros_like(q_block))
                g_head = jnp.where(mask, g_block, jnp.zeros_like(g_block))
                scores = [
                    jnp.where(same, dot_nt(q_head, key), MASKED)
                    for (key, _), same in zip(keys, sames)
                ]
                top = functools.reduce(
                    jnp.maximum, [jnp.max(s, axis=-1, keepdims=True) for s in scores]
                )
                powers = [jnp.exp(s - top) for s in scores]
                total = functools.reduce(
                    jnp.add, [jnp.sum(p, axis=-1, keepdims=True) for p in powers]
                )
                inverse = 1.0 / total
                g_head = (g_head.astype(F32) * inverse).astype(BF)
                pulls = [dot_nt(g_head, value) for _, value in keys]
                mean = functools.reduce(
                    jnp.add,
                    [jnp.sum(p * d, axis=-1, keepdims=True) for p, d in zip(powers, pulls)],
                ) * inverse
                slopes = [(p * (d - mean)).astype(BF) for p, d in zip(powers, pulls)]
                got = functools.reduce(
                    jnp.add, [dot_nn(s, key) for s, (key, _) in zip(slopes, keys)]
                )
                grads.append(got * 0.125)
                for (ref, begin, many), s, p in zip(sums, slopes, powers):
                    ref[0, pl.ds(begin, many), :] += dot_tn(s, q_head)
                    ref[1, pl.ds(begin, many), :] += dot_tn(p.astype(BF), g_head)
            whole = jnp.where(lane < HEAD_WIDTH, grads[0], grads[1])
            at = pl.ds(start, size)
            dq_ref[at, :] = (whole * c_ref[at, :] - turned(whole) * s_ref[at, :]).astype(BF)

        doc_keys = [
            (qkv_ref[1, :docs, :], qkv_ref[2, :docs, :]),
            (far_ref[0], far_ref[1]),
        ]
        for at in range(docs // block):
            labels = lc_ref[pl.ds(at * block, block), :]
            part(
                at * block,
                block,
                doc_keys,
                [labels == lo_ref[...], labels == lf_ref[...]],
                [(sums_own, 0, docs), (sums_far, 0, docs)],
            )
        row = lax.broadcasted_iota(jnp.int32, (asked, asked), 0) // QLEN
        col = lax.broadcasted_iota(jnp.int32, (asked, asked), 1) // QLEN
        part(
            docs,
            asked,
            [(qkv_ref[1, docs:, :], qkv_ref[2, docs:, :])],
            [row == col],
            [(sums_own, docs, asked)],
        )
        own_ref[0] = sums_own[0] * c_ref[...] - turned(sums_own[0]) * s_ref[...]
        own_ref[1] = sums_own[1]
        give_ref[0] = (sums_far[0] * fc_ref[...] - turned(sums_far[0]) * fs_ref[...]).astype(BF)
        give_ref[1] = sums_far[1].astype(BF)

    whole = lambda shape: pl.BlockSpec(shape, lambda h: (0, 0))
    return pl.pallas_call(
        kernel,
        grid=(count,),
        in_specs=[
            pl.BlockSpec((3, rows, 128), lambda h: (0, 0, h + first)),
            pl.BlockSpec((2, docs, 128), lambda h: (0, 0, h + first)),
            pl.BlockSpec((rows, 128), lambda h: (0, h + first)),
            whole((rows, 128)),
            whole((rows, 128)),
            whole((docs, 128)),
            whole((docs, 128)),
            whole((docs, 1)),
            whole((1, docs)),
            whole((1, docs)),
        ],
        out_specs=[
            pl.BlockSpec((rows, 128), lambda h: (0, h)),
            pl.BlockSpec((2, rows, 128), lambda h: (0, 0, h)),
            pl.BlockSpec((2, docs, 128), lambda h: (0, 0, h)),
        ],
        out_shape=[
            jax.ShapeDtypeStruct((rows, width), BF),
            jax.ShapeDtypeStruct((2, rows, width), F32),
            jax.ShapeDtypeStruct((2, docs, width), BF),
        ],
        scratch_shapes=[pltpu.VMEM((2, rows, 128), F32), pltpu.VMEM((2, docs, 128), F32)],
        compiler_params=pltpu.CompilerParams(vmem_limit_bytes=40 << 20),
        name="attend_backward",
        cost_estimate=pl.CostEstimate(
            flops=100 * rows * 2 * docs * width,
            bytes_accessed=4 * (6 * rows + 4 * docs) * width,
            transcendentals=rows * 2 * docs * width // 64,
        ),
    )(
        qkv, far_kv, grad, cosine, sine, far_cosine, far_sine, col_labels, own_labels, far_labels
    )


def project_and_attend(
    x, weights, bias, cosine, sine, col_labels, row_labels, out, params,
    doc_cot, query_cot, up, back,
):
    rows, width = x.shape
    docs = col_labels.shape[0]
    asked = rows - docs
    pairs = width // 128
    block = 256
    columns = 256
    steps = width // columns
    assert pairs == 8

    def kernel(
        x_ref, w_ref, b_ref, c_ref, s_ref, lc_ref, lr_ref, ow_ref, par_ref,
        cd_ref, cq_ref, up_ref, back_ref,
        qkv_o, far_o, mixed_o, resid_o, norm_o, low_o, cot_o, up_o, back_o,
        held, far, qkv, mixed, out_w, resid, norm, low, load_sem, far_send, far_recv, row_send, row_recv, send_sem, recv_sem, local_sem,
    ):
        h = pl.program_id(0)

        def parts():
            around = Around()
            moves = RowMoves(around, True, cd_ref, cq_ref, cot_o, row_send, row_recv)
            gather = WeightGather(
                around,
                [up_ref, back_ref],
                [up_o, back_o],
                [0, 1],
                [1, 0],
                [(2, 4), (4, 2)],
                send_sem,
                recv_sem,
                local_sem,
            )
            return around, moves, gather

        @pl.when(h == 0)
        def _():
            loads = [pltpu.make_async_copy(w_ref.at[j], held.at[j], load_sem.at[j]) for j in range(3)]
            for j in (1, 2, 0):
                loads[j].start()
            pltpu.make_async_copy(ow_ref, out_w, load_sem.at[4]).start()
            around, _, gather = parts()
            around.meet()
            gather.begin()
            copies = []
            for j in (1, 2, 0):
                loads[j].wait()
                for n in range(steps):
                    at = pl.ds(n * columns, columns)
                    got = dot_nn(x_ref[...], held[j, :, at]) + b_ref[j : j + 1, at]
                    for m in range(columns // 128):
                        piece = got[:, m * 128 : (m + 1) * 128]
                        if j < 2:
                            piece = piece * c_ref[...] + turned(piece) * s_ref[...]
                        if j == 0:
                            piece = piece * 0.125
                        qkv[j, :, n * columns + m * 128 : n * columns + (m + 1) * 128] = piece.astype(BF)
                    if j > 0:
                        copy = pltpu.make_async_remote_copy(
                            src_ref=qkv.at[j, pl.ds(0, docs), at],
                            dst_ref=far.at[j - 1, :, at],
                            send_sem=far_send.at[j - 1, n],
                            recv_sem=far_recv.at[j - 1, n],
                            device_id=around.other(1),
                            device_id_type=MESH,
                        )
                        copy.start()
                        copies.append(copy)
            for copy in copies:
                copy.wait()
            pltpu.make_async_copy(far, far_o, load_sem.at[3]).start()
            pltpu.make_async_copy(qkv, qkv_o, load_sem.at[5]).start()

        @pl.when(h == 1)
        def _():
            parts()[2].hop(1)

        @pl.when(h == 4)
        def _():
            _, moves, gather = parts()
            gather.hop(2)
            moves.start()

        @pl.when(h == 7)
        def _():
            parts()[2].hop(3)

        lane = lax.broadcasted_iota(jnp.int32, (1, 128), 1)
        pair = pl.ds(pl.multiple_of(h * 128, 128), 128)

        def part(start, size, keys, sames):
            q_block = qkv[0, pl.ds(start, size), pair]
            outs = []
            for head in range(2):
                mask = (lane // HEAD_WIDTH) == head
                q_head = jnp.where(mask, q_block, jnp.zeros_like(q_block))
                scores = [
                    jnp.where(same, dot_nt(q_head, key), MASKED)
                    for (key, _), same in zip(keys, sames)
                ]
                top = functools.reduce(
                    jnp.maximum, [jnp.max(s, axis=-1, keepdims=True) for s in scores]
                )
                powers = [jnp.exp(s - top) for s in scores]
                total = functools.reduce(
                    jnp.add, [jnp.sum(p, axis=-1, keepdims=True) for p in powers]
                )
                blend = functools.reduce(
                    jnp.add, [dot_nn(p.astype(BF), value) for p, (_, value) in zip(powers, keys)]
                )
                outs.append(blend * (1.0 / total))
            both = jnp.where(lane < HEAD_WIDTH, outs[0], outs[1]).astype(BF)
            mixed[pl.ds(start, size), pair] = both

        doc_keys = [
            (qkv[1, :docs, pair], qkv[2, :docs, pair]),
            (far[0, :, pair], far[1, :, pair]),
        ]
        for at in range(docs // block):
            labels = lc_ref[pl.ds(at * block, block), :]
            part(at * block, block, doc_keys, [labels == lr_ref[0:1, :], labels == lr_ref[1:2, :]])
        row = lax.broadcasted_iota(jnp.int32, (asked, asked), 0) // QLEN
        col = lax.broadcasted_iota(jnp.int32, (asked, asked), 1) // QLEN
        part(docs, asked, [(qkv[1, docs:, pair], qkv[2, docs:, pair])], [row == col])

        @pl.when(h == pairs - 1)
        def _():
            _, moves, gather = parts()
            pltpu.make_async_copy(ow_ref, out_w, load_sem.at[4]).wait()
            for at in range(0, rows, rows // 4):
                span = pl.ds(at, rows // 4)
                total = x_ref[span, :].astype(F32) + dot_nn(mixed[span, :], out_w[...])
                total = total + par_ref[0:1, :]
                resid[span, :] = total
                total = layer_norm(total, par_ref[1:2, :], par_ref[2:3, :])
                norm[span, :] = total
                low[span, :] = total.astype(BF)
            stores = [
                pltpu.make_async_copy(src, dst, load_sem.at[6 + n])
                for n, (src, dst) in enumerate(
                    ((mixed, mixed_o), (resid, resid_o), (norm, norm_o), (low, low_o))
                )
            ]
            for store in stores:
                store.start()
            gather.finish()
            moves.wait()
            pltpu.make_async_copy(far, far_o, load_sem.at[3]).wait()
            pltpu.make_async_copy(qkv, qkv_o, load_sem.at[5]).wait()
            for store in stores:
                store.wait()

    def whole(shape):
        return pl.BlockSpec(shape, lambda h: (0,) * len(shape))

    anywhere = pl.BlockSpec(memory_space=pl.ANY)
    dma = pltpu.SemaphoreType.DMA
    return pl.pallas_call(
        kernel,
        grid=(pairs,),
        in_specs=[
            whole((rows, width)),
            anywhere,
            whole((3, width)),
            whole((rows, 128)),
            whole((rows, 128)),
            whole((docs, 1)),
            whole((2, docs)),
            anywhere,
            whole(params.shape),
        ]
        + [anywhere] * 4,
        out_specs=[anywhere] * 9,
        out_shape=[
            jax.ShapeDtypeStruct((3, rows, width), BF),
            jax.ShapeDtypeStruct((2, docs, width), BF),
            jax.ShapeDtypeStruct((rows, width), BF),
            jax.ShapeDtypeStruct((rows, width), F32),
            jax.ShapeDtypeStruct((rows, width), F32),
            jax.ShapeDtypeStruct((rows, width), BF),
            jax.ShapeDtypeStruct((rows, width), doc_cot.dtype),
            gathered(up, 0, 1),
            gathered(back, 1, 0),
        ],
        scratch_shapes=[
            pltpu.VMEM((3, width, width), BF),
            pltpu.VMEM((2, docs, width), BF),
            pltpu.VMEM((3, rows, width), BF),
            pltpu.VMEM((rows, width), BF),
            pltpu.VMEM((width, width), BF),
            pltpu.VMEM((rows, width), F32),
            pltpu.VMEM((rows, width), F32),
            pltpu.VMEM((rows, width), BF),
            dma((10,)),
            dma((2, steps)),
            dma((2, steps)),
            dma((2, 2)),
            dma((2, 2)),
            dma((2, WeightGather.slots)),
            dma((2, WeightGather.slots)),
            dma((2,)),
        ],
        compiler_params=pltpu.CompilerParams(
            vmem_limit_bytes=60 << 20, collective_id=4, has_side_effects=True
        ),
        name="project_and_attend",
        cost_estimate=pl.CostEstimate(
            flops=64 * rows * 2 * docs * width,
            bytes_accessed=2 * (4 * rows + 2 * docs) * width,
            transcendentals=rows * 2 * docs * width // 64,
        ),
    )(
        x, weights, bias, cosine, sine, col_labels, row_labels, out, params,
        doc_cot, query_cot, up, back,
    )


def feed_forward(hidden, up, bias, back, normed, params, proj):
    rows, width = hidden.shape
    units = up.shape[1]
    columns, piece = 1024, 1024

    def kernel(
        h_ref, u_ref, b_ref, w_ref, n_ref, par_ref, p_ref, a_ref, d_ref, o_ref, y_ref, q_ref
    ):
        @pl.when(pl.program_id(0) == 0)
        def _():
            o_ref[...] = jnp.zeros_like(o_ref)

        for at in range(0, columns, piece):
            z = dot_nn(h_ref[...], u_ref[:, at : at + piece]) + b_ref[:, at : at + piece]
            bell = jnp.exp(-0.5 * z * z)
            t = 1.0 / (1.0 + 0.23164189 * jnp.abs(z))
            tail = 0.5 * t * (
                0.254829592
                + t * (-0.284496736 + t * (1.421413741 + t * (-1.453152027 + t * 1.061405429)))
            ) * bell
            below = jnp.where(z < 0.0, tail, 1.0 - tail)
            low = (z * below).astype(BF)
            a_ref[:, at : at + piece] = low
            d_ref[:, at : at + piece] = (below + z * (bell * 0.3989422804014327)).astype(BF)
            o_ref[...] += dot_nn(low, w_ref[at : at + piece, :])

        @pl.when(pl.program_id(0) == units // columns - 1)
        def _():
            for at in range(0, rows, rows // 4):
                span = pl.ds(at, rows // 4)
                total = n_ref[span, :] + o_ref[span, :] + par_ref[3:4, :]
                o_ref[span, :] = total
                low = layer_norm(total, par_ref[4:5, :], par_ref[5:6, :]).astype(BF)
                y_ref[span, :] = low
                q_ref[span, :] = dot_nn(low, p_ref[...])

    return pl.pallas_call(
        kernel,
        grid=(units // columns,),
        in_specs=[
            pl.BlockSpec((rows, width), lambda n: (0, 0)),
            pl.BlockSpec((width, columns), lambda n: (0, n)),
            pl.BlockSpec((1, columns), lambda n: (0, n)),
            pl.BlockSpec((columns, width), lambda n: (n, 0)),
            pl.BlockSpec((rows, width), lambda n: (0, 0)),
            pl.BlockSpec(params.shape, lambda n: (0, 0)),
            pl.BlockSpec(proj.shape, lambda n: (0, 0)),
        ],
        out_specs=[
            pl.BlockSpec((rows, columns), lambda n: (0, n)),
            pl.BlockSpec((rows, columns), lambda n: (0, n)),
            pl.BlockSpec((rows, width), lambda n: (0, 0)),
            pl.BlockSpec((rows, width), lambda n: (0, 0)),
            pl.BlockSpec((rows, proj.shape[1]), lambda n: (0, 0)),
        ],
        out_shape=[
            jax.ShapeDtypeStruct((rows, units), BF),
            jax.ShapeDtypeStruct((rows, units), BF),
            jax.ShapeDtypeStruct((rows, width), F32),
            jax.ShapeDtypeStruct((rows, width), BF),
            jax.ShapeDtypeStruct((rows, proj.shape[1]), F32),
        ],
        compiler_params=pltpu.CompilerParams(vmem_limit_bytes=60 << 20),
        name="feed_forward",
    )(hidden, up, bias, back, normed, params, proj)


def norm_backward(values, gain, grad):
    center = values - jnp.mean(values, axis=-1, keepdims=True)
    rate = lax.rsqrt(jnp.mean(center * center, axis=-1, keepdims=True) + EPS)
    unit = center * rate
    inner = grad * gain
    pull = inner - jnp.mean(inner, axis=-1, keepdims=True)
    pull = pull - unit * jnp.mean(inner * unit, axis=-1, keepdims=True)
    return (
        pull * rate,
        jnp.sum(grad * unit, axis=0, keepdims=True),
        jnp.sum(grad, axis=0, keepdims=True),
    )


def feed_forward_backward(
    cot, proj_low, proj, resid_two, output_low, params, back, slope, up, hidden, active,
    resid_one, out,
):
    rows, width = cot.shape
    units = up.shape[1]
    columns = 512
    steps = units // columns
    piece = rows // 4

    def kernel(
        c_ref, pl_ref, p_ref, r2_ref, y_ref, par_ref, w_ref, d_ref, u_ref, h_ref, a_ref,
        r1_ref, out_ref,
        one_ref, low_ref, mix_ref, du_ref, dw_ref, db_ref, dp_ref, vec_ref,
        two, g, total, r1, out_w, sem,
    ):
        step = pl.program_id(0)

        @pl.when(step == 0)
        def _():
            pltpu.make_async_copy(r1_ref, r1, sem.at[0]).start()
            pltpu.make_async_copy(out_ref, out_w, sem.at[1]).start()
            total[...] = jnp.zeros_like(total)
            vec_ref[...] = jnp.zeros_like(vec_ref)
            for at in range(0, rows, piece):
                span = pl.ds(at, piece)
                grad = c_ref[span, :].astype(F32) + dot_nt(pl_ref[span, :], p_ref[...])
                pull, gain, shift = norm_backward(r2_ref[span, :], par_ref[4:5, :], grad)
                two[span, :] = pull
                low = pull.astype(BF)
                g[span, :] = low
                vec_ref[3:4, :] += jnp.sum(low.astype(F32), axis=0, keepdims=True)
                vec_ref[4:5, :] += gain
                vec_ref[5:6, :] += shift
            dp_ref[...] = dot_tn(y_ref[...], pl_ref[...])

        dw_ref[...] = dot_tn(a_ref[...], g[...]).astype(BF)
        low = (dot_nt(g[...], w_ref[...]) * d_ref[...].astype(F32)).astype(BF)
        db_ref[...] = jnp.sum(low.astype(F32), axis=0, keepdims=True)
        total[...] += dot_nt(low, u_ref[...])
        du_ref[...] = dot_tn(h_ref[...], low).astype(BF)

        @pl.when(step == steps - 1)
        def _():
            pltpu.make_async_copy(r1_ref, r1, sem.at[0]).wait()
            pltpu.make_async_copy(out_ref, out_w, sem.at[1]).wait()
            for at in range(0, rows, piece):
                span = pl.ds(at, piece)
                grad = total[span, :] + two[span, :]
                pull, gain, shift = norm_backward(r1[span, :], par_ref[1:2, :], grad)
                one_ref[span, :] = pull
                low = pull.astype(BF)
                low_ref[span, :] = low
                vec_ref[0:1, :] += jnp.sum(low.astype(F32), axis=0, keepdims=True)
                vec_ref[1:2, :] += gain
                vec_ref[2:3, :] += shift
                mix_ref[span, :] = dot_nt(low, out_w[...]).astype(BF)

    def whole(shape):
        return pl.BlockSpec(shape, lambda n: (0,) * len(shape))

    anywhere = pl.BlockSpec(memory_space=pl.ANY)
    vmem = pltpu.VMEM
    return pl.pallas_call(
        kernel,
        grid=(steps,),
        in_specs=[
            whole((rows, width)),
            whole(proj_low.shape),
            whole(proj.shape),
            whole((rows, width)),
            whole((rows, width)),
            whole(params.shape),
            pl.BlockSpec((columns, width), lambda n: (n, 0)),
            pl.BlockSpec((rows, columns), lambda n: (0, n)),
            pl.BlockSpec((width, columns), lambda n: (0, n)),
            whole((rows, width)),
            pl.BlockSpec((rows, columns), lambda n: (0, n)),
            anywhere,
            anywhere,
        ],
        out_specs=[
            whole((rows, width)),
            whole((rows, width)),
            whole((rows, width)),
            pl.BlockSpec((width, columns), lambda n: (0, n)),
            pl.BlockSpec((columns, width), lambda n: (n, 0)),
            pl.BlockSpec((1, columns), lambda n: (0, n)),
            whole(proj.shape),
            whole((8, width)),
        ],
        out_shape=[
            jax.ShapeDtypeStruct((rows, width), F32),
            jax.ShapeDtypeStruct((rows, width), BF),
            jax.ShapeDtypeStruct((rows, width), BF),
            jax.ShapeDtypeStruct((width, units), BF),
            jax.ShapeDtypeStruct((units, width), BF),
            jax.ShapeDtypeStruct((1, units), F32),
            jax.ShapeDtypeStruct(proj.shape, F32),
            jax.ShapeDtypeStruct((8, width), F32),
        ],
        scratch_shapes=[
            vmem((rows, width), F32),
            vmem((rows, width), BF),
            vmem((rows, width), F32),
            vmem((rows, width), F32),
            vmem((width, width), BF),
            pltpu.SemaphoreType.DMA((2,)),
        ],
        compiler_params=pltpu.CompilerParams(vmem_limit_bytes=60 << 20),
        name="feed_forward_backward",
    )(
        cot, proj_low, proj, resid_two, output_low, params, back, slope, up, hidden, active,
        resid_one, out,
    )


def emit_kernel(arrays, dtypes):
    def kernel(*refs):
        for src, dst in zip(refs[: len(arrays)], refs[len(arrays) :]):
            dst[...] = src[...].astype(dst.dtype)

    def whole(x):
        return pl.BlockSpec(x.shape, lambda: (0,) * len(x.shape))

    return pl.pallas_call(
        kernel,
        in_specs=[whole(x) for x in arrays],
        out_specs=[whole(x) for x in arrays],
        out_shape=[jax.ShapeDtypeStruct(x.shape, t) for x, t in zip(arrays, dtypes)],
        compiler_params=pltpu.CompilerParams(vmem_limit_bytes=60 << 20),
        name="emit",
    )(*arrays)


def loss_kernel(projection, labels, log_counts, picks):
    rows, columns = projection.shape
    docs = labels.shape[0]
    own = rows - docs
    tokens = 16 * own
    units, segments = 8, 4
    chunk = 64

    def kernel(
        p_ref, lab_ref, cnt_ref, pick_ref,
        grad_ref, loss_ref,
        asked_all, weight, sums, sums_all, coef_all, slope, part, part_low, got, tile, tile_got,
        send_sem, recv_sem, tile_send, tile_recv,
    ):
        around = Around()
        rank, column, core, base = around.rank, around.column, around.core, around.base
        chip, side = rank // 2, column % 2
        mine = (chip * 2 + side) * 2 + core
        unit = chip * 2 + side

        def flip(value, bit, on):
            return value + bit - 2 * bit * ((value // bit) % 2) if on else value

        def peer(i):
            to = flip(flip(flip(rank, 1, i & 1), 2, i & 4), 4, i & 8)
            return (to, flip(column, 1, i & 2))

        def index_of(i):
            to, z = peer(i)
            return ((to // 2) * 2 + z % 2) * 2 + to % 2

        barrier = pltpu.get_barrier_semaphore()
        peers = [peer(i) for i in range(1, 16)]
        for dt in (2, 3):
            for dc in range(2):
                away, z = around.along(dt)
                peers.append((flip(rank, 1, dc), z))
        for to in peers:
            pl.semaphore_signal(barrier, inc=1, device_id=to, device_id_type=MESH)
        pl.semaphore_wait(barrier, len(peers))

        values = p_ref[...]
        rate = lax.rsqrt(jnp.sum(values * values, axis=-1, keepdims=True) + 1e-06)
        unit_wide = values * rate
        unit_low = unit_wide.astype(BF)
        own_at = pl.ds(pl.multiple_of(mine * own, own), own)
        asked_all[own_at, :] = unit_low[docs:]

        def all_to_all(kind, src, dst):
            copies = []
            for i in range(1, 16):
                copy = pltpu.make_async_remote_copy(
                    src_ref=src(i),
                    dst_ref=dst(i),
                    send_sem=send_sem.at[kind, i],
                    recv_sem=recv_sem.at[kind, i],
                    device_id=peer(i),
                    device_id_type=MESH,
                )
                copy.start()
                copies.append(copy)
            return copies

        first = all_to_all(0, lambda i: asked_all.at[own_at, :], lambda i: asked_all.at[own_at, :])
        doc_low = unit_low[:docs]
        seg_of = lab_ref[...]
        for copy in first:
            copy.wait_recv()
        queries = asked_all[...]
        sums[...] = jnp.zeros_like(sums)
        for at in range(0, docs, chunk):
            cosines = dot_nt(doc_low[at : at + chunk], queries)
            power = jnp.exp(TAU * (cosines - 1.0))
            weight[at : at + chunk, :] = power
            for s in range(segments):
                chosen = seg_of[at : at + chunk] == s
                sums[s : s + 1, :] += jnp.sum(
                    jnp.where(chosen, power, 0.0), axis=0, keepdims=True
                )
        second = all_to_all(1, lambda i: sums, lambda i: sums_all.at[mine])
        sums_all[mine] = sums[...]
        for copy in second:
            copy.wait_recv()
        row = lax.broadcasted_iota(jnp.int32, (8, tokens), 0)
        lane = lax.broadcasted_iota(jnp.int32, (8, tokens), 1)
        valid = row < segments
        totals, logits = [], []
        for n in range(units):
            total = jnp.where(valid, sums_all[2 * n] + sums_all[2 * n + 1], 1.0)
            best = (jnp.log(total) - cnt_ref[8 * n : 8 * n + 8, :]) / TAU + 1.0
            for step in (1, 2, 4, 8, 16):
                other = jnp.where(
                    (lane // step) % 2 == 1,
                    pltpu.roll(best, step, 1),
                    pltpu.roll(best, tokens - step, 1),
                )
                best = best + other
            totals.append(total)
            logits.append(jnp.where(valid, LOGIT_SCALE * best, MASKED))
        peak = functools.reduce(
            jnp.maximum, [jnp.max(x, axis=0, keepdims=True) for x in logits]
        )
        powers = [jnp.exp(x - peak) for x in logits]
        mass = functools.reduce(jnp.add, [jnp.sum(x, axis=0, keepdims=True) for x in powers])
        picked = jnp.zeros_like(peak)
        for n in range(units):
            hit = jnp.logical_and(valid, pick_ref[...] == n * segments + row)
            picked = picked + jnp.sum(jnp.where(hit, logits[n], 0.0), axis=0, keepdims=True)
            slope_n = LOGIT_SCALE * (powers[n] / mass - jnp.where(hit, 1.0, 0.0))
            coef_all[n] = slope_n / totals[n]
        losses = peak + jnp.log(mass) - picked
        tiles = []
        for q in range(2):
            at = mine * own + q * QLEN
            value = jnp.sum(
                jnp.where(lane[:1] == at, losses, 0.0), axis=1, keepdims=True
            )
            tile[q, 0] = jnp.broadcast_to(value, (8, 128))
            tile[q, 1] = jnp.zeros((8, 128), F32)
        lonely = 3 * core == column
        for q in range(2):
            here = jnp.logical_and(lonely, core == q)
            slot = column // 2
            away = pltpu.make_async_remote_copy(
                src_ref=tile.at[q],
                dst_ref=tile_got.at[slot],
                send_sem=tile_send.at[q],
                recv_sem=tile_recv.at[slot],
                device_id=(base + column % 2, 2 * core + q),
                device_id_type=MESH,
            )
            tiles.append((here, away))

            @pl.when(here)
            def _(q=q):
                tile_got[slot] = tile[q]

            @pl.when(jnp.logical_not(here))
            def _(away=away):
                away.start()

        coef = coef_all[unit]
        doc_grads = []
        part[...] = jnp.zeros_like(part)
        for at in range(0, docs, chunk):
            spread = jnp.zeros((chunk, tokens), F32)
            for s in range(segments):
                chosen = seg_of[at : at + chunk] == s
                spread = jnp.where(chosen, coef[s : s + 1, :], spread)
            low = (weight[at : at + chunk, :] * spread).astype(BF)
            slope[at : at + chunk, :] = low
            doc_grads.append(dot_nn(low, queries))
        part[...] = dot_tn(slope[...], doc_low)
        part_low[...] = part[...].astype(BF)

        def theirs(i):
            return part_low.at[pl.ds(pl.multiple_of(index_of(i) * own, own), own), :]

        third = all_to_all(2, theirs, lambda i: got.at[i])

        def pull(grad, begin, size):
            v, r = unit_wide[begin : begin + size], rate[begin : begin + size]
            inner = jnp.sum(v * grad, axis=-1, keepdims=True)
            return ((grad - v * inner) * r).astype(BF)

        for n, at in enumerate(range(0, docs, chunk)):
            grad_ref[at : at + chunk, :] = pull(doc_grads[n], at, chunk)
        total = part[own_at, :]
        for copy in third:
            copy.wait_recv()
        for i in range(1, 16):
            total = total + got[i].astype(F32)
        grad_ref[docs:, :] = pull(total, docs, own)
        for n in range(2):
            here = jnp.logical_and(lonely, column // 2 == n)
            came = pltpu.make_async_remote_copy(
                src_ref=tile.at[n],
                dst_ref=tile_got.at[n],
                send_sem=tile_send.at[n],
                recv_sem=tile_recv.at[n],
                device_id=peer(1),
                device_id_type=MESH,
            )

            @pl.when(jnp.logical_not(here))
            def _(came=came):
                came.wait_recv()

        loss_ref[...] = tile_got[:, 0]
        for here, away in tiles:

            @pl.when(jnp.logical_not(here))
            def _(away=away):
                away.wait_send()

        for copy in first + second + third:
            copy.wait_send()

    def whole(shape):
        return pl.BlockSpec(shape, lambda: (0,) * len(shape))

    vmem = pltpu.VMEM
    dma = pltpu.SemaphoreType.DMA
    return pl.pallas_call(
        kernel,
        in_specs=[
            whole(projection.shape),
            whole(labels.shape),
            whole(log_counts.shape),
            whole(picks.shape),
        ],
        out_specs=[whole((rows, columns)), whole((2, 8, 128))],
        out_shape=[
            jax.ShapeDtypeStruct((rows, columns), BF),
            jax.ShapeDtypeStruct((2, 8, 128), F32),
        ],
        scratch_shapes=[
            vmem((tokens, columns), BF),
            vmem((docs, tokens), F32),
            vmem((8, tokens), F32),
            vmem((16, 8, tokens), F32),
            vmem((units, 8, tokens), F32),
            vmem((docs, tokens), BF),
            vmem((tokens, columns), F32),
            vmem((tokens, columns), BF),
            vmem((16, own, columns), BF),
            vmem((2, 2, 8, 128), F32),
            vmem((2, 2, 8, 128), F32),
            dma((3, 16)),
            dma((3, 16)),
            dma((2,)),
            dma((2,)),
        ],
        compiler_params=pltpu.CompilerParams(
            collective_id=5, has_side_effects=True, vmem_limit_bytes=60 << 20
        ),
        name="loss",
        cost_estimate=pl.CostEstimate(
            flops=100 * docs * tokens * columns,
            bytes_accessed=8 * rows * columns,
            transcendentals=docs * tokens,
        ),
    )(projection, labels, log_counts, picks)


class MatrixSum:
    def __init__(
        self, around, send, axis, across, own, got, next_, near, far, home, local_sems,
        away=None, extras=(),
    ):
        self.axis, self.own, self.got, self.next, self.near = axis, own, got, next_, near
        self.block = own.shape[axis] // 4
        first, second = (2, 4) if across else (4, 2)
        self.gone, self.later = ((1, 3), 2) if across else ((2, 3), 1)
        self.cores = [send(src, dst, around.other(1)) for src, dst in far]
        self.loads = [
            pltpu.make_async_copy(src, dst, sem) for (src, dst), sem in zip(home, local_sems)
        ]
        self.firsts = [
            send(self.at(own, n), self.at(next_, slot), around.other(first))
            for slot, n in enumerate(self.gone)
        ]
        self.second = send(self.at(own, self.later), near, around.other(second))
        self.extras = extras
        self.away = None
        if away is not None:
            self.away = send(self.at(own, 0), away[1], around.along(away[0]))

    def at(self, ref, n):
        span = pl.ds(n * self.block, self.block)
        return ref.at[span, :] if self.axis == 0 else ref.at[:, span]

    def begin(self):
        for copy in self.cores + self.loads:
            copy.start()

    def add(self, n, ref, m):
        rows = self.block if self.axis == 0 else self.own.shape[0]
        step = 16 if self.axis == 0 else 128
        block = self.block

        @pl.loop(0, rows // step)
        def _(k):
            if self.axis == 0:
                to = (pl.ds(pl.multiple_of(n * block + k * step, step), step), slice(None))
                fr = (pl.ds(pl.multiple_of(m * block + k * step, step), step), slice(None))
            else:
                at = pl.ds(pl.multiple_of(k * step, step), step)
                to, fr = (at, pl.ds(n * block, block)), (at, pl.ds(m * block, block))
            self.own[to] = self.own[to] + ref[fr]

    def first_axis(self):
        for load in self.loads:
            load.wait()
        for copy in self.cores:
            copy.wait_recv()
        for n, copy in zip(self.gone, self.firsts):
            self.add(n, self.got, n)
            copy.start()
        for n in (self.later, 0):
            self.add(n, self.got, n)

    def second_axis(self):
        for copy in self.firsts:
            copy.wait_recv()
        self.add(self.later, self.next, 1)
        self.second.start()
        self.add(0, self.next, 0)

    def tensor(self):
        self.second.wait_recv()
        self.add(0, self.near, 0)
        for buffer, copy in self.extras:
            copy.wait_recv()
            self.add(0, buffer, 0)
        if self.away is not None:
            self.away.start()


class SmallSum:
    def __init__(self, around, send, got, run, bits=(1, 4, 2), tensor=(1, 2)):
        self.got, self.run = got, run
        tos = [around.other(bit) for bit in bits] + [around.along(dt) for dt in tensor]
        self.copies = [send(run.at[n], got.at[n], to) for n, to in enumerate(tos)]

    def begin(self):
        self.copies[0].start()

    def hop(self, n):
        self.copies[n].wait_recv()
        self.run[n + 1] = self.run[n] + self.got[n]
        if n + 1 < len(self.copies):
            self.copies[n + 1].start()


class ProjSum:
    def __init__(self, around, send, ref, run, got):
        self.ref, self.run, self.got = ref, run, got
        rows = ref.shape[0]
        self.half = [rows // 2, rows // 4, rows // 8]
        starts = [0, rows // 2, 3 * rows // 4]
        self.starts = starts
        self.copies = [
            send(ref.at[self.half[0] :, :], got.at[pl.ds(starts[0], self.half[0]), :], around.other(1))
        ]
        for n, bit in ((1, 4), (2, 2)):
            self.copies.append(
                send(
                    run.at[pl.ds(self.half[n], self.half[n]), :],
                    got.at[pl.ds(starts[n], self.half[n]), :],
                    around.other(bit),
                )
            )
        last = self.half[2]
        self.last = last
        base = rows
        for n, dt in ((0, 1), (1, 2)):
            self.copies.append(
                send(
                    run.at[pl.ds(rows // 2 + n * last, last), :],
                    got.at[pl.ds(base + n * last, last), :],
                    around.along(dt),
                )
            )

    def begin(self):
        self.copies[0].start()

    def hop(self, n):
        self.copies[n].wait_recv()
        rows = self.ref.shape[0]
        last = self.last
        if n < 3:
            size = self.half[n]
            old = self.ref if n == 0 else self.run
            total = old[:size, :] + self.got[pl.ds(self.starts[n], size), :]
            if n < 2:
                self.run[:size, :] = total
            else:
                self.run[pl.ds(rows // 2, last), :] = total
        else:
            at = rows // 2 + (n - 3) * last
            got = self.got[pl.ds(rows + (n - 3) * last, last), :]
            self.run[pl.ds(at + last, last), :] = self.run[pl.ds(at, last), :] + got
        if n + 1 < len(self.copies):
            self.copies[n + 1].start()

    def result(self):
        return self.run[pl.ds(self.ref.shape[0] // 2 + 2 * self.last, self.last), :]


def finish_kernel(x, weights, pre, mixed, branch, resid, head_bias, inner_bias):
    ways = 4
    rows, width = x.shape
    half, block = width // 2, width // 8
    share = width // ways
    docs = rows // 9 * 8
    quarter, asked = docs // 2, (rows - docs) // 2
    part = 3 * share
    units = inner_bias.shape[1] // ways
    lines = 16
    assert (3 * share + units) // 128 <= lines

    def kernel(
        x_ref, w_ref, p_ref, m_ref, g_ref, r_ref, hb_ref, ib_ref,
        qkv_o, out_o, doc_o, ask_o, ten_o,
        xs, ws, ps, ms, gs, rs, low, qf, qa, q0, q1, q2, q3, of, oa, o0, o1, o2, o3,
        t_got, t_run, tz, send_sem, recv_sem, local_sem, row_send, row_recv,
    ):
        around = Around()
        around.greet()
        loads = {}
        for n, (name, src, dst) in enumerate(
            [("p", p_ref, ps), ("r", r_ref, rs)]
            + [(j, w_ref.at[j], ws.at[j]) for j in range(3)]
            + [("x", x_ref, xs), ("m", m_ref, ms), ("g", g_ref, gs)]
        ):
            loads[name] = pltpu.make_async_copy(src, dst, local_sem.at[n])
            loads[name].start()
        send = Sender(send_sem, recv_sem)
        small = SmallSum(around, send, t_got, t_run, tensor=())
        spread = [send(t_run.at[3, dt], tz.at[dt - 1], around.along(dt)) for dt in range(1, ways)]
        heads, feats = [None] * ways, [None] * ways
        for n in (3, 2, 1, 0):
            step = {3: (1, 1), 2: (2, 2), 1: (1, 0), 0: None}[n]
            heads[n] = MatrixSum(
                around, send, 0, n % 2 == 0, qa.at[n], q0.at[n], q1.at[n], q2.at[n],
                [(qf.at[n], q0.at[n])], [], [],
                None if step is None else (step[0], q3.at[step[1]]),
                [(q3.at[1], heads[3].away)] if n == 2 else [],
            )
            feats[n] = MatrixSum(
                around, send, 1, n % 2 == 0, oa.at[n], o0.at[n], o1.at[n], o2.at[n],
                [(of.at[n], o0.at[n])], [], [],
                None if step is None else (step[0], o3.at[step[1]]),
                [(o3.at[1], feats[3].away)] if n == 2 else [],
            )
        names = [("h", 3), ("h", 2), ("f", 3), ("f", 2), ("h", 1), ("h", 0), ("f", 1), ("f", 0)]
        items = [(heads if kind == "h" else feats)[n] for kind, n in names]

        def compute(k):
            kind, n = names[k]
            at = pl.ds(n * share, share)
            for side, to in ((1, qf if kind == "h" else of), (0, qa if kind == "h" else oa)):
                span = pl.ds(side * half, half)
                if kind == "h":
                    for j in range(3):
                        to[n, :, j * share : (j + 1) * share] = dot_tn(
                            xs[:, span], ps[j, :, at]
                        ).astype(BF)
                else:
                    to[n] = dot_tn(ms[:, at], gs[:, span]).astype(BF)
                if side == 1:
                    items[k].begin()

        loads["p"].wait()
        loads["r"].wait()
        for j in range(3):
            loads[j].wait()
        t_run[0] = jnp.zeros((ways, lines, 128), F32)
        for dt in range(ways):
            for j in range(3):
                for m in range(share // 128):
                    fr = dt * share + m * 128
                    row = j * (share // 128) + m
                    t_run[0, dt, row : row + 1, :] = hb_ref[j : j + 1, fr : fr + 128]
            for m in range(units // 128):
                fr = dt * units + m * 128
                row = 3 * share // 128 + m
                t_run[0, dt, row : row + 1, :] = ib_ref[:, fr : fr + 128]

        for at in range(0, width, share):
            total = rs[:, at : at + share]
            for j in range(3):
                total = total + dot_nt(ps[j], ws[j, at : at + share, :])
            low[:, at : at + share] = total.astype(BF)
        around.await_all()
        home = RowMoves(around, False, doc_o, ask_o, low, row_send, row_recv)
        home.start()
        small.begin()
        for name in ("x", "m", "g"):
            loads[name].wait()
        compute(0)
        compute(1)
        for n in range(0, len(items) + 4, 2):
            if 0 < n < 8:
                small.hop(n // 2 - 1)
            if n == 6:
                for copy in spread:
                    copy.start()
            for item in items[n - 2 : n] if n >= 2 else []:
                item.second_axis()
            for item in items[n : n + 2]:
                item.first_axis()
            for k in (n + 2, n + 3):
                if k < len(items):
                    compute(k)
            for m in (n - 4, n - 3):
                if 0 <= m < len(items):
                    items[m].tensor()

        home.wait()
        for copy in spread:
            copy.wait_recv()
        ten_o[...] = t_run[3, 0] + tz[0] + tz[1] + tz[2]
        for group in (heads, feats):
            group[1].away.wait_recv()
            group[2].away.wait_recv()
        for j in range(3):
            at = pl.ds(j * share, share)
            total = qa[0, :block, at].astype(F32) + q3[0, :, at].astype(F32)
            qkv_o[j] = total + q3[2, :, at].astype(F32)
        total = oa[0, :, :block].astype(F32) + o3[0].astype(F32)
        out_o[...] = total + o3[2].astype(F32)
        send.drain()

    def whole(x):
        return pl.BlockSpec(x.shape, lambda: (0,) * len(x.shape))

    out_shape = [
        jax.ShapeDtypeStruct((3, block, share), F32),
        jax.ShapeDtypeStruct((share, block), F32),
        jax.ShapeDtypeStruct((2, quarter, width), BF),
        jax.ShapeDtypeStruct((2, asked, width), BF),
        jax.ShapeDtypeStruct((lines, 128), F32),
    ]
    anywhere = pl.BlockSpec(memory_space=pl.ANY)
    vmem = pltpu.VMEM
    dma = pltpu.SemaphoreType.DMA
    count = 6 + 2 * (ways * 4 + 3)
    return pl.pallas_call(
        kernel,
        out_shape=out_shape,
        in_specs=[anywhere] * 6 + [whole(head_bias), whole(inner_bias)],
        out_specs=[
            whole(out_shape[0]),
            whole(out_shape[1]),
            anywhere,
            anywhere,
            whole(out_shape[4]),
        ],
        scratch_shapes=[
            vmem((rows, width), BF),
            vmem((3, width, width), BF),
            vmem((3, rows, width), BF),
            vmem((rows, width), BF),
            vmem((rows, width), BF),
            vmem((rows, width), F32),
            vmem((rows, width), BF),
            vmem((ways, half, part), BF),
            vmem((ways, half, part), BF),
            vmem((ways, half, part), BF),
            vmem((ways, 2 * block, part), BF),
            vmem((ways, block, part), BF),
            vmem((ways - 1, block, part), BF),
            vmem((ways, share, half), BF),
            vmem((ways, share, half), BF),
            vmem((ways, share, half), BF),
            vmem((ways, share, 2 * block), BF),
            vmem((ways, share, block), BF),
            vmem((ways - 1, share, block), BF),
            vmem((3, ways, lines, 128), F32),
            vmem((4, ways, lines, 128), F32),
            vmem((ways - 1, lines, 128), F32),
            dma((count,)),
            dma((count,)),
            dma((8,)),
            dma((2, 2)),
            dma((2, 2)),
        ],
        compiler_params=pltpu.CompilerParams(
            collective_id=1, has_side_effects=True, vmem_limit_bytes=60 << 20
        ),
        name="last_sums",
    )(x, weights, pre, mixed, branch, resid, head_bias, inner_bias)


def attention_backward_kernel(
    qkv, far_kv, grad, cosine, sine, col_labels, row_labels,
    up, back, vectors, proj, y,
):
    rows, width = qkv.shape[1:]
    docs = far_kv.shape[1]
    pairs = width // 128
    block = docs
    asked = rows - docs
    ways = 4
    half, own_block = width // 2, width // 8
    share = up.shape[1] // ways
    count, piece = 2 * ways, share // 2
    assert pairs == 8

    def kernel(
        qkv_ref, far_ref, g_ref, c_ref, s_ref, lc_ref, lr_ref,
        up_ref, back_ref, vec_ref, proj_ref, y_ref,
        pre_ref, bias_ref, up_o, back_o, vec_o, proj_o, yd_ref, yq_ref,
        sums_own, sums_far, give, kept, got_kv,
        ua, u0, u1, u2, u3, ba, b0, b1, b2, b3, v_got, v_run, p_run, p_got,
        send_sem, recv_sem, local_sem, row_send, row_recv,
    ):
        h = pl.program_id(0)
        around = Around()
        send = Sender(send_sem, recv_sem)
        ups, backs = [None] * count, [None] * count
        for n in range(count - 1, -1, -1):
            span = pl.ds(n * piece, piece)
            dt, side = n // 2, n % 2
            step = {3: (1, 1), 2: (2, 2), 1: (1, 0), 0: None}[dt]
            ups[n] = MatrixSum(
                around, send, 0, False, ua.at[n], u0.at[n], u1.at[n], u2.at[n],
                [(up_ref.at[half:, span], u0.at[n])],
                [(up_ref.at[:half, span], ua.at[n])],
                [local_sem.at[n]],
                None if step is None else (step[0], u3.at[step[1], side]),
                [(u3.at[1, side], ups[n + 2].away)] if dt == 2 else [],
            )
            backs[n] = MatrixSum(
                around, send, 1, True, ba.at[n], b0.at[n], b1.at[n], b2.at[n],
                [(back_ref.at[span, half:], b0.at[n])],
                [(back_ref.at[span, :half], ba.at[n])],
                [local_sem.at[count + n]],
                None if step is None else (step[0], b3.at[step[1], side]),
                [(b3.at[1, side], backs[n + 2].away)] if dt == 2 else [],
            )
        couples = [(ups[n], backs[n]) for n in (6, 7, 4, 5, 2, 3, 0, 1)]
        small = SmallSum(around, send, v_got, v_run)
        mean_proj = ProjSum(around, send, proj_ref, p_run, p_got)
        gives = [send(give.at[n], got_kv.at[n], around.other(1)) for n in range(pairs)]
        home = RowMoves(around, False, yd_ref, yq_ref, y_ref, row_send, row_recv)
        lane = lax.broadcasted_iota(jnp.int32, (1, 128), 1)

        def finish(n):
            gives[n].wait_recv()
            at = pl.ds(n * 128, 128)
            for i in range(2):
                head = kept[n % 2, i, :docs, :] + got_kv[n, i].astype(F32)
                tail = kept[n % 2, i, docs:, :]
                if i == 0:
                    head = head * c_ref[:docs, :] - turned(head) * s_ref[:docs, :]
                    tail = tail * c_ref[docs:, :] - turned(tail) * s_ref[docs:, :]
                head, tail = head.astype(BF), tail.astype(BF)
                pre_ref[i + 1, :docs, at] = head
                pre_ref[i + 1, docs:, at] = tail
                total = jnp.sum(head.astype(F32), axis=0, keepdims=True)
                total = total + jnp.sum(tail.astype(F32), axis=0, keepdims=True)
                bias_ref[i + 1 : i + 2, at] = total

        for step in range(pairs):

            @pl.when(h == step)
            def _(step=step):
                if step == 0:
                    around.meet()
                    for p in range(8):
                        to = feature_block(around.rank, p) * own_block
                        at = pl.ds(pl.multiple_of(to, own_block), own_block)
                        v_run[0, :, at] = vec_ref[:, p * own_block : (p + 1) * own_block]
                    small.begin()
                    mean_proj.begin()
                    for n, many in ((0, 2), (2, 4), (4, 8)):
                        for couple in couples[n:many]:
                            for item in couple:
                                item.begin()
                        if n < 4:
                            for item in couples[n // 2]:
                                item.first_axis()
                    home.start()
                else:
                    firsts = {1: (2,), 2: (3, 4), 3: (5,), 4: (6,), 5: (7,)}
                    seconds = {1: (0,), 2: (1,), 3: (2,), 4: (3, 4), 5: (5,), 6: (6,), 7: (7,)}
                    tensors = {3: (0, 1), 4: (2,), 5: (3,), 6: (4,), 7: (5, 6)}
                    if step <= 5:
                        small.hop(step - 1)
                        mean_proj.hop(step - 1)
                    for n in seconds.get(step, ()):
                        for item in couples[n]:
                            item.second_axis()
                    for n in firsts.get(step, ()):
                        for item in couples[n]:
                            item.first_axis()
                    for n in tensors.get(step, ()):
                        for item in couples[n]:
                            item.tensor()
                    finish(step - 1)

        sums_own[...] = jnp.zeros_like(sums_own)
        sums_far[...] = jnp.zeros_like(sums_far)

        def part(start, size, keys, sames, sums):
            q_block = qkv_ref[0, pl.ds(start, size), :]
            g_block = g_ref[pl.ds(start, size), :]
            grads = []
            for head in range(2):
                mask = (lane // HEAD_WIDTH) == head
                q_head = jnp.where(mask, q_block, jnp.zeros_like(q_block))
                g_head = jnp.where(mask, g_block, jnp.zeros_like(g_block))
                scores = [
                    jnp.where(same, dot_nt(q_head, key), MASKED)
                    for (key, _), same in zip(keys, sames)
                ]
                top = functools.reduce(
                    jnp.maximum, [jnp.max(s, axis=-1, keepdims=True) for s in scores]
                )
                powers = [jnp.exp(s - top) for s in scores]
                total = functools.reduce(
                    jnp.add, [jnp.sum(p, axis=-1, keepdims=True) for p in powers]
                )
                inverse = 1.0 / total
                g_head = (g_head.astype(F32) * inverse).astype(BF)
                pulls = [dot_nt(g_head, value) for _, value in keys]
                mean = functools.reduce(
                    jnp.add,
                    [jnp.sum(p * d, axis=-1, keepdims=True) for p, d in zip(powers, pulls)],
                ) * inverse
                slopes = [(p * (d - mean)).astype(BF) for p, d in zip(powers, pulls)]
                got = functools.reduce(
                    jnp.add, [dot_nn(s, key) for s, (key, _) in zip(slopes, keys)]
                )
                grads.append(got * 0.125)
                for (ref, begin, many), s, p in zip(sums, slopes, powers):
                    ref[0, pl.ds(begin, many), :] += dot_tn(s, q_head)
                    ref[1, pl.ds(begin, many), :] += dot_tn(p.astype(BF), g_head)
            total = jnp.where(lane < HEAD_WIDTH, grads[0], grads[1])
            at = pl.ds(start, size)
            low = (total * c_ref[at, :] - turned(total) * s_ref[at, :]).astype(BF)
            pre_ref[0, at, pl.ds(pl.multiple_of(h * 128, 128), 128)] = low
            return jnp.sum(low.astype(F32), axis=0, keepdims=True)

        doc_keys = [
            (qkv_ref[1, :docs, :], qkv_ref[2, :docs, :]),
            (far_ref[0], far_ref[1]),
        ]
        bias = jnp.zeros((1, 128), F32)
        for at in range(docs // block):
            labels = lc_ref[pl.ds(at * block, block), :]
            bias = bias + part(
                at * block,
                block,
                doc_keys,
                [labels == lr_ref[0:1, :], labels == lr_ref[1:2, :]],
                [(sums_own, 0, docs), (sums_far, 0, docs)],
            )
        row = lax.broadcasted_iota(jnp.int32, (asked, asked), 0) // QLEN
        col = lax.broadcasted_iota(jnp.int32, (asked, asked), 1) // QLEN
        bias = bias + part(
            docs,
            asked,
            [(qkv_ref[1, docs:, :], qkv_ref[2, docs:, :])],
            [row == col],
            [(sums_own, docs, asked)],
        )
        bias_ref[0:1, pl.ds(pl.multiple_of(h * 128, 128), 128)] = bias
        side = h % 2
        kept[side] = sums_own[...]
        give[h] = sums_far[...].astype(BF)
        for step in range(pairs):

            @pl.when(h == step)
            def _(step=step):
                gives[step].start()

        @pl.when(h == pairs - 1)
        def _():
            finish(pairs - 1)
            for couple in couples[7:]:
                for item in couple:
                    item.tensor()
            for group, acc, came, o in ((ups, ua, u3, up_o), (backs, ba, b3, back_o)):
                for n in range(2):
                    group[n + 2].away.wait_recv()
                    group[n + 4].away.wait_recv()
                    at = pl.ds(n * piece, piece)
                    if acc is ua:
                        total = acc[n, :own_block, :].astype(F32)
                    else:
                        total = acc[n, :, :own_block].astype(F32)
                    total = total + came[0, n].astype(F32) + came[2, n].astype(F32)
                    if acc is ua:
                        o[:, at] = total
                    else:
                        o[at, :] = total
            vec_o[...] = v_run[5]
            proj_o[...] = mean_proj.result()
            home.wait()
            send.drain()

    def whole(shape):
        return pl.BlockSpec(shape, lambda h: (0,) * len(shape))

    anywhere = pl.BlockSpec(memory_space=pl.ANY)
    vmem = pltpu.VMEM
    dma = pltpu.SemaphoreType.DMA
    columns = proj.shape[1]
    out_shape = [
        jax.ShapeDtypeStruct((3, rows, width), BF),
        jax.ShapeDtypeStruct((8, width), F32),
        jax.ShapeDtypeStruct((own_block, share), F32),
        jax.ShapeDtypeStruct((share, own_block), F32),
        jax.ShapeDtypeStruct(vectors.shape, F32),
        jax.ShapeDtypeStruct((own_block, columns), F32),
    ]
    slots = 2 * (count * 4 + 6) + 5 + 5 + pairs
    return pl.pallas_call(
        kernel,
        grid=(pairs,),
        in_specs=[
            pl.BlockSpec((3, rows, 128), lambda h: (0, 0, h)),
            pl.BlockSpec((2, docs, 128), lambda h: (0, 0, h)),
            pl.BlockSpec((rows, 128), lambda h: (0, h)),
            whole((rows, 128)),
            whole((rows, 128)),
            whole((docs, 1)),
            whole((2, docs)),
            anywhere,
            anywhere,
            whole(vectors.shape),
            whole(proj.shape),
            anywhere,
        ],
        out_specs=[whole(x.shape) for x in out_shape] + [anywhere, anywhere],
        out_shape=out_shape
        + [
            jax.ShapeDtypeStruct((2, docs // 2, width), BF),
            jax.ShapeDtypeStruct((2, asked // 2, width), BF),
        ],
        scratch_shapes=[
            vmem((2, rows, 128), F32),
            vmem((2, docs, 128), F32),
            vmem((pairs, 2, docs, 128), BF),
            vmem((2, 2, rows, 128), F32),
            vmem((pairs, 2, docs, 128), BF),
            vmem((count, half, piece), BF),
            vmem((count, half, piece), BF),
            vmem((count, 2 * own_block, piece), BF),
            vmem((count, own_block, piece), BF),
            vmem((ways - 1, 2, own_block, piece), BF),
            vmem((count, piece, half), BF),
            vmem((count, piece, half), BF),
            vmem((count, piece, 2 * own_block), BF),
            vmem((count, piece, own_block), BF),
            vmem((ways - 1, 2, piece, own_block), BF),
            vmem((5,) + vectors.shape, F32),
            vmem((6,) + vectors.shape, F32),
            vmem((width, columns), F32),
            vmem((width + 2 * own_block, columns), F32),
            dma((slots,)),
            dma((slots,)),
            dma((2 * count,)),
            dma((2, 2)),
            dma((2, 2)),
        ],
        compiler_params=pltpu.CompilerParams(
            collective_id=2, has_side_effects=True, vmem_limit_bytes=60 << 20
        ),
        name="attend_backward_and_sum",
        cost_estimate=pl.CostEstimate(
            flops=100 * rows * 2 * docs * width,
            bytes_accessed=4 * (6 * rows + 4 * docs) * width,
            transcendentals=rows * 2 * docs * width // 64,
        ),
    )(
        qkv, far_kv, grad, cosine, sine, col_labels, row_labels,
        up, back, vectors, proj, y,
    )


def body(
    x_doc,
    x_query,
    doc_cot,
    query_cot,
    lengths,
    positives,
    w_qkv,
    b_qkv,
    w_out,
    b_out,
    gain_one,
    shift_one,
    w_in,
    b_in,
    w_back,
    b_back,
    gain_two,
    shift_two,
    w_proj,
):
    ways = lax.axis_size("tensor")
    groups = lax.axis_size("dp")
    column = lax.axis_index("tensor")
    rank = lax.axis_index("dp")
    core = rank % 2
    chip = rank // 2
    chips = groups // 2
    micro, quarter, width = x_doc.shape
    asked = x_query.shape[1]
    segments = lengths.shape[2] - 1
    proj_width = w_proj.shape[1]
    heads_local = w_qkv.shape[2]
    units_local = w_in.shape[1]
    block = width // groups
    assert ways == 2 * micro and ways == 4

    def exchange(value, dr=0, dt=0):
        pairs = [
            (r * ways + t, (r ^ dr) * ways + (t ^ dt)) for r in range(groups) for t in range(ways)
        ]
        return lax.ppermute(value, AXES, pairs)

    chip_bits = []
    bit = 2
    while bit < groups:
        chip_bits.append(bit)
        bit *= 2

    def gather_weights(pack, reverse):
        pieces = [pack] + [exchange(pack, dt=j) for j in range(1, ways)]
        pieces = [(0, jnp.concatenate(pieces, axis=-1))]
        order = chip_bits[::-1] if reverse and len(chip_bits) == 2 else chip_bits
        for dr in order:
            pieces = pieces + [(j + dr // 2, exchange(p, dr=dr)) for j, p in pieces]
            if len(pieces) >= 4 or dr == order[-1]:
                pieces.sort(key=lambda item: item[0])
                pieces = [(0, jnp.concatenate([p for _, p in pieces], axis=-2))]
        (_, half), = pieces
        return jnp.concatenate([half, exchange(half, dr=1)], axis=-2)

    def gather_proj(pack):
        for dr in chip_bits + [1]:
            pack = jnp.concatenate([pack, exchange(pack, dr=dr)], axis=0)
        return pack

    unit_micro = column // 2
    unit_row = chip * 2 + column % 2

    def rows_in(docs, queries):
        blocks = jnp.concatenate([docs, queries], axis=1)
        got = []
        for j in range(2):
            send = jnp.where((column + j) % 2 == 0, blocks[0], blocks[1])
            pairs = []
            for r in range(groups):
                for t in range(ways):
                    m = (t + j) % 2
                    pairs.append(
                        (r * ways + t, ((r // 2) * 2 + t // 2) * ways + 2 * m + r % 2)
                    )
            got.append(lax.ppermute(send, AXES, pairs))
        first = jnp.where(unit_micro == 0, got[0], got[1])
        second = jnp.where(unit_micro == 0, got[1], got[0])
        return jnp.concatenate(
            [first[:quarter], second[:quarter], first[quarter:], second[quarter:]], axis=0
        )

    def quarters_out(first, second):
        got = []
        for j in range(2):
            send = jnp.where((unit_micro + j) % 2 == 0, first, second)
            pairs = []
            for r in range(groups):
                for t in range(ways):
                    m = t // 2
                    pairs.append(
                        (
                            r * ways + t,
                            ((r // 2) * 2 + t % 2) * ways + 2 * (r % 2) + (m + j) % 2,
                        )
                    )
            got.append(lax.ppermute(send, AXES, pairs))
        even = jnp.where(column % 2 == 0, got[0], got[1])
        odd = jnp.where(column % 2 == 0, got[1], got[0])
        return jnp.stack([even, odd])

    def rows_out(values):
        docs = 2 * quarter
        first = jnp.concatenate([values[:quarter], values[docs : docs + asked]], axis=0)
        second = jnp.concatenate([values[quarter:docs], values[docs + asked :]], axis=0)
        blocks = quarters_out(first, second)
        return blocks[:, :quarter], blocks[:, quarter:]

    place = jnp.arange(width, dtype=jnp.int32)
    step = place // block
    actual = (rank ^ (2 * (step % chips) + step // chips)) * block + place % block
    turn = (place[:, None] == actual[None, :]).astype(BF)

    docs = 2 * quarter
    queries = 2 * asked
    rows = docs + queries
    sizes_all = lengths[unit_micro]
    sizes = sizes_all[unit_row]
    ends = jnp.cumsum(sizes[:-1])
    half = HEAD_WIDTH // 2
    rates = 10000.0 ** (-(2.0 * jnp.arange(half, dtype=F32)) / HEAD_WIDTH)
    own_picks = jnp.zeros((8, 128), jnp.int32).at[:micro, : positives.shape[1]].set(positives)
    params = [b_out, gain_one, shift_one, b_back, gain_two, shift_two]
    if chips == 4:
        (
            own_x, full_qkv, full_out, full_proj, picks_rel,
            bias_qkv, bias_in, cosine, sine, col_labels, row_labels, *cots, params,
        ) = gather_kernel(
            x_doc, x_query, w_qkv, w_out, w_proj, b_qkv, b_in[None], own_picks,
            doc_cot, query_cot, ends, jnp.tile(rates, 4)[None], params,
        )
        full_proj = full_proj.reshape(width, proj_width)
    else:
        own_x = rows_in(x_doc, x_query)
        own_cot = rows_in(doc_cot.astype(BF), query_cot.astype(BF))
        full_qkv = gather_weights(w_qkv, False)
        full_out = gather_weights(w_out.T, False).T
        full_in = gather_weights(w_in, False)
        full_back = gather_weights(w_back.T, False).T
        full_proj = gather_proj(w_proj)
        picks_rel = gather_proj(own_picks[None])
        bias_pack = jnp.concatenate([b_qkv.reshape(-1), b_in])
        biases = [bias_pack] + [exchange(bias_pack[None], dt=j)[0] for j in range(1, ways)]
        bias_qkv = jnp.concatenate(
            [b[: 3 * heads_local].reshape(3, heads_local) for b in biases], axis=1
        )
        bias_in = jnp.concatenate([b[3 * heads_local :] for b in biases])
        params = jnp.dot(
            jnp.stack(params + [b_out, b_out]), turn.astype(F32), precision=FULL_PRECISION
        )
        starts = jnp.concatenate([jnp.zeros((1,), jnp.int32), ends])

        def layout(first):
            index = first + jnp.arange(docs, dtype=jnp.int32)
            segment = jnp.sum((index[:, None] >= ends[None, :]).astype(jnp.int32), axis=1)
            labels = jnp.arange(starts.shape[0], dtype=jnp.int32)
            begin = jnp.sum(
                jnp.where(segment[:, None] == labels[None, :], starts[None, :], 0), axis=1
            )
            return segment, index - begin

        def rotation(places):
            angle = places.astype(F32)[:, None] * rates[None, :]
            turned_sine = jnp.sin(angle)
            return (
                jnp.tile(jnp.cos(angle), (1, 4)),
                jnp.concatenate([-turned_sine, turned_sine] * 2, axis=1),
            )

        own_labels, own_places = layout(core * docs)
        far_labels, far_places = layout((1 - core) * docs)
        own_places = jnp.concatenate([own_places, jnp.arange(queries, dtype=jnp.int32) % QLEN])
        cosine, sine = rotation(own_places)
        far_cosine, far_sine = rotation(far_places)
        label_args = (own_labels[:, None], own_labels[None, :], far_labels[None, :])
    picks_rel = picks_rel[:, :micro, : positives.shape[1]].astype(F32)
    b_out, gain_one, shift_one, b_back, gain_two, shift_two = [params[n] for n in range(6)]

    if chips == 4:
        x_low = own_x
        qkv, far_kv, mixed, resid_one, normed, normed_low, own_cot, full_in, full_back = (
            project_and_attend(
                own_x, full_qkv, bias_qkv, cosine, sine, col_labels, row_labels, full_out, params,
                *cots, w_in, w_back,
            )
        )
        active_low, active_slope, resid_two, output_low, projection = feed_forward(
            normed_low, full_in, bias_in, full_back, normed, params, full_proj
        )
        y_low = output_low
    else:
        x_low = dot_nn(own_x, turn).astype(BF)
        qkv = project_heads(
            x_low,
            full_qkv,
            bias_qkv,
            jnp.stack([cosine * 0.125, cosine, jnp.ones_like(cosine)]),
            jnp.stack([sine * 0.125, sine, jnp.zeros_like(sine)]),
        )
        far_kv = exchange(qkv[1:, :docs], dr=1)
        mixed = attention_forward(qkv, far_kv, *label_args)
        resid_one = x_low.astype(F32) + dot_nn(mixed, full_out) + b_out
        normed, norm_one_pull = jax.vjp(layer_norm, resid_one, gain_one, shift_one)
        normed_low = normed.astype(BF)
        inner = dot_nn(normed_low, full_in) + bias_in
        active, gelu_pull = jax.vjp(gelu_exact, inner)
        active_low = active.astype(BF)
        resid_two = normed + dot_nn(active_low, full_back) + b_back
        output, norm_two_pull = jax.vjp(layer_norm, resid_two, gain_two, shift_two)
        output_low = output.astype(BF)
        y_low = dot_nt(output_low, turn).astype(BF)
        projection = dot_nn(output_low, full_proj)
    held = jnp.arange(groups, dtype=jnp.int32)
    held = rank ^ (2 * (held % chips) + held // chips)
    order = (jnp.arange(groups, dtype=jnp.int32)[:, None] == held[None, :]).astype(F32)
    picks = jnp.where(unit_micro == 0, picks_rel[:, 0], picks_rel[:, 1])
    picks = jnp.dot(order, picks, precision=FULL_PRECISION).astype(jnp.int32).reshape(-1)
    counts = sizes_all[:, :segments].reshape(-1).astype(F32)

    if chips == 4:
        log_counts = jnp.pad(
            jnp.log(counts).reshape(-1, segments), ((0, 0), (0, 8 - segments))
        ).reshape(-1, 1)
        proj_low, loss_out = loss_kernel(
            projection, col_labels, log_counts, jnp.repeat(picks, QLEN)[None]
        )
        loss_out = loss_out[:, : asked // QLEN, 0]
    else:
        y_doc, y_query = rows_out(y_low)
        unit, unit_pull = jax.vjp(normalize, projection)
        unit_low = unit.astype(BF)

        doc_unit = unit_low[:docs]
        query_unit = unit_low[docs:]

        def bit_of(dr, dt):
            return (rank // dr) % 2 == 1 if dr else (column // dt) % 2 == 1

        def join(value, dr, dt, axis=0):
            got = exchange(value, dr=dr, dt=dt)
            on = bit_of(dr, dt)
            low = jnp.where(on, got, value)
            high = jnp.where(on, value, got)
            return jnp.concatenate([low, high], axis=axis)

        def split_sum(value, dr, dt):
            on = bit_of(dr, dt)
            size = value.shape[0] // 2
            send = jnp.where(on, value[:size], value[size:])
            keep = jnp.where(on, value[size:], value[:size])
            return keep + exchange(send.astype(BF), dr=dr, dt=dt).astype(F32)

        steps = [(1, 0), (0, 1)] + [(dr, 0) for dr in chip_bits]
        all_queries = query_unit
        for dr, dt in steps:
            all_queries = join(all_queries, dr, dt)
        seg_labels = jnp.arange(segments, dtype=jnp.int32)
        member = (own_labels[:, None] == seg_labels[None, :]).astype(F32)
        cosines = dot_nt(doc_unit, all_queries)
        weight = jnp.exp(TAU * (cosines - 1.0))
        totals = jnp.einsum("js,ji->si", member, weight, precision=FULL_PRECISION)
        totals = totals + exchange(totals, dr=1)
        for dr, dt in steps[1:]:
            totals = join(totals, dr, dt)
        best = (jnp.log(totals) - jnp.log(counts)[:, None]) / TAU + 1.0
        score = jnp.sum(best.reshape(best.shape[0], -1, QLEN), axis=-1)
        logits = LOGIT_SCALE * score
        documents = jnp.arange(logits.shape[0], dtype=jnp.int32)
        chosen = (documents[:, None] == picks[None, :]).astype(F32)
        peak = jnp.max(logits, axis=0, keepdims=True)
        powers = jnp.exp(logits - peak)
        mass = jnp.sum(powers, axis=0, keepdims=True)
        losses = (peak + jnp.log(mass))[0] - jnp.sum(chosen * logits, axis=0)
        logit_grad = LOGIT_SCALE * (powers / mass - chosen)
        own_grad = lax.dynamic_slice_in_dim(logit_grad, unit_row * segments, segments, axis=0)
        own_total = lax.dynamic_slice_in_dim(totals, unit_row * segments, segments, axis=0)
        coef = jnp.repeat(own_grad, QLEN, axis=1) / own_total
        spread = jnp.einsum("js,si->ji", member, coef, precision=FULL_PRECISION)
        cosine_grad = (weight * spread).astype(BF)
        doc_grad = dot_nn(cosine_grad, all_queries)
        query_grad = dot_tn(cosine_grad, doc_unit)
        for dr, dt in steps[::-1]:
            query_grad = split_sum(query_grad, dr, dt)
        own_losses = lax.dynamic_slice_in_dim(losses, unit_row * (4 * asked // QLEN) + core * 2 * (asked // QLEN), 2 * (asked // QLEN))
        per = asked // QLEN
        loss_tiles = [
            jnp.broadcast_to(own_losses[i * per : (i + 1) * per, None], (per, 128)) for i in range(2)
        ]
        loss_out = quarters_out(loss_tiles[0], loss_tiles[1])[:, :, 0]

        unit_grad = jnp.concatenate([doc_grad, query_grad], axis=0)
        (proj_grad,) = unit_pull(unit_grad)
        proj_low = proj_grad.astype(BF)

    class Reduction:
        def __init__(self, half, axis, reverse, last):
            self.bits = chip_bits if reverse and len(chip_bits) == 2 else chip_bits[::-1]
            self.left = sorted(chip_bits)
            self.axis, self.last = axis, last
            self.sends = [half(1).astype(BF)]
            self.hops = [(1, 0)]
            self.kept = lambda: half(0)
            self.stage = 0

        def advance(self):
            total = self.kept()
            for s, (dr, dt) in zip(self.sends, self.hops):
                got = exchange(s, dr=dr, dt=dt).astype(F32)
                total = got if total is None else total + got
            if self.stage == len(self.bits) + 1:
                return total
            if self.stage < len(self.bits):
                dr = self.bits[self.stage]
                at = self.left.index(dr)
                self.left.remove(dr)
                size = block << at
                stay, send = [
                    jnp.concatenate(
                        [
                            lax.slice_in_dim(total, b, b + size, axis=self.axis)
                            for b in range(side * size, total.shape[self.axis], 2 * size)
                        ],
                        axis=self.axis,
                    )
                    for side in (0, 1)
                ]
                self.sends = [send.astype(BF)]
                self.hops = [(dr, 0)]
            else:
                stay, sends = self.last(total)
                self.sends = [piece.astype(BF) for _, piece in sends]
                self.hops = [(0, dt) for dt, _ in sends]
            self.kept = lambda: stay
            self.stage += 1
            return None

        def finish(self):
            total = None
            while total is None:
                total = self.advance()
            return total

    def weight_sum(left, right, axis, reverse):
        size = width // 2

        def half(n):
            if axis == 0:
                return dot_tn(left[:, n * size : (n + 1) * size], right)
            return dot_tn(left, right[:, n * size : (n + 1) * size])

        def last(total):
            size = total.shape[1 - axis] // ways
            pieces = [
                lax.slice_in_dim(total, j * size, (j + 1) * size, axis=1 - axis)
                for j in range(ways)
            ]
            return pieces[0], [(j, pieces[j]) for j in range(1, ways)]

        return Reduction(half, axis, reverse, last)

    def after(value, reductions):
        sends = [r.sends for r in reductions]
        value, sends = lax.optimization_barrier((value, sends))
        for r, s in zip(reductions, sends):
            r.sends = s
        return value

    whole_path = chips == 4
    if whole_path:
        (
            resid_one_grad, branch_low, mixed_grad, in_grad, back_grad, inner_bias, grad_proj, vectors,
        ) = feed_forward_backward(
            own_cot, proj_low, full_proj, resid_two, output_low, params, full_back, active_slope,
            full_in, normed_low, active_low, resid_one, full_out,
        )
    else:
        out_grad = dot_nn(own_cot, turn) + dot_nt(proj_low, full_proj)
        resid_two_grad, gain_two_grad, shift_two_grad = norm_two_pull(out_grad)
        update_low = resid_two_grad.astype(BF)
        sum_back = weight_sum(active_low, update_low, 1, True)
        (inner_grad,) = gelu_pull(dot_nt(update_low, full_back))
        inner_low = inner_grad.astype(BF)
        sum_in = weight_sum(normed_low, inner_low, 0, False)
        inner_bias = jnp.sum(inner_low.astype(F32), axis=0)
        normed_grad = dot_nt(inner_low, full_in) + resid_two_grad
        resid_one_grad, gain_one_grad, shift_one_grad = norm_one_pull(normed_grad)
        branch_low = resid_one_grad.astype(BF)
        mixed_grad = dot_nt(branch_low, full_out).astype(BF)
        grad_proj = dot_tn(output_low, proj_low)
        zero = jnp.zeros((width,), F32)
        vectors = jnp.stack(
            [
                jnp.sum(branch_low.astype(F32), axis=0),
                gain_one_grad,
                shift_one_grad,
                jnp.sum(update_low.astype(F32), axis=0),
                gain_two_grad,
                shift_two_grad,
                zero,
                zero,
            ]
        )
        vectors = lax.dot_general(
            vectors, turn.astype(F32), (((1,), (1,)), ((), ())), precision=FULL_PRECISION
        )

    def heads_sum(rights, first_block, blocks, reverse):
        size = width // 2
        many = rights.shape[1] // 3 // blocks

        def half(n):
            return dot_tn(x_low[:, n * size : (n + 1) * size], rights)

        def last(total):
            stay, sends = None, []
            for b in range(blocks):
                piece = jnp.stack(
                    [total[:, (j * blocks + b) * many : (j * blocks + b + 1) * many] for j in range(3)]
                )
                if first_block + b == 0:
                    stay = piece
                else:
                    sends.append((first_block + b, piece))
            return stay, sends

        return Reduction(half, 0, reverse, last)

    if whole_path:
        pre, head_bias, out_in, out_back, vectors, grad_proj, y_doc, y_query = (
            attention_backward_kernel(
                qkv,
                far_kv,
                mixed_grad,
                cosine,
                sine,
                col_labels,
                row_labels,
                in_grad,
                back_grad,
                vectors,
                grad_proj,
                y_low,
            )
        )
    else:
        head_sums, head_rights = [], []
        running = [sum_back, sum_in]
        per_block = heads_local // 128
        sum_out = weight_sum(mixed, branch_low, 1, False)
        for first_block, blocks in ((0, 2), (2, 1), (3, 1)):
            for item in running:
                item.advance()
            mixed_grad = after(mixed_grad, running)
            dq, own_grads, give = attention_backward(
                first_block * per_block,
                blocks * per_block,
                qkv,
                far_kv,
                mixed_grad,
                cosine,
                sine,
                far_cosine,
                far_sine,
                *label_args,
            )
            got = exchange(give, dr=1).astype(F32)
            rights = [dq] + [
                jnp.concatenate(
                    [own_grads[i, :docs] + got[i], own_grads[i, docs:]], axis=0
                ).astype(BF)
                for i in range(2)
            ]
            head_rights.append(rights)
            head_sums.append(
                heads_sum(jnp.concatenate(rights, axis=1), first_block, blocks, first_block > 0)
            )
        out_back = sum_back.finish()
        out_in = sum_in.finish()
        pre = [jnp.concatenate([part[j] for part in head_rights], axis=1) for j in range(3)]
        head_bias = jnp.stack([jnp.sum(p.astype(F32), axis=0) for p in pre])
        head_bias = head_bias.reshape(3, ways, heads_local)
    if whole_path:
        out_qkv, out_out, gx_doc, gx_query, tensor_grads = finish_kernel(
            x_low,
            full_qkv,
            pre,
            mixed,
            branch_low,
            resid_one_grad,
            head_bias,
            inner_bias,
        )
        y_doc, y_query, gx_doc, gx_query, out_qkv, out_out, out_in, out_back, grad_proj = emit_kernel(
            [y_doc, y_query, gx_doc, gx_query, out_qkv, out_out, out_in, out_back, grad_proj],
            [BF, BF] + [F32] * 7,
        )
        tensor_grads = tensor_grads[: (3 * heads_local + units_local) // 128].reshape(-1)
    else:
        tensor_grads = jnp.concatenate(
            [
                jnp.swapaxes(head_bias, 0, 1).reshape(ways, 3 * heads_local),
                inner_bias.reshape(ways, units_local),
            ],
            axis=1,
        )
        x_grad = resid_one_grad
        for j in range(3):
            x_grad = x_grad + dot_nt(pre[j], full_qkv[j])
        x_grad = dot_nt(x_grad.astype(BF), turn).astype(BF)
        gx_doc, gx_query = rows_out(x_grad)
        gx_doc, gx_query = gx_doc.astype(F32), gx_query.astype(F32)
        out_out = sum_out.finish()
        out_qkv = functools.reduce(jnp.add, [item.finish() for item in head_sums])
        for dr in [1] + chip_bits[::-1]:
            size = grad_proj.shape[0] // 2
            got = exchange(grad_proj[size:].astype(BF), dr=dr)
            grad_proj = grad_proj[:size] + got.astype(F32)
        for dt in (1, 2):
            grad_proj = grad_proj + exchange(grad_proj, dt=dt)
        for dt in (2, 1):
            tensor_grads = tensor_grads[:dt] + exchange(tensor_grads[dt:], dt=dt)
            vectors = vectors + exchange(vectors, dt=dt)
        for dr in [1] + chip_bits:
            tensor_grads = tensor_grads + exchange(tensor_grads, dr=dr)
            vectors = vectors + exchange(vectors, dr=dr)
        tensor_grads = tensor_grads[0]
    return (
        y_doc,
        y_query,
        loss_out,
        gx_doc,
        gx_query,
        out_qkv,
        tensor_grads[: 3 * heads_local].reshape(3, heads_local),
        out_out,
        vectors[0],
        vectors[1],
        vectors[2],
        out_in,
        tensor_grads[3 * heads_local :],
        out_back,
        vectors[3],
        vectors[4],
        vectors[5],
        grad_proj,
    )


def solution(mesh):
    rows = P(None, ("dp", "tensor"), None)
    in_specs = (
        rows,
        rows,
        rows,
        rows,
        P(),
        P(None, "dp"),
        P(None, "dp", "tensor"),
        P(None, "tensor"),
        P("tensor", "dp"),
        P(),
        P(),
        P(),
        P("dp", "tensor"),
        P("tensor"),
        P("tensor", "dp"),
        P(),
        P(),
        P(),
        P("dp", None),
    )
    out_specs = (
        rows,
        rows,
        P(None, ("dp", "tensor")),
        rows,
        rows,
        P(None, "dp", "tensor"),
        P(None, "tensor"),
        P("tensor", "dp"),
        P(),
        P(),
        P(),
        P("dp", "tensor"),
        P("tensor"),
        P("tensor", "dp"),
        P(),
        P(),
        P(),
        P("dp", None),
    )
    return jax.shard_map(body, mesh=mesh, in_specs=in_specs, out_specs=out_specs, check_vma=False)
```
